32 devices in a mesh: fsdp: 8 (over y, x, core), tensor: 4 (over z).
Axes of the slice: x: 2, y: 2, z: 4, core: 2. Of those that a mesh axis runs over, the one named last changes fastest.
Arguments:
- tokens: bfloat16 [8192, 2048], P(('fsdp', 'tensor')), may hold values from -6 to 6
- segments: int32 [8, 1024], P('fsdp'), may hold values from 0 to 23, never falling along the last dimension, each value on 1 to 256 neighbouring positions
- routes: int32 [8192, 8], P(('fsdp', 'tensor')), may hold values from 0 to 31, all different within a row; in each aligned block of 256 rows (0 to 255, 256 to 511, ...) at most 80 rows name the same one
- adapter_index: int32 [8], replicated, may hold values from 0 to 7
- cotangent: bfloat16 [8192, 2048], P(('fsdp', 'tensor')), may hold values from -6 to 6
- attn_gain: bfloat16 [2048], replicated, may hold values from 0.25 to 1.75
- moe_gain: bfloat16 [2048], replicated, may hold values from 0.25 to 1.75
- q_gain: bfloat16 [128], replicated, may hold values from 0.25 to 1.75
- key_norm_gain: bfloat16 [128], replicated, may hold values from 0.25 to 1.75
- w_query: bfloat16 [2048, 4096], P('fsdp', 'tensor'), may hold values from -0.125 to 0.125
- key_projection_weight: bfloat16 [2048, 512], P('fsdp', 'tensor'), may hold values from -0.125 to 0.125
- value_projection_weight: bfloat16 [2048, 512], P('fsdp', 'tensor'), may hold values from -0.125 to 0.125
- w_out: bfloat16 [4096, 2048], P('tensor', 'fsdp'), may hold values from -0.25 to 0.25
- w_router: bfloat16 [2048, 32], P('fsdp'), may hold values from -0.0625 to 0.0625
- expert_gate_weight: bfloat16 [32, 2048, 768], P(('fsdp', 'tensor')), may hold values from -0.125 to 0.125
- expert_up_weight: bfloat16 [32, 2048, 768], P(('fsdp', 'tensor')), may hold values from -0.125 to 0.125
- expert_down_weight: bfloat16 [32, 768, 2048], P(('fsdp', 'tensor')), may hold values from -1 to 1
- query_in: bfloat16 [8, 2048, 16], replicated, may hold values from -0.125 to 0.125
- query_out: bfloat16 [8, 16, 4096], P(None, None, 'tensor'), may hold values from -0.5 to 0.5
- key_in: bfloat16 [8, 2048, 16], replicated, may hold values from -0.125 to 0.125
- key_second_weight: bfloat16 [8, 16, 512], P(None, None, 'tensor'), may hold values from -0.5 to 0.5
- value_in: bfloat16 [8, 2048, 16], replicated, may hold values from -0.125 to 0.125
- value_second_weight: bfloat16 [8, 16, 512], P(None, None, 'tensor'), may hold values from -0.5 to 0.5
- attn_in: bfloat16 [8, 4096, 16], P(None, 'tensor'), may hold values from -0.09375 to 0.09375
- attn_out: bfloat16 [8, 16, 2048], replicated, may hold values from -1.5 to 1.5
- router_in: bfloat16 [8, 2048, 16], replicated, may hold values from -0.125 to 0.125
- router_out: bfloat16 [8, 16, 32], replicated, may hold values from -0.25 to 0.25
- gate_in: bfloat16 [32, 8, 2048, 16], P(('fsdp', 'tensor')), may hold values from -0.125 to 0.125
- gate_out: bfloat16 [32, 8, 16, 768], P(('fsdp', 'tensor')), may hold values from -0.5 to 0.5
- upward_in: bfloat16 [32, 8, 2048, 16], P(('fsdp', 'tensor')), may hold values from -0.125 to 0.125
- upward_out: bfloat16 [32, 8, 16, 768], P(('fsdp', 'tensor')), may hold values from -0.5 to 0.5
- downward_in: bfloat16 [32, 8, 768, 16], P(('fsdp', 'tensor')), may hold values from -0.21875 to 0.21875
- downward_out: bfloat16 [32, 8, 16, 2048], P(('fsdp', 'tensor')), may hold values from -2.5 to 2.5
Outputs:
- output: bfloat16 [8192, 2048], P(('fsdp', 'tensor'))
- input_grad: float32 [8192, 2048], P(('fsdp', 'tensor'))
- grad_query_in: float32 [8, 2048, 16], P(None, ('fsdp', 'tensor'))
- grad_query_out: float32 [8, 16, 4096], P(None, None, ('fsdp', 'tensor'))
- grad_key_in: float32 [8, 2048, 16], P(None, ('fsdp', 'tensor'))
- grad_key_out: float32 [8, 16, 512], P(None, None, ('fsdp', 'tensor'))
- grad_value_in: float32 [8, 2048, 16], P(None, ('fsdp', 'tensor'))
- grad_value_out: float32 [8, 16, 512], P(None, None, ('fsdp', 'tensor'))
- grad_attn_in: float32 [8, 4096, 16], P(None, ('fsdp', 'tensor'))
- grad_attn_out: float32 [8, 16, 2048], P(None, None, ('fsdp', 'tensor'))
- grad_router_in: float32 [8, 2048, 16], P(None, ('fsdp', 'tensor'))
- grad_router_out: float32 [8, 16, 32], P(None, None, ('fsdp', 'tensor'))
- grad_gate_in: float32 [32, 8, 2048, 16], P(('fsdp', 'tensor'))
- grad_gate_out: float32 [32, 8, 16, 768], P(('fsdp', 'tensor'))
- grad_upward_in: float32 [32, 8, 2048, 16], P(('fsdp', 'tensor'))
- grad_upward_out: float32 [32, 8, 16, 768], P(('fsdp', 'tensor'))
- grad_downward_in: float32 [32, 8, 768, 16], P(('fsdp', 'tensor'))
- grad_downward_out: float32 [32, 8, 16, 2048], P(('fsdp', 'tensor'))
The draws below stay inside these ranges and needn't reach their ends.
Inputs may be any that keep to these rules, and one draw needn't show every extreme that they name: `routes`: every row names 8 different experts; among the rows of one device no expert is named more than 80 times, a bound that some block reaches. `segments`: along each sequence segment numbers never fall; segment 0 is padding; every segment holds 1 to 256 positions and one holds exactly that many.
All inputs are finite; a program needn't handle non-finite values.
Results may differ from the reference program's by a relative error of at most 0.025.
Values may be sent and summed in bfloat16 or wider, within the bound.
A program may use at most 448 MiB of HBM per device.

```python
import math
import jax
import jax.numpy as jnp
import numpy as np
from jax import lax

MODEL_DIM = 2048
QUERY_HEADS = 32
KEY_VALUE_HEADS = 4
HEAD_SIZE = 128
FF = 768
TOPK = 8
ADAPTER_RANK = 16
ADAPTER_CHOICES = 8
TOK_DEV = 256
SEQ = 1024
TOKENS = 8192
EXPERTS = 32
CAP = 80
N_FSDP = 8
N_TENSOR = 4


def place_ends(values, key, smallest, high):
    longest = values.shape.index(max(values.shape))
    spots = []
    for shift in (0, 1):
        where = [jax.random.randint(jax.random.fold_in(key, axis), (), 0, length) for axis, length in enumerate(values.shape)]
        where[longest] = (where[longest] + shift) % values.shape[longest]
        spots.append(tuple(where))
    return values.at[spots[0]].set(smallest).at[spots[1]].set(high)


def block_scale(key, dims, split, least, largest):
    gain = 1.0
    for axis_at, shards_of in split:
        steps = jax.random.uniform(jax.random.fold_in(jax.random.fold_in(key, 6), axis_at), (shards_of,), jnp.float32, least / len(split), largest / len(split))
        gain = gain * jnp.repeat(jnp.exp(steps), dims[axis_at] // shards_of).reshape((-1,) + (1,) * (len(dims) - 1 - axis_at))
    return gain


def profile(count, total, bound, lean):
    portions = [(1 << 20) // math.isqrt(grade ** lean) + 1 for grade in range(2, count + 1)]
    surplus, counts = total - bound - (count - 1), [1] * (count - 1)
    while surplus > 0:
        free = [i for i in range(count - 1) if counts[i] < bound]
        whole, remaining = sum([portions[i] for i in free]), surplus
        for i in free:
            extra = min(bound - counts[i], max(1, remaining * portions[i] // whole), surplus)
            counts[i] = counts[i] + extra
            surplus = surplus - extra
    return np.array([bound] + counts)


def uneven(own_key, amount, total, bound, skew):
    if amount == 2:
        one = jax.random.randint(own_key, (), max(1, total - bound), min(bound, total - 1) + 1)
        return jnp.stack([one, total - one])
    sizes = jnp.asarray(profile(amount, total, bound, skew), jnp.int32)
    pairs = (amount - 1) // 2
    donor, sink = sizes[1:1 + 2 * pairs:2], sizes[2:2 + 2 * pairs:2]
    margin = jnp.minimum(donor - 1, bound - sink)
    passed = jax.random.randint(jax.random.fold_in(own_key, 1), (pairs,), 0, 1 << 20) % (margin + 1)
    sizes = sizes.at[1:1 + 2 * pairs:2].set(donor - passed).at[2:2 + 2 * pairs:2].set(sink + passed)
    return sizes[jax.random.permutation(jax.random.fold_in(own_key, 2), amount)]


def assign_block(stream_key, own, number, rows, count, top, reach, skew):
    sequence = jax.random.permutation(stream_key, count)
    packed, usual = portions_of(count, rows * top, reach, skew, True), portions_of(count, rows * top, reach, skew, False)
    places = jnp.arange(count)

    def named(lengths, rotation):
        used = int((lengths > 0).sum())
        fixed = max(1, used // 4)
        shifted = fixed + (places - fixed + rotation * (used - fixed)) % max(1, count - fixed)
        return jnp.zeros((count,), jnp.int32).at[sequence[jnp.where(places < fixed, places, shifted)]].set(jnp.asarray(lengths, jnp.int32))

    lengths = jnp.where(number % 4 == 0, named(packed, number // 4), named(usual, number - number // 4 - 1))
    mixed = jax.random.permutation(jax.random.fold_in(own, 3), count)
    source_of, sink = mixed[0:count // 2 * 2:2], mixed[1:count // 2 * 2:2]
    room = jnp.minimum(lengths[source_of] - 1, reach - lengths[sink]) // 2
    room = jnp.where((source_of == sequence[0]) | (sink == sequence[0]) | (lengths[sink] == 0), 0, jnp.maximum(room, 0))
    shifted = jax.random.randint(jax.random.fold_in(own, 4), (count // 2,), 0, 1 << 20) % (room + 1)
    lengths = lengths.at[source_of].add(-shifted).at[sink].add(shifted)
    labels = jnp.searchsorted(jnp.cumsum(lengths), jnp.arange(rows * top), side="right").astype(jnp.int32)
    grid = labels.reshape(top, rows).T
    grid = grid[jax.random.permutation(jax.random.fold_in(own, 1), rows)]
    rotation = jax.random.randint(jax.random.fold_in(own, 2), (rows, 1), 0, top)
    return jnp.take_along_axis(grid, (jnp.arange(top)[None, :] + rotation) % top, axis=1)


def portions_of(count, total, limit, skew, full):
    weights = [(1 << 20) // math.isqrt(grade ** skew) + 1 for grade in range(1, count + 1)]
    largest = limit if full else min(limit, max(-(-total // count), total * weights[0] // sum(weights)))
    least = 1 if total - largest >= count - 1 else 0
    given, surplus = [largest] + [least] * (count - 1), total - largest - least * (count - 1)
    while surplus > 0:
        movable = [i for i in range(1, count) if given[i] < largest] or [i for i in range(1, count) if given[i] < limit]
        pool, budget = sum([weights[i] for i in movable]), surplus
        for i in movable:
            more = min(limit - given[i], max(1, budget * weights[i] // pool), surplus)
            given[i] = given[i] + more
            surplus = surplus - more
    return np.array(given)


def normal_values(own_key, dims, width, reach, pieces=(), held_as=jnp.bfloat16):
    factor_of = block_scale(own_key, dims, pieces, -0.22, 0.18) if pieces else 1.0
    values = jax.random.normal(own_key, dims, jnp.float32) * width * factor_of
    return jnp.minimum(jnp.maximum(values, -reach), reach).astype(held_as)


def setup_inputs(seed: int = 0) -> dict:
    arg_keys = jax.random.split(jax.random.key(seed), 34)
    tokens = normal_values(arg_keys[0], (TOKENS, MODEL_DIM), 1.0, 6.0, ((0, 32),))
    segments = jax.vmap(lambda own: jnp.searchsorted(jnp.cumsum(uneven(own, 24, SEQ, SEQ // 4, 2)), jnp.arange(SEQ), side="right"))(jax.random.split(arg_keys[1], N_FSDP)).reshape((N_FSDP, SEQ)).astype(jnp.int32)
    routes_keys = jax.random.split(jax.random.fold_in(arg_keys[2], 1), TOKENS // TOK_DEV)
    routes_turns = jax.random.permutation(jax.random.fold_in(arg_keys[2], 3), TOKENS // TOK_DEV)
    routes = jax.vmap(lambda own, number: assign_block(jax.random.fold_in(arg_keys[2], 2), own, number, TOK_DEV, EXPERTS, TOPK, CAP, 2))(routes_keys, routes_turns).reshape((TOKENS, TOPK))
    adapter_index = place_ends(jax.random.randint(arg_keys[3], (N_FSDP,), 0, ADAPTER_CHOICES), jax.random.fold_in(arg_keys[3], 1), 0, ADAPTER_CHOICES - 1).astype(jnp.int32)
    cotangent = normal_values(arg_keys[4], (TOKENS, MODEL_DIM), 1.0, 6.0, ((0, 32),))
    attn_gain = jnp.clip(1.0 + 0.15 * jax.random.normal(arg_keys[5], (MODEL_DIM,), jnp.float32), 0.25, 1.75).astype(jnp.bfloat16)
    moe_gain = jnp.clip(1.0 + 0.15 * jax.random.normal(arg_keys[6], (MODEL_DIM,), jnp.float32), 0.25, 1.75).astype(jnp.bfloat16)
    q_gain = jnp.clip(1.0 + 0.15 * jax.random.normal(arg_keys[7], (HEAD_SIZE,), jnp.float32), 0.25, 1.75).astype(jnp.bfloat16)
    key_norm_gain = jnp.clip(1.0 + 0.15 * jax.random.normal(arg_keys[8], (HEAD_SIZE,), jnp.float32), 0.25, 1.75).astype(jnp.bfloat16)
    w_query = normal_values(arg_keys[9], (MODEL_DIM, QUERY_HEADS * HEAD_SIZE), MODEL_DIM ** -0.5, 0.125, ((0, 8), (1, 4)))
    key_projection_weight = normal_values(arg_keys[10], (MODEL_DIM, KEY_VALUE_HEADS * HEAD_SIZE), MODEL_DIM ** -0.5, 0.125, ((0, 8), (1, 4)))
    value_projection_weight = normal_values(arg_keys[11], (MODEL_DIM, KEY_VALUE_HEADS * HEAD_SIZE), MODEL_DIM ** -0.5, 0.125, ((0, 8), (1, 4)))
    w_out = normal_values(arg_keys[12], (QUERY_HEADS * HEAD_SIZE, MODEL_DIM), (QUERY_HEADS * HEAD_SIZE // 8) ** -0.5, 0.25, ((0, 4), (1, 8)))
    w_router = normal_values(arg_keys[13], (MODEL_DIM, EXPERTS), (4 * MODEL_DIM) ** -0.5, 0.0625, ((0, 8),))
    expert_gate_weight = normal_values(arg_keys[14], (EXPERTS, MODEL_DIM, FF), MODEL_DIM ** -0.5, 0.125, ((0, 32),))
    expert_up_weight = normal_values(arg_keys[15], (EXPERTS, MODEL_DIM, FF), MODEL_DIM ** -0.5, 0.125, ((0, 32),))
    expert_down_weight = normal_values(arg_keys[16], (EXPERTS, FF, MODEL_DIM), (FF // 24) ** -0.5, 1.0, ((0, 32),))
    query_in = normal_values(arg_keys[17], (ADAPTER_CHOICES, MODEL_DIM, ADAPTER_RANK), MODEL_DIM ** -0.5, 0.125)
    query_out = normal_values(arg_keys[18], (ADAPTER_CHOICES, ADAPTER_RANK, QUERY_HEADS * HEAD_SIZE), 0.08, 0.5, ((2, 4),))
    key_in = normal_values(arg_keys[19], (ADAPTER_CHOICES, MODEL_DIM, ADAPTER_RANK), MODEL_DIM ** -0.5, 0.125)
    key_second_weight = normal_values(arg_keys[20], (ADAPTER_CHOICES, ADAPTER_RANK, KEY_VALUE_HEADS * HEAD_SIZE), 0.08, 0.5, ((2, 4),))
    value_in = normal_values(arg_keys[21], (ADAPTER_CHOICES, MODEL_DIM, ADAPTER_RANK), MODEL_DIM ** -0.5, 0.125)
    value_second_weight = normal_values(arg_keys[22], (ADAPTER_CHOICES, ADAPTER_RANK, KEY_VALUE_HEADS * HEAD_SIZE), 0.08, 0.5, ((2, 4),))
    attn_in = normal_values(arg_keys[23], (ADAPTER_CHOICES, QUERY_HEADS * HEAD_SIZE, ADAPTER_RANK), (QUERY_HEADS * HEAD_SIZE) ** -0.5, 0.09375, ((1, 4),))
    attn_out = normal_values(arg_keys[24], (ADAPTER_CHOICES, ADAPTER_RANK, MODEL_DIM), 0.25, 1.5)
    router_in = normal_values(arg_keys[25], (ADAPTER_CHOICES, MODEL_DIM, ADAPTER_RANK), MODEL_DIM ** -0.5, 0.125)
    router_out = normal_values(arg_keys[26], (ADAPTER_CHOICES, ADAPTER_RANK, EXPERTS), 0.04, 0.25)
    gate_in = normal_values(arg_keys[27], (EXPERTS, ADAPTER_CHOICES, MODEL_DIM, ADAPTER_RANK), MODEL_DIM ** -0.5, 0.125, ((0, 32),))
    gate_out = normal_values(arg_keys[28], (EXPERTS, ADAPTER_CHOICES, ADAPTER_RANK, FF), 0.08, 0.5, ((0, 32),))
    upward_in = normal_values(arg_keys[29], (EXPERTS, ADAPTER_CHOICES, MODEL_DIM, ADAPTER_RANK), MODEL_DIM ** -0.5, 0.125, ((0, 32),))
    upward_out = normal_values(arg_keys[30], (EXPERTS, ADAPTER_CHOICES, ADAPTER_RANK, FF), 0.08, 0.5, ((0, 32),))
    downward_in = normal_values(arg_keys[31], (EXPERTS, ADAPTER_CHOICES, FF, ADAPTER_RANK), FF ** -0.5, 0.21875, ((0, 32),))
    downward_out = normal_values(arg_keys[32], (EXPERTS, ADAPTER_CHOICES, ADAPTER_RANK, MODEL_DIM), 0.4, 2.5, ((0, 32),))
    return {"tokens": tokens, "segments": segments, "routes": routes, "adapter_index": adapter_index, "cotangent": cotangent, "attn_gain": attn_gain, "moe_gain": moe_gain, "q_gain": q_gain, "key_norm_gain": key_norm_gain, "w_query": w_query, "key_projection_weight": key_projection_weight, "value_projection_weight": value_projection_weight, "w_out": w_out, "w_router": w_router, "expert_gate_weight": expert_gate_weight, "expert_up_weight": expert_up_weight, "expert_down_weight": expert_down_weight, "query_in": query_in, "query_out": query_out, "key_in": key_in, "key_second_weight": key_second_weight, "value_in": value_in, "value_second_weight": value_second_weight, "attn_in": attn_in, "attn_out": attn_out, "router_in": router_in, "router_out": router_out, "gate_in": gate_in, "gate_out": gate_out, "upward_in": upward_in, "upward_out": upward_out, "downward_in": downward_in, "downward_out": downward_out}


NORM_EPSILON = 1e-06
ROPE_THETA = 1000000.0
EXACT_MODE = lax.Precision.HIGHEST

@jax.custom_vjp
def narrow_rows(v):
    return lax.optimization_barrier(v.astype(jnp.bfloat16)).astype(jnp.float32)

@jax.custom_vjp
def low_back(v):
    return v

def low_keep(v):
    return (narrow_rows(v), None)

def low_pass(kept, grad):
    return (grad,)

def back_keep(v):
    return (v, None)

def back_low(kept, grad):
    return (narrow_rows(grad),)
narrow_rows.defvjp(low_keep, low_pass)
low_back.defvjp(back_keep, back_low)

def matrix_product(first_op, second_op):
    return jnp.dot(first_op, second_op, precision=EXACT_MODE, preferred_element_type=jnp.float32)

def batched(first_op, second_op):
    return jnp.einsum('esd,edf->esf', first_op, second_op, precision=EXACT_MODE, preferred_element_type=jnp.float32)

def normalized_rows(values, gain_vec):
    return values * lax.rsqrt(lax.optimization_barrier(jnp.mean(values * values, axis=-1, keepdims=True)) + NORM_EPSILON) * gain_vec

def rope_tables(sequence_length, head_width):
    half_width = head_width // 2
    inverse = jnp.power(ROPE_THETA, -2.0 * jnp.arange(half_width, dtype=jnp.float32) / head_width)
    angles = jnp.arange(sequence_length, dtype=jnp.float32)[:, None] * inverse[None, :]
    return (jnp.cos(angles)[:, None, :], jnp.sin(angles)[:, None, :])

def rotated_rows(values, cosine_table, sine_table):
    half_width = values.shape[-1] // 2
    leading = values[..., :half_width]
    trailing = values[..., half_width:]
    return jnp.concatenate([leading * cosine_table - trailing * sine_table, trailing * cosine_table + leading * sine_table], axis=-1)

def adapted(inputs, down_map, up_map):
    return matrix_product(narrow_rows(low_back(matrix_product(inputs, down_map))), up_map)

def expert_adapted(inputs, down_map, up_map):
    return batched(narrow_rows(low_back(batched(inputs, down_map))), up_map)

def sequence_forward(hidden_in, seg_ids, route_ids, weights, adapters):
    attn_gain, moe_gain, q_gain, key_norm_gain, w_query, key_projection_weight, value_projection_weight, w_out, w_router, expert_gate_weight, expert_up_weight, expert_down_weight = weights
    query_in, query_out, key_in, key_second_weight, value_in, value_second_weight, attn_in, attn_out, router_in, router_out, gate_in, gate_out, upward_in, upward_out, downward_in, downward_out = adapters
    sequence_length = hidden_in.shape[0]
    normed_in = narrow_rows(normalized_rows(hidden_in, attn_gain))
    query_linear = low_back(matrix_product(normed_in, w_query) + adapted(normed_in, query_in, query_out))
    key_linear = low_back(matrix_product(normed_in, key_projection_weight) + adapted(normed_in, key_in, key_second_weight))
    value_narrow = narrow_rows(low_back(matrix_product(normed_in, value_projection_weight) + adapted(normed_in, value_in, value_second_weight)))
    cosine_table, sine_table = rope_tables(sequence_length, HEAD_SIZE)
    query_narrow = narrow_rows(rotated_rows(normalized_rows(query_linear.reshape(sequence_length, QUERY_HEADS, HEAD_SIZE), q_gain), cosine_table, sine_table))
    key_narrow = narrow_rows(rotated_rows(normalized_rows(key_linear.reshape(sequence_length, KEY_VALUE_HEADS, HEAD_SIZE), key_norm_gain), cosine_table, sine_table))
    grouped_heads = query_narrow.reshape(sequence_length, KEY_VALUE_HEADS, QUERY_HEADS // KEY_VALUE_HEADS, HEAD_SIZE)
    scores = low_back(jnp.einsum('ikgd,jkd->kgij', grouped_heads, key_narrow, precision=EXACT_MODE, preferred_element_type=jnp.float32) * (1.0 / math.sqrt(HEAD_SIZE)))
    positions = jnp.arange(sequence_length, dtype=jnp.int32)
    allowed = (positions[None, :] == positions[:, None]) | (positions[None, :] < positions[:, None]) & (seg_ids[:, None] == seg_ids[None, :]) & (seg_ids[None, :] != 0)
    attention_likelihoods = jax.nn.softmax(jnp.where(allowed, scores, -1e+30), axis=-1)
    blended_heads = jnp.einsum('qnzb,bqs->zqns', narrow_rows(attention_likelihoods), value_narrow.reshape(sequence_length, KEY_VALUE_HEADS, HEAD_SIZE), precision=EXACT_MODE, preferred_element_type=jnp.float32)
    heads_narrow = narrow_rows(low_back(blended_heads.reshape(sequence_length, QUERY_HEADS * HEAD_SIZE)))
    attn_branch = low_back(matrix_product(heads_narrow, w_out) + adapted(heads_narrow, attn_in, attn_out))
    residual_stream = hidden_in + attn_branch
    moe_in = narrow_rows(normalized_rows(residual_stream, moe_gain))
    router_logits = low_back(matrix_product(moe_in, w_router) + adapted(moe_in, router_in, router_out))
    gate_weights = jax.nn.softmax(jnp.take_along_axis(router_logits, route_ids, axis=1), axis=-1)
    flat_routes = route_ids.reshape(-1)
    entries = flat_routes.shape[0]
    onehot = (flat_routes[:, None] == jnp.arange(EXPERTS, dtype=jnp.int32)[None, :]).astype(jnp.int32)
    slot_rank = lax.optimization_barrier(jnp.sum((jnp.cumsum(onehot, axis=0, dtype=jnp.int32) - onehot) * onehot, axis=1, dtype=jnp.int32))
    slot_depth = N_TENSOR * CAP
    slot_entry = jnp.full((EXPERTS * slot_depth,), entries, jnp.int32).at[flat_routes * slot_depth + slot_rank].set(jnp.arange(entries, dtype=jnp.int32))
    slot_token = slot_entry // TOPK
    padded = jnp.concatenate([moe_in, jnp.zeros((1, MODEL_DIM), jnp.float32)], axis=0)
    expert_rows = low_back(padded[slot_token].reshape(EXPERTS, slot_depth, MODEL_DIM))
    gate_pad = jnp.concatenate([gate_weights.reshape(-1), jnp.zeros((1,), jnp.float32)])[slot_entry].reshape(EXPERTS, slot_depth)
    gate_linear = low_back(batched(expert_rows, expert_gate_weight) + expert_adapted(expert_rows, gate_in, gate_out))
    up_linear = low_back(batched(expert_rows, expert_up_weight) + expert_adapted(expert_rows, upward_in, upward_out))
    inner_act = narrow_rows(jax.nn.silu(gate_linear) * up_linear)
    returned = narrow_rows(low_back(batched(inner_act, expert_down_weight) + expert_adapted(inner_act, downward_in, downward_out)))
    weighted = (gate_pad[:, :, None] * returned).reshape(EXPERTS * slot_depth, MODEL_DIM)
    combined = jnp.zeros((sequence_length + 1, MODEL_DIM), jnp.float32).at[slot_token].add(weighted)[:sequence_length]
    return residual_stream + combined

def reference(tokens, segments, routes, adapter_index, cotangent, attn_gain, moe_gain, q_gain, key_norm_gain, w_query, key_projection_weight, value_projection_weight, w_out, w_router, expert_gate_weight, expert_up_weight, expert_down_weight, query_in, query_out, key_in, key_second_weight, value_in, value_second_weight, attn_in, attn_out, router_in, router_out, gate_in, gate_out, upward_in, upward_out, downward_in, downward_out):
    weights = tuple((array_in.astype(jnp.float32) for array_in in (attn_gain, moe_gain, q_gain, key_norm_gain, w_query, key_projection_weight, value_projection_weight, w_out, w_router, expert_gate_weight, expert_up_weight, expert_down_weight)))
    attn_tables = tuple((array_in.astype(jnp.float32) for array_in in (query_in, query_out, key_in, key_second_weight, value_in, value_second_weight, attn_in, attn_out, router_in, router_out)))
    expert_tables = tuple((array_in.astype(jnp.float32) for array_in in (gate_in, gate_out, upward_in, upward_out, downward_in, downward_out)))
    seqs_in = tokens.reshape(N_FSDP, SEQ, MODEL_DIM)
    route_seqs = routes.reshape(N_FSDP, SEQ, TOPK)
    cot_seqs = cotangent.reshape(N_FSDP, SEQ, MODEL_DIM)

    def per_sequence(totals, inputs):
        hidden_in, seg_ids, route_ids, cot_rows, adapter_pick = inputs
        chosen = tuple((lax.dynamic_index_in_dim(array_in, adapter_pick, 0, keepdims=False) for array_in in attn_tables)) + tuple((lax.dynamic_index_in_dim(array_in, adapter_pick, 1, keepdims=False) for array_in in expert_tables))

        def forward(hidden_rows, adapters):
            return sequence_forward(hidden_rows, seg_ids, route_ids, weights, adapters)
        result, pullback = jax.vjp(forward, hidden_in.astype(jnp.float32), chosen)
        grad_rows, grad_tables = pullback(cot_rows.astype(jnp.float32))
        updated = []
        for index_pos, (running, addend) in enumerate(zip(totals, grad_tables)):
            axis_pos = 0 if index_pos < 10 else 1
            current = lax.dynamic_index_in_dim(running, adapter_pick, axis_pos, keepdims=False)
            updated.append(lax.dynamic_update_index_in_dim(running, current + addend, adapter_pick, axis_pos))
        return (tuple(updated), (result.astype(jnp.bfloat16), grad_rows))
    initial = tuple((jnp.zeros(array_in.shape, jnp.float32) for array_in in attn_tables + expert_tables))
    totals, (outputs, grads) = lax.scan(per_sequence, initial, (seqs_in, segments, route_seqs, cot_seqs, adapter_index))
    return (outputs.reshape(TOKENS, MODEL_DIM), grads.reshape(TOKENS, MODEL_DIM), totals[0], totals[1], totals[2], totals[3], totals[4], totals[5], totals[6], totals[7], totals[8], totals[9], totals[10], totals[11], totals[12], totals[13], totals[14], totals[15])
```

```python
import math

import jax
import jax.numpy as jnp
from jax import lax
from jax.sharding import PartitionSpec as P

NORM_EPSILON = 1e-06
ROPE_THETA = 1000000.0


def matrix_product(first_op, second_op):
    return jnp.dot(first_op, second_op, preferred_element_type=jnp.float32)


def flipped_left_operand(first_op, second_op):
    return lax.dot_general(
        first_op, second_op, (((0,), (0,)), ((), ())), preferred_element_type=jnp.float32
    )


def flipped_right_operand(first_op, second_op):
    return lax.dot_general(
        first_op, second_op, (((1,), (1,)), ((), ())), preferred_element_type=jnp.float32
    )


def norm_forward(values, gain_vec):
    factor = lax.rsqrt(jnp.mean(values * values, axis=-1, keepdims=True) + NORM_EPSILON)
    return (values * factor * gain_vec, factor)


def norm_backward(values, factor, gain_vec, upstream):
    scaled = upstream * gain_vec
    return factor * scaled - values * (factor * factor * factor) * jnp.mean(
        values * scaled, axis=-1, keepdims=True
    )


def rope_tables(sequence_length, head_width):
    half_width = head_width // 2
    inverse = jnp.power(ROPE_THETA, -2.0 * jnp.arange(half_width, dtype=jnp.float32) / head_width)
    angles = jnp.arange(sequence_length, dtype=jnp.float32)[:, None] * inverse[None, :]
    return (jnp.cos(angles)[:, None, :], jnp.sin(angles)[:, None, :])


def rotated_rows(values, cosine_table, sine_table):
    half_width = values.shape[-1] // 2
    leading = values[..., :half_width]
    trailing = values[..., half_width:]
    return jnp.concatenate(
        [
            leading * cosine_table - trailing * sine_table,
            trailing * cosine_table + leading * sine_table,
        ],
        axis=-1,
    )


def unrotated(upstream, cosine_table, sine_table):
    half_width = upstream.shape[-1] // 2
    leading = upstream[..., :half_width]
    trailing = upstream[..., half_width:]
    return jnp.concatenate(
        [
            leading * cosine_table + trailing * sine_table,
            trailing * cosine_table - leading * sine_table,
        ],
        axis=-1,
    )


def route_rows(block_rows):
    return lax.all_to_all(block_rows, ("fsdp", "tensor"), split_axis=0, concat_axis=0, tiled=True)


def per_device(
    tokens,
    segments,
    routes,
    adapter_index,
    cotangent,
    attn_gain,
    moe_gain,
    q_gain,
    key_norm_gain,
    w_query,
    key_projection_weight,
    value_projection_weight,
    w_out,
    w_router,
    expert_gate_weight,
    expert_up_weight,
    expert_down_weight,
    query_in,
    query_out,
    key_in,
    key_second_weight,
    value_in,
    value_second_weight,
    attn_in,
    attn_out,
    router_in,
    router_out,
    gate_in,
    gate_out,
    upward_in,
    upward_out,
    downward_in,
    downward_out,
):
    tensor_count = lax.axis_size("tensor")
    tensor_pos = lax.axis_index("tensor")
    fsdp_pos = lax.axis_index("fsdp")
    zero_pos = fsdp_pos * 0
    tok_rows, model_width = tokens.shape
    seq_rows = tok_rows * tensor_count
    rank_columns = query_in.shape[2]
    adapter_count = query_in.shape[0]
    head_dim = q_gain.shape[0]
    local_cols = query_out.shape[2]
    local_kv_cols = key_second_weight.shape[2]
    local_heads = local_cols // head_dim
    local_groups = local_kv_cols // head_dim
    group_size = local_heads // local_groups
    expert_count = w_router.shape[1]
    top_count = routes.shape[1]
    capacity = 5 * tok_rows * top_count // (4 * expert_count)
    score_scale = 1.0 / math.sqrt(head_dim)
    broad_columns = adapter_count * rank_columns
    adapter_pick = lax.dynamic_index_in_dim(adapter_index, fsdp_pos, 0, keepdims=False)

    def select_adapter(adapter_table):
        return lax.dynamic_index_in_dim(adapter_table, adapter_pick, 0, keepdims=False)

    input_first_factor = jnp.concatenate(
        [select_adapter(query_in), select_adapter(key_in), select_adapter(value_in)], axis=1
    )
    query_second_factor = select_adapter(query_out)
    key_second_factor = select_adapter(key_second_weight)
    value_second_factor = select_adapter(value_second_weight)
    attention_down_factor = select_adapter(attn_in)
    attention_up_factor = select_adapter(attn_out)
    router_first_factor = select_adapter(router_in)
    router_second_factor = select_adapter(router_out)
    gain_attn = attn_gain.astype(jnp.float32)
    gain_moe = moe_gain.astype(jnp.float32)
    gain_query = q_gain.astype(jnp.float32)
    gain_key = key_norm_gain.astype(jnp.float32)
    gathered = (
        lax.all_gather(w_query, "fsdp", axis=0, tiled=True),
        lax.all_gather(key_projection_weight, "fsdp", axis=0, tiled=True),
        lax.all_gather(value_projection_weight, "fsdp", axis=0, tiled=True),
        lax.all_gather(w_out, "fsdp", axis=1, tiled=True),
        lax.all_gather(w_router, "fsdp", axis=0, tiled=True),
    )
    complete_query, complete_key, complete_value, full_out, complete_router = gathered
    token_value_rows = tokens.astype(jnp.float32)
    attn_normed, attn_factor = norm_forward(token_value_rows, gain_attn)
    attention_narrow = attn_normed.astype(jnp.bfloat16)
    input_adapter = matrix_product(attention_narrow, input_first_factor).astype(jnp.bfloat16)
    sequence_normalized, sequence_adapter = (
        lax.all_gather(attention_narrow, "tensor", axis=0, tiled=True),
        lax.all_gather(input_adapter, "tensor", axis=0, tiled=True),
    )
    query_linear = matrix_product(sequence_normalized, complete_query) + matrix_product(
        sequence_adapter[:, :rank_columns], query_second_factor
    )
    key_linear = matrix_product(sequence_normalized, complete_key) + matrix_product(
        sequence_adapter[:, rank_columns : 2 * rank_columns], key_second_factor
    )
    value_narrow = (
        matrix_product(sequence_normalized, complete_value)
        + matrix_product(sequence_adapter[:, 2 * rank_columns :], value_second_factor)
    ).astype(jnp.bfloat16)
    cosine_table, sine_table = rope_tables(seq_rows, head_dim)
    query_heads = query_linear.reshape(seq_rows, local_heads, head_dim)
    query_normed, query_factor = norm_forward(query_heads, gain_query)
    query_narrow = rotated_rows(query_normed, cosine_table, sine_table).astype(jnp.bfloat16)
    key_heads = key_linear.reshape(seq_rows, local_groups, head_dim)
    key_normed, key_factor = norm_forward(key_heads, gain_key)
    key_narrow = rotated_rows(key_normed, cosine_table, sine_table).astype(jnp.bfloat16)
    value_heads = value_narrow.reshape(seq_rows, local_groups, head_dim)
    seg_ids = segments[0]
    block_rows = min(512, seq_rows)
    block_count = seq_rows // block_rows
    key_pos = jnp.arange(seq_rows, dtype=jnp.int32)

    def block_scores(row_start):
        query_pos = row_start + jnp.arange(block_rows, dtype=jnp.int32)
        query_seg = seg_ids[row_start : row_start + block_rows]
        allowed = (key_pos[None, :] == query_pos[:, None]) | (
            key_pos[None, :] < query_pos[:, None]
        ) & (query_seg[:, None] == seg_ids[None, :]) & (seg_ids[None, :] != 0)
        query_block = query_narrow[row_start : row_start + block_rows].reshape(
            block_rows, local_groups, group_size, head_dim
        )
        raw_scores = (
            jnp.einsum(
                "ikgd,jkd->kgij", query_block, key_narrow, preferred_element_type=jnp.float32
            )
            * score_scale
        )
        return (jnp.where(allowed[None, None], raw_scores, -1e30), query_block)

    block_outputs = []
    block_lse = []
    for block_idx in range(block_count):
        row_start = block_idx * block_rows
        masked, query_block = block_scores(row_start)
        row_peak = jnp.max(masked, axis=-1, keepdims=True)
        expo_scores = jnp.exp(masked - row_peak)
        row_total = jnp.sum(expo_scores, axis=-1, keepdims=True)
        probs_low = (expo_scores / row_total).astype(jnp.bfloat16)
        block_lse.append(row_peak + jnp.log(row_total))
        block_outputs.append(
            jnp.einsum(
                "qnzb,bqs->zqns", probs_low, value_heads, preferred_element_type=jnp.float32
            ).reshape(block_rows, local_cols)
        )
    heads_narrow = jnp.concatenate(block_outputs, axis=0).astype(jnp.bfloat16)
    out_part = matrix_product(heads_narrow, full_out)
    attention_adapter_share = matrix_product(heads_narrow, attention_down_factor)
    attention_total, attention_adapter_total = (
        lax.psum_scatter(
            out_part.astype(jnp.bfloat16), "tensor", scatter_dimension=0, tiled=True
        ).astype(jnp.float32),
        lax.psum_scatter(
            attention_adapter_share.astype(jnp.bfloat16), "tensor", scatter_dimension=0, tiled=True
        ).astype(jnp.float32),
    )
    attention_adapter_narrow = attention_adapter_total.astype(jnp.bfloat16)
    residual_stream = (
        token_value_rows
        + attention_total
        + matrix_product(attention_adapter_narrow, attention_up_factor)
    )
    moe_normed, moe_factor = norm_forward(residual_stream, gain_moe)
    experts_narrow = moe_normed.astype(jnp.bfloat16)
    router_adapter = matrix_product(experts_narrow, router_first_factor).astype(jnp.bfloat16)
    router_logits = matrix_product(experts_narrow, complete_router) + matrix_product(
        router_adapter, router_second_factor
    )
    expert_ids = jnp.arange(expert_count, dtype=jnp.int32)
    onehot = (routes[:, :, None] == expert_ids[None, None, :]).astype(jnp.float32)
    chosen = jnp.sum(onehot * router_logits[:, None, :], axis=-1)
    chosen_exp = jnp.exp(chosen - jnp.max(chosen, axis=-1, keepdims=True))
    gate_weights = chosen_exp / jnp.sum(chosen_exp, axis=-1, keepdims=True)
    flat_routes = routes.reshape(-1)
    entries = flat_routes.shape[0]
    flat_onehot = (flat_routes[:, None] == expert_ids[None, :]).astype(jnp.int32)
    slot_rank = jnp.sum(
        (jnp.cumsum(flat_onehot, axis=0, dtype=jnp.int32) - flat_onehot) * flat_onehot,
        axis=1,
        dtype=jnp.int32,
    )
    destination = flat_routes * capacity + slot_rank
    slot_entry = (
        jnp.full((expert_count * capacity,), entries, jnp.int32)
        .at[destination]
        .set(jnp.arange(entries, dtype=jnp.int32))
    )
    slot_token = slot_entry // top_count
    padded_low = jnp.concatenate(
        [experts_narrow, jnp.zeros((1, model_width), jnp.bfloat16)], axis=0
    )
    send_rows = padded_low[slot_token].reshape(expert_count, capacity, model_width)
    expert_input = route_rows(send_rows).reshape(expert_count * capacity, model_width)
    source_seq = jnp.arange(expert_count, dtype=jnp.int32) // tensor_count
    source_adapter = adapter_index[source_seq]
    column_adapter = jnp.arange(broad_columns, dtype=jnp.int32) // rank_columns
    source_mask = (source_adapter[:, None] == column_adapter[None, :]).astype(jnp.float32)
    row_validity_mask = jnp.broadcast_to(
        source_mask[:, None, :], (expert_count, capacity, broad_columns)
    ).reshape(expert_count * capacity, broad_columns)
    paired_mask = jnp.concatenate([row_validity_mask, row_validity_mask], axis=1)

    def flat_down(adapter_table):
        return jnp.transpose(adapter_table[0], (1, 0, 2)).reshape(
            adapter_table.shape[2], broad_columns
        )

    def flat_up(adapter_table):
        return adapter_table[0].reshape(broad_columns, adapter_table.shape[3])

    paired_first_factor = jnp.concatenate([flat_down(gate_in), flat_down(upward_in)], axis=1)
    gate_second_factor = flat_up(gate_out)
    upward_second_factor = flat_up(upward_out)
    down_first_factor = flat_down(downward_in)
    down_second_factor = flat_up(downward_out)
    paired_adapter = (matrix_product(expert_input, paired_first_factor) * paired_mask).astype(
        jnp.bfloat16
    )
    gate_linear = matrix_product(expert_input, expert_gate_weight[0]) + matrix_product(
        paired_adapter[:, :broad_columns], gate_second_factor
    )
    up_linear = matrix_product(expert_input, expert_up_weight[0]) + matrix_product(
        paired_adapter[:, broad_columns:], upward_second_factor
    )
    gate_sig = jax.nn.sigmoid(gate_linear)
    gate_act = gate_linear * gate_sig
    inner_narrow = (gate_act * up_linear).astype(jnp.bfloat16)
    down_adapter = (matrix_product(inner_narrow, down_first_factor) * row_validity_mask).astype(
        jnp.bfloat16
    )
    expert_output = (
        matrix_product(inner_narrow, expert_down_weight[0])
        + matrix_product(down_adapter, down_second_factor)
    ).astype(jnp.bfloat16)
    back_rows = route_rows(expert_output.reshape(expert_count, capacity, model_width)).reshape(
        expert_count * capacity, model_width
    )
    route_out = back_rows[destination].reshape(tok_rows, top_count, model_width)
    final_rows = residual_stream + jnp.sum(gate_weights[:, :, None] * route_out, axis=1)
    output = final_rows.astype(jnp.bfloat16)
    out_grad = cotangent.astype(jnp.float32)
    back_weights = (
        lax.all_gather(w_query, "fsdp", axis=0, tiled=True),
        lax.all_gather(key_projection_weight, "fsdp", axis=0, tiled=True),
        lax.all_gather(value_projection_weight, "fsdp", axis=0, tiled=True),
        lax.all_gather(w_out, "fsdp", axis=1, tiled=True),
        lax.all_gather(w_router, "fsdp", axis=0, tiled=True),
    )
    complete_query, complete_key, complete_value, full_out, complete_router = back_weights
    gate_grad = jnp.sum(out_grad[:, None, :] * route_out, axis=-1)
    route_grad = (
        (gate_weights[:, :, None] * out_grad[:, None, :])
        .astype(jnp.bfloat16)
        .reshape(entries, model_width)
    )
    padded_grad = jnp.concatenate([route_grad, jnp.zeros((1, model_width), jnp.bfloat16)], axis=0)
    grad_send = padded_grad[slot_entry].reshape(expert_count, capacity, model_width)
    expert_gradient = route_rows(grad_send).reshape(expert_count * capacity, model_width)
    down_adapter_gradient = (
        flipped_right_operand(expert_gradient, down_second_factor) * row_validity_mask
    ).astype(jnp.bfloat16)
    inner_grad = flipped_right_operand(
        expert_gradient, expert_down_weight[0]
    ) + flipped_right_operand(down_adapter_gradient, down_first_factor)
    down_first_gradient = flipped_left_operand(inner_narrow, down_adapter_gradient)
    down_second_gradient = flipped_left_operand(down_adapter, expert_gradient)
    gate_linear_gradient = (
        inner_grad * up_linear * (gate_sig * (1.0 + gate_linear * (1.0 - gate_sig)))
    ).astype(jnp.bfloat16)
    up_linear_gradient = (inner_grad * gate_act).astype(jnp.bfloat16)
    pair_grad = (
        jnp.concatenate(
            [
                flipped_right_operand(gate_linear_gradient, gate_second_factor),
                flipped_right_operand(up_linear_gradient, upward_second_factor),
            ],
            axis=1,
        )
        * paired_mask
    ).astype(jnp.bfloat16)
    rows_grad = (
        flipped_right_operand(gate_linear_gradient, expert_gate_weight[0])
        + flipped_right_operand(up_linear_gradient, expert_up_weight[0])
        + flipped_right_operand(pair_grad, paired_first_factor)
    )
    grad_pair_down = flipped_left_operand(expert_input, pair_grad)
    gate_second_gradient = flipped_left_operand(
        paired_adapter[:, :broad_columns], gate_linear_gradient
    )
    upward_second_gradient = flipped_left_operand(
        paired_adapter[:, broad_columns:], up_linear_gradient
    )
    back_grad = route_rows(
        rows_grad.astype(jnp.bfloat16).reshape(expert_count, capacity, model_width)
    ).reshape(expert_count * capacity, model_width)
    moe_grad = jnp.sum(
        back_grad[destination].reshape(tok_rows, top_count, model_width), axis=1, dtype=jnp.float32
    )
    chosen_grad = gate_weights * (
        gate_grad - jnp.sum(gate_weights * gate_grad, axis=-1, keepdims=True)
    )
    logit_gradient = jnp.sum(onehot * chosen_grad[:, :, None], axis=1).astype(jnp.bfloat16)
    router_adapter_gradient = flipped_right_operand(logit_gradient, router_second_factor).astype(
        jnp.bfloat16
    )
    moe_grad = (
        moe_grad
        + flipped_right_operand(logit_gradient, complete_router)
        + flipped_right_operand(router_adapter_gradient, router_first_factor)
    )
    router_first_gradient = flipped_left_operand(experts_narrow, router_adapter_gradient)
    router_second_gradient = flipped_left_operand(router_adapter, logit_gradient)
    residual_grad = out_grad + norm_backward(residual_stream, moe_factor, gain_moe, moe_grad)
    branch_gradient = residual_grad.astype(jnp.bfloat16)
    attention_adapter_grad = flipped_right_operand(branch_gradient, attention_up_factor).astype(
        jnp.bfloat16
    )
    attention_up_gradient = flipped_left_operand(attention_adapter_narrow, branch_gradient)
    sequence_branch_gradient, sequence_attention_adapter_grad = (
        lax.all_gather(branch_gradient, "tensor", axis=0, tiled=True),
        lax.all_gather(attention_adapter_grad, "tensor", axis=0, tiled=True),
    )
    heads_grad = (
        flipped_right_operand(sequence_branch_gradient, full_out)
        + flipped_right_operand(sequence_attention_adapter_grad, attention_down_factor)
    ).astype(jnp.bfloat16)
    attention_down_gradient = flipped_left_operand(heads_narrow, sequence_attention_adapter_grad)
    heads_grad_view = heads_grad.reshape(seq_rows, local_groups, group_size, head_dim)
    value_grad = jnp.zeros((seq_rows, local_groups, head_dim), jnp.float32)
    key_grad = jnp.zeros((seq_rows, local_groups, head_dim), jnp.float32)
    query_grads = []
    for block_idx in range(block_count):
        row_start = block_idx * block_rows
        masked, query_block = block_scores(row_start)
        block_probs = jnp.exp(masked - block_lse[block_idx])
        probs_low = block_probs.astype(jnp.bfloat16)
        grad_block = heads_grad_view[row_start : row_start + block_rows]
        prob_grad = jnp.einsum(
            "ikgd,jkd->kgij", grad_block, value_heads, preferred_element_type=jnp.float32
        )
        score_grad = (
            block_probs * (prob_grad - jnp.sum(block_probs * prob_grad, axis=-1, keepdims=True))
        ).astype(jnp.bfloat16)
        value_grad = value_grad + jnp.einsum(
            "kgij,ikgd->jkd", probs_low, grad_block, preferred_element_type=jnp.float32
        )
        key_grad = (
            key_grad
            + jnp.einsum(
                "kgij,ikgd->jkd", score_grad, query_block, preferred_element_type=jnp.float32
            )
            * score_scale
        )
        query_grads.append(
            jnp.einsum(
                "qnzb,bqs->zqns", score_grad, key_narrow, preferred_element_type=jnp.float32
            ).reshape(block_rows, local_heads, head_dim)
            * score_scale
        )
    query_grad = jnp.concatenate(query_grads, axis=0)
    query_linear_gradient = (
        norm_backward(
            query_heads, query_factor, gain_query, unrotated(query_grad, cosine_table, sine_table)
        )
        .reshape(seq_rows, local_cols)
        .astype(jnp.bfloat16)
    )
    key_linear_gradient = (
        norm_backward(
            key_heads, key_factor, gain_key, unrotated(key_grad, cosine_table, sine_table)
        )
        .reshape(seq_rows, local_kv_cols)
        .astype(jnp.bfloat16)
    )
    value_linear_gradient = value_grad.reshape(seq_rows, local_kv_cols).astype(jnp.bfloat16)
    normed_part = (
        flipped_right_operand(query_linear_gradient, complete_query)
        + flipped_right_operand(key_linear_gradient, complete_key)
        + flipped_right_operand(value_linear_gradient, complete_value)
    )
    adapter_share = jnp.concatenate(
        [
            flipped_right_operand(query_linear_gradient, query_second_factor),
            flipped_right_operand(key_linear_gradient, key_second_factor),
            flipped_right_operand(value_linear_gradient, value_second_factor),
        ],
        axis=1,
    )
    query_second_gradient = flipped_left_operand(
        sequence_adapter[:, :rank_columns], query_linear_gradient
    )
    key_second_gradient = flipped_left_operand(
        sequence_adapter[:, rank_columns : 2 * rank_columns], key_linear_gradient
    )
    value_second_gradient = flipped_left_operand(
        sequence_adapter[:, 2 * rank_columns :], value_linear_gradient
    )
    normalized_gradient, input_adapter_gradient = (
        lax.psum_scatter(
            normed_part.astype(jnp.bfloat16), "tensor", scatter_dimension=0, tiled=True
        ).astype(jnp.float32),
        lax.psum_scatter(
            adapter_share.astype(jnp.bfloat16), "tensor", scatter_dimension=0, tiled=True
        ).astype(jnp.float32),
    )
    input_adapter_narrow = input_adapter_gradient.astype(jnp.bfloat16)
    normalized_gradient = normalized_gradient + flipped_right_operand(
        input_adapter_narrow, input_first_factor
    )
    input_first_gradient = flipped_left_operand(attention_narrow, input_adapter_narrow)
    input_grad = residual_grad + norm_backward(
        token_value_rows, attn_factor, gain_attn, normalized_gradient
    )
    device_count = lax.axis_size("fsdp") * tensor_count
    fsdp_count = lax.axis_size("fsdp")
    adapter_ids = jnp.arange(adapter_count, dtype=jnp.int32)
    source_rows = jnp.arange(device_count, dtype=jnp.int32) // tensor_count
    owner_onehot = (adapter_ids[:, None] == adapter_index[source_rows][None, :]).astype(
        jnp.bfloat16
    )

    def everywhere(addend):
        return addend.reshape(device_count, -1)

    def columns_everywhere(addend):
        ranks = addend.shape[0]
        return jnp.transpose(addend.reshape(ranks, device_count, -1), (1, 0, 2)).reshape(
            device_count, -1
        )

    def from_heads(pieces):
        holder = jnp.zeros((device_count, pieces.shape[1]), pieces.dtype)
        return lax.dynamic_update_slice(
            holder, pieces, (tensor_pos * fsdp_count, zero_pos)
        )

    def owner_sums(parts):
        widths = [part.shape[1] for part in parts]
        packed = jnp.concatenate([part.astype(jnp.bfloat16) for part in parts], axis=1)
        received = route_rows(packed)
        total = matrix_product(owner_onehot, received)
        pieces = []
        start = 0
        for width in widths:
            pieces.append(total[:, start : start + width])
            start += width
        return pieces

    def head_columns(addend):
        ranks = addend.shape[0]
        return from_heads(
            jnp.transpose(addend.reshape(ranks, fsdp_count, -1), (1, 0, 2)).reshape(
                fsdp_count, -1
            )
        )

    early = owner_sums(
        [
            everywhere(router_first_gradient),
            columns_everywhere(attention_up_gradient),
            columns_everywhere(router_second_gradient),
            from_heads(attention_down_gradient.reshape(fsdp_count, -1)),
        ]
    )
    late = owner_sums(
        [
            everywhere(input_first_gradient),
            head_columns(query_second_gradient),
            head_columns(key_second_gradient),
            head_columns(value_second_gradient),
        ]
    )
    first_sums = late[0].reshape(adapter_count, -1, 3 * rank_columns)

    def by_row(piece):
        return piece.reshape(adapter_count, -1, rank_columns)

    def by_column(piece):
        return piece.reshape(adapter_count, rank_columns, -1)

    summed = (
        first_sums[:, :, :rank_columns],
        by_column(late[1]),
        first_sums[:, :, rank_columns : 2 * rank_columns],
        by_column(late[2]),
        first_sums[:, :, 2 * rank_columns :],
        by_column(late[3]),
        by_row(early[3]),
        by_column(early[1]),
        by_row(early[0]),
        by_column(early[2]),
    )
    grad_gate_in = jnp.transpose(
        grad_pair_down[:, :broad_columns].reshape(model_width, adapter_count, rank_columns),
        (1, 0, 2),
    )[None]
    grad_upward_in = jnp.transpose(
        grad_pair_down[:, broad_columns:].reshape(model_width, adapter_count, rank_columns),
        (1, 0, 2),
    )[None]
    grad_gate_out = gate_second_gradient.reshape(
        adapter_count, rank_columns, gate_second_factor.shape[1]
    )[None]
    grad_upward_out = upward_second_gradient.reshape(
        adapter_count, rank_columns, upward_second_factor.shape[1]
    )[None]
    grad_downward_in = jnp.transpose(
        down_first_gradient.reshape(down_first_factor.shape[0], adapter_count, rank_columns),
        (1, 0, 2),
    )[None]
    grad_downward_out = down_second_gradient.reshape(adapter_count, rank_columns, model_width)[None]
    return (
        output,
        input_grad,
        summed[0],
        summed[1],
        summed[2],
        summed[3],
        summed[4],
        summed[5],
        summed[6],
        summed[7],
        summed[8],
        summed[9],
        grad_gate_in,
        grad_gate_out,
        grad_upward_in,
        grad_upward_out,
        grad_downward_in,
        grad_downward_out,
    )


def solution(mesh):
    placed = (
        P(("fsdp", "tensor"), None),
        P("fsdp", None),
        P(("fsdp", "tensor"), None),
        P(),
        P(("fsdp", "tensor"), None),
        P(),
        P(),
        P(),
        P(),
        P("fsdp", "tensor"),
        P("fsdp", "tensor"),
        P("fsdp", "tensor"),
        P("tensor", "fsdp"),
        P("fsdp", None),
        P(("fsdp", "tensor"), None, None),
        P(("fsdp", "tensor"), None, None),
        P(("fsdp", "tensor"), None, None),
        P(),
        P(None, None, "tensor"),
        P(),
        P(None, None, "tensor"),
        P(),
        P(None, None, "tensor"),
        P(None, "tensor", None),
        P(),
        P(),
        P(),
        P(("fsdp", "tensor"), None, None, None),
        P(("fsdp", "tensor"), None, None, None),
        P(("fsdp", "tensor"), None, None, None),
        P(("fsdp", "tensor"), None, None, None),
        P(("fsdp", "tensor"), None, None, None),
        P(("fsdp", "tensor"), None, None, None),
    )
    return jax.shard_map(
        per_device,
        mesh=mesh,
        in_specs=placed,
        out_specs=(
            P(("fsdp", "tensor"), None),
            P(("fsdp", "tensor"), None),
            P(None, ("fsdp", "tensor"), None),
            P(None, None, ("fsdp", "tensor")),
            P(None, ("fsdp", "tensor"), None),
            P(None, None, ("fsdp", "tensor")),
            P(None, ("fsdp", "tensor"), None),
            P(None, None, ("fsdp", "tensor")),
            P(None, ("fsdp", "tensor"), None),
            P(None, None, ("fsdp", "tensor")),
            P(None, ("fsdp", "tensor"), None),
            P(None, None, ("fsdp", "tensor")),
            P(("fsdp", "tensor"), None, None, None),
            P(("fsdp", "tensor"), None, None, None),
            P(("fsdp", "tensor"), None, None, None),
            P(("fsdp", "tensor"), None, None, None),
            P(("fsdp", "tensor"), None, None, None),
            P(("fsdp", "tensor"), None, None, None),
        ),
        check_vma=False,
    )
```

```python
import functools
import math

import jax
import jax.numpy as jnp
from jax import lax
from jax.experimental import pallas as pl
from jax.experimental.pallas import tpu as pltpu
from jax.sharding import PartitionSpec as P

NORM_EPSILON = 1e-06
ROPE_THETA = 1000000.0
BF16 = jnp.bfloat16
F32 = jnp.float32
WINDOW = 256
MEBI = 1 << 20


def matrix_product(first_op, second_op):
    return jnp.dot(first_op, second_op, preferred_element_type=F32)


def flipped_left_operand(first_op, second_op):
    return lax.dot_general(
        first_op, second_op, (((0,), (0,)), ((), ())), preferred_element_type=F32
    )


def flipped_right_operand(first_op, second_op):
    return lax.dot_general(
        first_op, second_op, (((1,), (1,)), ((), ())), preferred_element_type=F32
    )


def norm_forward(values, gain_vec):
    factor = lax.rsqrt(jnp.mean(values * values, axis=-1, keepdims=True) + NORM_EPSILON)
    return (values * factor * gain_vec, factor)


def norm_backward(values, factor, gain_vec, upstream):
    scaled = upstream * gain_vec
    return factor * scaled - values * (factor * factor * factor) * jnp.mean(
        values * scaled, axis=-1, keepdims=True
    )


def rope_tables(sequence_length, head_width):
    half_width = head_width // 2
    inverse = jnp.power(ROPE_THETA, -2.0 * jnp.arange(half_width, dtype=F32) / head_width)
    angles = jnp.arange(sequence_length, dtype=F32)[:, None] * inverse[None, :]
    cosine, sine = jnp.cos(angles), jnp.sin(angles)
    return (
        jnp.concatenate([cosine, cosine], axis=1),
        jnp.concatenate([-sine, sine], axis=1),
    )


def swapped(values):
    return pltpu.roll(values, values.shape[-1] // 2, 1)


def route_rows(block_rows):
    return lax.all_to_all(block_rows, ("fsdp", "tensor"), split_axis=0, concat_axis=0, tiled=True)


def plane_rows(block_rows):
    return lax.all_to_all(block_rows, "fsdp", split_axis=0, concat_axis=0, tiled=True)


def params(mebibytes, axes=1):
    return pltpu.CompilerParams(
        vmem_limit_bytes=mebibytes * MEBI, dimension_semantics=("arbitrary",) * axes
    )


def whole(shape):
    rank = len(shape)
    return pl.BlockSpec(shape, lambda *_: (0,) * rank)


def head_values(linear, low, second, gain, cosine, sine):
    values = linear + matrix_product(low, second)
    normed, factor = norm_forward(values, gain)
    turned = (normed * cosine + swapped(normed) * sine).astype(BF16)
    return values, factor, turned


def head_values_gradient(values, factor, gain, cosine, sine, upstream):
    back = upstream * cosine - swapped(upstream) * sine
    return norm_backward(values, factor, gain, back).astype(BF16)


def allowed_keys(block, start, width, seg_column, seg_row):
    rows = block * WINDOW + lax.broadcasted_iota(jnp.int32, (WINDOW, width), 0)
    keys = start + lax.broadcasted_iota(jnp.int32, (WINDOW, width), 1)
    mine = seg_column[block * WINDOW : (block + 1) * WINDOW]
    theirs = seg_row[:, start : start + width]
    return (keys == rows) | ((keys < rows) & (mine == theirs) & (theirs != 0))


def block_bounds(block):
    start = max(block - 1, 0) * WINDOW
    return start, (block + 1) * WINDOW - start


def attention_forward_body(
    rank,
    scale,
    lin_ref,
    key_lin_ref,
    value_lin_ref,
    low_ref,
    q_second_ref,
    k_second_ref,
    v_second_ref,
    q_gain_ref,
    k_gain_ref,
    cos_ref,
    sin_ref,
    seg_column_ref,
    seg_row_ref,
    heads_ref,
    key_scratch,
    value_scratch,
):
    cosine, sine = cos_ref[...], sin_ref[...]

    @pl.when(pl.program_id(0) == 0)
    def _():
        key_scratch[...] = head_values(
            key_lin_ref[...],
            low_ref[:, rank : 2 * rank],
            k_second_ref[...],
            k_gain_ref[...],
            cosine,
            sine,
        )[2]
        value_scratch[...] = (
            value_lin_ref[...]
            + matrix_product(low_ref[:, 2 * rank : 3 * rank], v_second_ref[...])
        ).astype(BF16)

    query = head_values(
        lin_ref[...], low_ref[:, :rank], q_second_ref[...], q_gain_ref[...], cosine, sine
    )[2]
    seg_column, seg_row = seg_column_ref[...], seg_row_ref[...]
    for block in range(query.shape[0] // WINDOW):
        start, width = block_bounds(block)
        rows = pl.ds(block * WINDOW, WINDOW)
        scores = (
            flipped_right_operand(
                query[block * WINDOW : (block + 1) * WINDOW], key_scratch[pl.ds(start, width)]
            )
            * scale
        )
        scores = jnp.where(
            allowed_keys(block, start, width, seg_column, seg_row), scores, -1e30
        )
        expo = jnp.exp(scores - jnp.max(scores, axis=-1, keepdims=True))
        probs = (expo / jnp.sum(expo, axis=-1, keepdims=True)).astype(BF16)
        heads_ref[rows, :] = matrix_product(probs, value_scratch[pl.ds(start, width)]).astype(
            BF16
        )


def attention_forward(
    linear, low, q_second, k_second, v_second, q_gain, k_gain, tables, seg_column, seg_row, scale
):
    rows, head_dim = linear.shape[0], q_gain.shape[1]
    heads = q_second.shape[1] // head_dim
    rank = q_second.shape[0]
    column = pl.BlockSpec((rows, head_dim), lambda h: (0, h))
    return pl.pallas_call(
        functools.partial(attention_forward_body, rank, scale),
        grid=(heads,),
        out_shape=jax.ShapeDtypeStruct((rows, heads * head_dim), BF16),
        in_specs=[
            column,
            pl.BlockSpec((rows, head_dim), lambda h: (0, heads)),
            pl.BlockSpec((rows, head_dim), lambda h: (0, heads + 1)),
            whole(low.shape),
            pl.BlockSpec((rank, head_dim), lambda h: (0, h)),
            whole(k_second.shape),
            whole(v_second.shape),
            whole(q_gain.shape),
            whole(k_gain.shape),
            whole(tables[0].shape),
            whole(tables[1].shape),
            whole(seg_column.shape),
            whole(seg_row.shape),
        ],
        out_specs=column,
        scratch_shapes=[pltpu.VMEM((rows, head_dim), BF16), pltpu.VMEM((rows, head_dim), BF16)],
        compiler_params=params(40),
        cost_estimate=pl.CostEstimate(
            flops=8 * heads * rows * WINDOW * head_dim,
            transcendentals=2 * heads * rows * WINDOW,
            bytes_accessed=6 * rows * heads * head_dim,
        ),
        name="attention_forward",
    )(
        linear,
        linear,
        linear,
        low,
        q_second,
        k_second,
        v_second,
        q_gain,
        k_gain,
        *tables,
        seg_column,
        seg_row,
    )


def attention_backward_body(
    rank,
    scale,
    lin_ref,
    key_lin_ref,
    value_lin_ref,
    low_ref,
    q_second_ref,
    k_second_ref,
    v_second_ref,
    q_gain_ref,
    k_gain_ref,
    cos_ref,
    sin_ref,
    seg_column_ref,
    seg_row_ref,
    heads_ref,
    heads_grad_ref,
    low_grad_ref,
    down_ref,
    q_grad_ref,
    k_grad_ref,
    v_grad_ref,
    share_ref,
    q_second_grad_ref,
    k_second_grad_ref,
    v_second_grad_ref,
    down_grad_ref,
    key_scratch,
    value_scratch,
    key_sum,
    value_sum,
    query_sum,
    share_sum,
):
    cosine, sine = cos_ref[...], sin_ref[...]
    head = pl.program_id(0)

    @pl.when(head == 0)
    def _():
        key_scratch[...] = head_values(
            key_lin_ref[...],
            low_ref[:, rank : 2 * rank],
            k_second_ref[...],
            k_gain_ref[...],
            cosine,
            sine,
        )[2]
        value_scratch[...] = (
            value_lin_ref[...]
            + matrix_product(low_ref[:, 2 * rank : 3 * rank], v_second_ref[...])
        ).astype(BF16)
        key_sum[...] = jnp.zeros_like(key_sum)
        value_sum[...] = jnp.zeros_like(value_sum)
        share_sum[...] = jnp.zeros_like(share_sum)

    low_q = low_ref[:, :rank]
    values, factor, query = head_values(
        lin_ref[...], low_q, q_second_ref[...], q_gain_ref[...], cosine, sine
    )
    low_grad = low_grad_ref[...]
    upstream = (heads_grad_ref[...] + matrix_product(low_grad, down_ref[...])).astype(BF16)
    down_grad_ref[...] = flipped_left_operand(low_grad, heads_ref[...])
    seg_column, seg_row = seg_column_ref[...], seg_row_ref[...]
    for block in range(query.shape[0] // WINDOW):
        start, width = block_bounds(block)
        rows = pl.ds(block * WINDOW, WINDOW)
        keys = pl.ds(start, width)
        query_block = query[block * WINDOW : (block + 1) * WINDOW]
        upstream_block = upstream[block * WINDOW : (block + 1) * WINDOW]
        scores = flipped_right_operand(query_block, key_scratch[keys]) * scale
        scores = jnp.where(
            allowed_keys(block, start, width, seg_column, seg_row), scores, -1e30
        )
        expo = jnp.exp(scores - jnp.max(scores, axis=-1, keepdims=True))
        probs = expo / jnp.sum(expo, axis=-1, keepdims=True)
        prob_grad = flipped_right_operand(upstream_block, value_scratch[keys])
        score_grad = (
            probs * (prob_grad - jnp.sum(probs * prob_grad, axis=-1, keepdims=True))
        ).astype(BF16)
        value_sum[keys, :] += flipped_left_operand(probs.astype(BF16), upstream_block)
        key_sum[keys, :] += flipped_left_operand(score_grad, query_block)
        query_sum[rows, :] = matrix_product(score_grad, key_scratch[keys]) * scale
    q_grad = head_values_gradient(
        values, factor, q_gain_ref[...], cosine, sine, query_sum[...]
    )
    q_grad_ref[...] = q_grad
    q_second_grad_ref[...] = flipped_left_operand(low_q, q_grad)
    share_sum[:, :rank] += flipped_right_operand(q_grad, q_second_ref[...])

    @pl.when(head == pl.num_programs(0) - 1)
    def _():
        low_k = low_ref[:, rank : 2 * rank]
        low_v = low_ref[:, 2 * rank : 3 * rank]
        key_values, key_factor, _turned = head_values(
            key_lin_ref[...], low_k, k_second_ref[...], k_gain_ref[...], cosine, sine
        )
        k_grad = head_values_gradient(
            key_values, key_factor, k_gain_ref[...], cosine, sine, key_sum[...] * scale
        )
        v_grad = value_sum[...].astype(BF16)
        k_grad_ref[...] = k_grad
        v_grad_ref[...] = v_grad
        k_second_grad_ref[...] = flipped_left_operand(low_k, k_grad)
        v_second_grad_ref[...] = flipped_left_operand(low_v, v_grad)
        share_sum[:, rank : 2 * rank] = flipped_right_operand(k_grad, k_second_ref[...])
        share_sum[:, 2 * rank : 3 * rank] = flipped_right_operand(v_grad, v_second_ref[...])
        share_ref[...] = share_sum[...].astype(BF16)


def attention_backward(
    linear,
    low,
    q_second,
    k_second,
    v_second,
    q_gain,
    k_gain,
    tables,
    seg_column,
    seg_row,
    scale,
    heads_low,
    heads_grad,
    low_grad,
    down_first,
):
    rows, head_dim = linear.shape[0], q_gain.shape[1]
    rank, columns = q_second.shape
    heads = columns // head_dim
    column = pl.BlockSpec((rows, head_dim), lambda h: (0, h))
    narrow = pl.BlockSpec((rank, head_dim), lambda h: (0, h))
    single = (rows, head_dim)
    return pl.pallas_call(
        functools.partial(attention_backward_body, rank, scale),
        grid=(heads,),
        out_shape=(
            jax.ShapeDtypeStruct((rows, columns), BF16),
            jax.ShapeDtypeStruct(single, BF16),
            jax.ShapeDtypeStruct(single, BF16),
            jax.ShapeDtypeStruct((rows, 3 * rank), BF16),
            jax.ShapeDtypeStruct((rank, columns), F32),
            jax.ShapeDtypeStruct((rank, head_dim), F32),
            jax.ShapeDtypeStruct((rank, head_dim), F32),
            jax.ShapeDtypeStruct((rank, columns), F32),
        ),
        in_specs=[
            column,
            pl.BlockSpec((rows, head_dim), lambda h: (0, heads)),
            pl.BlockSpec((rows, head_dim), lambda h: (0, heads + 1)),
            whole(low.shape),
            narrow,
            whole(k_second.shape),
            whole(v_second.shape),
            whole(q_gain.shape),
            whole(k_gain.shape),
            whole(tables[0].shape),
            whole(tables[1].shape),
            whole(seg_column.shape),
            whole(seg_row.shape),
            column,
            column,
            whole(low_grad.shape),
            narrow,
        ],
        out_specs=(
            column,
            whole(single),
            whole(single),
            whole((rows, 3 * rank)),
            narrow,
            whole((rank, head_dim)),
            whole((rank, head_dim)),
            narrow,
        ),
        scratch_shapes=[
            pltpu.VMEM(single, BF16),
            pltpu.VMEM(single, BF16),
            pltpu.VMEM(single, F32),
            pltpu.VMEM(single, F32),
            pltpu.VMEM(single, F32),
            pltpu.VMEM((rows, 3 * rank), F32),
        ],
        compiler_params=params(48),
        cost_estimate=pl.CostEstimate(
            flops=20 * heads * rows * WINDOW * head_dim,
            transcendentals=2 * heads * rows * WINDOW,
            bytes_accessed=12 * rows * columns,
        ),
        name="attention_backward",
    )(
        linear,
        linear,
        linear,
        low,
        q_second,
        k_second,
        v_second,
        q_gain,
        k_gain,
        *tables,
        seg_column,
        seg_row,
        heads_low,
        heads_grad,
        low_grad,
        down_first,
    )


def slot_choice(ranks, slots):
    experts, tokens = ranks.shape
    places = lax.broadcasted_iota(jnp.int32, (slots, tokens), 0)
    return jnp.concatenate(
        [(places == ranks[e : e + 1, :]).astype(F32) for e in range(experts)], axis=0
    ).astype(BF16)


def to_slots_body(rank_ref, rows_ref, out_ref):
    experts, _, slots, width = out_ref.shape
    chosen = matrix_product(slot_choice(rank_ref[0], slots), rows_ref[...])
    out_ref[...] = chosen.astype(BF16).reshape(out_ref.shape)


def to_slots(ranks, rows, slots):
    blocks, experts, tokens = ranks.shape
    width = rows.shape[1]
    return pl.pallas_call(
        to_slots_body,
        grid=(blocks,),
        out_shape=jax.ShapeDtypeStruct((experts, blocks, slots, width), BF16),
        in_specs=[
            pl.BlockSpec((1, experts, tokens), lambda z: (z, 0, 0)),
            pl.BlockSpec((tokens, width), lambda z: (z, 0)),
        ],
        out_specs=pl.BlockSpec((experts, 1, slots, width), lambda z: (0, z, 0, 0)),
        compiler_params=params(40),
        cost_estimate=pl.CostEstimate(
            flops=2 * blocks * experts * slots * tokens * width,
            transcendentals=0,
            bytes_accessed=2 * blocks * width * (experts * slots + tokens),
        ),
        name="to_slots",
    )(ranks, rows)


def from_slots_body(rank_ref, slot_ref, out_ref):
    experts, _, slots, width = slot_ref.shape
    choice = slot_choice(rank_ref[0], slots)
    out_ref[...] = flipped_left_operand(
        choice, slot_ref[...].reshape(experts * slots, width)
    ).astype(BF16)


def from_slots(ranks, slotted):
    blocks, experts, tokens = ranks.shape
    slots, width = slotted.shape[2:]
    return pl.pallas_call(
        from_slots_body,
        grid=(blocks,),
        out_shape=jax.ShapeDtypeStruct((blocks * tokens, width), BF16),
        in_specs=[
            pl.BlockSpec((1, experts, tokens), lambda z: (z, 0, 0)),
            pl.BlockSpec((experts, 1, slots, width), lambda z: (0, z, 0, 0)),
        ],
        out_specs=pl.BlockSpec((tokens, width), lambda z: (z, 0)),
        compiler_params=params(40),
        cost_estimate=pl.CostEstimate(
            flops=2 * blocks * experts * slots * tokens * width,
            transcendentals=0,
            bytes_accessed=2 * blocks * width * (experts * slots + tokens),
        ),
        name="from_slots",
    )(ranks, slotted)


def ranks_of(mask):
    tokens = mask.shape[-1]
    order = jnp.arange(tokens, dtype=jnp.int32)
    before = (order[:, None] < order[None, :]).astype(BF16)
    counts = matrix_product(mask.astype(BF16), before)
    return jnp.where(mask, counts, -1.0).astype(jnp.int32)


def experts_body(
    tile,
    pick_ref,
    rows_ref,
    up_rows_ref,
    rank_ref,
    weight_ref,
    gate_w_ref,
    up_w_ref,
    down_w_ref,
    pair_in_ref,
    gate_out_ref,
    up_out_ref,
    down_in_ref,
    down_out_ref,
    y_ref,
    rows_grad_ref,
    gate_grad_ref,
    pair_in_grad_ref,
    gate_out_grad_ref,
    up_out_grad_ref,
    down_in_grad_ref,
    down_out_grad_ref,
    gate_scratch,
    up_scratch,
    inner_scratch,
    route_scratch,
    gate_lin_scratch,
    up_lin_scratch,
):
    step = pl.program_id(0)

    @pl.when(step == 0)
    def _():
        for ref in (
            pair_in_grad_ref,
            gate_out_grad_ref,
            up_out_grad_ref,
            down_in_grad_ref,
            down_out_grad_ref,
        ):
            ref[...] = jnp.zeros_like(ref)

    pick = pick_ref[step]
    row_count, width = rows_ref.shape[1:]
    hidden = gate_w_ref.shape[1]
    rank = gate_out_ref.shape[1]
    blocks, tokens = rank_ref.shape[1:]
    slots = row_count // blocks
    places = lax.broadcasted_iota(jnp.int32, (slots, tokens), 0)
    held = [places == rank_ref[0, z : z + 1, :] for z in range(blocks)]
    weight = jnp.concatenate(
        [
            jnp.sum(jnp.where(held[z], weight_ref[0, z : z + 1, :], 0.0), axis=1, keepdims=True)
            for z in range(blocks)
        ],
        axis=0,
    )
    rows = rows_ref[0]
    pair = flipped_right_operand(rows, pair_in_ref[pick]).astype(BF16)
    gate_low, up_low = pair[:, :rank], pair[:, rank:]

    @pl.loop(0, hidden // tile)
    def _(j):
        columns = pl.ds(pl.multiple_of(j * tile, tile), tile)
        gate_lin = matrix_product(rows, gate_w_ref[:, columns]) + matrix_product(
            gate_low, gate_out_ref[pick, :, columns]
        )
        up_lin = matrix_product(rows, up_w_ref[:, columns]) + matrix_product(
            up_low, up_out_ref[pick, :, columns]
        )
        gate_scratch[:, columns] = gate_lin
        up_scratch[:, columns] = up_lin
        inner_scratch[:, columns] = (gate_lin * jax.nn.sigmoid(gate_lin) * up_lin).astype(BF16)

    inner = inner_scratch[...]
    down_low = flipped_right_operand(inner, down_in_ref[pick]).astype(BF16)

    def down_step(j, total):
        columns = pl.ds(pl.multiple_of(j * tile, tile), tile)
        result = (
            matrix_product(inner, down_w_ref[:, columns])
            + matrix_product(down_low, down_out_ref[pick, :, columns])
        ).astype(BF16)
        wide = result.astype(F32)
        upstream = up_rows_ref[0, :, columns].astype(F32)
        y_ref[0, :, columns] = (weight * wide).astype(BF16)
        route_scratch[:, columns] = (weight * upstream).astype(BF16)
        return total + jnp.sum(upstream * wide, axis=1, keepdims=True)

    gate_grad = lax.fori_loop(
        0, width // tile, down_step, jnp.zeros((row_count, 1), F32)
    )
    for z in range(blocks):
        gate_grad_ref[0, z : z + 1, :] = jnp.sum(
            jnp.where(held[z], gate_grad[z * slots : (z + 1) * slots], 0.0),
            axis=0,
            keepdims=True,
        )
    route = route_scratch[...]
    down_low_grad = flipped_right_operand(route, down_out_ref[pick]).astype(BF16)
    down_in_grad_ref[pick] += flipped_left_operand(down_low_grad, inner)
    down_out_grad_ref[pick] += flipped_left_operand(down_low, route)

    @pl.loop(0, hidden // tile)
    def _(j):
        columns = pl.ds(pl.multiple_of(j * tile, tile), tile)
        inner_grad = flipped_right_operand(route, down_w_ref[columns, :]) + matrix_product(
            down_low_grad, down_in_ref[pick, :, columns]
        )
        gate_lin, up_lin = gate_scratch[:, columns], up_scratch[:, columns]
        sig = jax.nn.sigmoid(gate_lin)
        gate_lin_scratch[:, columns] = (
            inner_grad * up_lin * (sig * (1.0 + gate_lin * (1.0 - sig)))
        ).astype(BF16)
        up_lin_scratch[:, columns] = (inner_grad * (gate_lin * sig)).astype(BF16)

    gate_lin_grad, up_lin_grad = gate_lin_scratch[...], up_lin_scratch[...]
    gate_low_grad = flipped_right_operand(gate_lin_grad, gate_out_ref[pick]).astype(BF16)
    up_low_grad = flipped_right_operand(up_lin_grad, up_out_ref[pick]).astype(BF16)
    gate_out_grad_ref[pick] += flipped_left_operand(gate_low, gate_lin_grad)
    up_out_grad_ref[pick] += flipped_left_operand(up_low, up_lin_grad)
    pair_grad = jnp.concatenate([gate_low_grad, up_low_grad], axis=1)
    pair_in_grad_ref[pick] += flipped_left_operand(pair_grad, rows)

    @pl.loop(0, width // tile)
    def _(j):
        columns = pl.ds(pl.multiple_of(j * tile, tile), tile)
        rows_grad_ref[0, :, columns] = (
            flipped_right_operand(gate_lin_grad, gate_w_ref[columns, :])
            + flipped_right_operand(up_lin_grad, up_w_ref[columns, :])
            + matrix_product(pair_grad, pair_in_ref[pick, :, columns])
        ).astype(BF16)


def experts(
    picks,
    rows,
    up_rows,
    ranks,
    weights,
    gate_w,
    up_w,
    down_w,
    pair_in,
    gate_out,
    up_out,
    down_in,
    down_out,
):
    sources, row_count, width = rows.shape
    hidden = gate_w.shape[1]
    adapters, rank = gate_out.shape[:2]
    token_spec = pl.BlockSpec((1,) + ranks.shape[1:], lambda s, _: (s, 0, 0))
    row_spec = pl.BlockSpec((1, row_count, width), lambda s, _: (s, 0, 0))

    def resident(array):
        return pl.BlockSpec(
            array.shape, lambda s, _: (0,) * array.ndim, pipeline_mode=pl.Buffered(1)
        )

    grads = [
        jax.ShapeDtypeStruct(shape, F32)
        for shape in (
            (adapters, 2 * rank, width),
            (adapters, rank, hidden),
            (adapters, rank, hidden),
            (adapters, rank, hidden),
            (adapters, rank, width),
        )
    ]
    return pl.pallas_call(
        functools.partial(experts_body, 256),
        grid_spec=pltpu.PrefetchScalarGridSpec(
            num_scalar_prefetch=1,
            grid=(sources,),
            in_specs=[row_spec, row_spec, token_spec, token_spec]
            + [
                resident(array)
                for array in (gate_w, up_w, down_w, pair_in, gate_out, up_out, down_in, down_out)
            ],
            out_specs=[row_spec, row_spec, token_spec]
            + [
                pl.BlockSpec(grad.shape, lambda s, _: (0, 0, 0), pipeline_mode=pl.Buffered(1))
                for grad in grads
            ],
            scratch_shapes=[
                pltpu.VMEM((row_count, hidden), F32),
                pltpu.VMEM((row_count, hidden), F32),
                pltpu.VMEM((row_count, hidden), BF16),
                pltpu.VMEM((row_count, width), BF16),
                pltpu.VMEM((row_count, hidden), BF16),
                pltpu.VMEM((row_count, hidden), BF16),
            ],
        ),
        out_shape=[
            jax.ShapeDtypeStruct(rows.shape, BF16),
            jax.ShapeDtypeStruct(rows.shape, BF16),
            jax.ShapeDtypeStruct(ranks.shape, F32),
        ]
        + grads,
        compiler_params=params(60),
        cost_estimate=pl.CostEstimate(
            flops=12 * sources * row_count * width * hidden,
            transcendentals=4 * sources * row_count * hidden,
            bytes_accessed=8 * sources * row_count * width + 6 * width * hidden,
        ),
        name="experts",
    )(
        picks,
        rows,
        up_rows,
        ranks,
        weights,
        gate_w,
        up_w,
        down_w,
        pair_in,
        gate_out,
        up_out,
        down_in,
        down_out,
    )


def per_device(
    tokens,
    segments,
    routes,
    adapter_index,
    cotangent,
    attn_gain,
    moe_gain,
    q_gain,
    key_norm_gain,
    w_query,
    key_projection_weight,
    value_projection_weight,
    w_out,
    w_router,
    expert_gate_weight,
    expert_up_weight,
    expert_down_weight,
    query_in,
    query_out,
    key_in,
    key_second_weight,
    value_in,
    value_second_weight,
    attn_in,
    attn_out,
    router_in,
    router_out,
    gate_in,
    gate_out,
    upward_in,
    upward_out,
    downward_in,
    downward_out,
):
    tensor_count = lax.axis_size("tensor")
    fsdp_count = lax.axis_size("fsdp")
    device_count = fsdp_count * tensor_count
    tensor_pos = lax.axis_index("tensor")
    fsdp_pos = lax.axis_index("fsdp")
    zero_pos = fsdp_pos * 0
    tok_rows, model_width = tokens.shape
    seq_rows = tok_rows * tensor_count
    rank = query_in.shape[2]
    adapter_count = query_in.shape[0]
    head_dim = q_gain.shape[0]
    local_cols = query_out.shape[2]
    local_kv_cols = key_second_weight.shape[2]
    expert_count = w_router.shape[1]
    top_count = routes.shape[1]
    capacity = 5 * tok_rows * top_count // (4 * expert_count)
    slots = -(-capacity // 16) * 16
    score_scale = 1.0 / math.sqrt(head_dim)
    adapter_pick = lax.dynamic_index_in_dim(adapter_index, fsdp_pos, 0, keepdims=False)

    def select_adapter(adapter_table):
        return lax.dynamic_index_in_dim(adapter_table, adapter_pick, 0, keepdims=False)

    def transposed(adapter_table):
        return jnp.swapaxes(adapter_table, -1, -2)

    input_first = jnp.concatenate(
        [select_adapter(transposed(table)) for table in (query_in, key_in, value_in)], axis=0
    )
    q_second = select_adapter(query_out)
    k_second = select_adapter(key_second_weight)
    v_second = select_adapter(value_second_weight)
    attention_first = select_adapter(transposed(attn_in))
    attention_second = select_adapter(attn_out)
    router_first = select_adapter(transposed(router_in))
    router_second = select_adapter(router_out)
    gain_attn = attn_gain.astype(F32)
    gain_moe = moe_gain.astype(F32)
    gain_query = q_gain.astype(F32)[None, :]
    gain_key = key_norm_gain.astype(F32)[None, :]

    packed_weights = lax.all_gather(
        jnp.concatenate(
            [w_query, key_projection_weight, value_projection_weight, w_router], axis=1
        ),
        "fsdp",
        axis=0,
        tiled=True,
    )
    linear_cols = local_cols + 2 * local_kv_cols
    complete_linear = packed_weights[:, :linear_cols]
    complete_router = packed_weights[:, linear_cols:]
    full_out = lax.all_gather(w_out, "fsdp", axis=1, tiled=True)
    sequence_tokens = lax.all_gather(tokens, "tensor", axis=0, tiled=True)
    sequence_routes = lax.all_gather(routes, "tensor", axis=0, tiled=True)
    sequence_cotangent = lax.all_gather(cotangent, "tensor", axis=0, tiled=True)
    plane_experts = jnp.arange(fsdp_count, dtype=jnp.int32) * tensor_count + tensor_pos
    route_blocks = sequence_routes.reshape(tensor_count, 1, tok_rows, top_count)
    plane_mask = jnp.any(route_blocks == plane_experts[None, :, None, None], axis=-1)
    plane_ranks = ranks_of(plane_mask)
    up_rows = plane_rows(
        to_slots(plane_ranks, sequence_cotangent, slots).reshape(
            fsdp_count, tensor_count * slots, model_width
        )
    )

    token_values = tokens.astype(F32)
    attn_normed, attn_factor = norm_forward(token_values, gain_attn)
    attention_narrow = attn_normed.astype(BF16)
    sequence_normalized = norm_forward(sequence_tokens.astype(F32), gain_attn)[0].astype(BF16)
    linear = matrix_product(sequence_normalized, complete_linear)
    low = flipped_right_operand(sequence_normalized, input_first).astype(BF16)
    tables = rope_tables(seq_rows, head_dim)
    seg_row = segments
    seg_column = jnp.transpose(segments, (1, 0))
    attention_operands = (
        linear,
        low,
        q_second,
        k_second,
        v_second,
        gain_query,
        gain_key,
        tables,
        seg_column,
        seg_row,
        score_scale,
    )
    heads_narrow = attention_forward(*attention_operands)
    attention_low = flipped_right_operand(heads_narrow, attention_first).astype(BF16)
    out_part = matrix_product(heads_narrow, full_out) + matrix_product(
        attention_low, attention_second
    )
    attention_total = lax.psum_scatter(
        out_part.astype(BF16), "tensor", scatter_dimension=0, tiled=True
    ).astype(F32)
    residual_stream = token_values + attention_total
    moe_normed, moe_factor = norm_forward(residual_stream, gain_moe)
    experts_narrow = moe_normed.astype(BF16)

    router_low = flipped_right_operand(experts_narrow, router_first).astype(BF16)
    router_logits = matrix_product(experts_narrow, complete_router) + matrix_product(
        router_low, router_second
    )
    expert_ids = jnp.arange(expert_count, dtype=jnp.int32)
    chosen = jnp.any(routes[:, :, None] == expert_ids[None, None, :], axis=1)
    chosen_logits = jnp.where(chosen, router_logits, -jnp.inf)
    chosen_exp = jnp.exp(chosen_logits - jnp.max(chosen_logits, axis=-1, keepdims=True))
    gate_weights = chosen_exp / jnp.sum(chosen_exp, axis=-1, keepdims=True)
    sent_weights = jnp.transpose(jnp.where(chosen, gate_weights, -1.0), (1, 0))
    own_weights = route_rows(sent_weights).reshape(fsdp_count, tensor_count, tok_rows)
    own_ranks = ranks_of(own_weights >= 0.0)

    sequence_experts = lax.all_gather(experts_narrow, "tensor", axis=0, tiled=True)
    expert_rows = plane_rows(
        to_slots(plane_ranks, sequence_experts, slots).reshape(
            fsdp_count, tensor_count * slots, model_width
        )
    )
    gate_in_t, upward_in_t = transposed(gate_in[0]), transposed(upward_in[0])
    (
        expert_output,
        rows_grad,
        gate_dots,
        pair_in_grad,
        gate_out_grad,
        upward_out_grad,
        downward_in_grad,
        downward_out_grad,
    ) = experts(
        adapter_index,
        expert_rows,
        up_rows,
        own_ranks,
        own_weights,
        expert_gate_weight[0],
        expert_up_weight[0],
        expert_down_weight[0],
        jnp.concatenate([gate_in_t, upward_in_t], axis=1),
        gate_out[0],
        upward_out[0],
        transposed(downward_in[0]),
        downward_out[0],
    )
    gate_grad = jnp.transpose(
        route_rows(gate_dots.reshape(device_count, tok_rows)), (1, 0)
    )

    def returned(slotted):
        combined = from_slots(
            plane_ranks,
            plane_rows(slotted).reshape(fsdp_count, tensor_count, slots, model_width),
        )
        return lax.psum_scatter(combined, "tensor", scatter_dimension=0, tiled=True).astype(F32)

    moe_grad = returned(rows_grad)
    output = (residual_stream + returned(expert_output)).astype(BF16)

    out_grad = cotangent.astype(F32)
    logit_gradient = (
        gate_weights * (gate_grad - jnp.sum(gate_weights * gate_grad, axis=-1, keepdims=True))
    ).astype(BF16)
    router_low_gradient = flipped_right_operand(logit_gradient, router_second).astype(BF16)
    moe_grad = (
        moe_grad
        + flipped_right_operand(logit_gradient, complete_router)
        + matrix_product(router_low_gradient, router_first)
    )
    router_first_gradient = flipped_left_operand(router_low_gradient, experts_narrow)
    router_second_gradient = flipped_left_operand(router_low, logit_gradient)
    residual_grad = out_grad + norm_backward(residual_stream, moe_factor, gain_moe, moe_grad)

    sequence_branch = lax.all_gather(
        residual_grad.astype(BF16), "tensor", axis=0, tiled=True
    )
    attention_low_grad = flipped_right_operand(sequence_branch, attention_second).astype(BF16)
    attention_second_gradient = flipped_left_operand(attention_low, sequence_branch)
    heads_grad = flipped_right_operand(sequence_branch, full_out)
    (
        q_grad,
        k_grad,
        v_grad,
        low_share,
        q_second_gradient,
        k_second_gradient,
        v_second_gradient,
        attention_first_gradient,
    ) = attention_backward(
        *attention_operands,
        heads_narrow,
        heads_grad,
        attention_low_grad,
        attention_first,
    )
    linear_grad = jnp.concatenate([q_grad, k_grad, v_grad], axis=1)
    normed_part = flipped_right_operand(linear_grad, complete_linear) + matrix_product(
        low_share, input_first
    )
    input_first_gradient = flipped_left_operand(low_share, sequence_normalized)
    normalized_gradient = lax.psum_scatter(
        normed_part.astype(BF16), "tensor", scatter_dimension=0, tiled=True
    ).astype(F32)
    input_grad = residual_grad + norm_backward(
        token_values, attn_factor, gain_attn, normalized_gradient
    )

    source_adapter = jnp.repeat(adapter_index, tensor_count)
    owner_onehot = (
        jnp.arange(adapter_count, dtype=jnp.int32)[:, None] == source_adapter[None, :]
    ).astype(BF16)

    def to_all(addend):
        lines = addend.shape[0]
        return jnp.transpose(
            addend.astype(BF16).reshape(lines, device_count, -1), (1, 0, 2)
        ).reshape(device_count, -1)

    def to_head_owners(addend):
        lines = addend.shape[0]
        pieces = jnp.transpose(
            addend.astype(BF16).reshape(lines, fsdp_count, -1), (1, 0, 2)
        ).reshape(fsdp_count, -1)
        holder = jnp.zeros((device_count, pieces.shape[1]), BF16)
        return lax.dynamic_update_slice(holder, pieces, (tensor_pos * fsdp_count, zero_pos))

    def owner_sums(parts):
        widths = [part.shape[1] for part in parts]
        total = matrix_product(owner_onehot, route_rows(jnp.concatenate(parts, axis=1)))
        pieces = []
        start = 0
        for width in widths:
            pieces.append(total[:, start : start + width])
            start += width
        return pieces

    early = owner_sums(
        [
            to_all(router_first_gradient),
            to_all(attention_second_gradient),
            to_all(router_second_gradient),
        ]
    )
    late = owner_sums(
        [
            to_all(input_first_gradient),
            to_head_owners(q_second_gradient),
            to_head_owners(k_second_gradient),
            to_head_owners(v_second_gradient),
            to_head_owners(attention_first_gradient),
        ]
    )

    def lines_of(piece, lines):
        return piece.reshape(adapter_count, lines, -1)

    first_sums = lines_of(late[0], 3 * rank)
    return (
        output,
        input_grad,
        transposed(first_sums[:, :rank]),
        lines_of(late[1], rank),
        transposed(first_sums[:, rank : 2 * rank]),
        lines_of(late[2], rank),
        transposed(first_sums[:, 2 * rank :]),
        lines_of(late[3], rank),
        transposed(lines_of(late[4], rank)),
        lines_of(early[1], rank),
        transposed(lines_of(early[0], rank)),
        lines_of(early[2], rank),
        transposed(pair_in_grad[:, :rank])[None],
        gate_out_grad[None],
        transposed(pair_in_grad[:, rank:])[None],
        upward_out_grad[None],
        transposed(downward_in_grad)[None],
        downward_out_grad[None],
    )


def solution(mesh):
    placed = (
        P(("fsdp", "tensor"), None),
        P("fsdp", None),
        P(("fsdp", "tensor"), None),
        P(),
        P(("fsdp", "tensor"), None),
        P(),
        P(),
        P(),
        P(),
        P("fsdp", "tensor"),
        P("fsdp", "tensor"),
        P("fsdp", "tensor"),
        P("tensor", "fsdp"),
        P("fsdp", None),
        P(("fsdp", "tensor"), None, None),
        P(("fsdp", "tensor"), None, None),
        P(("fsdp", "tensor"), None, None),
        P(),
        P(None, None, "tensor"),
        P(),
        P(None, None, "tensor"),
        P(),
        P(None, None, "tensor"),
        P(None, "tensor", None),
        P(),
        P(),
        P(),
        P(("fsdp", "tensor"), None, None, None),
        P(("fsdp", "tensor"), None, None, None),
        P(("fsdp", "tensor"), None, None, None),
        P(("fsdp", "tensor"), None, None, None),
        P(("fsdp", "tensor"), None, None, None),
        P(("fsdp", "tensor"), None, None, None),
    )
    return jax.shard_map(
        per_device,
        mesh=mesh,
        in_specs=placed,
        out_specs=(
            P(("fsdp", "tensor"), None),
            P(("fsdp", "tensor"), None),
            P(None, ("fsdp", "tensor"), None),
            P(None, None, ("fsdp", "tensor")),
            P(None, ("fsdp", "tensor"), None),
            P(None, None, ("fsdp", "tensor")),
            P(None, ("fsdp", "tensor"), None),
            P(None, None, ("fsdp", "tensor")),
            P(None, ("fsdp", "tensor"), None),
            P(None, None, ("fsdp", "tensor")),
            P(None, ("fsdp", "tensor"), None),
            P(None, None, ("fsdp", "tensor")),
            P(("fsdp", "tensor"), None, None, None),
            P(("fsdp", "tensor"), None, None, None),
            P(("fsdp", "tensor"), None, None, None),
            P(("fsdp", "tensor"), None, None, None),
            P(("fsdp", "tensor"), None, None, None),
            P(("fsdp", "tensor"), None, None, None),
        ),
        check_vma=False,
    )
```

```python
import functools
import math

import jax
import jax.numpy as jnp
from jax import lax
from jax.experimental import pallas as pl
from jax.experimental.pallas import tpu as pltpu
from jax.sharding import PartitionSpec as P

NORM_EPSILON = 1e-06
ROPE_THETA = 1000000.0
BF16 = jnp.bfloat16
F32 = jnp.float32
WINDOW = 256
MEBI = 1 << 20


def matrix_product(first_op, second_op):
    return jnp.dot(first_op, second_op, preferred_element_type=F32)


def flipped_left_operand(first_op, second_op):
    return lax.dot_general(
        first_op, second_op, (((0,), (0,)), ((), ())), preferred_element_type=F32
    )


def flipped_right_operand(first_op, second_op):
    return lax.dot_general(
        first_op, second_op, (((1,), (1,)), ((), ())), preferred_element_type=F32
    )


def norm_forward(values, gain_vec):
    factor = lax.rsqrt(jnp.mean(values * values, axis=-1, keepdims=True) + NORM_EPSILON)
    return (values * factor * gain_vec, factor)


def norm_backward(values, factor, gain_vec, upstream):
    scaled = upstream * gain_vec
    return factor * scaled - values * (factor * factor * factor) * jnp.mean(
        values * scaled, axis=-1, keepdims=True
    )


def rope_tables(sequence_length, head_width):
    half_width = head_width // 2
    inverse = jnp.power(ROPE_THETA, -2.0 * jnp.arange(half_width, dtype=F32) / head_width)
    angles = jnp.arange(sequence_length, dtype=F32)[:, None] * inverse[None, :]
    cosine, sine = jnp.cos(angles), jnp.sin(angles)
    return (
        jnp.concatenate([cosine, cosine], axis=1),
        jnp.concatenate([-sine, sine], axis=1),
    )


def swapped(values):
    return pltpu.roll(values, values.shape[-1] // 2, 1)


def route_rows(block_rows):
    return lax.all_to_all(block_rows, ("fsdp", "tensor"), split_axis=0, concat_axis=0, tiled=True)


def plane_rows(block_rows):
    return lax.all_to_all(block_rows, "fsdp", split_axis=0, concat_axis=0, tiled=True)


def params(mebibytes, axes=1):
    return pltpu.CompilerParams(
        vmem_limit_bytes=mebibytes * MEBI, dimension_semantics=("arbitrary",) * axes
    )


def whole(shape):
    rank = len(shape)
    return pl.BlockSpec(shape, lambda *_: (0,) * rank)


def head_values(linear, low, second, gain, cosine, sine):
    values = linear + matrix_product(low, second)
    normed, factor = norm_forward(values, gain)
    turned = (normed * cosine + swapped(normed) * sine).astype(BF16)
    return values, factor, turned


def head_values_gradient(values, factor, gain, cosine, sine, upstream):
    back = upstream * cosine - swapped(upstream) * sine
    return norm_backward(values, factor, gain, back).astype(BF16)


def allowed_keys(block, start, width, seg_column, seg_row):
    rows = block * WINDOW + lax.broadcasted_iota(jnp.int32, (WINDOW, width), 0)
    keys = start + lax.broadcasted_iota(jnp.int32, (WINDOW, width), 1)
    mine = seg_column[block * WINDOW : (block + 1) * WINDOW]
    theirs = seg_row[:, start : start + width]
    return (keys == rows) | ((keys < rows) & (mine == theirs) & (theirs != 0))


def block_bounds(block):
    start = max(block - 1, 0) * WINDOW
    return start, (block + 1) * WINDOW - start


def attention_forward_body(
    rank,
    scale,
    lin_ref,
    key_lin_ref,
    value_lin_ref,
    low_ref,
    q_second_ref,
    k_second_ref,
    v_second_ref,
    q_gain_ref,
    k_gain_ref,
    cos_ref,
    sin_ref,
    seg_column_ref,
    seg_row_ref,
    heads_ref,
    key_scratch,
    value_scratch,
):
    cosine, sine = cos_ref[...], sin_ref[...]

    @pl.when(pl.program_id(0) == 0)
    def _():
        key_scratch[...] = head_values(
            key_lin_ref[...],
            low_ref[:, rank : 2 * rank],
            k_second_ref[...],
            k_gain_ref[...],
            cosine,
            sine,
        )[2]
        value_scratch[...] = (
            value_lin_ref[...]
            + matrix_product(low_ref[:, 2 * rank : 3 * rank], v_second_ref[...])
        ).astype(BF16)

    query = head_values(
        lin_ref[...], low_ref[:, :rank], q_second_ref[...], q_gain_ref[...], cosine, sine
    )[2]
    seg_column, seg_row = seg_column_ref[...], seg_row_ref[...]
    for block in range(query.shape[0] // WINDOW):
        start, width = block_bounds(block)
        rows = pl.ds(block * WINDOW, WINDOW)
        scores = (
            flipped_right_operand(
                query[block * WINDOW : (block + 1) * WINDOW], key_scratch[pl.ds(start, width)]
            )
            * scale
        )
        scores = jnp.where(
            allowed_keys(block, start, width, seg_column, seg_row), scores, -1e30
        )
        expo = jnp.exp(scores - jnp.max(scores, axis=-1, keepdims=True))
        probs = (expo / jnp.sum(expo, axis=-1, keepdims=True)).astype(BF16)
        heads_ref[rows, :] = matrix_product(probs, value_scratch[pl.ds(start, width)]).astype(
            BF16
        )


def attention_forward(
    linear, low, q_second, k_second, v_second, q_gain, k_gain, tables, seg_column, seg_row, scale
):
    rows, head_dim = linear.shape[0], q_gain.shape[1]
    heads = q_second.shape[1] // head_dim
    rank = q_second.shape[0]
    column = pl.BlockSpec((rows, head_dim), lambda h: (0, h))
    return pl.pallas_call(
        functools.partial(attention_forward_body, rank, scale),
        grid=(heads,),
        out_shape=jax.ShapeDtypeStruct((rows, heads * head_dim), BF16),
        in_specs=[
            column,
            pl.BlockSpec((rows, head_dim), lambda h: (0, heads)),
            pl.BlockSpec((rows, head_dim), lambda h: (0, heads + 1)),
            whole(low.shape),
            pl.BlockSpec((rank, head_dim), lambda h: (0, h)),
            whole(k_second.shape),
            whole(v_second.shape),
            whole(q_gain.shape),
            whole(k_gain.shape),
            whole(tables[0].shape),
            whole(tables[1].shape),
            whole(seg_column.shape),
            whole(seg_row.shape),
        ],
        out_specs=column,
        scratch_shapes=[pltpu.VMEM((rows, head_dim), BF16), pltpu.VMEM((rows, head_dim), BF16)],
        compiler_params=params(40),
        cost_estimate=pl.CostEstimate(
            flops=8 * heads * rows * WINDOW * head_dim,
            transcendentals=2 * heads * rows * WINDOW,
            bytes_accessed=6 * rows * heads * head_dim,
        ),
        name="attention_forward",
    )(
        linear,
        linear,
        linear,
        low,
        q_second,
        k_second,
        v_second,
        q_gain,
        k_gain,
        *tables,
        seg_column,
        seg_row,
    )


def attention_backward_body(
    rank,
    scale,
    lin_ref,
    key_lin_ref,
    value_lin_ref,
    low_ref,
    q_second_ref,
    k_second_ref,
    v_second_ref,
    q_gain_ref,
    k_gain_ref,
    cos_ref,
    sin_ref,
    seg_column_ref,
    seg_row_ref,
    heads_ref,
    heads_grad_ref,
    low_grad_ref,
    down_ref,
    q_grad_ref,
    k_grad_ref,
    v_grad_ref,
    share_ref,
    q_second_grad_ref,
    k_second_grad_ref,
    v_second_grad_ref,
    down_grad_ref,
    key_scratch,
    value_scratch,
    key_sum,
    value_sum,
    query_sum,
    share_sum,
):
    cosine, sine = cos_ref[...], sin_ref[...]
    head = pl.program_id(0)

    @pl.when(head == 0)
    def _():
        key_scratch[...] = head_values(
            key_lin_ref[...],
            low_ref[:, rank : 2 * rank],
            k_second_ref[...],
            k_gain_ref[...],
            cosine,
            sine,
        )[2]
        value_scratch[...] = (
            value_lin_ref[...]
            + matrix_product(low_ref[:, 2 * rank : 3 * rank], v_second_ref[...])
        ).astype(BF16)
        key_sum[...] = jnp.zeros_like(key_sum)
        value_sum[...] = jnp.zeros_like(value_sum)
        share_sum[...] = jnp.zeros_like(share_sum)

    low_q = low_ref[:, :rank]
    values, factor, query = head_values(
        lin_ref[...], low_q, q_second_ref[...], q_gain_ref[...], cosine, sine
    )
    low_grad = low_grad_ref[...]
    upstream = (heads_grad_ref[...] + matrix_product(low_grad, down_ref[...])).astype(BF16)
    down_grad_ref[...] = flipped_left_operand(low_grad, heads_ref[...])
    seg_column, seg_row = seg_column_ref[...], seg_row_ref[...]
    for block in range(query.shape[0] // WINDOW):
        start, width = block_bounds(block)
        rows = pl.ds(block * WINDOW, WINDOW)
        keys = pl.ds(start, width)
        query_block = query[block * WINDOW : (block + 1) * WINDOW]
        upstream_block = upstream[block * WINDOW : (block + 1) * WINDOW]
        scores = flipped_right_operand(query_block, key_scratch[keys]) * scale
        scores = jnp.where(
            allowed_keys(block, start, width, seg_column, seg_row), scores, -1e30
        )
        expo = jnp.exp(scores - jnp.max(scores, axis=-1, keepdims=True))
        probs = expo / jnp.sum(expo, axis=-1, keepdims=True)
        prob_grad = flipped_right_operand(upstream_block, value_scratch[keys])
        score_grad = (
            probs * (prob_grad - jnp.sum(probs * prob_grad, axis=-1, keepdims=True))
        ).astype(BF16)
        value_sum[keys, :] += flipped_left_operand(probs.astype(BF16), upstream_block)
        key_sum[keys, :] += flipped_left_operand(score_grad, query_block)
        query_sum[rows, :] = matrix_product(score_grad, key_scratch[keys]) * scale
    q_grad = head_values_gradient(
        values, factor, q_gain_ref[...], cosine, sine, query_sum[...]
    )
    q_grad_ref[...] = q_grad
    q_second_grad_ref[...] = flipped_left_operand(low_q, q_grad)
    share_sum[:, :rank] += flipped_right_operand(q_grad, q_second_ref[...])

    @pl.when(head == pl.num_programs(0) - 1)
    def _():
        low_k = low_ref[:, rank : 2 * rank]
        low_v = low_ref[:, 2 * rank : 3 * rank]
        key_values, key_factor, _turned = head_values(
            key_lin_ref[...], low_k, k_second_ref[...], k_gain_ref[...], cosine, sine
        )
        k_grad = head_values_gradient(
            key_values, key_factor, k_gain_ref[...], cosine, sine, key_sum[...] * scale
        )
        v_grad = value_sum[...].astype(BF16)
        k_grad_ref[...] = k_grad
        v_grad_ref[...] = v_grad
        k_second_grad_ref[...] = flipped_left_operand(low_k, k_grad)
        v_second_grad_ref[...] = flipped_left_operand(low_v, v_grad)
        share_sum[:, rank : 2 * rank] = flipped_right_operand(k_grad, k_second_ref[...])
        share_sum[:, 2 * rank : 3 * rank] = flipped_right_operand(v_grad, v_second_ref[...])
        share_ref[...] = share_sum[...].astype(BF16)


def attention_backward(
    linear,
    low,
    q_second,
    k_second,
    v_second,
    q_gain,
    k_gain,
    tables,
    seg_column,
    seg_row,
    scale,
    heads_low,
    heads_grad,
    low_grad,
    down_first,
):
    rows, head_dim = linear.shape[0], q_gain.shape[1]
    rank, columns = q_second.shape
    heads = columns // head_dim
    column = pl.BlockSpec((rows, head_dim), lambda h: (0, h))
    narrow = pl.BlockSpec((rank, head_dim), lambda h: (0, h))
    single = (rows, head_dim)
    return pl.pallas_call(
        functools.partial(attention_backward_body, rank, scale),
        grid=(heads,),
        out_shape=(
            jax.ShapeDtypeStruct((rows, columns), BF16),
            jax.ShapeDtypeStruct(single, BF16),
            jax.ShapeDtypeStruct(single, BF16),
            jax.ShapeDtypeStruct((rows, 3 * rank), BF16),
            jax.ShapeDtypeStruct((rank, columns), F32),
            jax.ShapeDtypeStruct((rank, head_dim), F32),
            jax.ShapeDtypeStruct((rank, head_dim), F32),
            jax.ShapeDtypeStruct((rank, columns), F32),
        ),
        in_specs=[
            column,
            pl.BlockSpec((rows, head_dim), lambda h: (0, heads)),
            pl.BlockSpec((rows, head_dim), lambda h: (0, heads + 1)),
            whole(low.shape),
            narrow,
            whole(k_second.shape),
            whole(v_second.shape),
            whole(q_gain.shape),
            whole(k_gain.shape),
            whole(tables[0].shape),
            whole(tables[1].shape),
            whole(seg_column.shape),
            whole(seg_row.shape),
            column,
            column,
            whole(low_grad.shape),
            narrow,
        ],
        out_specs=(
            column,
            whole(single),
            whole(single),
            whole((rows, 3 * rank)),
            narrow,
            whole((rank, head_dim)),
            whole((rank, head_dim)),
            narrow,
        ),
        scratch_shapes=[
            pltpu.VMEM(single, BF16),
            pltpu.VMEM(single, BF16),
            pltpu.VMEM(single, F32),
            pltpu.VMEM(single, F32),
            pltpu.VMEM(single, F32),
            pltpu.VMEM((rows, 3 * rank), F32),
        ],
        compiler_params=params(48),
        cost_estimate=pl.CostEstimate(
            flops=20 * heads * rows * WINDOW * head_dim,
            transcendentals=2 * heads * rows * WINDOW,
            bytes_accessed=12 * rows * columns,
        ),
        name="attention_backward",
    )(
        linear,
        linear,
        linear,
        low,
        q_second,
        k_second,
        v_second,
        q_gain,
        k_gain,
        *tables,
        seg_column,
        seg_row,
        heads_low,
        heads_grad,
        low_grad,
        down_first,
    )


def slot_choice(ranks, slots):
    experts, tokens = ranks.shape
    places = lax.broadcasted_iota(jnp.int32, (slots, tokens), 0)
    return jnp.concatenate(
        [(places == ranks[e : e + 1, :]).astype(F32) for e in range(experts)], axis=0
    ).astype(BF16)


def to_slots_body(_block_ref, rank_ref, rows_ref, out_ref):
    slots = out_ref.shape[1]
    chosen = matrix_product(slot_choice(rank_ref[0], slots), rows_ref[...])
    out_ref[...] = chosen.astype(BF16).reshape(out_ref.shape)


def to_slots(block, ranks, rows, slots):
    experts, tokens = ranks.shape[1:]
    width = rows.shape[1]
    half = width // 2
    return pl.pallas_call(
        to_slots_body,
        grid_spec=pltpu.PrefetchScalarGridSpec(
            num_scalar_prefetch=1,
            grid=(2,),
            in_specs=[
                pl.BlockSpec((1, experts, tokens), lambda j, at: (at[0], 0, 0)),
                pl.BlockSpec((tokens, half), lambda j, at: (0, j)),
            ],
            out_specs=pl.BlockSpec((experts, slots, half), lambda j, at: (0, 0, j)),
        ),
        out_shape=jax.ShapeDtypeStruct((experts, slots, width), BF16),
        compiler_params=params(32),
        cost_estimate=pl.CostEstimate(
            flops=2 * experts * slots * tokens * width,
            transcendentals=0,
            bytes_accessed=2 * width * (experts * slots + tokens),
        ),
        name="to_slots",
    )(block, ranks, rows)


def from_slots_body(_block_ref, rank_ref, slot_ref, out_ref):
    experts, slots, width = slot_ref.shape
    choice = slot_choice(rank_ref[0], slots)
    out_ref[...] = flipped_left_operand(
        choice, slot_ref[...].reshape(experts * slots, width)
    ).astype(BF16)


def from_slots(block, ranks, slotted):
    experts, tokens = ranks.shape[1:]
    slots, width = slotted.shape[1:]
    half = width // 2
    return pl.pallas_call(
        from_slots_body,
        grid_spec=pltpu.PrefetchScalarGridSpec(
            num_scalar_prefetch=1,
            grid=(2,),
            in_specs=[
                pl.BlockSpec((1, experts, tokens), lambda j, at: (at[0], 0, 0)),
                pl.BlockSpec((experts, slots, half), lambda j, at: (0, 0, j)),
            ],
            out_specs=pl.BlockSpec((tokens, half), lambda j, at: (0, j)),
        ),
        out_shape=jax.ShapeDtypeStruct((tokens, width), BF16),
        compiler_params=params(32),
        cost_estimate=pl.CostEstimate(
            flops=2 * experts * slots * tokens * width,
            transcendentals=0,
            bytes_accessed=2 * width * (experts * slots + tokens),
        ),
        name="from_slots",
    )(block, ranks, slotted)


def all_to_slots_body(rank_ref, rows_ref, out_ref):
    slots = out_ref.shape[2]
    chosen = matrix_product(slot_choice(rank_ref[0], slots), rows_ref[...])
    out_ref[...] = chosen.astype(BF16).reshape(out_ref.shape)


def all_to_slots(ranks, rows, slots):
    blocks, experts, tokens = ranks.shape
    width = rows.shape[1]
    return pl.pallas_call(
        all_to_slots_body,
        grid=(blocks,),
        out_shape=jax.ShapeDtypeStruct((experts, blocks, slots, width), BF16),
        in_specs=[
            pl.BlockSpec((1, experts, tokens), lambda z: (z, 0, 0)),
            pl.BlockSpec((tokens, width), lambda z: (z, 0)),
        ],
        out_specs=pl.BlockSpec((experts, 1, slots, width), lambda z: (0, z, 0, 0)),
        compiler_params=params(40),
        cost_estimate=pl.CostEstimate(
            flops=2 * blocks * experts * slots * tokens * width,
            transcendentals=0,
            bytes_accessed=2 * blocks * width * (experts * slots + tokens),
        ),
        name="all_to_slots",
    )(ranks, rows)


def all_from_slots_body(_start_ref, rank_ref, slot_ref, out_ref):
    experts, _, slots, width = slot_ref.shape
    choice = slot_choice(rank_ref[0], slots)
    out_ref[...] = flipped_left_operand(
        choice, slot_ref[...].reshape(experts * slots, width)
    ).astype(BF16)


def all_from_slots(start, ranks, slotted):
    blocks, experts, tokens = ranks.shape
    slots, width = slotted.shape[2:]
    return pl.pallas_call(
        all_from_slots_body,
        grid_spec=pltpu.PrefetchScalarGridSpec(
            num_scalar_prefetch=1,
            grid=(blocks,),
            in_specs=[
                pl.BlockSpec((1, experts, tokens), lambda z, at: ((at[0] + z) % blocks, 0, 0)),
                pl.BlockSpec((experts, 1, slots, width), lambda z, at: (0, z, 0, 0)),
            ],
            out_specs=pl.BlockSpec((tokens, width), lambda z, at: ((at[0] + z) % blocks, 0)),
        ),
        out_shape=jax.ShapeDtypeStruct((blocks * tokens, width), BF16),
        compiler_params=params(40),
        cost_estimate=pl.CostEstimate(
            flops=2 * blocks * experts * slots * tokens * width,
            transcendentals=0,
            bytes_accessed=2 * blocks * width * (experts * slots + tokens),
        ),
        name="all_from_slots",
    )(start, ranks, slotted)


def ranks_of(mask):
    tokens = mask.shape[-1]
    order = jnp.arange(tokens, dtype=jnp.int32)
    before = (order[:, None] < order[None, :]).astype(BF16)
    counts = matrix_product(mask.astype(BF16), before)
    return jnp.where(mask, counts, -1.0).astype(jnp.int32)


def tiles(width, tile, body):
    @pl.loop(0, width // tile)
    def _(j):
        body(pl.ds(pl.multiple_of(j * tile, tile), tile))


def expert_math(
    tile, rows_ref, up_ref, ranks, weights, keep_dots, sent_y, mask_ref, tables, sums, scratch
):
    gate_w, up_w, down_w, pair_in, gate_out, up_out, down_in, down_out = tables
    pair_in_sum, gate_out_sum, up_out_sum, down_in_sum, down_out_sum = sums
    gate_lin_ref, up_lin_ref, inner_ref, route_ref, gate_grad_ref, up_grad_ref = scratch
    sources, slots, width = rows_ref.shape
    row_count = sources * slots
    hidden = gate_w.shape[1]
    broad = gate_out.shape[0]
    places = lax.broadcasted_iota(jnp.int32, (slots, ranks.shape[1]), 0)

    def held(source):
        return places == ranks[source : source + 1, :]

    def all_rows():
        return rows_ref[...].reshape(row_count, width)

    def pair_mask():
        mask = mask_ref[...].astype(F32)
        return jnp.concatenate([mask, mask], axis=1)

    weight = jnp.concatenate(
        [
            jnp.sum(
                jnp.where(held(source), weights[source : source + 1, :], 0.0),
                axis=1,
                keepdims=True,
            )
            for source in range(sources)
        ],
        axis=0,
    )
    pair = (flipped_right_operand(all_rows(), pair_in[...]) * pair_mask()).astype(BF16)
    gate_low, up_low = pair[:, :broad], pair[:, broad:]

    def inner_step(columns):
        rows = all_rows()
        gate_lin = matrix_product(rows, gate_w[:, columns]) + matrix_product(
            gate_low, gate_out[:, columns]
        )
        up_lin = matrix_product(rows, up_w[:, columns]) + matrix_product(
            up_low, up_out[:, columns]
        )
        gate_lin_ref[:, columns] = gate_lin
        up_lin_ref[:, columns] = up_lin
        inner_ref[:, columns] = (gate_lin * jax.nn.sigmoid(gate_lin) * up_lin).astype(BF16)

    tiles(hidden, tile, inner_step)
    down_low = (
        flipped_right_operand(inner_ref[...], down_in[...]) * mask_ref[...].astype(F32)
    ).astype(BF16)

    def down_step(j, total):
        columns = pl.ds(pl.multiple_of(j * tile, tile), tile)
        result = (
            matrix_product(inner_ref[...], down_w[:, columns])
            + matrix_product(down_low, down_out[:, columns])
        ).astype(BF16)
        wide = result.astype(F32)
        upstream = up_ref[:, :, columns].reshape(row_count, tile).astype(F32)
        up_ref[:, :, columns] = (weight * wide).astype(BF16).reshape(sources, slots, tile)
        route_ref[:, columns] = (weight * upstream).astype(BF16)
        return total + jnp.sum(upstream * wide, axis=1, keepdims=True)

    gate_dots = lax.fori_loop(0, width // tile, down_step, jnp.zeros((row_count, 1), F32))
    sent_y()
    for source in range(sources):
        keep_dots(
            source,
            jnp.sum(
                jnp.where(held(source), gate_dots[source * slots : (source + 1) * slots], 0.0),
                axis=0,
                keepdims=True,
            ),
        )
    down_low_grad = (
        flipped_right_operand(route_ref[...], down_out[...]) * mask_ref[...].astype(F32)
    ).astype(BF16)
    down_in_sum[...] += flipped_left_operand(down_low_grad, inner_ref[...])

    def down_out_step(columns):
        down_out_sum[:, columns] += flipped_left_operand(down_low, route_ref[:, columns])

    tiles(width, 2 * tile, down_out_step)

    def inner_grad_step(columns):
        inner_grad = flipped_right_operand(route_ref[...], down_w[columns, :]) + matrix_product(
            down_low_grad, down_in[:, columns]
        )
        gate_lin, up_lin = gate_lin_ref[:, columns], up_lin_ref[:, columns]
        sig = jax.nn.sigmoid(gate_lin)
        gate_grad_ref[:, columns] = (
            inner_grad * up_lin * (sig * (1.0 + gate_lin * (1.0 - sig)))
        ).astype(BF16)
        up_grad_ref[:, columns] = (inner_grad * (gate_lin * sig)).astype(BF16)

    tiles(hidden, tile, inner_grad_step)
    pair_grad = (
        jnp.concatenate(
            [
                flipped_right_operand(gate_grad_ref[...], gate_out[...]),
                flipped_right_operand(up_grad_ref[...], up_out[...]),
            ],
            axis=1,
        )
        * pair_mask()
    ).astype(BF16)
    gate_out_sum[...] += flipped_left_operand(gate_low, gate_grad_ref[...])
    up_out_sum[...] += flipped_left_operand(up_low, up_grad_ref[...])

    def rows_grad_step(columns):
        before = rows_ref[:, :, columns].reshape(row_count, tile)
        pair_in_sum[:, columns] += flipped_left_operand(pair_grad, before)
        rows_ref[:, :, columns] = (
            (
                flipped_right_operand(gate_grad_ref[...], gate_w[columns, :])
                + flipped_right_operand(up_grad_ref[...], up_w[columns, :])
                + matrix_product(pair_grad, pair_in[:, columns])
            )
            .astype(BF16)
            .reshape(sources, slots, tile)
        )

    tiles(width, tile, rows_grad_step)


def expert_sums(tables):
    gate_w, _up_w, _down_w, pair_in, gate_out, _up_out, down_in, down_out = tables
    return [
        jax.ShapeDtypeStruct(table.shape, F32)
        for table in (pair_in, gate_out, gate_out, down_in, down_out)
    ]


def expert_scratch(row_count, hidden, width):
    return [
        pltpu.VMEM((row_count, hidden), F32),
        pltpu.VMEM((row_count, hidden), F32),
        pltpu.VMEM((row_count, hidden), BF16),
        pltpu.VMEM((row_count, width), BF16),
        pltpu.VMEM((row_count, hidden), BF16),
        pltpu.VMEM((row_count, hidden), BF16),
    ]


def experts_body(_block_ref, rows_in, up_in, rank_ref, weight_ref, mask_ref, *rest):
    tables, sums_before, rest = rest[:8], rest[8:13], rest[13:]
    y_ref, rows_grad_ref, dots_ref = rest[:3]
    sums, rest = rest[3:8], rest[8:]
    for total, before in zip(sums, sums_before):
        total[...] = before[...]
    rows_grad_ref[...] = rows_in[...]
    y_ref[...] = up_in[...]

    def keep_dots(source, dots):
        dots_ref[source : source + 1, :] = dots

    expert_math(
        256,
        rows_grad_ref,
        y_ref,
        rank_ref[0],
        weight_ref[0],
        keep_dots,
        lambda: None,
        mask_ref,
        tables,
        sums,
        rest,
    )


def experts(block, rows, up_rows, ranks, weights, mask, tables, sums_before):
    sources, slots, width = rows.shape
    hidden = tables[0].shape[1]
    tokens = ranks.shape[2]
    token_spec = pl.BlockSpec((1, sources, tokens), lambda _, at: (at[0], 0, 0))

    def resident(array):
        return pl.BlockSpec(
            array.shape, lambda *_: (0,) * len(array.shape), pipeline_mode=pl.Buffered(1)
        )

    sums = expert_sums(tables)
    outs = [
        jax.ShapeDtypeStruct(rows.shape, BF16),
        jax.ShapeDtypeStruct(rows.shape, BF16),
        jax.ShapeDtypeStruct((sources, tokens), F32),
    ] + sums
    operands = [rows, up_rows, ranks, weights, mask, *tables, *sums_before]
    specs = (
        [resident(rows), resident(up_rows), token_spec, token_spec, resident(mask)]
        + [resident(table) for table in tables]
        + [resident(each) for each in sums_before]
    )
    return pl.pallas_call(
        experts_body,
        grid_spec=pltpu.PrefetchScalarGridSpec(
            num_scalar_prefetch=1,
            grid=(1,),
            in_specs=specs,
            out_specs=[resident(out) for out in outs],
            scratch_shapes=expert_scratch(sources * slots, hidden, width),
        ),
        out_shape=outs,
        input_output_aliases={
            1 + len(operands) - len(sums) + at: 3 + at for at in range(len(sums))
        },
        compiler_params=params(63),
        name="experts",
    )(block, *operands)


def moe_body(
    plane,
    line,
    own_ref,
    up_hbm,
    plane_rank_ref,
    rank_ref,
    weight_ref,
    mask_ref,
    *rest,
):
    tables_hbm, rest = rest[:8], rest[8:]
    total_ref, dots_ref, y_hbm, back_hbm = rest[:4]
    sums, rest = rest[4:9], rest[9:]
    tables, rest = rest[:8], rest[8:]
    (
        blocks,
        partials,
        partials_in,
        sent_slots,
        rows,
        up_rows,
        back_rows,
        choice,
        dots,
        dots_back,
        dots_pass,
        dots_in,
    ) = rest[:12]
    scratch, rest = rest[12:18], rest[18:]
    (
        table_sem,
        up_sem,
        y_sem,
        back_sem,
        own_sem,
        block_send,
        block_recv,
        row_send,
        row_recv,
        back_send,
        back_recv,
        partial_send,
        partial_recv,
        dots_send,
        dots_recv,
        dots_in_send,
        dots_in_recv,
    ) = rest
    width = own_ref.shape[1]
    slots = rows.shape[2]
    tile = 256
    me, at_line = lax.axis_index("fsdp"), lax.axis_index("tensor")

    barrier = pltpu.get_barrier_semaphore()

    @pl.loop(1, plane)
    def _(d):
        pl.semaphore_signal(barrier, inc=1, device_id={"fsdp": lax.rem(me + d, plane)})

    @pl.loop(1, line)
    def _(d):
        pl.semaphore_signal(barrier, inc=1, device_id={"tensor": lax.rem(at_line + d, line)})

    pl.semaphore_wait(barrier, plane + line - 2)

    def block_copy(r):
        return pltpu.make_async_remote_copy(
            src_ref=own_ref,
            dst_ref=blocks.at[r],
            send_sem=block_send.at[r - 1],
            recv_sem=block_recv.at[r - 1],
            device_id={"tensor": lax.rem(at_line + line - r, line)},
        )

    def row_copy(r, d):
        target = lax.rem(me + d, plane)
        return pltpu.make_async_remote_copy(
            src_ref=sent_slots.at[lax.rem(r, 2), target],
            dst_ref=rows.at[r, me],
            send_sem=row_send.at[r, d],
            recv_sem=row_recv.at[r, d],
            device_id={"fsdp": target},
        )

    def own_rows(r):
        return pltpu.make_async_copy(
            sent_slots.at[lax.rem(r, 2), me], rows.at[r, me], own_sem.at[0]
        )

    def back_copy(r, d):
        target = lax.rem(me + d, plane)
        return pltpu.make_async_remote_copy(
            src_ref=rows.at[r, target],
            dst_ref=back_hbm.at[r, me],
            send_sem=back_send.at[r, d],
            recv_sem=back_recv.at[r, d],
            device_id={"fsdp": target},
        )

    def own_back(r):
        return pltpu.make_async_copy(rows.at[r, me], back_hbm.at[r, me], own_sem.at[1])

    def dots_copy(r, d):
        target = lax.rem(me + d, plane)
        return pltpu.make_async_remote_copy(
            src_ref=dots.at[r, target],
            dst_ref=dots_back.at[r, me],
            send_sem=dots_send.at[r, d],
            recv_sem=dots_recv.at[r, d],
            device_id={"fsdp": target},
        )

    def dots_in_copy(r):
        return pltpu.make_async_remote_copy(
            src_ref=dots_pass.at[r],
            dst_ref=dots_in.at[r],
            send_sem=dots_in_send.at[r - 1],
            recv_sem=dots_in_recv.at[r - 1],
            device_id={"tensor": lax.rem(at_line + r, line)},
        )

    def partial_copy(r):
        return pltpu.make_async_remote_copy(
            src_ref=partials.at[r - 1],
            dst_ref=partials_in.at[r - 1],
            send_sem=partial_send.at[r - 1],
            recv_sem=partial_recv.at[r - 1],
            device_id={"tensor": lax.rem(at_line + r, line)},
        )

    def up_copy(r):
        return pltpu.make_async_copy(
            up_hbm.at[:, lax.rem(at_line + r, line)], up_rows, up_sem
        )

    def y_copy(r):
        return pltpu.make_async_copy(up_rows, y_hbm.at[:, r], y_sem)

    @pl.loop(1, line)
    def _(r):
        block_copy(r).start()

    first_block = pltpu.make_async_copy(own_ref, blocks.at[0], own_sem.at[2])
    first_block.start()
    up_copy(0).start()
    table_copies = [
        pltpu.make_async_copy(source, target, table_sem.at[at])
        for at, (source, target) in enumerate(zip(tables_hbm, tables))
    ]
    for each in table_copies:
        each.start()
    for total in sums:
        total[...] = jnp.zeros_like(total)
    first_block.wait()

    @pl.loop(0, line + 2)
    def _(step):
        @pl.when(step < line)
        def _():
            @pl.when(step > 0)
            def _():
                block_copy(step).wait_recv()

            @pl.when(step > 1)
            def _():
                @pl.loop(1, plane)
                def _(d):
                    row_copy(step - 2, d).wait_send()

            choice[...] = slot_choice(plane_rank_ref[lax.rem(at_line + step, line)], slots)

            def slot_step(columns):
                sent_slots[lax.rem(step, 2), :, :, columns] = (
                    matrix_product(choice[...], blocks[step, :, columns])
                    .astype(BF16)
                    .reshape(plane, slots, 2 * tile)
                )

            tiles(width, 2 * tile, slot_step)

            @pl.loop(1, plane)
            def _(d):
                row_copy(step, d).start()

        @pl.when((step >= 1) & (step <= line))
        def _():
            r = step - 1
            block = lax.rem(at_line + r, line)

            @pl.when(r == 0)
            def _():
                for each in table_copies:
                    each.wait()

            own_rows(r).start()
            own_rows(r).wait()

            @pl.loop(1, plane)
            def _(d):
                row_copy(r, d).wait_recv()

            up_copy(r).wait()

            def keep_dots(source, values):
                dots[r, source] = jnp.broadcast_to(values, (8, values.shape[1]))

            expert_math(
                tile,
                rows.at[r],
                up_rows,
                rank_ref[block],
                weight_ref[block],
                keep_dots,
                lambda: y_copy(r).start(),
                mask_ref,
                tables,
                sums,
                scratch,
            )

            @pl.loop(1, plane)
            def _(d):
                dots_copy(r, d).start()
                back_copy(r, d).start()

            own_back(r).start()
            dots_back[r, me] = dots[r, me]
            y_copy(r).wait()

            @pl.when(r + 1 < line)
            def _():
                up_copy(r + 1).start()

            own_back(r).wait()

        @pl.when(step >= 2)
        def _():
            r = step - 2

            @pl.loop(1, plane)
            def _(d):
                dots_copy(r, d).wait_recv()
                back_copy(r, d).wait_recv()

            dots_pass[r] = dots_back[r, :, 0, :]
            load = pltpu.make_async_copy(back_hbm.at[r], back_rows, back_sem)
            load.start()
            choice[...] = slot_choice(plane_rank_ref[lax.rem(at_line + r, line)], slots)
            load.wait()

            def combined(columns):
                return flipped_left_operand(
                    choice[...], back_rows[:, :, columns].reshape(plane * slots, 2 * tile)
                )

            @pl.when(r == 0)
            def _():
                def keep(columns):
                    total_ref[:, columns] = combined(columns)

                tiles(width, 2 * tile, keep)
                dots_ref[at_line] = dots_pass[0]

            @pl.when(r > 0)
            def _():
                def pass_on(columns):
                    partials[r - 1, :, columns] = combined(columns).astype(BF16)

                dots_in_copy(r).start()
                tiles(width, 2 * tile, pass_on)
                partial_copy(r).start()

    @pl.loop(1, line)
    def _(r):
        dots_in_copy(r).wait_recv()
        dots_ref[lax.rem(at_line + line - r, line)] = dots_in[r]
        partial_copy(r).wait_recv()
        total_ref[...] += partials_in[r - 1].astype(F32)

    @pl.loop(1, line)
    def _(r):
        partial_copy(r).wait_send()
        dots_in_copy(r).wait_send()
        block_copy(r).wait_send()

    @pl.loop(1, plane)
    def _(d):
        row_copy(line - 2, d).wait_send()
        row_copy(line - 1, d).wait_send()

    @pl.loop(0, line)
    def _(r):
        @pl.loop(1, plane)
        def _(d):
            back_copy(r, d).wait_send()
            dots_copy(r, d).wait_send()


def moe_layer(own, up_rows, plane_ranks, ranks, weights, mask, tables, identity):
    line, plane, tokens = plane_ranks.shape
    slots, width = up_rows.shape[2:]
    hidden = tables[0].shape[1]
    sums = expert_sums(tables)
    anywhere = pl.BlockSpec(memory_space=pl.ANY)
    local = pl.BlockSpec(memory_space=pltpu.VMEM)
    grouped = (plane, slots, width)
    dma = pltpu.SemaphoreType.DMA
    return pl.pallas_call(
        functools.partial(moe_body, plane, line),
        out_shape=[
            jax.ShapeDtypeStruct((tokens, width), F32),
            jax.ShapeDtypeStruct((line, plane, tokens), F32),
            jax.ShapeDtypeStruct((plane, line, slots, width), BF16),
            jax.ShapeDtypeStruct((line,) + grouped, BF16),
        ]
        + sums,
        in_specs=[anywhere, anywhere, local, local, local, local] + [anywhere] * len(tables),
        out_specs=[local, local, anywhere, anywhere] + [local] * len(sums),
        scratch_shapes=[pltpu.VMEM(table.shape, table.dtype) for table in tables]
        + [
            pltpu.VMEM((line, tokens, width), BF16),
            pltpu.VMEM((line - 1, tokens, width), BF16),
            pltpu.VMEM((line - 1, tokens, width), BF16),
            pltpu.VMEM((2,) + grouped, BF16),
            pltpu.VMEM((line,) + grouped, BF16),
            pltpu.VMEM(grouped, BF16),
            pltpu.VMEM(grouped, BF16),
            pltpu.VMEM((plane * slots, tokens), BF16),
            pltpu.VMEM((line, plane, 8, tokens), F32),
            pltpu.VMEM((line, plane, 8, tokens), F32),
            pltpu.VMEM((line, plane, tokens), F32),
            pltpu.VMEM((line, plane, tokens), F32),
        ]
        + expert_scratch(plane * slots, hidden, width)
        + [dma((len(tables),)), dma, dma, dma, dma((3,))]
        + [dma((line - 1,))] * 2
        + [dma((line, plane))] * 4
        + [dma((line - 1,))] * 2
        + [dma((line, plane))] * 2
        + [dma((line - 1,))] * 2,
        compiler_params=pltpu.CompilerParams(
            collective_id=identity, has_side_effects=True, vmem_limit_bytes=63 * MEBI
        ),
        name="moe_layer",
    )(own, up_rows, plane_ranks, ranks, weights, mask, *tables)


def greet_line(me, count):
    barrier = pltpu.get_barrier_semaphore()

    @pl.when(me > 0)
    def _():
        pl.semaphore_signal(barrier, inc=1, device_id={"tensor": me - 1})

    @pl.when(me < count - 1)
    def _():
        pl.semaphore_signal(barrier, inc=1, device_id={"tensor": me + 1})

    @pl.when((me > 0) & (me < count - 1))
    def _():
        pl.semaphore_wait(barrier, 2)

    @pl.when((me == 0) | (me == count - 1))
    def _():
        pl.semaphore_wait(barrier, 1)


def gather_line_body(count, chunks, *refs):
    arrays = len(chunks)
    ins, outs = refs[:arrays], refs[arrays : 2 * arrays]
    right_send, right_recv, left_send, left_recv, own_sem = refs[2 * arrays :]
    me = lax.axis_index("tensor")
    pieces = []
    for at in range(arrays):
        size = ins[at].shape[0] // chunks[at]
        for piece in range(chunks[at]):
            pieces.append((at, pl.ds(piece * size, size)))

    def copy(at, rows, place, hop, origin, target, send, recv):
        source = ins[at].at[rows] if hop == 0 else outs[at].at[origin, rows]
        return pltpu.make_async_remote_copy(
            src_ref=source,
            dst_ref=outs[at].at[origin, rows],
            send_sem=send.at[hop, place],
            recv_sem=recv.at[hop, place],
            device_id={"tensor": target},
        )

    def rightward(place, hop):
        at, rows = pieces[place]
        return copy(at, rows, place, hop, me - hop, me + 1, right_send, right_recv)

    def leftward(place, hop):
        at, rows = pieces[place]
        return copy(at, rows, place, hop, me + hop, me - 1, left_send, left_recv)

    greet_line(me, count)
    own = [
        pltpu.make_async_copy(ins[at], outs[at].at[me], own_sem.at[at]) for at in range(arrays)
    ]
    for hop in range(count):
        for place in range(len(pieces)):
            if hop > 0:

                @pl.when(me - hop >= 0)
                def _():
                    at, rows = pieces[place]
                    copy(
                        at, rows, place, hop - 1, me - hop, me - 1, right_send, right_recv
                    ).wait_recv()

            if hop < count - 1:

                @pl.when((me - hop >= 0) & (me + 1 < count))
                def _():
                    rightward(place, hop).start()

            if hop > 0:

                @pl.when(me + hop < count)
                def _():
                    at, rows = pieces[place]
                    copy(
                        at, rows, place, hop - 1, me + hop, me + 1, left_send, left_recv
                    ).wait_recv()

            if hop < count - 1:

                @pl.when((me + hop < count) & (me > 0))
                def _():
                    leftward(place, hop).start()

        if hop == 0:
            for each in own:
                each.start()
    for each in own:
        each.wait()
    for hop in range(count - 1):
        for place in range(len(pieces)):

            @pl.when((me - hop >= 0) & (me + 1 < count))
            def _():
                rightward(place, hop).wait_send()

            @pl.when((me + hop < count) & (me > 0))
            def _():
                leftward(place, hop).wait_send()


def gather_line(arrays, chunks, identity):
    count = lax.axis_size("tensor")
    total = sum(chunks)
    anywhere = pl.BlockSpec(memory_space=pl.ANY)
    return pl.pallas_call(
        functools.partial(gather_line_body, count, chunks),
        out_shape=[jax.ShapeDtypeStruct((count,) + a.shape, a.dtype) for a in arrays],
        in_specs=[anywhere] * len(arrays),
        out_specs=[anywhere] * len(arrays),
        scratch_shapes=[pltpu.SemaphoreType.DMA((count - 1, total))] * 4
        + [pltpu.SemaphoreType.DMA((len(arrays),))],
        compiler_params=pltpu.CompilerParams(collective_id=identity, has_side_effects=True),
        name="gather_line",
    )(*arrays)


def sum_line_body(
    count,
    chunks,
    part_ref,
    out_ref,
    left_buf,
    right_buf,
    right_send,
    right_recv,
    left_send,
    left_recv,
):
    me = lax.axis_index("tensor")
    size = part_ref.shape[1] // chunks

    def rightward(rows, piece, far, source):
        return pltpu.make_async_remote_copy(
            src_ref=source,
            dst_ref=left_buf.at[far - 1, rows],
            send_sem=right_send.at[far - 1, piece],
            recv_sem=right_recv.at[far - 1, piece],
            device_id={"tensor": me + 1},
        )

    def leftward(rows, piece, far, source):
        return pltpu.make_async_remote_copy(
            src_ref=source,
            dst_ref=right_buf.at[far - 1, rows],
            send_sem=left_send.at[far - 1, piece],
            recv_sem=left_recv.at[far - 1, piece],
            device_id={"tensor": me - 1},
        )

    greet_line(me, count)
    for far in range(count - 1, 0, -1):
        for piece in range(chunks):
            rows = pl.ds(piece * size, size)

            @pl.when((me == 0) & (me + far < count))
            def _():
                rightward(rows, piece, far, part_ref.at[me + far, rows]).start()

            @pl.when((me == count - 1) & (me - far >= 0))
            def _():
                leftward(rows, piece, far, part_ref.at[me - far, rows]).start()

            if far < count - 1:

                @pl.when((me > 0) & (me + far < count))
                def _():
                    rightward(rows, piece, far + 1, left_buf.at[far, rows]).wait_recv()
                    left_buf[far, rows, :] = (
                        left_buf[far, rows, :].astype(F32)
                        + part_ref[me + far, rows, :].astype(F32)
                    ).astype(BF16)
                    rightward(rows, piece, far, left_buf.at[far, rows]).start()

                @pl.when((me < count - 1) & (me - far >= 0))
                def _():
                    leftward(rows, piece, far + 1, right_buf.at[far, rows]).wait_recv()
                    right_buf[far, rows, :] = (
                        right_buf[far, rows, :].astype(F32)
                        + part_ref[me - far, rows, :].astype(F32)
                    ).astype(BF16)
                    leftward(rows, piece, far, right_buf.at[far, rows]).start()

    for piece in range(chunks):
        rows = pl.ds(piece * size, size)
        out_ref[rows, :] = part_ref[me, rows, :].astype(F32)

        @pl.when(me > 0)
        def _():
            rightward(rows, piece, 1, left_buf.at[0, rows]).wait_recv()
            out_ref[rows, :] += left_buf[0, rows, :].astype(F32)

        @pl.when(me < count - 1)
        def _():
            leftward(rows, piece, 1, right_buf.at[0, rows]).wait_recv()
            out_ref[rows, :] += right_buf[0, rows, :].astype(F32)

    for far in range(count - 1, 0, -1):
        for piece in range(chunks):
            rows = pl.ds(piece * size, size)

            @pl.when((me == 0) & (me + far < count))
            def _():
                rightward(rows, piece, far, part_ref.at[me + far, rows]).wait_send()

            @pl.when((me == count - 1) & (me - far >= 0))
            def _():
                leftward(rows, piece, far, part_ref.at[me - far, rows]).wait_send()

            if far < count - 1:

                @pl.when((me > 0) & (me + far < count))
                def _():
                    rightward(rows, piece, far, left_buf.at[far, rows]).wait_send()

                @pl.when((me < count - 1) & (me - far >= 0))
                def _():
                    leftward(rows, piece, far, right_buf.at[far, rows]).wait_send()


def sum_line(part, chunks, identity):
    count, rows, width = part.shape
    semaphores = pltpu.SemaphoreType.DMA((count - 1, chunks))
    return pl.pallas_call(
        functools.partial(sum_line_body, count, chunks),
        out_shape=jax.ShapeDtypeStruct((rows, width), F32),
        in_specs=[pl.BlockSpec(memory_space=pltpu.VMEM)],
        out_specs=pl.BlockSpec(memory_space=pltpu.VMEM),
        scratch_shapes=[
            pltpu.VMEM((count - 1, rows, width), BF16),
            pltpu.VMEM((count - 1, rows, width), BF16),
        ]
        + [semaphores] * 4,
        compiler_params=pltpu.CompilerParams(
            collective_id=identity, has_side_effects=True, vmem_limit_bytes=32 * MEBI
        ),
        name="sum_line",
    )(part)


def per_device(
    tokens,
    segments,
    routes,
    adapter_index,
    cotangent,
    attn_gain,
    moe_gain,
    q_gain,
    key_norm_gain,
    w_query,
    key_projection_weight,
    value_projection_weight,
    w_out,
    w_router,
    expert_gate_weight,
    expert_up_weight,
    expert_down_weight,
    query_in,
    query_out,
    key_in,
    key_second_weight,
    value_in,
    value_second_weight,
    attn_in,
    attn_out,
    router_in,
    router_out,
    gate_in,
    gate_out,
    upward_in,
    upward_out,
    downward_in,
    downward_out,
):
    tensor_count = lax.axis_size("tensor")
    fsdp_count = lax.axis_size("fsdp")
    device_count = fsdp_count * tensor_count
    tensor_pos = lax.axis_index("tensor")
    fsdp_pos = lax.axis_index("fsdp")
    zero_pos = fsdp_pos * 0
    tok_rows, model_width = tokens.shape
    seq_rows = tok_rows * tensor_count
    rank = query_in.shape[2]
    adapter_count = query_in.shape[0]
    head_dim = q_gain.shape[0]
    local_cols = query_out.shape[2]
    local_kv_cols = key_second_weight.shape[2]
    expert_count = w_router.shape[1]
    top_count = routes.shape[1]
    capacity = 5 * tok_rows * top_count // (4 * expert_count)
    slots = -(-capacity // 16) * 16
    score_scale = 1.0 / math.sqrt(head_dim)
    adapter_pick = lax.dynamic_index_in_dim(adapter_index, fsdp_pos, 0, keepdims=False)

    def select_adapter(adapter_table):
        return lax.dynamic_index_in_dim(adapter_table, adapter_pick, 0, keepdims=False)

    def transposed(adapter_table):
        return jnp.swapaxes(adapter_table, -1, -2)

    input_first = jnp.concatenate(
        [select_adapter(transposed(table)) for table in (query_in, key_in, value_in)], axis=0
    )
    q_second = select_adapter(query_out)
    k_second = select_adapter(key_second_weight)
    v_second = select_adapter(value_second_weight)
    attention_first = select_adapter(transposed(attn_in))
    attention_second = select_adapter(attn_out)
    router_first = select_adapter(transposed(router_in))
    router_second = select_adapter(router_out)
    gain_attn = attn_gain.astype(F32)
    gain_moe = moe_gain.astype(F32)
    gain_query = q_gain.astype(F32)[None, :]
    gain_key = key_norm_gain.astype(F32)[None, :]

    packed_weights = lax.all_gather(
        jnp.concatenate(
            [w_query, key_projection_weight, value_projection_weight, w_router], axis=1
        ),
        "fsdp",
        axis=0,
        tiled=True,
    )
    linear_cols = local_cols + 2 * local_kv_cols
    complete_linear = packed_weights[:, :linear_cols]
    complete_router = packed_weights[:, linear_cols:]
    full_out = lax.all_gather(w_out, "fsdp", axis=1, tiled=True)
    sequence_tokens, sequence_routes, sequence_cotangent = gather_line(
        [tokens, jnp.transpose(routes, (1, 0)), cotangent], (4, 1, 4), 0
    )
    sequence_tokens = sequence_tokens.reshape(seq_rows, model_width)
    plane_experts = jnp.arange(fsdp_count, dtype=jnp.int32) * tensor_count + tensor_pos
    plane_mask = jnp.any(
        sequence_routes[:, None, :, :] == plane_experts[None, :, None, None], axis=2
    )
    plane_ranks = ranks_of(plane_mask)
    offsets = [0] + [sign * step for step in range(1, tensor_count) for sign in (1, -1)]
    offsets = [offset % tensor_count for offset in offsets[:tensor_count]]
    line_blocks = [((tensor_pos + offset) % tensor_count)[None] for offset in offsets]

    def fetched(block, offset):
        if offset == 0:
            return block
        pairs = [((at + offset) % tensor_count, at) for at in range(tensor_count)]
        return lax.ppermute(block, "tensor", pairs)

    def delivered(block, offset):
        if offset == 0:
            return block
        pairs = [(at, (at + offset) % tensor_count) for at in range(tensor_count)]
        return lax.ppermute(block, "tensor", pairs)

    def dispatched(block):
        return [
            plane_rows(to_slots(at, plane_ranks, fetched(block, offset), slots))
            for offset, at in zip(offsets, line_blocks)
        ]

    in_kernel = fsdp_count * slots <= 640
    if in_kernel:
        slotted = all_to_slots(
            plane_ranks, sequence_cotangent.reshape(seq_rows, model_width), slots
        )
        slotted, sequence_tokens = lax.optimization_barrier((slotted, sequence_tokens))
        up_rows = plane_rows(
            slotted.reshape(fsdp_count, tensor_count * slots, model_width)
        ).reshape(fsdp_count, tensor_count, slots, model_width)
    else:
        up_rows = dispatched(cotangent)

    token_values = tokens.astype(F32)
    attn_normed, attn_factor = norm_forward(token_values, gain_attn)
    attention_narrow = attn_normed.astype(BF16)
    sequence_normalized = norm_forward(sequence_tokens.astype(F32), gain_attn)[0].astype(BF16)
    linear = matrix_product(sequence_normalized, complete_linear)
    low = flipped_right_operand(sequence_normalized, input_first).astype(BF16)
    tables = rope_tables(seq_rows, head_dim)
    seg_row = segments
    seg_column = jnp.transpose(segments, (1, 0))
    attention_operands = (
        linear,
        low,
        q_second,
        k_second,
        v_second,
        gain_query,
        gain_key,
        tables,
        seg_column,
        seg_row,
        score_scale,
    )
    heads_narrow = attention_forward(*attention_operands)
    attention_low = flipped_right_operand(heads_narrow, attention_first).astype(BF16)
    out_part = matrix_product(heads_narrow, full_out) + matrix_product(
        attention_low, attention_second
    )
    attention_total = sum_line(
        out_part.astype(BF16).reshape(tensor_count, tok_rows, model_width), 4, 1
    )
    up_rows, attention_total = lax.optimization_barrier((up_rows, attention_total))
    residual_stream = token_values + attention_total
    moe_normed, moe_factor = norm_forward(residual_stream, gain_moe)
    experts_narrow = moe_normed.astype(BF16)

    router_low = flipped_right_operand(experts_narrow, router_first).astype(BF16)
    router_logits = matrix_product(experts_narrow, complete_router) + matrix_product(
        router_low, router_second
    )
    expert_ids = jnp.arange(expert_count, dtype=jnp.int32)
    chosen = jnp.any(routes[:, :, None] == expert_ids[None, None, :], axis=1)
    chosen_logits = jnp.where(chosen, router_logits, -jnp.inf)
    chosen_exp = jnp.exp(chosen_logits - jnp.max(chosen_logits, axis=-1, keepdims=True))
    gate_weights = chosen_exp / jnp.sum(chosen_exp, axis=-1, keepdims=True)
    sent_weights = jnp.transpose(jnp.where(chosen, gate_weights, -1.0), (1, 0))
    own_weights = jnp.transpose(
        route_rows(sent_weights).reshape(fsdp_count, tensor_count, tok_rows), (1, 0, 2)
    )
    own_ranks = ranks_of(own_weights >= 0.0)

    broad = adapter_count * rank
    gate_in_t, upward_in_t = transposed(gate_in[0]), transposed(upward_in[0])
    expert_tables = (
        expert_gate_weight[0],
        expert_up_weight[0],
        expert_down_weight[0],
        jnp.concatenate(
            [gate_in_t.reshape(broad, model_width), upward_in_t.reshape(broad, model_width)],
            axis=0,
        ),
        gate_out[0].reshape(broad, -1),
        upward_out[0].reshape(broad, -1),
        transposed(downward_in[0]).reshape(broad, -1),
        downward_out[0].reshape(broad, model_width),
    )
    column_adapter = jnp.arange(broad, dtype=jnp.int32) // rank
    adapter_mask = jnp.repeat(
        (adapter_index[:, None] == column_adapter[None, :]).astype(BF16), slots, axis=0
    )
    ordered = [None] * tensor_count
    if in_kernel:
        moe_grad, gate_dots, expert_output, _landed, *sums = moe_layer(
            experts_narrow,
            up_rows,
            plane_ranks,
            own_ranks,
            own_weights,
            adapter_mask,
            expert_tables,
            3,
        )
    else:
        expert_rows = dispatched(experts_narrow)
        expert_output, rows_grad, gate_dots = [], [], []
        sums = [jnp.zeros(each.shape, F32) for each in expert_sums(expert_tables)]
        for at, rows, upstream in zip(line_blocks, expert_rows, up_rows):
            y_rows, grad_rows, dots, *sums = experts(
                at, rows, upstream, own_ranks, own_weights, adapter_mask, expert_tables, sums
            )
            expert_output.append(y_rows)
            rows_grad.append(grad_rows)
            gate_dots.append(dots)
        for offset, dots in zip(offsets, gate_dots):
            ordered[offset] = dots
        gate_dots = jnp.roll(jnp.stack(ordered), tensor_pos, axis=0)
    pair_in_grad, gate_out_grad, upward_out_grad, downward_in_grad, downward_out_grad = sums
    if in_kernel:
        gate_grad = jnp.transpose(gate_dots, (2, 1, 0)).reshape(tok_rows, expert_count)
    else:
        gate_grad = jnp.transpose(
            route_rows(jnp.transpose(gate_dots, (1, 0, 2)).reshape(device_count, tok_rows)),
            (1, 0),
        )

    def returned(slotted):
        total = 0.0
        for offset, at, rows in zip(offsets, line_blocks, slotted):
            combined = from_slots(at, plane_ranks, plane_rows(rows))
            total = total + delivered(combined, offset).astype(F32)
        return total

    if not in_kernel:
        moe_grad = returned(rows_grad)

    out_grad = cotangent.astype(F32)
    logit_gradient = (
        gate_weights * (gate_grad - jnp.sum(gate_weights * gate_grad, axis=-1, keepdims=True))
    ).astype(BF16)
    router_low_gradient = flipped_right_operand(logit_gradient, router_second).astype(BF16)
    moe_grad = (
        moe_grad
        + flipped_right_operand(logit_gradient, complete_router)
        + matrix_product(router_low_gradient, router_first)
    )
    router_first_gradient = flipped_left_operand(router_low_gradient, experts_narrow)
    router_second_gradient = flipped_left_operand(router_low, logit_gradient)
    residual_grad = out_grad + norm_backward(residual_stream, moe_factor, gain_moe, moe_grad)

    (sequence_branch,) = gather_line([residual_grad.astype(BF16)], (4,), 2)
    sequence_branch = sequence_branch.reshape(seq_rows, model_width)
    if in_kernel:
        back_output = plane_rows(
            expert_output.reshape(fsdp_count, tensor_count * slots, model_width)
        ).reshape(fsdp_count, tensor_count, slots, model_width)
        back_output, sequence_branch = lax.optimization_barrier((back_output, sequence_branch))
        combined = all_from_slots(tensor_pos[None], plane_ranks, back_output)
        moe_output = lax.psum_scatter(combined, "tensor", scatter_dimension=0, tiled=True)
        output = (residual_stream + moe_output.astype(F32)).astype(BF16)
    else:
        output = (residual_stream + returned(expert_output)).astype(BF16)
    attention_low_grad = flipped_right_operand(sequence_branch, attention_second).astype(BF16)
    attention_second_gradient = flipped_left_operand(attention_low, sequence_branch)
    heads_grad = flipped_right_operand(sequence_branch, full_out)
    (
        q_grad,
        k_grad,
        v_grad,
        low_share,
        q_second_gradient,
        k_second_gradient,
        v_second_gradient,
        attention_first_gradient,
    ) = attention_backward(
        *attention_operands,
        heads_narrow,
        heads_grad,
        attention_low_grad,
        attention_first,
    )
    linear_grad = jnp.concatenate([q_grad, k_grad, v_grad], axis=1)
    normed_part = flipped_right_operand(linear_grad, complete_linear) + matrix_product(
        low_share, input_first
    )
    input_first_gradient = flipped_left_operand(low_share, sequence_normalized)
    normalized_gradient = sum_line(
        normed_part.astype(BF16).reshape(tensor_count, tok_rows, model_width), 4, 1
    )
    input_grad = residual_grad + norm_backward(
        token_values, attn_factor, gain_attn, normalized_gradient
    )

    source_adapter = jnp.repeat(adapter_index, tensor_count)
    owner_onehot = (
        jnp.arange(adapter_count, dtype=jnp.int32)[:, None] == source_adapter[None, :]
    ).astype(BF16)

    def to_all(addend):
        lines = addend.shape[0]
        return jnp.transpose(
            addend.astype(BF16).reshape(lines, device_count, -1), (1, 0, 2)
        ).reshape(device_count, -1)

    def to_head_owners(addend):
        lines = addend.shape[0]
        pieces = jnp.transpose(
            addend.astype(BF16).reshape(lines, fsdp_count, -1), (1, 0, 2)
        ).reshape(fsdp_count, -1)
        holder = jnp.zeros((device_count, pieces.shape[1]), BF16)
        return lax.dynamic_update_slice(holder, pieces, (tensor_pos * fsdp_count, zero_pos))

    def owner_sums(parts):
        widths = [part.shape[1] for part in parts]
        total = matrix_product(owner_onehot, route_rows(jnp.concatenate(parts, axis=1)))
        pieces = []
        start = 0
        for width in widths:
            pieces.append(total[:, start : start + width])
            start += width
        return pieces

    early = owner_sums(
        [
            to_all(router_first_gradient),
            to_all(attention_second_gradient),
            to_all(router_second_gradient),
        ]
    )
    late = owner_sums(
        [
            to_all(input_first_gradient),
            to_head_owners(q_second_gradient),
            to_head_owners(k_second_gradient),
            to_head_owners(v_second_gradient),
            to_head_owners(attention_first_gradient),
        ]
    )

    def lines_of(piece, lines):
        return piece.reshape(adapter_count, lines, -1)

    first_sums = lines_of(late[0], 3 * rank)
    return (
        output,
        input_grad,
        transposed(first_sums[:, :rank]),
        lines_of(late[1], rank),
        transposed(first_sums[:, rank : 2 * rank]),
        lines_of(late[2], rank),
        transposed(first_sums[:, 2 * rank :]),
        lines_of(late[3], rank),
        transposed(lines_of(late[4], rank)),
        lines_of(early[1], rank),
        transposed(lines_of(early[0], rank)),
        lines_of(early[2], rank),
        transposed(lines_of(pair_in_grad[:broad], rank))[None],
        lines_of(gate_out_grad, rank)[None],
        transposed(lines_of(pair_in_grad[broad:], rank))[None],
        lines_of(upward_out_grad, rank)[None],
        transposed(lines_of(downward_in_grad, rank))[None],
        lines_of(downward_out_grad, rank)[None],
    )


def solution(mesh):
    placed = (
        P(("fsdp", "tensor"), None),
        P("fsdp", None),
        P(("fsdp", "tensor"), None),
        P(),
        P(("fsdp", "tensor"), None),
        P(),
        P(),
        P(),
        P(),
        P("fsdp", "tensor"),
        P("fsdp", "tensor"),
        P("fsdp", "tensor"),
        P("tensor", "fsdp"),
        P("fsdp", None),
        P(("fsdp", "tensor"), None, None),
        P(("fsdp", "tensor"), None, None),
        P(("fsdp", "tensor"), None, None),
        P(),
        P(None, None, "tensor"),
        P(),
        P(None, None, "tensor"),
        P(),
        P(None, None, "tensor"),
        P(None, "tensor", None),
        P(),
        P(),
        P(),
        P(("fsdp", "tensor"), None, None, None),
        P(("fsdp", "tensor"), None, None, None),
        P(("fsdp", "tensor"), None, None, None),
        P(("fsdp", "tensor"), None, None, None),
        P(("fsdp", "tensor"), None, None, None),
        P(("fsdp", "tensor"), None, None, None),
    )
    return jax.shard_map(
        per_device,
        mesh=mesh,
        in_specs=placed,
        out_specs=(
            P(("fsdp", "tensor"), None),
            P(("fsdp", "tensor"), None),
            P(None, ("fsdp", "tensor"), None),
            P(None, None, ("fsdp", "tensor")),
            P(None, ("fsdp", "tensor"), None),
            P(None, None, ("fsdp", "tensor")),
            P(None, ("fsdp", "tensor"), None),
            P(None, None, ("fsdp", "tensor")),
            P(None, ("fsdp", "tensor"), None),
            P(None, None, ("fsdp", "tensor")),
            P(None, ("fsdp", "tensor"), None),
            P(None, None, ("fsdp", "tensor")),
            P(("fsdp", "tensor"), None, None, None),
            P(("fsdp", "tensor"), None, None, None),
            P(("fsdp", "tensor"), None, None, None),
            P(("fsdp", "tensor"), None, None, None),
            P(("fsdp", "tensor"), None, None, None),
            P(("fsdp", "tensor"), None, None, None),
        ),
        check_vma=False,
    )
```

```python
import functools
import math

import jax
import jax.numpy as jnp
from jax import lax
from jax.experimental import pallas as pl
from jax.experimental.pallas import tpu as pltpu
from jax.sharding import PartitionSpec as P

NORM_EPSILON = 1e-06
ROPE_THETA = 1000000.0
BF16 = jnp.bfloat16
F32 = jnp.float32
WINDOW = 256
MEBI = 1 << 20


def matrix_product(first_op, second_op):
    return jnp.dot(first_op, second_op, preferred_element_type=F32)


def flipped_left_operand(first_op, second_op):
    return lax.dot_general(
        first_op, second_op, (((0,), (0,)), ((), ())), preferred_element_type=F32
    )


def flipped_right_operand(first_op, second_op):
    return lax.dot_general(
        first_op, second_op, (((1,), (1,)), ((), ())), preferred_element_type=F32
    )


def norm_forward(values, gain_vec):
    factor = lax.rsqrt(jnp.mean(values * values, axis=-1, keepdims=True) + NORM_EPSILON)
    return (values * factor * gain_vec, factor)


def norm_backward(values, factor, gain_vec, upstream):
    scaled = upstream * gain_vec
    return factor * scaled - values * (factor * factor * factor) * jnp.mean(
        values * scaled, axis=-1, keepdims=True
    )


def rope_tables(sequence_length, head_width):
    half_width = head_width // 2
    inverse = jnp.power(ROPE_THETA, -2.0 * jnp.arange(half_width, dtype=F32) / head_width)
    angles = jnp.arange(sequence_length, dtype=F32)[:, None] * inverse[None, :]
    cosine, sine = jnp.cos(angles), jnp.sin(angles)
    return (
        jnp.concatenate([cosine, cosine], axis=1),
        jnp.concatenate([-sine, sine], axis=1),
    )


def swapped(values):
    return pltpu.roll(values, values.shape[-1] // 2, 1)


def route_rows(block_rows):
    return lax.all_to_all(block_rows, ("fsdp", "tensor"), split_axis=0, concat_axis=0, tiled=True)


def plane_rows(block_rows):
    return lax.all_to_all(block_rows, "fsdp", split_axis=0, concat_axis=0, tiled=True)


def params(mebibytes, axes=1):
    return pltpu.CompilerParams(
        vmem_limit_bytes=mebibytes * MEBI, dimension_semantics=("arbitrary",) * axes
    )


def whole(shape):
    rank = len(shape)
    return pl.BlockSpec(shape, lambda *_: (0,) * rank)


def head_values(linear, low, second, gain, cosine, sine):
    values = linear + matrix_product(low, second)
    normed, factor = norm_forward(values, gain)
    turned = (normed * cosine + swapped(normed) * sine).astype(BF16)
    return values, factor, turned


def head_values_gradient(values, factor, gain, cosine, sine, upstream):
    back = upstream * cosine - swapped(upstream) * sine
    return norm_backward(values, factor, gain, back).astype(BF16)


def allowed_keys(block, start, width, seg_column, seg_row):
    rows = block * WINDOW + lax.broadcasted_iota(jnp.int32, (WINDOW, width), 0)
    keys = start + lax.broadcasted_iota(jnp.int32, (WINDOW, width), 1)
    mine = seg_column[block * WINDOW : (block + 1) * WINDOW]
    theirs = seg_row[:, start : start + width]
    return (keys == rows) | ((keys < rows) & (mine == theirs) & (theirs != 0))


def block_bounds(block):
    start = max(block - 1, 0) * WINDOW
    return start, (block + 1) * WINDOW - start


def attention_forward_body(
    rank,
    scale,
    lin_ref,
    key_lin_ref,
    value_lin_ref,
    low_ref,
    q_second_ref,
    k_second_ref,
    v_second_ref,
    q_gain_ref,
    k_gain_ref,
    cos_ref,
    sin_ref,
    seg_column_ref,
    seg_row_ref,
    heads_ref,
    key_scratch,
    value_scratch,
):
    cosine, sine = cos_ref[...], sin_ref[...]

    @pl.when(pl.program_id(0) == 0)
    def _():
        key_scratch[...] = head_values(
            key_lin_ref[...],
            low_ref[:, rank : 2 * rank],
            k_second_ref[...],
            k_gain_ref[...],
            cosine,
            sine,
        )[2]
        value_scratch[...] = (
            value_lin_ref[...]
            + matrix_product(low_ref[:, 2 * rank : 3 * rank], v_second_ref[...])
        ).astype(BF16)

    query = head_values(
        lin_ref[...], low_ref[:, :rank], q_second_ref[...], q_gain_ref[...], cosine, sine
    )[2]
    seg_column, seg_row = seg_column_ref[...], seg_row_ref[...]
    for block in range(query.shape[0] // WINDOW):
        start, width = block_bounds(block)
        rows = pl.ds(block * WINDOW, WINDOW)
        scores = (
            flipped_right_operand(
                query[block * WINDOW : (block + 1) * WINDOW], key_scratch[pl.ds(start, width)]
            )
            * scale
        )
        scores = jnp.where(
            allowed_keys(block, start, width, seg_column, seg_row), scores, -1e30
        )
        expo = jnp.exp(scores - jnp.max(scores, axis=-1, keepdims=True))
        probs = (expo / jnp.sum(expo, axis=-1, keepdims=True)).astype(BF16)
        heads_ref[rows, :] = matrix_product(probs, value_scratch[pl.ds(start, width)]).astype(
            BF16
        )


def attention_forward(
    linear, low, q_second, k_second, v_second, q_gain, k_gain, tables, seg_column, seg_row, scale
):
    rows, head_dim = linear.shape[0], q_gain.shape[1]
    heads = q_second.shape[1] // head_dim
    rank = q_second.shape[0]
    column = pl.BlockSpec((rows, head_dim), lambda h: (0, h))
    return pl.pallas_call(
        functools.partial(attention_forward_body, rank, scale),
        grid=(heads,),
        out_shape=jax.ShapeDtypeStruct((rows, heads * head_dim), BF16),
        in_specs=[
            column,
            pl.BlockSpec((rows, head_dim), lambda h: (0, heads)),
            pl.BlockSpec((rows, head_dim), lambda h: (0, heads + 1)),
            whole(low.shape),
            pl.BlockSpec((rank, head_dim), lambda h: (0, h)),
            whole(k_second.shape),
            whole(v_second.shape),
            whole(q_gain.shape),
            whole(k_gain.shape),
            whole(tables[0].shape),
            whole(tables[1].shape),
            whole(seg_column.shape),
            whole(seg_row.shape),
        ],
        out_specs=column,
        scratch_shapes=[pltpu.VMEM((rows, head_dim), BF16), pltpu.VMEM((rows, head_dim), BF16)],
        compiler_params=params(40),
        cost_estimate=pl.CostEstimate(
            flops=8 * heads * rows * WINDOW * head_dim,
            transcendentals=2 * heads * rows * WINDOW,
            bytes_accessed=6 * rows * heads * head_dim,
        ),
        name="attention_forward",
    )(
        linear,
        linear,
        linear,
        low,
        q_second,
        k_second,
        v_second,
        q_gain,
        k_gain,
        *tables,
        seg_column,
        seg_row,
    )


def attention_backward_body(
    rank,
    scale,
    lin_ref,
    key_lin_ref,
    value_lin_ref,
    low_ref,
    q_second_ref,
    k_second_ref,
    v_second_ref,
    q_gain_ref,
    k_gain_ref,
    cos_ref,
    sin_ref,
    seg_column_ref,
    seg_row_ref,
    heads_ref,
    heads_grad_ref,
    low_grad_ref,
    down_ref,
    q_grad_ref,
    k_grad_ref,
    v_grad_ref,
    share_ref,
    q_second_grad_ref,
    k_second_grad_ref,
    v_second_grad_ref,
    down_grad_ref,
    key_scratch,
    value_scratch,
    key_sum,
    value_sum,
    query_sum,
    share_sum,
):
    cosine, sine = cos_ref[...], sin_ref[...]
    head = pl.program_id(0)

    @pl.when(head == 0)
    def _():
        key_scratch[...] = head_values(
            key_lin_ref[...],
            low_ref[:, rank : 2 * rank],
            k_second_ref[...],
            k_gain_ref[...],
            cosine,
            sine,
        )[2]
        value_scratch[...] = (
            value_lin_ref[...]
            + matrix_product(low_ref[:, 2 * rank : 3 * rank], v_second_ref[...])
        ).astype(BF16)
        key_sum[...] = jnp.zeros_like(key_sum)
        value_sum[...] = jnp.zeros_like(value_sum)
        share_sum[...] = jnp.zeros_like(share_sum)

    low_q = low_ref[:, :rank]
    values, factor, query = head_values(
        lin_ref[...], low_q, q_second_ref[...], q_gain_ref[...], cosine, sine
    )
    low_grad = low_grad_ref[...]
    upstream = (heads_grad_ref[...] + matrix_product(low_grad, down_ref[...])).astype(BF16)
    down_grad_ref[...] = flipped_left_operand(low_grad, heads_ref[...])
    seg_column, seg_row = seg_column_ref[...], seg_row_ref[...]
    for block in range(query.shape[0] // WINDOW):
        start, width = block_bounds(block)
        rows = pl.ds(block * WINDOW, WINDOW)
        keys = pl.ds(start, width)
        query_block = query[block * WINDOW : (block + 1) * WINDOW]
        upstream_block = upstream[block * WINDOW : (block + 1) * WINDOW]
        scores = flipped_right_operand(query_block, key_scratch[keys]) * scale
        scores = jnp.where(
            allowed_keys(block, start, width, seg_column, seg_row), scores, -1e30
        )
        expo = jnp.exp(scores - jnp.max(scores, axis=-1, keepdims=True))
        probs = expo / jnp.sum(expo, axis=-1, keepdims=True)
        prob_grad = flipped_right_operand(upstream_block, value_scratch[keys])
        score_grad = (
            probs * (prob_grad - jnp.sum(probs * prob_grad, axis=-1, keepdims=True))
        ).astype(BF16)
        value_sum[keys, :] += flipped_left_operand(probs.astype(BF16), upstream_block)
        key_sum[keys, :] += flipped_left_operand(score_grad, query_block)
        query_sum[rows, :] = matrix_product(score_grad, key_scratch[keys]) * scale
    q_grad = head_values_gradient(
        values, factor, q_gain_ref[...], cosine, sine, query_sum[...]
    )
    q_grad_ref[...] = q_grad
    q_second_grad_ref[...] = flipped_left_operand(low_q, q_grad)
    share_sum[:, :rank] += flipped_right_operand(q_grad, q_second_ref[...])

    @pl.when(head == pl.num_programs(0) - 1)
    def _():
        low_k = low_ref[:, rank : 2 * rank]
        low_v = low_ref[:, 2 * rank : 3 * rank]
        key_values, key_factor, _turned = head_values(
            key_lin_ref[...], low_k, k_second_ref[...], k_gain_ref[...], cosine, sine
        )
        k_grad = head_values_gradient(
            key_values, key_factor, k_gain_ref[...], cosine, sine, key_sum[...] * scale
        )
        v_grad = value_sum[...].astype(BF16)
        k_grad_ref[...] = k_grad
        v_grad_ref[...] = v_grad
        k_second_grad_ref[...] = flipped_left_operand(low_k, k_grad)
        v_second_grad_ref[...] = flipped_left_operand(low_v, v_grad)
        share_sum[:, rank : 2 * rank] = flipped_right_operand(k_grad, k_second_ref[...])
        share_sum[:, 2 * rank : 3 * rank] = flipped_right_operand(v_grad, v_second_ref[...])
        share_ref[...] = share_sum[...].astype(BF16)


def attention_backward(
    linear,
    low,
    q_second,
    k_second,
    v_second,
    q_gain,
    k_gain,
    tables,
    seg_column,
    seg_row,
    scale,
    heads_low,
    heads_grad,
    low_grad,
    down_first,
):
    rows, head_dim = linear.shape[0], q_gain.shape[1]
    rank, columns = q_second.shape
    heads = columns // head_dim
    column = pl.BlockSpec((rows, head_dim), lambda h: (0, h))
    narrow = pl.BlockSpec((rank, head_dim), lambda h: (0, h))
    single = (rows, head_dim)
    return pl.pallas_call(
        functools.partial(attention_backward_body, rank, scale),
        grid=(heads,),
        out_shape=(
            jax.ShapeDtypeStruct((rows, columns), BF16),
            jax.ShapeDtypeStruct(single, BF16),
            jax.ShapeDtypeStruct(single, BF16),
            jax.ShapeDtypeStruct((rows, 3 * rank), BF16),
            jax.ShapeDtypeStruct((rank, columns), F32),
            jax.ShapeDtypeStruct((rank, head_dim), F32),
            jax.ShapeDtypeStruct((rank, head_dim), F32),
            jax.ShapeDtypeStruct((rank, columns), F32),
        ),
        in_specs=[
            column,
            pl.BlockSpec((rows, head_dim), lambda h: (0, heads)),
            pl.BlockSpec((rows, head_dim), lambda h: (0, heads + 1)),
            whole(low.shape),
            narrow,
            whole(k_second.shape),
            whole(v_second.shape),
            whole(q_gain.shape),
            whole(k_gain.shape),
            whole(tables[0].shape),
            whole(tables[1].shape),
            whole(seg_column.shape),
            whole(seg_row.shape),
            column,
            column,
            whole(low_grad.shape),
            narrow,
        ],
        out_specs=(
            column,
            whole(single),
            whole(single),
            whole((rows, 3 * rank)),
            narrow,
            whole((rank, head_dim)),
            whole((rank, head_dim)),
            narrow,
        ),
        scratch_shapes=[
            pltpu.VMEM(single, BF16),
            pltpu.VMEM(single, BF16),
            pltpu.VMEM(single, F32),
            pltpu.VMEM(single, F32),
            pltpu.VMEM(single, F32),
            pltpu.VMEM((rows, 3 * rank), F32),
        ],
        compiler_params=params(48),
        cost_estimate=pl.CostEstimate(
            flops=20 * heads * rows * WINDOW * head_dim,
            transcendentals=2 * heads * rows * WINDOW,
            bytes_accessed=12 * rows * columns,
        ),
        name="attention_backward",
    )(
        linear,
        linear,
        linear,
        low,
        q_second,
        k_second,
        v_second,
        q_gain,
        k_gain,
        *tables,
        seg_column,
        seg_row,
        heads_low,
        heads_grad,
        low_grad,
        down_first,
    )


def slot_choice(ranks, slots):
    experts, tokens = ranks.shape
    places = lax.broadcasted_iota(jnp.int32, (slots, tokens), 0).astype(ranks.dtype)
    return jnp.concatenate(
        [(places == ranks[e : e + 1, :]).astype(F32) for e in range(experts)], axis=0
    ).astype(BF16)


def to_slots_body(_block_ref, rank_ref, rows_ref, out_ref):
    slots = out_ref.shape[1]
    chosen = matrix_product(slot_choice(rank_ref[0], slots), rows_ref[...])
    out_ref[...] = chosen.astype(BF16).reshape(out_ref.shape)


def to_slots(block, ranks, rows, slots):
    experts, tokens = ranks.shape[1:]
    width = rows.shape[1]
    half = width // 2
    return pl.pallas_call(
        to_slots_body,
        grid_spec=pltpu.PrefetchScalarGridSpec(
            num_scalar_prefetch=1,
            grid=(2,),
            in_specs=[
                pl.BlockSpec((1, experts, tokens), lambda j, at: (at[0], 0, 0)),
                pl.BlockSpec((tokens, half), lambda j, at: (0, j)),
            ],
            out_specs=pl.BlockSpec((experts, slots, half), lambda j, at: (0, 0, j)),
        ),
        out_shape=jax.ShapeDtypeStruct((experts, slots, width), BF16),
        compiler_params=params(32),
        cost_estimate=pl.CostEstimate(
            flops=2 * experts * slots * tokens * width,
            transcendentals=0,
            bytes_accessed=2 * width * (experts * slots + tokens),
        ),
        name="to_slots",
    )(block, ranks, rows)


def from_slots_body(_block_ref, rank_ref, slot_ref, out_ref):
    experts, slots, width = slot_ref.shape
    choice = slot_choice(rank_ref[0], slots)
    out_ref[...] = flipped_left_operand(
        choice, slot_ref[...].reshape(experts * slots, width)
    ).astype(BF16)


def from_slots(block, ranks, slotted):
    experts, tokens = ranks.shape[1:]
    slots, width = slotted.shape[1:]
    half = width // 2
    return pl.pallas_call(
        from_slots_body,
        grid_spec=pltpu.PrefetchScalarGridSpec(
            num_scalar_prefetch=1,
            grid=(2,),
            in_specs=[
                pl.BlockSpec((1, experts, tokens), lambda j, at: (at[0], 0, 0)),
                pl.BlockSpec((experts, slots, half), lambda j, at: (0, 0, j)),
            ],
            out_specs=pl.BlockSpec((tokens, half), lambda j, at: (0, j)),
        ),
        out_shape=jax.ShapeDtypeStruct((tokens, width), BF16),
        compiler_params=params(32),
        cost_estimate=pl.CostEstimate(
            flops=2 * experts * slots * tokens * width,
            transcendentals=0,
            bytes_accessed=2 * width * (experts * slots + tokens),
        ),
        name="from_slots",
    )(block, ranks, slotted)


def all_to_slots_body(rank_ref, rows_ref, out_ref):
    slots = out_ref.shape[2]
    chosen = matrix_product(slot_choice(rank_ref[0], slots), rows_ref[...])
    out_ref[...] = chosen.astype(BF16).reshape(out_ref.shape)


def all_to_slots(ranks, rows, slots):
    blocks, experts, tokens = ranks.shape
    width = rows.shape[1]
    return pl.pallas_call(
        all_to_slots_body,
        grid=(blocks,),
        out_shape=jax.ShapeDtypeStruct((experts, blocks, slots, width), BF16),
        in_specs=[
            pl.BlockSpec((1, experts, tokens), lambda z: (z, 0, 0)),
            pl.BlockSpec((tokens, width), lambda z: (z, 0)),
        ],
        out_specs=pl.BlockSpec((experts, 1, slots, width), lambda z: (0, z, 0, 0)),
        compiler_params=params(40),
        cost_estimate=pl.CostEstimate(
            flops=2 * blocks * experts * slots * tokens * width,
            transcendentals=0,
            bytes_accessed=2 * blocks * width * (experts * slots + tokens),
        ),
        name="all_to_slots",
    )(ranks, rows)


def all_from_slots_body(_start_ref, rank_ref, slot_ref, out_ref):
    experts, _, slots, width = slot_ref.shape
    choice = slot_choice(rank_ref[0], slots)
    out_ref[...] = flipped_left_operand(
        choice, slot_ref[...].reshape(experts * slots, width)
    ).astype(BF16)


def all_from_slots(start, ranks, slotted):
    blocks, experts, tokens = ranks.shape
    slots, width = slotted.shape[2:]
    return pl.pallas_call(
        all_from_slots_body,
        grid_spec=pltpu.PrefetchScalarGridSpec(
            num_scalar_prefetch=1,
            grid=(blocks,),
            in_specs=[
                pl.BlockSpec((1, experts, tokens), lambda z, at: ((at[0] + z) % blocks, 0, 0)),
                pl.BlockSpec((experts, 1, slots, width), lambda z, at: (0, z, 0, 0)),
            ],
            out_specs=pl.BlockSpec((tokens, width), lambda z, at: ((at[0] + z) % blocks, 0)),
        ),
        out_shape=jax.ShapeDtypeStruct((blocks * tokens, width), BF16),
        compiler_params=params(40),
        cost_estimate=pl.CostEstimate(
            flops=2 * blocks * experts * slots * tokens * width,
            transcendentals=0,
            bytes_accessed=2 * blocks * width * (experts * slots + tokens),
        ),
        name="all_from_slots",
    )(start, ranks, slotted)


def ranks_of(mask):
    tokens = mask.shape[-1]
    order = jnp.arange(tokens, dtype=jnp.int32)
    before = (order[:, None] < order[None, :]).astype(BF16)
    counts = matrix_product(mask.astype(BF16), before)
    return jnp.where(mask, counts, -1.0).astype(jnp.int32)


def tiles(width, tile, body):
    @pl.loop(0, width // tile)
    def _(j):
        body(pl.ds(pl.multiple_of(j * tile, tile), tile))


def expert_math(
    tile, rows_ref, up_ref, ranks, weights, keep_dots, sent_y, mask_ref, tables, sums, scratch
):
    gate_w, up_w, down_w, pair_in, gate_out, up_out, down_in, down_out = tables
    pair_in_sum, gate_out_sum, up_out_sum, down_in_sum, down_out_sum = sums
    gate_lin_ref, up_lin_ref, inner_ref, route_ref, gate_grad_ref, up_grad_ref = scratch
    sources, slots, width = rows_ref.shape
    row_count = sources * slots
    hidden = gate_w.shape[1]
    broad = gate_out.shape[0]
    places = lax.broadcasted_iota(jnp.int32, (slots, ranks.shape[1]), 0)

    def held(source):
        return places == ranks[source : source + 1, :]

    def all_rows():
        return rows_ref[...].reshape(row_count, width)

    def pair_mask():
        mask = mask_ref[...].astype(F32)
        return jnp.concatenate([mask, mask], axis=1)

    weight = jnp.concatenate(
        [
            jnp.sum(
                jnp.where(held(source), weights[source : source + 1, :], 0.0),
                axis=1,
                keepdims=True,
            )
            for source in range(sources)
        ],
        axis=0,
    )
    pair = (flipped_right_operand(all_rows(), pair_in[...]) * pair_mask()).astype(BF16)
    gate_low, up_low = pair[:, :broad], pair[:, broad:]

    def inner_step(columns):
        rows = all_rows()
        gate_lin = matrix_product(rows, gate_w[:, columns]) + matrix_product(
            gate_low, gate_out[:, columns]
        )
        up_lin = matrix_product(rows, up_w[:, columns]) + matrix_product(
            up_low, up_out[:, columns]
        )
        gate_lin_ref[:, columns] = gate_lin
        up_lin_ref[:, columns] = up_lin
        inner_ref[:, columns] = (gate_lin * jax.nn.sigmoid(gate_lin) * up_lin).astype(BF16)

    tiles(hidden, tile, inner_step)
    down_low = (
        flipped_right_operand(inner_ref[...], down_in[...]) * mask_ref[...].astype(F32)
    ).astype(BF16)

    def down_step(j, total):
        columns = pl.ds(pl.multiple_of(j * tile, tile), tile)
        result = (
            matrix_product(inner_ref[...], down_w[:, columns])
            + matrix_product(down_low, down_out[:, columns])
        ).astype(BF16)
        wide = result.astype(F32)
        upstream = up_ref[:, :, columns].reshape(row_count, tile).astype(F32)
        up_ref[:, :, columns] = (weight * wide).astype(BF16).reshape(sources, slots, tile)
        route_ref[:, columns] = (weight * upstream).astype(BF16)
        return total + jnp.sum(upstream * wide, axis=1, keepdims=True)

    gate_dots = lax.fori_loop(0, width // tile, down_step, jnp.zeros((row_count, 1), F32))
    sent_y()
    for source in range(sources):
        keep_dots(
            source,
            jnp.sum(
                jnp.where(held(source), gate_dots[source * slots : (source + 1) * slots], 0.0),
                axis=0,
                keepdims=True,
            ),
        )
    down_low_grad = (
        flipped_right_operand(route_ref[...], down_out[...]) * mask_ref[...].astype(F32)
    ).astype(BF16)
    down_in_sum[...] += flipped_left_operand(down_low_grad, inner_ref[...])

    def down_out_step(columns):
        down_out_sum[:, columns] += flipped_left_operand(down_low, route_ref[:, columns])

    tiles(width, 2 * tile, down_out_step)

    def inner_grad_step(columns):
        inner_grad = flipped_right_operand(route_ref[...], down_w[columns, :]) + matrix_product(
            down_low_grad, down_in[:, columns]
        )
        gate_lin, up_lin = gate_lin_ref[:, columns], up_lin_ref[:, columns]
        sig = jax.nn.sigmoid(gate_lin)
        gate_grad_ref[:, columns] = (
            inner_grad * up_lin * (sig * (1.0 + gate_lin * (1.0 - sig)))
        ).astype(BF16)
        up_grad_ref[:, columns] = (inner_grad * (gate_lin * sig)).astype(BF16)

    tiles(hidden, tile, inner_grad_step)
    pair_grad = (
        jnp.concatenate(
            [
                flipped_right_operand(gate_grad_ref[...], gate_out[...]),
                flipped_right_operand(up_grad_ref[...], up_out[...]),
            ],
            axis=1,
        )
        * pair_mask()
    ).astype(BF16)
    gate_out_sum[...] += flipped_left_operand(gate_low, gate_grad_ref[...])
    up_out_sum[...] += flipped_left_operand(up_low, up_grad_ref[...])

    def rows_grad_step(columns):
        before = rows_ref[:, :, columns].reshape(row_count, tile)
        pair_in_sum[:, columns] += flipped_left_operand(pair_grad, before)
        rows_ref[:, :, columns] = (
            (
                flipped_right_operand(gate_grad_ref[...], gate_w[columns, :])
                + flipped_right_operand(up_grad_ref[...], up_w[columns, :])
                + matrix_product(pair_grad, pair_in[:, columns])
            )
            .astype(BF16)
            .reshape(sources, slots, tile)
        )

    tiles(width, tile, rows_grad_step)


def expert_sums(tables):
    gate_w, _up_w, _down_w, pair_in, gate_out, _up_out, down_in, down_out = tables
    return [
        jax.ShapeDtypeStruct(table.shape, F32)
        for table in (pair_in, gate_out, gate_out, down_in, down_out)
    ]


def expert_scratch(row_count, hidden, width):
    return [
        pltpu.VMEM((row_count, hidden), F32),
        pltpu.VMEM((row_count, hidden), F32),
        pltpu.VMEM((row_count, hidden), BF16),
        pltpu.VMEM((row_count, width), BF16),
        pltpu.VMEM((row_count, hidden), BF16),
        pltpu.VMEM((row_count, hidden), BF16),
    ]


def experts_body(_block_ref, rows_in, up_in, rank_ref, weight_ref, mask_ref, *rest):
    tables, sums_before, rest = rest[:8], rest[8:13], rest[13:]
    y_ref, rows_grad_ref, dots_ref = rest[:3]
    sums, rest = rest[3:8], rest[8:]
    for total, before in zip(sums, sums_before):
        total[...] = before[...]
    rows_grad_ref[...] = rows_in[...]
    y_ref[...] = up_in[...]

    def keep_dots(source, dots):
        dots_ref[source : source + 1, :] = dots

    expert_math(
        256,
        rows_grad_ref,
        y_ref,
        rank_ref[0],
        weight_ref[0],
        keep_dots,
        lambda: None,
        mask_ref,
        tables,
        sums,
        rest,
    )


def experts(block, rows, up_rows, ranks, weights, mask, tables, sums_before):
    sources, slots, width = rows.shape
    hidden = tables[0].shape[1]
    tokens = ranks.shape[2]
    token_spec = pl.BlockSpec((1, sources, tokens), lambda _, at: (at[0], 0, 0))

    def resident(array):
        return pl.BlockSpec(
            array.shape, lambda *_: (0,) * len(array.shape), pipeline_mode=pl.Buffered(1)
        )

    sums = expert_sums(tables)
    outs = [
        jax.ShapeDtypeStruct(rows.shape, BF16),
        jax.ShapeDtypeStruct(rows.shape, BF16),
        jax.ShapeDtypeStruct((sources, tokens), F32),
    ] + sums
    operands = [rows, up_rows, ranks, weights, mask, *tables, *sums_before]
    specs = (
        [resident(rows), resident(up_rows), token_spec, token_spec, resident(mask)]
        + [resident(table) for table in tables]
        + [resident(each) for each in sums_before]
    )
    return pl.pallas_call(
        experts_body,
        grid_spec=pltpu.PrefetchScalarGridSpec(
            num_scalar_prefetch=1,
            grid=(1,),
            in_specs=specs,
            out_specs=[resident(out) for out in outs],
            scratch_shapes=expert_scratch(sources * slots, hidden, width),
        ),
        out_shape=outs,
        input_output_aliases={
            1 + len(operands) - len(sums) + at: 3 + at for at in range(len(sums))
        },
        compiler_params=params(63),
        name="experts",
    )(block, *operands)


def moe_body(
    plane,
    line,
    own_ref,
    up_hbm,
    plane_rank_ref,
    rank_ref,
    weight_ref,
    mask_ref,
    *rest,
):
    tables_hbm, rest = rest[:8], rest[8:]
    total_ref, dots_ref, y_hbm, back_hbm = rest[:4]
    sums, rest = rest[4:9], rest[9:]
    tables, rest = rest[:8], rest[8:]
    (
        blocks,
        partials,
        partials_in,
        sent_slots,
        rows,
        up_rows,
        back_rows,
        choice,
        dots,
        dots_back,
        dots_pass,
        dots_in,
    ) = rest[:12]
    scratch, rest = rest[12:18], rest[18:]
    (
        table_sem,
        up_sem,
        y_sem,
        back_sem,
        own_sem,
        block_send,
        block_recv,
        row_send,
        row_recv,
        back_send,
        back_recv,
        partial_send,
        partial_recv,
        dots_send,
        dots_recv,
        dots_in_send,
        dots_in_recv,
    ) = rest
    width = own_ref.shape[1]
    slots = rows.shape[2]
    tile = 256
    me, at_line = lax.axis_index("fsdp"), lax.axis_index("tensor")

    greet_line_and_plane(line, plane)

    def block_copy(r):
        return pltpu.make_async_remote_copy(
            src_ref=own_ref,
            dst_ref=blocks.at[r],
            send_sem=block_send.at[r - 1],
            recv_sem=block_recv.at[r - 1],
            device_id={"tensor": lax.rem(at_line + line - r, line)},
        )

    def row_copy(r, d):
        target = lax.rem(me + d, plane)
        return pltpu.make_async_remote_copy(
            src_ref=sent_slots.at[lax.rem(r, 2), target],
            dst_ref=rows.at[r, me],
            send_sem=row_send.at[r, d],
            recv_sem=row_recv.at[r, d],
            device_id={"fsdp": target},
        )

    def own_rows(r):
        return pltpu.make_async_copy(
            sent_slots.at[lax.rem(r, 2), me], rows.at[r, me], own_sem.at[0]
        )

    def back_copy(r, d):
        target = lax.rem(me + d, plane)
        return pltpu.make_async_remote_copy(
            src_ref=rows.at[r, target],
            dst_ref=back_hbm.at[r, me],
            send_sem=back_send.at[r, d],
            recv_sem=back_recv.at[r, d],
            device_id={"fsdp": target},
        )

    def own_back(r):
        return pltpu.make_async_copy(rows.at[r, me], back_hbm.at[r, me], own_sem.at[1])

    def dots_copy(r, d):
        target = lax.rem(me + d, plane)
        return pltpu.make_async_remote_copy(
            src_ref=dots.at[r, target],
            dst_ref=dots_back.at[r, me],
            send_sem=dots_send.at[r, d],
            recv_sem=dots_recv.at[r, d],
            device_id={"fsdp": target},
        )

    def dots_in_copy(r):
        return pltpu.make_async_remote_copy(
            src_ref=dots_pass.at[r],
            dst_ref=dots_in.at[r],
            send_sem=dots_in_send.at[r - 1],
            recv_sem=dots_in_recv.at[r - 1],
            device_id={"tensor": lax.rem(at_line + r, line)},
        )

    def partial_copy(r):
        return pltpu.make_async_remote_copy(
            src_ref=partials.at[r - 1],
            dst_ref=partials_in.at[r - 1],
            send_sem=partial_send.at[r - 1],
            recv_sem=partial_recv.at[r - 1],
            device_id={"tensor": lax.rem(at_line + r, line)},
        )

    def up_copy(r):
        return pltpu.make_async_copy(
            up_hbm.at[:, lax.rem(at_line + r, line)], up_rows, up_sem
        )

    def y_copy(r):
        return pltpu.make_async_copy(up_rows, y_hbm.at[:, r], y_sem)

    @pl.loop(1, line)
    def _(r):
        block_copy(r).start()

    first_block = pltpu.make_async_copy(own_ref, blocks.at[0], own_sem.at[2])
    first_block.start()
    up_copy(0).start()
    table_copies = [
        pltpu.make_async_copy(source, target, table_sem.at[at])
        for at, (source, target) in enumerate(zip(tables_hbm, tables))
    ]
    for each in table_copies:
        each.start()
    for total in sums:
        total[...] = jnp.zeros_like(total)
    first_block.wait()

    @pl.loop(0, line + 2)
    def _(step):
        @pl.when(step < line)
        def _():
            @pl.when(step > 0)
            def _():
                block_copy(step).wait_recv()

            @pl.when(step > 1)
            def _():
                @pl.loop(1, plane)
                def _(d):
                    row_copy(step - 2, d).wait_send()

            choice[...] = slot_choice(plane_rank_ref[lax.rem(at_line + step, line)], slots)

            def slot_step(columns):
                sent_slots[lax.rem(step, 2), :, :, columns] = (
                    matrix_product(choice[...], blocks[step, :, columns])
                    .astype(BF16)
                    .reshape(plane, slots, 2 * tile)
                )

            tiles(width, 2 * tile, slot_step)

            @pl.loop(1, plane)
            def _(d):
                row_copy(step, d).start()

        @pl.when((step >= 1) & (step <= line))
        def _():
            r = step - 1
            block = lax.rem(at_line + r, line)

            @pl.when(r == 0)
            def _():
                for each in table_copies:
                    each.wait()

            own_rows(r).start()
            own_rows(r).wait()

            @pl.loop(1, plane)
            def _(d):
                row_copy(r, d).wait_recv()

            up_copy(r).wait()

            def keep_dots(source, values):
                dots[r, source] = jnp.broadcast_to(values, (8, values.shape[1]))

            expert_math(
                tile,
                rows.at[r],
                up_rows,
                rank_ref[block],
                weight_ref[block],
                keep_dots,
                lambda: y_copy(r).start(),
                mask_ref,
                tables,
                sums,
                scratch,
            )

            @pl.loop(1, plane)
            def _(d):
                dots_copy(r, d).start()
                back_copy(r, d).start()

            own_back(r).start()
            dots_back[r, me] = dots[r, me]
            y_copy(r).wait()

            @pl.when(r + 1 < line)
            def _():
                up_copy(r + 1).start()

            own_back(r).wait()

        @pl.when(step >= 2)
        def _():
            r = step - 2

            @pl.loop(1, plane)
            def _(d):
                dots_copy(r, d).wait_recv()
                back_copy(r, d).wait_recv()

            dots_pass[r] = dots_back[r, :, 0, :]
            load = pltpu.make_async_copy(back_hbm.at[r], back_rows, back_sem)
            load.start()
            choice[...] = slot_choice(plane_rank_ref[lax.rem(at_line + r, line)], slots)
            load.wait()

            def combined(columns):
                return flipped_left_operand(
                    choice[...], back_rows[:, :, columns].reshape(plane * slots, 2 * tile)
                )

            @pl.when(r == 0)
            def _():
                def keep(columns):
                    total_ref[:, columns] = combined(columns)

                tiles(width, 2 * tile, keep)
                dots_ref[at_line] = dots_pass[0]

            @pl.when(r > 0)
            def _():
                def pass_on(columns):
                    partials[r - 1, :, columns] = combined(columns).astype(BF16)

                dots_in_copy(r).start()
                tiles(width, 2 * tile, pass_on)
                partial_copy(r).start()

    @pl.loop(1, line)
    def _(r):
        dots_in_copy(r).wait_recv()
        dots_ref[lax.rem(at_line + line - r, line)] = dots_in[r]
        partial_copy(r).wait_recv()
        total_ref[...] += partials_in[r - 1].astype(F32)

    @pl.loop(1, line)
    def _(r):
        partial_copy(r).wait_send()
        dots_in_copy(r).wait_send()
        block_copy(r).wait_send()

    @pl.loop(1, plane)
    def _(d):
        row_copy(line - 2, d).wait_send()
        row_copy(line - 1, d).wait_send()

    @pl.loop(0, line)
    def _(r):
        @pl.loop(1, plane)
        def _(d):
            back_copy(r, d).wait_send()
            dots_copy(r, d).wait_send()


def moe_layer(own, up_rows, plane_ranks, ranks, weights, mask, tables, identity):
    line, plane, tokens = plane_ranks.shape
    slots, width = up_rows.shape[2:]
    hidden = tables[0].shape[1]
    sums = expert_sums(tables)
    anywhere = pl.BlockSpec(memory_space=pl.ANY)
    local = pl.BlockSpec(memory_space=pltpu.VMEM)
    grouped = (plane, slots, width)
    dma = pltpu.SemaphoreType.DMA
    return pl.pallas_call(
        functools.partial(moe_body, plane, line),
        out_shape=[
            jax.ShapeDtypeStruct((tokens, width), F32),
            jax.ShapeDtypeStruct((line, plane, tokens), F32),
            jax.ShapeDtypeStruct((plane, line, slots, width), BF16),
            jax.ShapeDtypeStruct((line,) + grouped, BF16),
        ]
        + sums,
        in_specs=[anywhere, anywhere, local, local, local, local] + [anywhere] * len(tables),
        out_specs=[local, local, anywhere, anywhere] + [local] * len(sums),
        scratch_shapes=[pltpu.VMEM(table.shape, table.dtype) for table in tables]
        + [
            pltpu.VMEM((line, tokens, width), BF16),
            pltpu.VMEM((line - 1, tokens, width), BF16),
            pltpu.VMEM((line - 1, tokens, width), BF16),
            pltpu.VMEM((2,) + grouped, BF16),
            pltpu.VMEM((line,) + grouped, BF16),
            pltpu.VMEM(grouped, BF16),
            pltpu.VMEM(grouped, BF16),
            pltpu.VMEM((plane * slots, tokens), BF16),
            pltpu.VMEM((line, plane, 8, tokens), F32),
            pltpu.VMEM((line, plane, 8, tokens), F32),
            pltpu.VMEM((line, plane, tokens), F32),
            pltpu.VMEM((line, plane, tokens), F32),
        ]
        + expert_scratch(plane * slots, hidden, width)
        + [dma((len(tables),)), dma, dma, dma, dma((3,))]
        + [dma((line - 1,))] * 2
        + [dma((line, plane))] * 4
        + [dma((line - 1,))] * 2
        + [dma((line, plane))] * 2
        + [dma((line - 1,))] * 2,
        compiler_params=pltpu.CompilerParams(
            collective_id=identity, has_side_effects=True, vmem_limit_bytes=63 * MEBI
        ),
        name="moe_layer",
    )(own, up_rows, plane_ranks, ranks, weights, mask, *tables)


def greet_line(me, count):
    barrier = pltpu.get_barrier_semaphore()

    @pl.when(me > 0)
    def _():
        pl.semaphore_signal(barrier, inc=1, device_id={"tensor": me - 1})

    @pl.when(me < count - 1)
    def _():
        pl.semaphore_signal(barrier, inc=1, device_id={"tensor": me + 1})

    @pl.when((me > 0) & (me < count - 1))
    def _():
        pl.semaphore_wait(barrier, 2)

    @pl.when((me == 0) | (me == count - 1))
    def _():
        pl.semaphore_wait(barrier, 1)


def gather_line_body(count, chunks, *refs):
    arrays = len(chunks)
    ins, outs = refs[:arrays], refs[arrays : 2 * arrays]
    semaphores, own_sem = refs[2 * arrays : -1], refs[-1]
    me = lax.axis_index("tensor")
    advance, finish = line_relay(me, count, ins, outs, chunks, semaphores)
    greet_line(me, count)
    own = [
        pltpu.make_async_copy(ins[at], outs[at].at[me], own_sem.at[at]) for at in range(arrays)
    ]
    everything = tuple(range(arrays))
    advance(0, everything)
    for each in own:
        each.start()
    for hop in range(1, count):
        advance(hop, everything)
    for each in own:
        each.wait()
    finish(everything, range(count - 1))


def gather_line(arrays, chunks, identity):
    count = lax.axis_size("tensor")
    total = sum(chunks)
    anywhere = pl.BlockSpec(memory_space=pl.ANY)
    return pl.pallas_call(
        functools.partial(gather_line_body, count, chunks),
        out_shape=[jax.ShapeDtypeStruct((count,) + a.shape, a.dtype) for a in arrays],
        in_specs=[anywhere] * len(arrays),
        out_specs=[anywhere] * len(arrays),
        scratch_shapes=[pltpu.SemaphoreType.DMA((count - 1, total))] * 4
        + [pltpu.SemaphoreType.DMA((len(arrays),))],
        compiler_params=pltpu.CompilerParams(collective_id=identity, has_side_effects=True),
        name="gather_line",
    )(*arrays)


def sum_line_body(count, chunks, part_ref, out_ref, left_buf, right_buf, *semaphores):
    me = lax.axis_index("tensor")
    advance, finish = line_sum(
        me, count, chunks, part_ref, out_ref, left_buf, right_buf, semaphores
    )
    greet_line(me, count)
    for far in range(count - 1, 0, -1):
        advance(far)
    finish()


def sum_line(part, chunks, identity):
    count, rows, width = part.shape
    semaphores = pltpu.SemaphoreType.DMA((count - 1, chunks))
    return pl.pallas_call(
        functools.partial(sum_line_body, count, chunks),
        out_shape=jax.ShapeDtypeStruct((rows, width), F32),
        in_specs=[pl.BlockSpec(memory_space=pltpu.VMEM)],
        out_specs=pl.BlockSpec(memory_space=pltpu.VMEM),
        scratch_shapes=[
            pltpu.VMEM((count - 1, rows, width), BF16),
            pltpu.VMEM((count - 1, rows, width), BF16),
        ]
        + [semaphores] * 4,
        compiler_params=pltpu.CompilerParams(
            collective_id=identity, has_side_effects=True, vmem_limit_bytes=32 * MEBI
        ),
        name="sum_line",
    )(part)


def line_relay(me, count, ins, outs, chunks, semaphores):
    right_send, right_recv, left_send, left_recv = semaphores
    pieces = []
    for at in range(len(ins)):
        size = ins[at].shape[0] // chunks[at]
        for piece in range(chunks[at]):
            pieces.append((at, pl.ds(piece * size, size)))

    def copy(place, hop, origin, target, send, recv):
        at, rows = pieces[place]
        source = ins[at].at[rows] if hop == 0 else outs[at].at[origin, rows]
        return pltpu.make_async_remote_copy(
            src_ref=source,
            dst_ref=outs[at].at[origin, rows],
            send_sem=send.at[hop, place],
            recv_sem=recv.at[hop, place],
            device_id={"tensor": target},
        )

    def places(arrays):
        return [place for place in range(len(pieces)) if pieces[place][0] in arrays]

    def advance(hop, arrays):
        for place in places(arrays):
            if hop > 0:

                @pl.when(me - hop >= 0)
                def _():
                    copy(place, hop - 1, me - hop, me - 1, right_send, right_recv).wait_recv()

            if hop < count - 1:

                @pl.when((me - hop >= 0) & (me + 1 < count))
                def _():
                    copy(place, hop, me - hop, me + 1, right_send, right_recv).start()

            if hop > 0:

                @pl.when(me + hop < count)
                def _():
                    copy(place, hop - 1, me + hop, me + 1, left_send, left_recv).wait_recv()

            if hop < count - 1:

                @pl.when((me + hop < count) & (me > 0))
                def _():
                    copy(place, hop, me + hop, me - 1, left_send, left_recv).start()

    def finish(arrays, hops):
        for hop in hops:
            for place in places(arrays):

                @pl.when((me - hop >= 0) & (me + 1 < count))
                def _():
                    copy(place, hop, me - hop, me + 1, right_send, right_recv).wait_send()

                @pl.when((me + hop < count) & (me > 0))
                def _():
                    copy(place, hop, me + hop, me - 1, left_send, left_recv).wait_send()

    return advance, finish


def line_sum(me, count, chunks, part_ref, out_ref, left_buf, right_buf, semaphores):
    right_send, right_recv, left_send, left_recv = semaphores
    size = part_ref.shape[1] // chunks

    def rightward(rows, piece, far, source):
        return pltpu.make_async_remote_copy(
            src_ref=source,
            dst_ref=left_buf.at[far - 1, rows],
            send_sem=right_send.at[far - 1, piece],
            recv_sem=right_recv.at[far - 1, piece],
            device_id={"tensor": me + 1},
        )

    def leftward(rows, piece, far, source):
        return pltpu.make_async_remote_copy(
            src_ref=source,
            dst_ref=right_buf.at[far - 1, rows],
            send_sem=left_send.at[far - 1, piece],
            recv_sem=left_recv.at[far - 1, piece],
            device_id={"tensor": me - 1},
        )

    def added(buffer, far, rows, block):
        buffer[far, rows, :] = (
            buffer[far, rows, :].astype(F32) + part_ref[block, rows, :].astype(F32)
        ).astype(BF16)

    def advance(far):
        for piece in range(chunks):
            rows = pl.ds(piece * size, size)

            @pl.when((me == 0) & (me + far < count))
            def _():
                rightward(rows, piece, far, part_ref.at[me + far, rows]).start()

            @pl.when((me == count - 1) & (me - far >= 0))
            def _():
                leftward(rows, piece, far, part_ref.at[me - far, rows]).start()

            if far < count - 1:

                @pl.when((me > 0) & (me + far < count))
                def _():
                    rightward(rows, piece, far + 1, left_buf.at[far, rows]).wait_recv()
                    added(left_buf, far, rows, me + far)
                    rightward(rows, piece, far, left_buf.at[far, rows]).start()

                @pl.when((me < count - 1) & (me - far >= 0))
                def _():
                    leftward(rows, piece, far + 1, right_buf.at[far, rows]).wait_recv()
                    added(right_buf, far, rows, me - far)
                    leftward(rows, piece, far, right_buf.at[far, rows]).start()

    def finish():
        for piece in range(chunks):
            rows = pl.ds(piece * size, size)
            out_ref[rows, :] = part_ref[me, rows, :].astype(F32)

            @pl.when(me > 0)
            def _():
                rightward(rows, piece, 1, left_buf.at[0, rows]).wait_recv()
                out_ref[rows, :] += left_buf[0, rows, :].astype(F32)

            @pl.when(me < count - 1)
            def _():
                leftward(rows, piece, 1, right_buf.at[0, rows]).wait_recv()
                out_ref[rows, :] += right_buf[0, rows, :].astype(F32)

        for far in range(count - 1, 0, -1):
            for piece in range(chunks):
                rows = pl.ds(piece * size, size)

                @pl.when((me == 0) & (me + far < count))
                def _():
                    rightward(rows, piece, far, part_ref.at[me + far, rows]).wait_send()

                @pl.when((me == count - 1) & (me - far >= 0))
                def _():
                    leftward(rows, piece, far, part_ref.at[me - far, rows]).wait_send()

                if far < count - 1:

                    @pl.when((me > 0) & (me + far < count))
                    def _():
                        rightward(rows, piece, far, left_buf.at[far, rows]).wait_send()

                    @pl.when((me < count - 1) & (me - far >= 0))
                    def _():
                        leftward(rows, piece, far, right_buf.at[far, rows]).wait_send()

    return advance, finish


def greet_line_and_plane(line, plane):
    me, at_line = lax.axis_index("fsdp"), lax.axis_index("tensor")
    barrier = pltpu.get_barrier_semaphore()

    @pl.loop(1, plane)
    def _(d):
        pl.semaphore_signal(barrier, inc=1, device_id={"fsdp": lax.rem(me + d, plane)})

    @pl.loop(1, line)
    def _(d):
        pl.semaphore_signal(barrier, inc=1, device_id={"tensor": lax.rem(at_line + d, line)})

    pl.semaphore_wait(barrier, plane + line - 2)


def front_body(
    plane,
    line,
    scale,
    places,
    tokens_hbm,
    cotangent_hbm,
    routes_hbm,
    weights_hbm,
    gain_ref,
    first_ref,
    q_second_ref,
    k_second_ref,
    v_second_ref,
    q_gain_ref,
    k_gain_ref,
    cos_ref,
    sin_ref,
    seg_column_ref,
    seg_row_ref,
    out_first_ref,
    out_second_ref,
    before_ref,
    total_ref,
    ranks_ref,
    low_ref,
    out_low_ref,
    linear_hbm,
    heads_hbm,
    normed_hbm,
    gathered_hbm,
    up_hbm,
    rows,
    upstream,
    routes,
    weights,
    linear,
    heads,
    keys,
    values,
    part,
    left_buf,
    right_buf,
    sent_slots,
    choice,
    own_sem,
    save_sem,
    relay_right_send,
    relay_right_recv,
    relay_left_send,
    relay_left_recv,
    weight_send,
    weight_recv,
    pass_send,
    pass_recv,
    sum_right_send,
    sum_right_recv,
    sum_left_send,
    sum_left_recv,
    slot_send,
    slot_recv,
):
    me, at_line = lax.axis_index("fsdp"), lax.axis_index("tensor")
    rank = q_second_ref.shape[0]
    head_dim = q_gain_ref.shape[1]
    tokens, width = tokens_hbm.shape
    slots = sent_slots.shape[2]
    tile = 256
    query_columns = q_second_ref.shape[1]
    linear_columns = linear.shape[1]
    out_start = places[1]

    greet_line_and_plane(line, plane)

    beside = me + 1 - 2 * lax.rem(me, 2)

    def weight_copy(k):
        target = lax.rem(me + 2 * k, plane)
        return pltpu.make_async_remote_copy(
            src_ref=weights_hbm,
            dst_ref=weights.at[me],
            send_sem=weight_send.at[k],
            recv_sem=weight_recv.at[k],
            device_id={"fsdp": target},
        )

    def weight_pass(k):
        origin = lax.rem(me + plane - 2 * k, plane)
        return pltpu.make_async_remote_copy(
            src_ref=weights_hbm if k == 0 else weights.at[origin],
            dst_ref=weights.at[origin],
            send_sem=pass_send.at[k],
            recv_sem=pass_recv.at[k],
            device_id={"fsdp": beside},
        )

    peers = plane // 2
    for k in range(1, peers):
        weight_copy(k).start()
    weight_pass(0).start()
    locals_in = [
        pltpu.make_async_copy(source, target, own_sem.at[at])
        for at, (source, target) in enumerate(
            [
                (tokens_hbm, rows.at[at_line]),
                (routes_hbm, routes.at[at_line]),
                (cotangent_hbm, upstream.at[at_line]),
                (weights_hbm, weights.at[me]),
            ]
        )
    ]
    advance, finish_relay = line_relay(
        at_line,
        line,
        [tokens_hbm, routes_hbm, cotangent_hbm],
        [rows, routes, upstream],
        (4, 1, 4),
        (relay_right_send, relay_right_recv, relay_left_send, relay_left_recv),
    )
    advance(0, (0, 1))
    advance(0, (2,))
    for each in locals_in:
        each.start()
    advance(1, (0, 1))
    advance(2, (0, 1))
    for k in range(1, peers):
        weight_copy(k).wait_recv()
        weight_pass(k).start()
    advance(3, (0, 1))
    for each in locals_in:
        each.wait()

    for block in range(line):
        named = [
            jnp.max(
                (routes[block] == expert * line + at_line).astype(F32), axis=0, keepdims=True
            )
            for expert in range(plane)
        ]
        mask = jnp.concatenate(named, axis=0)
        counts = matrix_product(mask.astype(BF16), before_ref[...])
        ranks_ref[block] = jnp.where(mask > 0.0, counts, -1.0)

    def slot_copy(block, d):
        target = lax.rem(me + d, plane)
        return pltpu.make_async_remote_copy(
            src_ref=sent_slots.at[block, target],
            dst_ref=up_hbm.at[me, block],
            send_sem=slot_send.at[block, d],
            recv_sem=slot_recv.at[block, d],
            device_id={"fsdp": target},
        )

    def own_slots(block):
        return pltpu.make_async_copy(
            sent_slots.at[block, me], up_hbm.at[me, block], save_sem.at[4 + block]
        )

    def dispatch(block):
        choice[...] = slot_choice(ranks_ref[block], slots)

        def slot_step(columns):
            sent_slots[block, :, :, columns] = (
                matrix_product(choice[...], upstream[block, :, columns])
                .astype(BF16)
                .reshape(plane, slots, 2 * tile)
            )

        tiles(width, 2 * tile, slot_step)

        @pl.loop(1, plane)
        def _(d):
            slot_copy(block, d).start()

    def dispatch_at(distance):
        if distance == 0:
            dispatch(at_line)
            return

        @pl.when(at_line - distance >= 0)
        def _():
            dispatch(at_line - distance)

        @pl.when(at_line + distance < line)
        def _():
            dispatch(at_line + distance)

    dispatch_at(0)

    finish_relay((0,), range(1, line - 1))

    @pl.loop(0, line * tokens // 128)
    def _(j):
        block, at = j // (tokens // 128), pl.ds((j % (tokens // 128)) * 128, 128)
        wide = rows[block, at, :].astype(F32)
        rows[block, at, :] = norm_forward(wide, gain_ref[...])[0].astype(BF16)

    for k in range(peers):
        weight_pass(k).wait_recv()
    saves = [
        pltpu.make_async_copy(rows, normed_hbm, save_sem.at[0]),
        pltpu.make_async_copy(weights, gathered_hbm, save_sem.at[1]),
        pltpu.make_async_copy(linear, linear_hbm, save_sem.at[2]),
        pltpu.make_async_copy(heads, heads_hbm, save_sem.at[3]),
    ]
    saves[0].start()
    saves[1].start()

    @pl.loop(0, line)
    def _(block):
        at = pl.ds(pl.multiple_of(block * tokens, tokens), tokens)
        low_ref[at, :] = flipped_right_operand(rows[block], first_ref[...]).astype(BF16)

        def project(columns):
            linear[at, columns] = matrix_product(
                rows[block], weights[:, :, columns].reshape(width, tile)
            )

        tiles(linear_columns, tile, project)

    saves[2].start()
    advance(1, (2,))
    dispatch_at(1)

    cosine, sine = cos_ref[...], sin_ref[...]
    keys[...] = head_values(
        linear[:, query_columns : query_columns + head_dim],
        low_ref[:, rank : 2 * rank],
        k_second_ref[...],
        k_gain_ref[...],
        cosine,
        sine,
    )[2]
    values[...] = (
        linear[:, query_columns + head_dim : query_columns + 2 * head_dim]
        + matrix_product(low_ref[:, 2 * rank : 3 * rank], v_second_ref[...])
    ).astype(BF16)

    @pl.loop(0, query_columns // head_dim)
    def _(head):
        columns = pl.ds(pl.multiple_of(head * head_dim, head_dim), head_dim)
        query = head_values(
            linear[:, columns],
            low_ref[:, :rank],
            q_second_ref[:, columns],
            q_gain_ref[...],
            cos_ref[...],
            sin_ref[...],
        )[2]
        seg_column, seg_row = seg_column_ref[...], seg_row_ref[...]
        for block in range(query.shape[0] // WINDOW):
            start, span = block_bounds(block)
            scores = (
                flipped_right_operand(
                    query[block * WINDOW : (block + 1) * WINDOW], keys[pl.ds(start, span)]
                )
                * scale
            )
            scores = jnp.where(
                allowed_keys(block, start, span, seg_column, seg_row), scores, -1e30
            )
            expo = jnp.exp(scores - jnp.max(scores, axis=-1, keepdims=True))
            probs = (expo / jnp.sum(expo, axis=-1, keepdims=True)).astype(BF16)
            heads[pl.ds(block * WINDOW, WINDOW), columns] = matrix_product(
                probs, values[pl.ds(start, span)]
            ).astype(BF16)

    saves[3].start()
    advance(2, (2,))
    dispatch_at(2)

    out_low_ref[...] = flipped_right_operand(heads[...], out_first_ref[...]).astype(BF16)

    @pl.loop(0, line)
    def _(block):
        at = pl.ds(pl.multiple_of(block * tokens, tokens), tokens)

        @pl.loop(0, plane)
        def _(shard):
            wide = width // plane
            columns = pl.ds(pl.multiple_of(shard * wide, wide), wide)
            part[block, :, columns] = (
                flipped_right_operand(heads[at, :], weights[shard, :, out_start:])
                + matrix_product(out_low_ref[at, :], out_second_ref[:, columns])
            ).astype(BF16)

    advance_sum, finish_sum = line_sum(
        at_line,
        line,
        4,
        part,
        total_ref,
        left_buf,
        right_buf,
        (sum_right_send, sum_right_recv, sum_left_send, sum_left_recv),
    )
    for far in range(line - 1, 0, -1):
        advance_sum(far)
        if far == 2:
            advance(3, (2,))
            dispatch_at(3)
    finish_sum()

    for block in range(line):
        own_slots(block).start()
    for each in saves:
        each.wait()
    finish_relay((0,), (0,))
    finish_relay((1, 2), range(line - 1))
    for k in range(1, peers):
        weight_copy(k).wait_send()
    for k in range(peers):
        weight_pass(k).wait_send()

    @pl.loop(0, line)
    def _(block):
        @pl.loop(1, plane)
        def _(d):
            slot_copy(block, d).wait_recv()
            slot_copy(block, d).wait_send()

    for block in range(line):
        own_slots(block).wait()


def front(
    tokens,
    cotangent,
    routes,
    packed,
    gain,
    first,
    q_second,
    k_second,
    v_second,
    q_gain,
    k_gain,
    tables,
    seg_column,
    seg_row,
    out_first,
    out_second,
    scale,
    slots,
    places,
    identity,
):
    line, plane = lax.axis_size("tensor"), lax.axis_size("fsdp")
    count, width = tokens.shape
    all_rows = line * count
    rank, query_columns = q_second.shape
    head_dim = q_gain.shape[1]
    linear_columns = query_columns + 2 * head_dim
    order = jnp.arange(count, dtype=jnp.int32)
    before = (order[:, None] < order[None, :]).astype(BF16)
    anywhere = pl.BlockSpec(memory_space=pl.ANY)
    local = pl.BlockSpec(memory_space=pltpu.VMEM)
    dma = pltpu.SemaphoreType.DMA
    up_shape = (plane, line, slots, width)
    operands = [
        gain,
        first,
        q_second,
        k_second,
        v_second,
        q_gain,
        k_gain,
        *tables,
        seg_column,
        seg_row,
        out_first,
        out_second,
        before,
    ]
    return pl.pallas_call(
        functools.partial(front_body, plane, line, scale, places),
        out_shape=[
            jax.ShapeDtypeStruct((count, width), F32),
            jax.ShapeDtypeStruct((line, plane, count), F32),
            jax.ShapeDtypeStruct((all_rows, 3 * rank), BF16),
            jax.ShapeDtypeStruct((all_rows, rank), BF16),
            jax.ShapeDtypeStruct((all_rows, linear_columns), F32),
            jax.ShapeDtypeStruct((all_rows, query_columns), BF16),
            jax.ShapeDtypeStruct((line, count, width), BF16),
            jax.ShapeDtypeStruct((plane,) + packed.shape, BF16),
            jax.ShapeDtypeStruct(up_shape, BF16),
        ],
        in_specs=[anywhere] * 4 + [local] * len(operands),
        out_specs=[local] * 4 + [anywhere] * 5,
        scratch_shapes=[
            pltpu.VMEM((line, count, width), BF16),
            pltpu.VMEM((line, count, width), BF16),
            pltpu.VMEM((line,) + routes.shape, jnp.int32),
            pltpu.VMEM((plane,) + packed.shape, BF16),
            pltpu.VMEM((all_rows, linear_columns), F32),
            pltpu.VMEM((all_rows, query_columns), BF16),
            pltpu.VMEM((all_rows, head_dim), BF16),
            pltpu.VMEM((all_rows, head_dim), BF16),
            pltpu.VMEM((line, count, width), BF16),
            pltpu.VMEM((line - 1, count, width), BF16),
            pltpu.VMEM((line - 1, count, width), BF16),
            pltpu.VMEM((line, plane, slots, width), BF16),
            pltpu.VMEM((plane * slots, count), BF16),
            dma((4,)),
            dma((4 + line,)),
        ]
        + [dma((line - 1, 9))] * 4
        + [dma((plane // 2,))] * 4
        + [dma((line - 1, 4))] * 4
        + [dma((line, plane))] * 2,
        compiler_params=pltpu.CompilerParams(
            collective_id=identity, has_side_effects=True, vmem_limit_bytes=63 * MEBI
        ),
        name="front",
    )(tokens, cotangent, routes, packed, *operands)


def per_device(
    tokens,
    segments,
    routes,
    adapter_index,
    cotangent,
    attn_gain,
    moe_gain,
    q_gain,
    key_norm_gain,
    w_query,
    key_projection_weight,
    value_projection_weight,
    w_out,
    w_router,
    expert_gate_weight,
    expert_up_weight,
    expert_down_weight,
    query_in,
    query_out,
    key_in,
    key_second_weight,
    value_in,
    value_second_weight,
    attn_in,
    attn_out,
    router_in,
    router_out,
    gate_in,
    gate_out,
    upward_in,
    upward_out,
    downward_in,
    downward_out,
):
    tensor_count = lax.axis_size("tensor")
    fsdp_count = lax.axis_size("fsdp")
    device_count = fsdp_count * tensor_count
    tensor_pos = lax.axis_index("tensor")
    fsdp_pos = lax.axis_index("fsdp")
    zero_pos = fsdp_pos * 0
    tok_rows, model_width = tokens.shape
    seq_rows = tok_rows * tensor_count
    rank = query_in.shape[2]
    adapter_count = query_in.shape[0]
    head_dim = q_gain.shape[0]
    local_cols = query_out.shape[2]
    local_kv_cols = key_second_weight.shape[2]
    expert_count = w_router.shape[1]
    top_count = routes.shape[1]
    capacity = 5 * tok_rows * top_count // (4 * expert_count)
    slots = -(-capacity // 16) * 16
    score_scale = 1.0 / math.sqrt(head_dim)
    adapter_pick = lax.dynamic_index_in_dim(adapter_index, fsdp_pos, 0, keepdims=False)

    def select_adapter(adapter_table):
        return lax.dynamic_index_in_dim(adapter_table, adapter_pick, 0, keepdims=False)

    def transposed(adapter_table):
        return jnp.swapaxes(adapter_table, -1, -2)

    input_first = jnp.concatenate(
        [select_adapter(transposed(table)) for table in (query_in, key_in, value_in)], axis=0
    )
    q_second = select_adapter(query_out)
    k_second = select_adapter(key_second_weight)
    v_second = select_adapter(value_second_weight)
    attention_first = select_adapter(transposed(attn_in))
    attention_second = select_adapter(attn_out)
    router_first = select_adapter(transposed(router_in))
    router_second = select_adapter(router_out)
    gain_attn = attn_gain.astype(F32)
    gain_moe = moe_gain.astype(F32)
    gain_query = q_gain.astype(F32)[None, :]
    gain_key = key_norm_gain.astype(F32)[None, :]

    in_kernel = fsdp_count * slots <= 640
    linear_cols = local_cols + 2 * local_kv_cols
    router_pad = -(-expert_count // 128) * 128
    out_start = linear_cols + router_pad
    packed = jnp.concatenate(
        [
            w_query,
            key_projection_weight,
            value_projection_weight,
            jnp.pad(w_router, ((0, 0), (0, router_pad - expert_count))),
            jnp.transpose(w_out, (1, 0)),
        ],
        axis=1,
    )
    tables = rope_tables(seq_rows, head_dim)
    seg_row = segments
    seg_column = jnp.transpose(segments, (1, 0))
    token_values = tokens.astype(F32)
    attn_normed, attn_factor = norm_forward(token_values, gain_attn)
    offsets = [0] + [sign * step for step in range(1, tensor_count) for sign in (1, -1)]
    offsets = [offset % tensor_count for offset in offsets[:tensor_count]]
    line_blocks = [((tensor_pos + offset) % tensor_count)[None] for offset in offsets]

    def fetched(block, offset):
        if offset == 0:
            return block
        pairs = [((at + offset) % tensor_count, at) for at in range(tensor_count)]
        return lax.ppermute(block, "tensor", pairs)

    def delivered(block, offset):
        if offset == 0:
            return block
        pairs = [(at, (at + offset) % tensor_count) for at in range(tensor_count)]
        return lax.ppermute(block, "tensor", pairs)

    def dispatched(block):
        return [
            plane_rows(to_slots(at, plane_ranks, fetched(block, offset), slots))
            for offset, at in zip(offsets, line_blocks)
        ]

    if in_kernel:
        (
            attention_total,
            plane_ranks,
            low,
            attention_low,
            linear,
            heads_narrow,
            sequence_normalized,
            gathered,
            up_rows,
        ) = front(
            tokens,
            cotangent,
            jnp.transpose(routes, (1, 0)),
            packed,
            gain_attn[None, :],
            input_first,
            q_second,
            k_second,
            v_second,
            gain_query,
            gain_key,
            tables,
            seg_column,
            seg_row,
            attention_first,
            attention_second,
            score_scale,
            slots,
            (linear_cols, out_start),
            0,
        )
        sequence_normalized = sequence_normalized.reshape(seq_rows, model_width)
        gathered = gathered.reshape(model_width, -1)
    else:
        gathered = lax.all_gather(packed, "fsdp", axis=0, tiled=True)
        sequence_tokens, sequence_routes = gather_line(
            [tokens, jnp.transpose(routes, (1, 0))], (4, 1), 0
        )
        sequence_tokens = sequence_tokens.reshape(seq_rows, model_width)
        plane_experts = jnp.arange(fsdp_count, dtype=jnp.int32) * tensor_count + tensor_pos
        plane_ranks = ranks_of(
            jnp.any(
                sequence_routes[:, None, :, :] == plane_experts[None, :, None, None], axis=2
            )
        )
        up_rows = dispatched(cotangent)
        sequence_normalized = norm_forward(sequence_tokens.astype(F32), gain_attn)[0].astype(
            BF16
        )
        linear = matrix_product(sequence_normalized, gathered[:, :linear_cols])
        low = flipped_right_operand(sequence_normalized, input_first).astype(BF16)
    complete_linear = gathered[:, :linear_cols]
    complete_router = gathered[:, linear_cols : linear_cols + expert_count]
    full_out_t = gathered[:, out_start:]
    attention_operands = (
        linear,
        low,
        q_second,
        k_second,
        v_second,
        gain_query,
        gain_key,
        tables,
        seg_column,
        seg_row,
        score_scale,
    )
    if not in_kernel:
        heads_narrow = attention_forward(*attention_operands)
        attention_low = flipped_right_operand(heads_narrow, attention_first).astype(BF16)
        out_part = flipped_right_operand(heads_narrow, full_out_t) + matrix_product(
            attention_low, attention_second
        )
        attention_total = sum_line(
            out_part.astype(BF16).reshape(tensor_count, tok_rows, model_width), 4, 1
        )
    residual_stream = token_values + attention_total
    moe_normed, moe_factor = norm_forward(residual_stream, gain_moe)
    experts_narrow = moe_normed.astype(BF16)

    router_low = flipped_right_operand(experts_narrow, router_first).astype(BF16)
    router_logits = matrix_product(experts_narrow, complete_router) + matrix_product(
        router_low, router_second
    )
    expert_ids = jnp.arange(expert_count, dtype=jnp.int32)
    chosen = jnp.any(routes[:, :, None] == expert_ids[None, None, :], axis=1)
    chosen_logits = jnp.where(chosen, router_logits, -jnp.inf)
    chosen_exp = jnp.exp(chosen_logits - jnp.max(chosen_logits, axis=-1, keepdims=True))
    gate_weights = chosen_exp / jnp.sum(chosen_exp, axis=-1, keepdims=True)
    sent_weights = jnp.transpose(jnp.where(chosen, gate_weights, -1.0), (1, 0))
    own_weights = jnp.transpose(
        route_rows(sent_weights).reshape(fsdp_count, tensor_count, tok_rows), (1, 0, 2)
    )
    own_ranks = ranks_of(own_weights >= 0.0)

    broad = adapter_count * rank
    gate_in_t, upward_in_t = transposed(gate_in[0]), transposed(upward_in[0])
    expert_tables = (
        expert_gate_weight[0],
        expert_up_weight[0],
        expert_down_weight[0],
        jnp.concatenate(
            [gate_in_t.reshape(broad, model_width), upward_in_t.reshape(broad, model_width)],
            axis=0,
        ),
        gate_out[0].reshape(broad, -1),
        upward_out[0].reshape(broad, -1),
        transposed(downward_in[0]).reshape(broad, -1),
        downward_out[0].reshape(broad, model_width),
    )
    column_adapter = jnp.arange(broad, dtype=jnp.int32) // rank
    adapter_mask = jnp.repeat(
        (adapter_index[:, None] == column_adapter[None, :]).astype(BF16), slots, axis=0
    )
    ordered = [None] * tensor_count
    if in_kernel:
        moe_grad, gate_dots, expert_output, _landed, *sums = moe_layer(
            experts_narrow,
            up_rows,
            plane_ranks,
            own_ranks,
            own_weights,
            adapter_mask,
            expert_tables,
            3,
        )
    else:
        expert_rows = dispatched(experts_narrow)
        expert_output, rows_grad, gate_dots = [], [], []
        sums = [jnp.zeros(each.shape, F32) for each in expert_sums(expert_tables)]
        for at, rows, upstream in zip(line_blocks, expert_rows, up_rows):
            y_rows, grad_rows, dots, *sums = experts(
                at, rows, upstream, own_ranks, own_weights, adapter_mask, expert_tables, sums
            )
            expert_output.append(y_rows)
            rows_grad.append(grad_rows)
            gate_dots.append(dots)
        for offset, dots in zip(offsets, gate_dots):
            ordered[offset] = dots
        gate_dots = jnp.roll(jnp.stack(ordered), tensor_pos, axis=0)
    pair_in_grad, gate_out_grad, upward_out_grad, downward_in_grad, downward_out_grad = sums
    if in_kernel:
        gate_grad = jnp.transpose(gate_dots, (2, 1, 0)).reshape(tok_rows, expert_count)
    else:
        gate_grad = jnp.transpose(
            route_rows(jnp.transpose(gate_dots, (1, 0, 2)).reshape(device_count, tok_rows)),
            (1, 0),
        )

    def returned(slotted):
        total = 0.0
        for offset, at, rows in zip(offsets, line_blocks, slotted):
            combined = from_slots(at, plane_ranks, plane_rows(rows))
            total = total + delivered(combined, offset).astype(F32)
        return total

    if not in_kernel:
        moe_grad = returned(rows_grad)

    out_grad = cotangent.astype(F32)
    logit_gradient = (
        gate_weights * (gate_grad - jnp.sum(gate_weights * gate_grad, axis=-1, keepdims=True))
    ).astype(BF16)
    router_low_gradient = flipped_right_operand(logit_gradient, router_second).astype(BF16)
    moe_grad = (
        moe_grad
        + flipped_right_operand(logit_gradient, complete_router)
        + matrix_product(router_low_gradient, router_first)
    )
    router_first_gradient = flipped_left_operand(router_low_gradient, experts_narrow)
    router_second_gradient = flipped_left_operand(router_low, logit_gradient)
    residual_grad = out_grad + norm_backward(residual_stream, moe_factor, gain_moe, moe_grad)

    (sequence_branch,) = gather_line([residual_grad.astype(BF16)], (4,), 2)
    sequence_branch = sequence_branch.reshape(seq_rows, model_width)
    if in_kernel:
        back_output = plane_rows(
            expert_output.reshape(fsdp_count, tensor_count * slots, model_width)
        ).reshape(fsdp_count, tensor_count, slots, model_width)
    else:
        output = (residual_stream + returned(expert_output)).astype(BF16)
    attention_low_grad = flipped_right_operand(sequence_branch, attention_second).astype(BF16)
    attention_second_gradient = flipped_left_operand(attention_low, sequence_branch)
    heads_grad = matrix_product(sequence_branch, full_out_t)
    if in_kernel:
        back_output, heads_grad = lax.optimization_barrier((back_output, heads_grad))
        combined = all_from_slots(tensor_pos[None], plane_ranks, back_output)
        moe_output = lax.psum_scatter(combined, "tensor", scatter_dimension=0, tiled=True)
        output = (residual_stream + moe_output.astype(F32)).astype(BF16)
    (
        q_grad,
        k_grad,
        v_grad,
        low_share,
        q_second_gradient,
        k_second_gradient,
        v_second_gradient,
        attention_first_gradient,
    ) = attention_backward(
        *attention_operands,
        heads_narrow,
        heads_grad,
        attention_low_grad,
        attention_first,
    )
    linear_grad = jnp.concatenate([q_grad, k_grad, v_grad], axis=1)
    normed_part = flipped_right_operand(linear_grad, complete_linear) + matrix_product(
        low_share, input_first
    )
    input_first_gradient = flipped_left_operand(low_share, sequence_normalized)
    normalized_gradient = sum_line(
        normed_part.astype(BF16).reshape(tensor_count, tok_rows, model_width), 4, 1
    )
    input_grad = residual_grad + norm_backward(
        token_values, attn_factor, gain_attn, normalized_gradient
    )

    source_adapter = jnp.repeat(adapter_index, tensor_count)
    owner_onehot = (
        jnp.arange(adapter_count, dtype=jnp.int32)[:, None] == source_adapter[None, :]
    ).astype(BF16)

    def to_all(addend):
        lines = addend.shape[0]
        return jnp.transpose(
            addend.astype(BF16).reshape(lines, device_count, -1), (1, 0, 2)
        ).reshape(device_count, -1)

    def to_head_owners(addend):
        lines = addend.shape[0]
        pieces = jnp.transpose(
            addend.astype(BF16).reshape(lines, fsdp_count, -1), (1, 0, 2)
        ).reshape(fsdp_count, -1)
        holder = jnp.zeros((device_count, pieces.shape[1]), BF16)
        return lax.dynamic_update_slice(holder, pieces, (tensor_pos * fsdp_count, zero_pos))

    def owner_sums(parts):
        widths = [part.shape[1] for part in parts]
        total = matrix_product(owner_onehot, route_rows(jnp.concatenate(parts, axis=1)))
        pieces = []
        start = 0
        for width in widths:
            pieces.append(total[:, start : start + width])
            start += width
        return pieces

    early = owner_sums(
        [
            to_all(router_first_gradient),
            to_all(attention_second_gradient),
            to_all(router_second_gradient),
        ]
    )
    late = owner_sums(
        [
            to_all(input_first_gradient),
            to_head_owners(q_second_gradient),
            to_head_owners(k_second_gradient),
            to_head_owners(v_second_gradient),
            to_head_owners(attention_first_gradient),
        ]
    )

    def lines_of(piece, lines):
        return piece.reshape(adapter_count, lines, -1)

    first_sums = lines_of(late[0], 3 * rank)
    return (
        output,
        input_grad,
        transposed(first_sums[:, :rank]),
        lines_of(late[1], rank),
        transposed(first_sums[:, rank : 2 * rank]),
        lines_of(late[2], rank),
        transposed(first_sums[:, 2 * rank :]),
        lines_of(late[3], rank),
        transposed(lines_of(late[4], rank)),
        lines_of(early[1], rank),
        transposed(lines_of(early[0], rank)),
        lines_of(early[2], rank),
        transposed(lines_of(pair_in_grad[:broad], rank))[None],
        lines_of(gate_out_grad, rank)[None],
        transposed(lines_of(pair_in_grad[broad:], rank))[None],
        lines_of(upward_out_grad, rank)[None],
        transposed(lines_of(downward_in_grad, rank))[None],
        lines_of(downward_out_grad, rank)[None],
    )


def solution(mesh):
    placed = (
        P(("fsdp", "tensor"), None),
        P("fsdp", None),
        P(("fsdp", "tensor"), None),
        P(),
        P(("fsdp", "tensor"), None),
        P(),
        P(),
        P(),
        P(),
        P("fsdp", "tensor"),
        P("fsdp", "tensor"),
        P("fsdp", "tensor"),
        P("tensor", "fsdp"),
        P("fsdp", None),
        P(("fsdp", "tensor"), None, None),
        P(("fsdp", "tensor"), None, None),
        P(("fsdp", "tensor"), None, None),
        P(),
        P(None, None, "tensor"),
        P(),
        P(None, None, "tensor"),
        P(),
        P(None, None, "tensor"),
        P(None, "tensor", None),
        P(),
        P(),
        P(),
        P(("fsdp", "tensor"), None, None, None),
        P(("fsdp", "tensor"), None, None, None),
        P(("fsdp", "tensor"), None, None, None),
        P(("fsdp", "tensor"), None, None, None),
        P(("fsdp", "tensor"), None, None, None),
        P(("fsdp", "tensor"), None, None, None),
    )
    return jax.shard_map(
        per_device,
        mesh=mesh,
        in_specs=placed,
        out_specs=(
            P(("fsdp", "tensor"), None),
            P(("fsdp", "tensor"), None),
            P(None, ("fsdp", "tensor"), None),
            P(None, None, ("fsdp", "tensor")),
            P(None, ("fsdp", "tensor"), None),
            P(None, None, ("fsdp", "tensor")),
            P(None, ("fsdp", "tensor"), None),
            P(None, None, ("fsdp", "tensor")),
            P(None, ("fsdp", "tensor"), None),
            P(None, None, ("fsdp", "tensor")),
            P(None, ("fsdp", "tensor"), None),
            P(None, None, ("fsdp", "tensor")),
            P(("fsdp", "tensor"), None, None, None),
            P(("fsdp", "tensor"), None, None, None),
            P(("fsdp", "tensor"), None, None, None),
            P(("fsdp", "tensor"), None, None, None),
            P(("fsdp", "tensor"), None, None, None),
            P(("fsdp", "tensor"), None, None, None),
        ),
        check_vma=False,
    )
```

```python
import functools
import math

import jax
import jax.numpy as jnp
from jax import lax
from jax.experimental import pallas as pl
from jax.experimental.pallas import tpu as pltpu
from jax.sharding import PartitionSpec as P

NORM_EPSILON = 1e-06
ROPE_THETA = 1000000.0
BF16 = jnp.bfloat16
F32 = jnp.float32
WINDOW = 256
MEBI = 1 << 20


def matrix_product(first_op, second_op):
    return jnp.dot(first_op, second_op, preferred_element_type=F32)


def flipped_left_operand(first_op, second_op):
    return lax.dot_general(
        first_op, second_op, (((0,), (0,)), ((), ())), preferred_element_type=F32
    )


def flipped_right_operand(first_op, second_op):
    return lax.dot_general(
        first_op, second_op, (((1,), (1,)), ((), ())), preferred_element_type=F32
    )


def norm_forward(values, gain_vec):
    factor = lax.rsqrt(jnp.mean(values * values, axis=-1, keepdims=True) + NORM_EPSILON)
    return (values * factor * gain_vec, factor)


def norm_backward(values, factor, gain_vec, upstream):
    scaled = upstream * gain_vec
    return factor * scaled - values * (factor * factor * factor) * jnp.mean(
        values * scaled, axis=-1, keepdims=True
    )


def rope_tables(sequence_length, head_width):
    half_width = head_width // 2
    inverse = jnp.power(ROPE_THETA, -2.0 * jnp.arange(half_width, dtype=F32) / head_width)
    angles = jnp.arange(sequence_length, dtype=F32)[:, None] * inverse[None, :]
    cosine, sine = jnp.cos(angles), jnp.sin(angles)
    return (
        jnp.concatenate([cosine, cosine], axis=1),
        jnp.concatenate([-sine, sine], axis=1),
    )


def swapped(values):
    return pltpu.roll(values, values.shape[-1] // 2, 1)


def route_rows(block_rows):
    return lax.all_to_all(block_rows, ("fsdp", "tensor"), split_axis=0, concat_axis=0, tiled=True)


def plane_rows(block_rows):
    return lax.all_to_all(block_rows, "fsdp", split_axis=0, concat_axis=0, tiled=True)


def params(mebibytes, axes=1):
    return pltpu.CompilerParams(
        vmem_limit_bytes=mebibytes * MEBI, dimension_semantics=("arbitrary",) * axes
    )


def whole(shape):
    rank = len(shape)
    return pl.BlockSpec(shape, lambda *_: (0,) * rank)


def head_values(linear, low, second, gain, cosine, sine):
    values = linear + matrix_product(low, second)
    normed, factor = norm_forward(values, gain)
    turned = (normed * cosine + swapped(normed) * sine).astype(BF16)
    return values, factor, turned


def head_values_gradient(values, factor, gain, cosine, sine, upstream):
    back = upstream * cosine - swapped(upstream) * sine
    return norm_backward(values, factor, gain, back).astype(BF16)


def allowed_keys(block, start, width, seg_column, seg_row):
    rows = block * WINDOW + lax.broadcasted_iota(jnp.int32, (WINDOW, width), 0)
    keys = start + lax.broadcasted_iota(jnp.int32, (WINDOW, width), 1)
    mine = seg_column[block * WINDOW : (block + 1) * WINDOW]
    theirs = seg_row[:, start : start + width]
    return (keys == rows) | ((keys < rows) & (mine == theirs) & (theirs != 0))


def block_bounds(block):
    start = max(block - 1, 0) * WINDOW
    return start, (block + 1) * WINDOW - start


def attention_forward_body(
    rank,
    scale,
    lin_ref,
    key_lin_ref,
    value_lin_ref,
    low_ref,
    q_second_ref,
    k_second_ref,
    v_second_ref,
    q_gain_ref,
    k_gain_ref,
    cos_ref,
    sin_ref,
    seg_column_ref,
    seg_row_ref,
    heads_ref,
    key_scratch,
    value_scratch,
):
    cosine, sine = cos_ref[...], sin_ref[...]

    @pl.when(pl.program_id(0) == 0)
    def _():
        key_scratch[...] = head_values(
            key_lin_ref[...],
            low_ref[:, rank : 2 * rank],
            k_second_ref[...],
            k_gain_ref[...],
            cosine,
            sine,
        )[2]
        value_scratch[...] = (
            value_lin_ref[...]
            + matrix_product(low_ref[:, 2 * rank : 3 * rank], v_second_ref[...])
        ).astype(BF16)

    query = head_values(
        lin_ref[...], low_ref[:, :rank], q_second_ref[...], q_gain_ref[...], cosine, sine
    )[2]
    seg_column, seg_row = seg_column_ref[...], seg_row_ref[...]
    for block in range(query.shape[0] // WINDOW):
        start, width = block_bounds(block)
        rows = pl.ds(block * WINDOW, WINDOW)
        scores = (
            flipped_right_operand(
                query[block * WINDOW : (block + 1) * WINDOW], key_scratch[pl.ds(start, width)]
            )
            * scale
        )
        scores = jnp.where(
            allowed_keys(block, start, width, seg_column, seg_row), scores, -1e30
        )
        expo = jnp.exp(scores - jnp.max(scores, axis=-1, keepdims=True))
        probs = (expo / jnp.sum(expo, axis=-1, keepdims=True)).astype(BF16)
        heads_ref[rows, :] = matrix_product(probs, value_scratch[pl.ds(start, width)]).astype(
            BF16
        )


def attention_forward(
    linear, low, q_second, k_second, v_second, q_gain, k_gain, tables, seg_column, seg_row, scale
):
    rows, head_dim = linear.shape[0], q_gain.shape[1]
    heads = q_second.shape[1] // head_dim
    rank = q_second.shape[0]
    column = pl.BlockSpec((rows, head_dim), lambda h: (0, h))
    return pl.pallas_call(
        functools.partial(attention_forward_body, rank, scale),
        grid=(heads,),
        out_shape=jax.ShapeDtypeStruct((rows, heads * head_dim), BF16),
        in_specs=[
            column,
            pl.BlockSpec((rows, head_dim), lambda h: (0, heads)),
            pl.BlockSpec((rows, head_dim), lambda h: (0, heads + 1)),
            whole(low.shape),
            pl.BlockSpec((rank, head_dim), lambda h: (0, h)),
            whole(k_second.shape),
            whole(v_second.shape),
            whole(q_gain.shape),
            whole(k_gain.shape),
            whole(tables[0].shape),
            whole(tables[1].shape),
            whole(seg_column.shape),
            whole(seg_row.shape),
        ],
        out_specs=column,
        scratch_shapes=[pltpu.VMEM((rows, head_dim), BF16), pltpu.VMEM((rows, head_dim), BF16)],
        compiler_params=params(40),
        cost_estimate=pl.CostEstimate(
            flops=8 * heads * rows * WINDOW * head_dim,
            transcendentals=2 * heads * rows * WINDOW,
            bytes_accessed=6 * rows * heads * head_dim,
        ),
        name="attention_forward",
    )(
        linear,
        linear,
        linear,
        low,
        q_second,
        k_second,
        v_second,
        q_gain,
        k_gain,
        *tables,
        seg_column,
        seg_row,
    )


def attention_backward_body(
    rank,
    scale,
    lin_ref,
    key_lin_ref,
    value_lin_ref,
    low_ref,
    q_second_ref,
    k_second_ref,
    v_second_ref,
    q_gain_ref,
    k_gain_ref,
    cos_ref,
    sin_ref,
    seg_column_ref,
    seg_row_ref,
    heads_ref,
    heads_grad_ref,
    low_grad_ref,
    down_ref,
    q_grad_ref,
    k_grad_ref,
    v_grad_ref,
    share_ref,
    q_second_grad_ref,
    k_second_grad_ref,
    v_second_grad_ref,
    down_grad_ref,
    key_scratch,
    value_scratch,
    key_sum,
    value_sum,
    query_sum,
    share_sum,
):
    cosine, sine = cos_ref[...], sin_ref[...]
    head = pl.program_id(0)

    @pl.when(head == 0)
    def _():
        key_scratch[...] = head_values(
            key_lin_ref[...],
            low_ref[:, rank : 2 * rank],
            k_second_ref[...],
            k_gain_ref[...],
            cosine,
            sine,
        )[2]
        value_scratch[...] = (
            value_lin_ref[...]
            + matrix_product(low_ref[:, 2 * rank : 3 * rank], v_second_ref[...])
        ).astype(BF16)
        key_sum[...] = jnp.zeros_like(key_sum)
        value_sum[...] = jnp.zeros_like(value_sum)
        share_sum[...] = jnp.zeros_like(share_sum)

    low_q = low_ref[:, :rank]
    values, factor, query = head_values(
        lin_ref[...], low_q, q_second_ref[...], q_gain_ref[...], cosine, sine
    )
    low_grad = low_grad_ref[...]
    upstream = (heads_grad_ref[...] + matrix_product(low_grad, down_ref[...])).astype(BF16)
    down_grad_ref[...] = flipped_left_operand(low_grad, heads_ref[...])
    seg_column, seg_row = seg_column_ref[...], seg_row_ref[...]
    for block in range(query.shape[0] // WINDOW):
        start, width = block_bounds(block)
        rows = pl.ds(block * WINDOW, WINDOW)
        keys = pl.ds(start, width)
        query_block = query[block * WINDOW : (block + 1) * WINDOW]
        upstream_block = upstream[block * WINDOW : (block + 1) * WINDOW]
        scores = flipped_right_operand(query_block, key_scratch[keys]) * scale
        scores = jnp.where(
            allowed_keys(block, start, width, seg_column, seg_row), scores, -1e30
        )
        expo = jnp.exp(scores - jnp.max(scores, axis=-1, keepdims=True))
        probs = expo / jnp.sum(expo, axis=-1, keepdims=True)
        prob_grad = flipped_right_operand(upstream_block, value_scratch[keys])
        score_grad = (
            probs * (prob_grad - jnp.sum(probs * prob_grad, axis=-1, keepdims=True))
        ).astype(BF16)
        value_sum[keys, :] += flipped_left_operand(probs.astype(BF16), upstream_block)
        key_sum[keys, :] += flipped_left_operand(score_grad, query_block)
        query_sum[rows, :] = matrix_product(score_grad, key_scratch[keys]) * scale
    q_grad = head_values_gradient(
        values, factor, q_gain_ref[...], cosine, sine, query_sum[...]
    )
    q_grad_ref[...] = q_grad
    q_second_grad_ref[...] = flipped_left_operand(low_q, q_grad)
    share_sum[:, :rank] += flipped_right_operand(q_grad, q_second_ref[...])

    @pl.when(head == pl.num_programs(0) - 1)
    def _():
        low_k = low_ref[:, rank : 2 * rank]
        low_v = low_ref[:, 2 * rank : 3 * rank]
        key_values, key_factor, _turned = head_values(
            key_lin_ref[...], low_k, k_second_ref[...], k_gain_ref[...], cosine, sine
        )
        k_grad = head_values_gradient(
            key_values, key_factor, k_gain_ref[...], cosine, sine, key_sum[...] * scale
        )
        v_grad = value_sum[...].astype(BF16)
        k_grad_ref[...] = k_grad
        v_grad_ref[...] = v_grad
        k_second_grad_ref[...] = flipped_left_operand(low_k, k_grad)
        v_second_grad_ref[...] = flipped_left_operand(low_v, v_grad)
        share_sum[:, rank : 2 * rank] = flipped_right_operand(k_grad, k_second_ref[...])
        share_sum[:, 2 * rank : 3 * rank] = flipped_right_operand(v_grad, v_second_ref[...])
        share_ref[...] = share_sum[...].astype(BF16)


def attention_backward(
    linear,
    low,
    q_second,
    k_second,
    v_second,
    q_gain,
    k_gain,
    tables,
    seg_column,
    seg_row,
    scale,
    heads_low,
    heads_grad,
    low_grad,
    down_first,
):
    rows, head_dim = linear.shape[0], q_gain.shape[1]
    rank, columns = q_second.shape
    heads = columns // head_dim
    column = pl.BlockSpec((rows, head_dim), lambda h: (0, h))
    narrow = pl.BlockSpec((rank, head_dim), lambda h: (0, h))
    single = (rows, head_dim)
    return pl.pallas_call(
        functools.partial(attention_backward_body, rank, scale),
        grid=(heads,),
        out_shape=(
            jax.ShapeDtypeStruct((rows, columns), BF16),
            jax.ShapeDtypeStruct(single, BF16),
            jax.ShapeDtypeStruct(single, BF16),
            jax.ShapeDtypeStruct((rows, 3 * rank), BF16),
            jax.ShapeDtypeStruct((rank, columns), F32),
            jax.ShapeDtypeStruct((rank, head_dim), F32),
            jax.ShapeDtypeStruct((rank, head_dim), F32),
            jax.ShapeDtypeStruct((rank, columns), F32),
        ),
        in_specs=[
            column,
            pl.BlockSpec((rows, head_dim), lambda h: (0, heads)),
            pl.BlockSpec((rows, head_dim), lambda h: (0, heads + 1)),
            whole(low.shape),
            narrow,
            whole(k_second.shape),
            whole(v_second.shape),
            whole(q_gain.shape),
            whole(k_gain.shape),
            whole(tables[0].shape),
            whole(tables[1].shape),
            whole(seg_column.shape),
            whole(seg_row.shape),
            column,
            column,
            whole(low_grad.shape),
            narrow,
        ],
        out_specs=(
            column,
            whole(single),
            whole(single),
            whole((rows, 3 * rank)),
            narrow,
            whole((rank, head_dim)),
            whole((rank, head_dim)),
            narrow,
        ),
        scratch_shapes=[
            pltpu.VMEM(single, BF16),
            pltpu.VMEM(single, BF16),
            pltpu.VMEM(single, F32),
            pltpu.VMEM(single, F32),
            pltpu.VMEM(single, F32),
            pltpu.VMEM((rows, 3 * rank), F32),
        ],
        compiler_params=params(48),
        cost_estimate=pl.CostEstimate(
            flops=20 * heads * rows * WINDOW * head_dim,
            transcendentals=2 * heads * rows * WINDOW,
            bytes_accessed=12 * rows * columns,
        ),
        name="attention_backward",
    )(
        linear,
        linear,
        linear,
        low,
        q_second,
        k_second,
        v_second,
        q_gain,
        k_gain,
        *tables,
        seg_column,
        seg_row,
        heads_low,
        heads_grad,
        low_grad,
        down_first,
    )


def slot_choice(ranks, slots):
    experts, tokens = ranks.shape
    places = lax.broadcasted_iota(jnp.int32, (slots, tokens), 0).astype(ranks.dtype)
    return jnp.concatenate(
        [(places == ranks[e : e + 1, :]).astype(F32) for e in range(experts)], axis=0
    ).astype(BF16)


def to_slots_body(_block_ref, rank_ref, rows_ref, out_ref):
    slots = out_ref.shape[1]
    chosen = matrix_product(slot_choice(rank_ref[0], slots), rows_ref[...])
    out_ref[...] = chosen.astype(BF16).reshape(out_ref.shape)


def to_slots(block, ranks, rows, slots):
    experts, tokens = ranks.shape[1:]
    width = rows.shape[1]
    half = width // 2
    return pl.pallas_call(
        to_slots_body,
        grid_spec=pltpu.PrefetchScalarGridSpec(
            num_scalar_prefetch=1,
            grid=(2,),
            in_specs=[
                pl.BlockSpec((1, experts, tokens), lambda j, at: (at[0], 0, 0)),
                pl.BlockSpec((tokens, half), lambda j, at: (0, j)),
            ],
            out_specs=pl.BlockSpec((experts, slots, half), lambda j, at: (0, 0, j)),
        ),
        out_shape=jax.ShapeDtypeStruct((experts, slots, width), BF16),
        compiler_params=params(32),
        cost_estimate=pl.CostEstimate(
            flops=2 * experts * slots * tokens * width,
            transcendentals=0,
            bytes_accessed=2 * width * (experts * slots + tokens),
        ),
        name="to_slots",
    )(block, ranks, rows)


def from_slots_body(_block_ref, rank_ref, slot_ref, out_ref):
    experts, slots, width = slot_ref.shape
    choice = slot_choice(rank_ref[0], slots)
    out_ref[...] = flipped_left_operand(
        choice, slot_ref[...].reshape(experts * slots, width)
    ).astype(BF16)


def from_slots(block, ranks, slotted):
    experts, tokens = ranks.shape[1:]
    slots, width = slotted.shape[1:]
    half = width // 2
    return pl.pallas_call(
        from_slots_body,
        grid_spec=pltpu.PrefetchScalarGridSpec(
            num_scalar_prefetch=1,
            grid=(2,),
            in_specs=[
                pl.BlockSpec((1, experts, tokens), lambda j, at: (at[0], 0, 0)),
                pl.BlockSpec((experts, slots, half), lambda j, at: (0, 0, j)),
            ],
            out_specs=pl.BlockSpec((tokens, half), lambda j, at: (0, j)),
        ),
        out_shape=jax.ShapeDtypeStruct((tokens, width), BF16),
        compiler_params=params(32),
        cost_estimate=pl.CostEstimate(
            flops=2 * experts * slots * tokens * width,
            transcendentals=0,
            bytes_accessed=2 * width * (experts * slots + tokens),
        ),
        name="from_slots",
    )(block, ranks, slotted)


def all_to_slots_body(rank_ref, rows_ref, out_ref):
    slots = out_ref.shape[2]
    chosen = matrix_product(slot_choice(rank_ref[0], slots), rows_ref[...])
    out_ref[...] = chosen.astype(BF16).reshape(out_ref.shape)


def all_to_slots(ranks, rows, slots):
    blocks, experts, tokens = ranks.shape
    width = rows.shape[1]
    return pl.pallas_call(
        all_to_slots_body,
        grid=(blocks,),
        out_shape=jax.ShapeDtypeStruct((experts, blocks, slots, width), BF16),
        in_specs=[
            pl.BlockSpec((1, experts, tokens), lambda z: (z, 0, 0)),
            pl.BlockSpec((tokens, width), lambda z: (z, 0)),
        ],
        out_specs=pl.BlockSpec((experts, 1, slots, width), lambda z: (0, z, 0, 0)),
        compiler_params=params(40),
        cost_estimate=pl.CostEstimate(
            flops=2 * blocks * experts * slots * tokens * width,
            transcendentals=0,
            bytes_accessed=2 * blocks * width * (experts * slots + tokens),
        ),
        name="all_to_slots",
    )(ranks, rows)


def all_from_slots_body(_start_ref, rank_ref, slot_ref, out_ref):
    experts, _, slots, width = slot_ref.shape
    choice = slot_choice(rank_ref[0], slots)
    out_ref[...] = flipped_left_operand(
        choice, slot_ref[...].reshape(experts * slots, width)
    ).astype(BF16)


def all_from_slots(start, ranks, slotted):
    blocks, experts, tokens = ranks.shape
    slots, width = slotted.shape[2:]
    return pl.pallas_call(
        all_from_slots_body,
        grid_spec=pltpu.PrefetchScalarGridSpec(
            num_scalar_prefetch=1,
            grid=(blocks,),
            in_specs=[
                pl.BlockSpec((1, experts, tokens), lambda z, at: ((at[0] + z) % blocks, 0, 0)),
                pl.BlockSpec((experts, 1, slots, width), lambda z, at: (0, z, 0, 0)),
            ],
            out_specs=pl.BlockSpec((tokens, width), lambda z, at: ((at[0] + z) % blocks, 0)),
        ),
        out_shape=jax.ShapeDtypeStruct((blocks * tokens, width), BF16),
        compiler_params=params(40),
        cost_estimate=pl.CostEstimate(
            flops=2 * blocks * experts * slots * tokens * width,
            transcendentals=0,
            bytes_accessed=2 * blocks * width * (experts * slots + tokens),
        ),
        name="all_from_slots",
    )(start, ranks, slotted)


def ranks_of(mask):
    tokens = mask.shape[-1]
    order = jnp.arange(tokens, dtype=jnp.int32)
    before = (order[:, None] < order[None, :]).astype(BF16)
    counts = matrix_product(mask.astype(BF16), before)
    return jnp.where(mask, counts, -1.0).astype(jnp.int32)


def tiles(width, tile, body):
    @pl.loop(0, width // tile)
    def _(j):
        body(pl.ds(pl.multiple_of(j * tile, tile), tile))


def expert_math(
    tile, rows_ref, up_ref, ranks, weights, keep_dots, sent_y, mask_ref, tables, sums, scratch
):
    gate_w, up_w, down_w, pair_in, gate_out, up_out, down_in, down_out = tables
    pair_in_sum, gate_out_sum, up_out_sum, down_in_sum, down_out_sum = sums
    gate_lin_ref, up_lin_ref, inner_ref, route_ref, gate_grad_ref, up_grad_ref = scratch
    sources, slots, width = rows_ref.shape
    row_count = sources * slots
    hidden = gate_w.shape[1]
    broad = gate_out.shape[0]
    places = lax.broadcasted_iota(jnp.int32, (slots, ranks.shape[1]), 0)

    def held(source):
        return places == ranks[source : source + 1, :]

    def all_rows():
        return rows_ref[...].reshape(row_count, width)

    def pair_mask():
        mask = mask_ref[...].astype(F32)
        return jnp.concatenate([mask, mask], axis=1)

    weight = jnp.concatenate(
        [
            jnp.sum(
                jnp.where(held(source), weights[source : source + 1, :], 0.0),
                axis=1,
                keepdims=True,
            )
            for source in range(sources)
        ],
        axis=0,
    )
    pair = (flipped_right_operand(all_rows(), pair_in[...]) * pair_mask()).astype(BF16)
    gate_low, up_low = pair[:, :broad], pair[:, broad:]

    def inner_step(columns):
        rows = all_rows()
        gate_lin = matrix_product(rows, gate_w[:, columns]) + matrix_product(
            gate_low, gate_out[:, columns]
        )
        up_lin = matrix_product(rows, up_w[:, columns]) + matrix_product(
            up_low, up_out[:, columns]
        )
        gate_lin_ref[:, columns] = gate_lin
        up_lin_ref[:, columns] = up_lin
        inner_ref[:, columns] = (gate_lin * jax.nn.sigmoid(gate_lin) * up_lin).astype(BF16)

    tiles(hidden, tile, inner_step)
    down_low = (
        flipped_right_operand(inner_ref[...], down_in[...]) * mask_ref[...].astype(F32)
    ).astype(BF16)

    def down_step(j, total):
        columns = pl.ds(pl.multiple_of(j * tile, tile), tile)
        result = (
            matrix_product(inner_ref[...], down_w[:, columns])
            + matrix_product(down_low, down_out[:, columns])
        ).astype(BF16)
        wide = result.astype(F32)
        upstream = up_ref[:, :, columns].reshape(row_count, tile).astype(F32)
        up_ref[:, :, columns] = (weight * wide).astype(BF16).reshape(sources, slots, tile)
        route_ref[:, columns] = (weight * upstream).astype(BF16)
        return total + jnp.sum(upstream * wide, axis=1, keepdims=True)

    gate_dots = lax.fori_loop(0, width // tile, down_step, jnp.zeros((row_count, 1), F32))
    sent_y()
    for source in range(sources):
        keep_dots(
            source,
            jnp.sum(
                jnp.where(held(source), gate_dots[source * slots : (source + 1) * slots], 0.0),
                axis=0,
                keepdims=True,
            ),
        )
    down_low_grad = (
        flipped_right_operand(route_ref[...], down_out[...]) * mask_ref[...].astype(F32)
    ).astype(BF16)
    down_in_sum[...] += flipped_left_operand(down_low_grad, inner_ref[...])

    def down_out_step(columns):
        down_out_sum[:, columns] += flipped_left_operand(down_low, route_ref[:, columns])

    tiles(width, 2 * tile, down_out_step)

    def inner_grad_step(columns):
        inner_grad = flipped_right_operand(route_ref[...], down_w[columns, :]) + matrix_product(
            down_low_grad, down_in[:, columns]
        )
        gate_lin, up_lin = gate_lin_ref[:, columns], up_lin_ref[:, columns]
        sig = jax.nn.sigmoid(gate_lin)
        gate_grad_ref[:, columns] = (
            inner_grad * up_lin * (sig * (1.0 + gate_lin * (1.0 - sig)))
        ).astype(BF16)
        up_grad_ref[:, columns] = (inner_grad * (gate_lin * sig)).astype(BF16)

    tiles(hidden, tile, inner_grad_step)
    pair_grad = (
        jnp.concatenate(
            [
                flipped_right_operand(gate_grad_ref[...], gate_out[...]),
                flipped_right_operand(up_grad_ref[...], up_out[...]),
            ],
            axis=1,
        )
        * pair_mask()
    ).astype(BF16)
    gate_out_sum[...] += flipped_left_operand(gate_low, gate_grad_ref[...])
    up_out_sum[...] += flipped_left_operand(up_low, up_grad_ref[...])

    def rows_grad_step(columns):
        before = rows_ref[:, :, columns].reshape(row_count, tile)
        pair_in_sum[:, columns] += flipped_left_operand(pair_grad, before)
        rows_ref[:, :, columns] = (
            (
                flipped_right_operand(gate_grad_ref[...], gate_w[columns, :])
                + flipped_right_operand(up_grad_ref[...], up_w[columns, :])
                + matrix_product(pair_grad, pair_in[:, columns])
            )
            .astype(BF16)
            .reshape(sources, slots, tile)
        )

    tiles(width, tile, rows_grad_step)


def expert_sums(tables):
    gate_w, _up_w, _down_w, pair_in, gate_out, _up_out, down_in, down_out = tables
    return [
        jax.ShapeDtypeStruct(table.shape, F32)
        for table in (pair_in, gate_out, gate_out, down_in, down_out)
    ]


def expert_scratch(row_count, hidden, width):
    return [
        pltpu.VMEM((row_count, hidden), F32),
        pltpu.VMEM((row_count, hidden), F32),
        pltpu.VMEM((row_count, hidden), BF16),
        pltpu.VMEM((row_count, width), BF16),
        pltpu.VMEM((row_count, hidden), BF16),
        pltpu.VMEM((row_count, hidden), BF16),
    ]


def experts_body(_block_ref, rows_in, up_in, rank_ref, weight_ref, mask_ref, *rest):
    tables, sums_before, rest = rest[:8], rest[8:13], rest[13:]
    y_ref, rows_grad_ref, dots_ref = rest[:3]
    sums, rest = rest[3:8], rest[8:]
    for total, before in zip(sums, sums_before):
        total[...] = before[...]
    rows_grad_ref[...] = rows_in[...]
    y_ref[...] = up_in[...]

    def keep_dots(source, dots):
        dots_ref[source : source + 1, :] = dots

    expert_math(
        256,
        rows_grad_ref,
        y_ref,
        rank_ref[0],
        weight_ref[0],
        keep_dots,
        lambda: None,
        mask_ref,
        tables,
        sums,
        rest,
    )


def experts(block, rows, up_rows, ranks, weights, mask, tables, sums_before):
    sources, slots, width = rows.shape
    hidden = tables[0].shape[1]
    tokens = ranks.shape[2]
    token_spec = pl.BlockSpec((1, sources, tokens), lambda _, at: (at[0], 0, 0))

    def resident(array):
        return pl.BlockSpec(
            array.shape, lambda *_: (0,) * len(array.shape), pipeline_mode=pl.Buffered(1)
        )

    sums = expert_sums(tables)
    outs = [
        jax.ShapeDtypeStruct(rows.shape, BF16),
        jax.ShapeDtypeStruct(rows.shape, BF16),
        jax.ShapeDtypeStruct((sources, tokens), F32),
    ] + sums
    operands = [rows, up_rows, ranks, weights, mask, *tables, *sums_before]
    specs = (
        [resident(rows), resident(up_rows), token_spec, token_spec, resident(mask)]
        + [resident(table) for table in tables]
        + [resident(each) for each in sums_before]
    )
    return pl.pallas_call(
        experts_body,
        grid_spec=pltpu.PrefetchScalarGridSpec(
            num_scalar_prefetch=1,
            grid=(1,),
            in_specs=specs,
            out_specs=[resident(out) for out in outs],
            scratch_shapes=expert_scratch(sources * slots, hidden, width),
        ),
        out_shape=outs,
        input_output_aliases={
            1 + len(operands) - len(sums) + at: 3 + at for at in range(len(sums))
        },
        compiler_params=params(63),
        name="experts",
    )(block, *operands)


def moe_body(
    plane,
    line,
    own_ref,
    up_hbm,
    plane_rank_ref,
    rank_ref,
    weight_ref,
    mask_ref,
    *rest,
):
    tables_hbm, rest = rest[:8], rest[8:]
    total_ref, dots_ref, y_hbm, back_hbm = rest[:4]
    sums, rest = rest[4:9], rest[9:]
    tables, rest = rest[:8], rest[8:]
    (
        blocks,
        partials,
        partials_in,
        sent_slots,
        rows,
        up_rows,
        back_rows,
        choice,
        dots,
        dots_back,
        dots_pass,
        dots_in,
    ) = rest[:12]
    scratch, rest = rest[12:18], rest[18:]
    (
        table_sem,
        up_sem,
        y_sem,
        back_sem,
        own_sem,
        block_send,
        block_recv,
        row_send,
        row_recv,
        back_send,
        back_recv,
        partial_send,
        partial_recv,
        dots_send,
        dots_recv,
        dots_in_send,
        dots_in_recv,
    ) = rest
    width = own_ref.shape[1]
    slots = rows.shape[2]
    tile = 256
    me, at_line = lax.axis_index("fsdp"), lax.axis_index("tensor")

    greet_line_and_plane(line, plane)

    def block_copy(r):
        return pltpu.make_async_remote_copy(
            src_ref=own_ref,
            dst_ref=blocks.at[r],
            send_sem=block_send.at[r - 1],
            recv_sem=block_recv.at[r - 1],
            device_id={"tensor": lax.rem(at_line + line - r, line)},
        )

    def row_copy(r, d):
        target = lax.rem(me + d, plane)
        return pltpu.make_async_remote_copy(
            src_ref=sent_slots.at[lax.rem(r, 2), target],
            dst_ref=rows.at[r, me],
            send_sem=row_send.at[r, d],
            recv_sem=row_recv.at[r, d],
            device_id={"fsdp": target},
        )

    def own_rows(r):
        return pltpu.make_async_copy(
            sent_slots.at[lax.rem(r, 2), me], rows.at[r, me], own_sem.at[0]
        )

    def back_copy(r, d):
        target = lax.rem(me + d, plane)
        return pltpu.make_async_remote_copy(
            src_ref=rows.at[r, target],
            dst_ref=back_hbm.at[r, me],
            send_sem=back_send.at[r, d],
            recv_sem=back_recv.at[r, d],
            device_id={"fsdp": target},
        )

    def own_back(r):
        return pltpu.make_async_copy(rows.at[r, me], back_hbm.at[r, me], own_sem.at[1])

    def dots_copy(r, d):
        target = lax.rem(me + d, plane)
        return pltpu.make_async_remote_copy(
            src_ref=dots.at[r, target],
            dst_ref=dots_back.at[r, me],
            send_sem=dots_send.at[r, d],
            recv_sem=dots_recv.at[r, d],
            device_id={"fsdp": target},
        )

    def dots_in_copy(r):
        return pltpu.make_async_remote_copy(
            src_ref=dots_pass.at[r],
            dst_ref=dots_in.at[r],
            send_sem=dots_in_send.at[r - 1],
            recv_sem=dots_in_recv.at[r - 1],
            device_id={"tensor": lax.rem(at_line + r, line)},
        )

    def partial_copy(r):
        return pltpu.make_async_remote_copy(
            src_ref=partials.at[r - 1],
            dst_ref=partials_in.at[r - 1],
            send_sem=partial_send.at[r - 1],
            recv_sem=partial_recv.at[r - 1],
            device_id={"tensor": lax.rem(at_line + r, line)},
        )

    def up_copy(r):
        return pltpu.make_async_copy(
            up_hbm.at[:, lax.rem(at_line + r, line)], up_rows, up_sem
        )

    def y_copy(r):
        return pltpu.make_async_copy(up_rows, y_hbm.at[:, r], y_sem)

    @pl.loop(1, line)
    def _(r):
        block_copy(r).start()

    first_block = pltpu.make_async_copy(own_ref, blocks.at[0], own_sem.at[2])
    first_block.start()
    up_copy(0).start()
    table_copies = [
        pltpu.make_async_copy(source, target, table_sem.at[at])
        for at, (source, target) in enumerate(zip(tables_hbm, tables))
    ]
    for each in table_copies:
        each.start()
    for total in sums:
        total[...] = jnp.zeros_like(total)
    first_block.wait()

    @pl.loop(0, line + 2)
    def _(step):
        @pl.when(step < line)
        def _():
            @pl.when(step > 0)
            def _():
                block_copy(step).wait_recv()

            @pl.when(step > 1)
            def _():
                @pl.loop(1, plane)
                def _(d):
                    row_copy(step - 2, d).wait_send()

            choice[...] = slot_choice(plane_rank_ref[lax.rem(at_line + step, line)], slots)

            def slot_step(columns):
                sent_slots[lax.rem(step, 2), :, :, columns] = (
                    matrix_product(choice[...], blocks[step, :, columns])
                    .astype(BF16)
                    .reshape(plane, slots, 2 * tile)
                )

            tiles(width, 2 * tile, slot_step)

            @pl.loop(1, plane)
            def _(d):
                row_copy(step, d).start()

        @pl.when((step >= 1) & (step <= line))
        def _():
            r = step - 1
            block = lax.rem(at_line + r, line)

            @pl.when(r == 0)
            def _():
                for each in table_copies:
                    each.wait()

            own_rows(r).start()
            own_rows(r).wait()

            @pl.loop(1, plane)
            def _(d):
                row_copy(r, d).wait_recv()

            up_copy(r).wait()

            def keep_dots(source, values):
                dots[r, source] = jnp.broadcast_to(values, (8, values.shape[1]))

            expert_math(
                tile,
                rows.at[r],
                up_rows,
                rank_ref[block],
                weight_ref[block],
                keep_dots,
                lambda: y_copy(r).start(),
                mask_ref,
                tables,
                sums,
                scratch,
            )

            @pl.loop(1, plane)
            def _(d):
                dots_copy(r, d).start()
                back_copy(r, d).start()

            own_back(r).start()
            dots_back[r, me] = dots[r, me]
            y_copy(r).wait()

            @pl.when(r + 1 < line)
            def _():
                up_copy(r + 1).start()

            own_back(r).wait()

        @pl.when(step >= 2)
        def _():
            r = step - 2

            @pl.loop(1, plane)
            def _(d):
                dots_copy(r, d).wait_recv()
                back_copy(r, d).wait_recv()

            dots_pass[r] = dots_back[r, :, 0, :]
            load = pltpu.make_async_copy(back_hbm.at[r], back_rows, back_sem)
            load.start()
            choice[...] = slot_choice(plane_rank_ref[lax.rem(at_line + r, line)], slots)
            load.wait()

            def combined(columns):
                return flipped_left_operand(
                    choice[...], back_rows[:, :, columns].reshape(plane * slots, 2 * tile)
                )

            @pl.when(r == 0)
            def _():
                def keep(columns):
                    total_ref[:, columns] = combined(columns)

                tiles(width, 2 * tile, keep)
                dots_ref[at_line] = dots_pass[0]

            @pl.when(r > 0)
            def _():
                def pass_on(columns):
                    partials[r - 1, :, columns] = combined(columns).astype(BF16)

                dots_in_copy(r).start()
                tiles(width, 2 * tile, pass_on)
                partial_copy(r).start()

    @pl.loop(1, line)
    def _(r):
        dots_in_copy(r).wait_recv()
        dots_ref[lax.rem(at_line + line - r, line)] = dots_in[r]
        partial_copy(r).wait_recv()
        total_ref[...] += partials_in[r - 1].astype(F32)

    @pl.loop(1, line)
    def _(r):
        partial_copy(r).wait_send()
        dots_in_copy(r).wait_send()
        block_copy(r).wait_send()

    @pl.loop(1, plane)
    def _(d):
        row_copy(line - 2, d).wait_send()
        row_copy(line - 1, d).wait_send()

    @pl.loop(0, line)
    def _(r):
        @pl.loop(1, plane)
        def _(d):
            back_copy(r, d).wait_send()
            dots_copy(r, d).wait_send()


def moe_layer(own, up_rows, plane_ranks, ranks, weights, mask, tables, identity):
    line, plane, tokens = plane_ranks.shape
    slots, width = up_rows.shape[2:]
    hidden = tables[0].shape[1]
    sums = expert_sums(tables)
    anywhere = pl.BlockSpec(memory_space=pl.ANY)
    local = pl.BlockSpec(memory_space=pltpu.VMEM)
    grouped = (plane, slots, width)
    dma = pltpu.SemaphoreType.DMA
    return pl.pallas_call(
        functools.partial(moe_body, plane, line),
        out_shape=[
            jax.ShapeDtypeStruct((tokens, width), F32),
            jax.ShapeDtypeStruct((line, plane, tokens), F32),
            jax.ShapeDtypeStruct((plane, line, slots, width), BF16),
            jax.ShapeDtypeStruct((line,) + grouped, BF16),
        ]
        + sums,
        in_specs=[anywhere, anywhere, local, local, local, local] + [anywhere] * len(tables),
        out_specs=[local, local, anywhere, anywhere] + [local] * len(sums),
        scratch_shapes=[pltpu.VMEM(table.shape, table.dtype) for table in tables]
        + [
            pltpu.VMEM((line, tokens, width), BF16),
            pltpu.VMEM((line - 1, tokens, width), BF16),
            pltpu.VMEM((line - 1, tokens, width), BF16),
            pltpu.VMEM((2,) + grouped, BF16),
            pltpu.VMEM((line,) + grouped, BF16),
            pltpu.VMEM(grouped, BF16),
            pltpu.VMEM(grouped, BF16),
            pltpu.VMEM((plane * slots, tokens), BF16),
            pltpu.VMEM((line, plane, 8, tokens), F32),
            pltpu.VMEM((line, plane, 8, tokens), F32),
            pltpu.VMEM((line, plane, tokens), F32),
            pltpu.VMEM((line, plane, tokens), F32),
        ]
        + expert_scratch(plane * slots, hidden, width)
        + [dma((len(tables),)), dma, dma, dma, dma((3,))]
        + [dma((line - 1,))] * 2
        + [dma((line, plane))] * 4
        + [dma((line - 1,))] * 2
        + [dma((line, plane))] * 2
        + [dma((line - 1,))] * 2,
        compiler_params=pltpu.CompilerParams(
            collective_id=identity, has_side_effects=True, vmem_limit_bytes=63 * MEBI
        ),
        name="moe_layer",
    )(own, up_rows, plane_ranks, ranks, weights, mask, *tables)


def greet_line(me, count):
    barrier = pltpu.get_barrier_semaphore()

    @pl.when(me > 0)
    def _():
        pl.semaphore_signal(barrier, inc=1, device_id={"tensor": me - 1})

    @pl.when(me < count - 1)
    def _():
        pl.semaphore_signal(barrier, inc=1, device_id={"tensor": me + 1})

    @pl.when((me > 0) & (me < count - 1))
    def _():
        pl.semaphore_wait(barrier, 2)

    @pl.when((me == 0) | (me == count - 1))
    def _():
        pl.semaphore_wait(barrier, 1)


def gather_line_body(count, chunks, *refs):
    arrays = len(chunks)
    ins, outs = refs[:arrays], refs[arrays : 2 * arrays]
    semaphores, own_sem = refs[2 * arrays : -1], refs[-1]
    me = lax.axis_index("tensor")
    advance, finish = line_relay(me, count, ins, outs, chunks, semaphores)
    greet_line(me, count)
    own = [
        pltpu.make_async_copy(ins[at], outs[at].at[me], own_sem.at[at]) for at in range(arrays)
    ]
    everything = tuple(range(arrays))
    advance(0, everything)
    for each in own:
        each.start()
    for hop in range(1, count):
        advance(hop, everything)
    for each in own:
        each.wait()
    finish(everything, range(count - 1))


def gather_line(arrays, chunks, identity):
    count = lax.axis_size("tensor")
    total = sum(chunks)
    anywhere = pl.BlockSpec(memory_space=pl.ANY)
    return pl.pallas_call(
        functools.partial(gather_line_body, count, chunks),
        out_shape=[jax.ShapeDtypeStruct((count,) + a.shape, a.dtype) for a in arrays],
        in_specs=[anywhere] * len(arrays),
        out_specs=[anywhere] * len(arrays),
        scratch_shapes=[pltpu.SemaphoreType.DMA((count - 1, total))] * 4
        + [pltpu.SemaphoreType.DMA((len(arrays),))],
        compiler_params=pltpu.CompilerParams(collective_id=identity, has_side_effects=True),
        name="gather_line",
    )(*arrays)


def sum_line_body(count, chunks, part_ref, out_ref, left_buf, right_buf, *semaphores):
    me = lax.axis_index("tensor")
    advance, finish = line_sum(
        me, count, chunks, part_ref, out_ref, left_buf, right_buf, semaphores
    )
    greet_line(me, count)
    for far in range(count - 1, 0, -1):
        advance(far)
    finish()


def sum_line(part, chunks, identity):
    count, rows, width = part.shape
    semaphores = pltpu.SemaphoreType.DMA((count - 1, chunks))
    return pl.pallas_call(
        functools.partial(sum_line_body, count, chunks),
        out_shape=jax.ShapeDtypeStruct((rows, width), F32),
        in_specs=[pl.BlockSpec(memory_space=pltpu.VMEM)],
        out_specs=pl.BlockSpec(memory_space=pltpu.VMEM),
        scratch_shapes=[
            pltpu.VMEM((count - 1, rows, width), BF16),
            pltpu.VMEM((count - 1, rows, width), BF16),
        ]
        + [semaphores] * 4,
        compiler_params=pltpu.CompilerParams(
            collective_id=identity, has_side_effects=True, vmem_limit_bytes=32 * MEBI
        ),
        name="sum_line",
    )(part)


def line_relay(me, count, ins, outs, chunks, semaphores):
    right_send, right_recv, left_send, left_recv = semaphores
    pieces = []
    for at in range(len(ins)):
        size = ins[at].shape[0] // chunks[at]
        for piece in range(chunks[at]):
            pieces.append((at, pl.ds(piece * size, size)))

    def copy(place, hop, origin, target, send, recv):
        at, rows = pieces[place]
        source = ins[at].at[rows] if hop == 0 else outs[at].at[origin, rows]
        return pltpu.make_async_remote_copy(
            src_ref=source,
            dst_ref=outs[at].at[origin, rows],
            send_sem=send.at[hop, place],
            recv_sem=recv.at[hop, place],
            device_id={"tensor": target},
        )

    def places(arrays):
        return [place for place in range(len(pieces)) if pieces[place][0] in arrays]

    def advance(hop, arrays):
        for place in places(arrays):
            if hop > 0:

                @pl.when(me - hop >= 0)
                def _():
                    copy(place, hop - 1, me - hop, me - 1, right_send, right_recv).wait_recv()

            if hop < count - 1:

                @pl.when((me - hop >= 0) & (me + 1 < count))
                def _():
                    copy(place, hop, me - hop, me + 1, right_send, right_recv).start()

            if hop > 0:

                @pl.when(me + hop < count)
                def _():
                    copy(place, hop - 1, me + hop, me + 1, left_send, left_recv).wait_recv()

            if hop < count - 1:

                @pl.when((me + hop < count) & (me > 0))
                def _():
                    copy(place, hop, me + hop, me - 1, left_send, left_recv).start()

    def finish(arrays, hops):
        for hop in hops:
            for place in places(arrays):

                @pl.when((me - hop >= 0) & (me + 1 < count))
                def _():
                    copy(place, hop, me - hop, me + 1, right_send, right_recv).wait_send()

                @pl.when((me + hop < count) & (me > 0))
                def _():
                    copy(place, hop, me + hop, me - 1, left_send, left_recv).wait_send()

    return advance, finish


def line_sum(me, count, chunks, part_ref, out_ref, left_buf, right_buf, semaphores):
    right_send, right_recv, left_send, left_recv = semaphores
    size = part_ref.shape[1] // chunks

    def rightward(rows, piece, far, source):
        return pltpu.make_async_remote_copy(
            src_ref=source,
            dst_ref=left_buf.at[far - 1, rows],
            send_sem=right_send.at[far - 1, piece],
            recv_sem=right_recv.at[far - 1, piece],
            device_id={"tensor": me + 1},
        )

    def leftward(rows, piece, far, source):
        return pltpu.make_async_remote_copy(
            src_ref=source,
            dst_ref=right_buf.at[far - 1, rows],
            send_sem=left_send.at[far - 1, piece],
            recv_sem=left_recv.at[far - 1, piece],
            device_id={"tensor": me - 1},
        )

    def added(buffer, far, rows, block):
        buffer[far, rows, :] = (
            buffer[far, rows, :].astype(F32) + part_ref[block, rows, :].astype(F32)
        ).astype(BF16)

    def advance(far):
        for piece in range(chunks):
            rows = pl.ds(piece * size, size)

            @pl.when((me == 0) & (me + far < count))
            def _():
                rightward(rows, piece, far, part_ref.at[me + far, rows]).start()

            @pl.when((me == count - 1) & (me - far >= 0))
            def _():
                leftward(rows, piece, far, part_ref.at[me - far, rows]).start()

            if far < count - 1:

                @pl.when((me > 0) & (me + far < count))
                def _():
                    rightward(rows, piece, far + 1, left_buf.at[far, rows]).wait_recv()
                    added(left_buf, far, rows, me + far)
                    rightward(rows, piece, far, left_buf.at[far, rows]).start()

                @pl.when((me < count - 1) & (me - far >= 0))
                def _():
                    leftward(rows, piece, far + 1, right_buf.at[far, rows]).wait_recv()
                    added(right_buf, far, rows, me - far)
                    leftward(rows, piece, far, right_buf.at[far, rows]).start()

    def finish():
        for piece in range(chunks):
            rows = pl.ds(piece * size, size)
            out_ref[rows, :] = part_ref[me, rows, :].astype(F32)

            @pl.when(me > 0)
            def _():
                rightward(rows, piece, 1, left_buf.at[0, rows]).wait_recv()
                out_ref[rows, :] += left_buf[0, rows, :].astype(F32)

            @pl.when(me < count - 1)
            def _():
                leftward(rows, piece, 1, right_buf.at[0, rows]).wait_recv()
                out_ref[rows, :] += right_buf[0, rows, :].astype(F32)

        for far in range(count - 1, 0, -1):
            for piece in range(chunks):
                rows = pl.ds(piece * size, size)

                @pl.when((me == 0) & (me + far < count))
                def _():
                    rightward(rows, piece, far, part_ref.at[me + far, rows]).wait_send()

                @pl.when((me == count - 1) & (me - far >= 0))
                def _():
                    leftward(rows, piece, far, part_ref.at[me - far, rows]).wait_send()

                if far < count - 1:

                    @pl.when((me > 0) & (me + far < count))
                    def _():
                        rightward(rows, piece, far, left_buf.at[far, rows]).wait_send()

                    @pl.when((me < count - 1) & (me - far >= 0))
                    def _():
                        leftward(rows, piece, far, right_buf.at[far, rows]).wait_send()

    return advance, finish


def greet_line_and_plane(line, plane):
    me, at_line = lax.axis_index("fsdp"), lax.axis_index("tensor")
    barrier = pltpu.get_barrier_semaphore()

    @pl.loop(1, plane)
    def _(d):
        pl.semaphore_signal(barrier, inc=1, device_id={"fsdp": lax.rem(me + d, plane)})

    @pl.loop(1, line)
    def _(d):
        pl.semaphore_signal(barrier, inc=1, device_id={"tensor": lax.rem(at_line + d, line)})

    pl.semaphore_wait(barrier, plane + line - 2)


def front_body(
    plane,
    line,
    scale,
    places,
    tokens_hbm,
    cotangent_hbm,
    routes_hbm,
    weights_hbm,
    gain_ref,
    first_ref,
    q_second_ref,
    k_second_ref,
    v_second_ref,
    q_gain_ref,
    k_gain_ref,
    cos_ref,
    sin_ref,
    seg_column_ref,
    seg_row_ref,
    out_first_ref,
    out_second_ref,
    before_ref,
    total_ref,
    ranks_ref,
    low_ref,
    out_low_ref,
    linear_hbm,
    heads_hbm,
    normed_hbm,
    gathered_hbm,
    up_hbm,
    rows,
    upstream,
    routes,
    weights,
    linear,
    heads,
    keys,
    values,
    part,
    left_buf,
    right_buf,
    sent_slots,
    choice,
    own_sem,
    save_sem,
    relay_right_send,
    relay_right_recv,
    relay_left_send,
    relay_left_recv,
    weight_send,
    weight_recv,
    pass_send,
    pass_recv,
    sum_right_send,
    sum_right_recv,
    sum_left_send,
    sum_left_recv,
    slot_send,
    slot_recv,
):
    me, at_line = lax.axis_index("fsdp"), lax.axis_index("tensor")
    rank = q_second_ref.shape[0]
    head_dim = q_gain_ref.shape[1]
    tokens, width = tokens_hbm.shape
    slots = sent_slots.shape[2]
    tile = 256
    query_columns = q_second_ref.shape[1]
    linear_columns = linear.shape[1]
    out_start = places[1]

    greet_line_and_plane(line, plane)

    beside = me + 1 - 2 * lax.rem(me, 2)

    def weight_copy(k):
        target = lax.rem(me + 2 * k, plane)
        return pltpu.make_async_remote_copy(
            src_ref=weights_hbm,
            dst_ref=weights.at[me],
            send_sem=weight_send.at[k],
            recv_sem=weight_recv.at[k],
            device_id={"fsdp": target},
        )

    def weight_pass(k):
        origin = lax.rem(me + plane - 2 * k, plane)
        return pltpu.make_async_remote_copy(
            src_ref=weights_hbm if k == 0 else weights.at[origin],
            dst_ref=weights.at[origin],
            send_sem=pass_send.at[k],
            recv_sem=pass_recv.at[k],
            device_id={"fsdp": beside},
        )

    peers = plane // 2
    for k in range(1, peers):
        weight_copy(k).start()
    weight_pass(0).start()
    locals_in = [
        pltpu.make_async_copy(source, target, own_sem.at[at])
        for at, (source, target) in enumerate(
            [
                (tokens_hbm, rows.at[at_line]),
                (routes_hbm, routes.at[at_line]),
                (cotangent_hbm, upstream.at[at_line]),
                (weights_hbm, weights.at[me]),
            ]
        )
    ]
    advance, finish_relay = line_relay(
        at_line,
        line,
        [tokens_hbm, routes_hbm, cotangent_hbm],
        [rows, routes, upstream],
        (4, 1, 4),
        (relay_right_send, relay_right_recv, relay_left_send, relay_left_recv),
    )
    advance(0, (0, 1))
    advance(0, (2,))
    for each in locals_in:
        each.start()
    advance(1, (0, 1))
    advance(2, (0, 1))
    for k in range(1, peers):
        weight_copy(k).wait_recv()
        weight_pass(k).start()
    advance(3, (0, 1))
    for each in locals_in:
        each.wait()

    for block in range(line):
        named = [
            jnp.max(
                (routes[block] == expert * line + at_line).astype(F32), axis=0, keepdims=True
            )
            for expert in range(plane)
        ]
        mask = jnp.concatenate(named, axis=0)
        counts = matrix_product(mask.astype(BF16), before_ref[...])
        ranks_ref[block] = jnp.where(mask > 0.0, counts, -1.0)

    def slot_copy(block, d):
        target = lax.rem(me + d, plane)
        return pltpu.make_async_remote_copy(
            src_ref=sent_slots.at[block, target],
            dst_ref=up_hbm.at[me, block],
            send_sem=slot_send.at[block, d],
            recv_sem=slot_recv.at[block, d],
            device_id={"fsdp": target},
        )

    def own_slots(block):
        return pltpu.make_async_copy(
            sent_slots.at[block, me], up_hbm.at[me, block], save_sem.at[4 + block]
        )

    def dispatch(block):
        choice[...] = slot_choice(ranks_ref[block], slots)

        def slot_step(columns):
            sent_slots[block, :, :, columns] = (
                matrix_product(choice[...], upstream[block, :, columns])
                .astype(BF16)
                .reshape(plane, slots, 2 * tile)
            )

        tiles(width, 2 * tile, slot_step)

        @pl.loop(1, plane)
        def _(d):
            slot_copy(block, d).start()

    def dispatch_at(distance):
        if distance == 0:
            dispatch(at_line)
            return

        @pl.when(at_line - distance >= 0)
        def _():
            dispatch(at_line - distance)

        @pl.when(at_line + distance < line)
        def _():
            dispatch(at_line + distance)

    dispatch_at(0)

    finish_relay((0,), range(1, line - 1))

    @pl.loop(0, line * tokens // 128)
    def _(j):
        block, at = j // (tokens // 128), pl.ds((j % (tokens // 128)) * 128, 128)
        wide = rows[block, at, :].astype(F32)
        rows[block, at, :] = norm_forward(wide, gain_ref[...])[0].astype(BF16)

    for k in range(peers):
        weight_pass(k).wait_recv()
    saves = [
        pltpu.make_async_copy(rows, normed_hbm, save_sem.at[0]),
        pltpu.make_async_copy(weights, gathered_hbm, save_sem.at[1]),
        pltpu.make_async_copy(linear, linear_hbm, save_sem.at[2]),
        pltpu.make_async_copy(heads, heads_hbm, save_sem.at[3]),
    ]
    saves[0].start()
    saves[1].start()

    @pl.loop(0, line)
    def _(block):
        at = pl.ds(pl.multiple_of(block * tokens, tokens), tokens)
        low_ref[at, :] = flipped_right_operand(rows[block], first_ref[...]).astype(BF16)

        def project(columns):
            linear[at, columns] = matrix_product(
                rows[block], weights[:, :, columns].reshape(width, tile)
            )

        tiles(linear_columns, tile, project)

    saves[2].start()
    advance(1, (2,))
    dispatch_at(1)

    cosine, sine = cos_ref[...], sin_ref[...]
    keys[...] = head_values(
        linear[:, query_columns : query_columns + head_dim],
        low_ref[:, rank : 2 * rank],
        k_second_ref[...],
        k_gain_ref[...],
        cosine,
        sine,
    )[2]
    values[...] = (
        linear[:, query_columns + head_dim : query_columns + 2 * head_dim]
        + matrix_product(low_ref[:, 2 * rank : 3 * rank], v_second_ref[...])
    ).astype(BF16)

    @pl.loop(0, query_columns // head_dim)
    def _(head):
        columns = pl.ds(pl.multiple_of(head * head_dim, head_dim), head_dim)
        query = head_values(
            linear[:, columns],
            low_ref[:, :rank],
            q_second_ref[:, columns],
            q_gain_ref[...],
            cos_ref[...],
            sin_ref[...],
        )[2]
        seg_column, seg_row = seg_column_ref[...], seg_row_ref[...]
        for block in range(query.shape[0] // WINDOW):
            start, span = block_bounds(block)
            scores = (
                flipped_right_operand(
                    query[block * WINDOW : (block + 1) * WINDOW], keys[pl.ds(start, span)]
                )
                * scale
            )
            scores = jnp.where(
                allowed_keys(block, start, span, seg_column, seg_row), scores, -1e30
            )
            expo = jnp.exp(scores - jnp.max(scores, axis=-1, keepdims=True))
            probs = (expo / jnp.sum(expo, axis=-1, keepdims=True)).astype(BF16)
            heads[pl.ds(block * WINDOW, WINDOW), columns] = matrix_product(
                probs, values[pl.ds(start, span)]
            ).astype(BF16)

    saves[3].start()
    advance(2, (2,))
    dispatch_at(2)

    out_low_ref[...] = flipped_right_operand(heads[...], out_first_ref[...]).astype(BF16)

    @pl.loop(0, line)
    def _(block):
        at = pl.ds(pl.multiple_of(block * tokens, tokens), tokens)

        @pl.loop(0, plane)
        def _(shard):
            wide = width // plane
            columns = pl.ds(pl.multiple_of(shard * wide, wide), wide)
            part[block, :, columns] = (
                flipped_right_operand(heads[at, :], weights[shard, :, out_start:])
                + matrix_product(out_low_ref[at, :], out_second_ref[:, columns])
            ).astype(BF16)

    advance_sum, finish_sum = line_sum(
        at_line,
        line,
        4,
        part,
        total_ref,
        left_buf,
        right_buf,
        (sum_right_send, sum_right_recv, sum_left_send, sum_left_recv),
    )
    for far in range(line - 1, 0, -1):
        advance_sum(far)
        if far == 2:
            advance(3, (2,))
            dispatch_at(3)
    finish_sum()

    for block in range(line):
        own_slots(block).start()
    for each in saves:
        each.wait()
    finish_relay((0,), (0,))
    finish_relay((1, 2), range(line - 1))
    for k in range(1, peers):
        weight_copy(k).wait_send()
    for k in range(peers):
        weight_pass(k).wait_send()

    @pl.loop(0, line)
    def _(block):
        @pl.loop(1, plane)
        def _(d):
            slot_copy(block, d).wait_recv()
            slot_copy(block, d).wait_send()

    for block in range(line):
        own_slots(block).wait()


def front(
    tokens,
    cotangent,
    routes,
    packed,
    gain,
    first,
    q_second,
    k_second,
    v_second,
    q_gain,
    k_gain,
    tables,
    seg_column,
    seg_row,
    out_first,
    out_second,
    scale,
    slots,
    places,
    identity,
):
    line, plane = lax.axis_size("tensor"), lax.axis_size("fsdp")
    count, width = tokens.shape
    all_rows = line * count
    rank, query_columns = q_second.shape
    head_dim = q_gain.shape[1]
    linear_columns = query_columns + 2 * head_dim
    order = jnp.arange(count, dtype=jnp.int32)
    before = (order[:, None] < order[None, :]).astype(BF16)
    anywhere = pl.BlockSpec(memory_space=pl.ANY)
    local = pl.BlockSpec(memory_space=pltpu.VMEM)
    dma = pltpu.SemaphoreType.DMA
    up_shape = (plane, line, slots, width)
    operands = [
        gain,
        first,
        q_second,
        k_second,
        v_second,
        q_gain,
        k_gain,
        *tables,
        seg_column,
        seg_row,
        out_first,
        out_second,
        before,
    ]
    return pl.pallas_call(
        functools.partial(front_body, plane, line, scale, places),
        out_shape=[
            jax.ShapeDtypeStruct((count, width), F32),
            jax.ShapeDtypeStruct((line, plane, count), F32),
            jax.ShapeDtypeStruct((all_rows, 3 * rank), BF16),
            jax.ShapeDtypeStruct((all_rows, rank), BF16),
            jax.ShapeDtypeStruct((all_rows, linear_columns), F32),
            jax.ShapeDtypeStruct((all_rows, query_columns), BF16),
            jax.ShapeDtypeStruct((line, count, width), BF16),
            jax.ShapeDtypeStruct((plane,) + packed.shape, BF16),
            jax.ShapeDtypeStruct(up_shape, BF16),
        ],
        in_specs=[anywhere] * 4 + [local] * len(operands),
        out_specs=[local] * 4 + [anywhere] * 5,
        scratch_shapes=[
            pltpu.VMEM((line, count, width), BF16),
            pltpu.VMEM((line, count, width), BF16),
            pltpu.VMEM((line,) + routes.shape, jnp.int32),
            pltpu.VMEM((plane,) + packed.shape, BF16),
            pltpu.VMEM((all_rows, linear_columns), F32),
            pltpu.VMEM((all_rows, query_columns), BF16),
            pltpu.VMEM((all_rows, head_dim), BF16),
            pltpu.VMEM((all_rows, head_dim), BF16),
            pltpu.VMEM((line, count, width), BF16),
            pltpu.VMEM((line - 1, count, width), BF16),
            pltpu.VMEM((line - 1, count, width), BF16),
            pltpu.VMEM((line, plane, slots, width), BF16),
            pltpu.VMEM((plane * slots, count), BF16),
            dma((4,)),
            dma((4 + line,)),
        ]
        + [dma((line - 1, 9))] * 4
        + [dma((plane // 2,))] * 4
        + [dma((line - 1, 4))] * 4
        + [dma((line, plane))] * 2,
        compiler_params=pltpu.CompilerParams(
            collective_id=identity, has_side_effects=True, vmem_limit_bytes=63 * MEBI
        ),
        name="front",
    )(tokens, cotangent, routes, packed, *operands)


def back_body(
    plane,
    line,
    scale,
    places,
    moe_total_ref,
    dots_ref,
    gates_ref,
    residual_ref,
    cotangent_ref,
    moe_gain_ref,
    router_ref,
    router_first_ref,
    router_second_ref,
    router_low_ref,
    moe_rows_ref,
    ranks_ref,
    low_ref,
    out_low_ref,
    first_out_ref,
    second_out_ref,
    q_second_ref,
    k_second_ref,
    v_second_ref,
    q_gain_ref,
    k_gain_ref,
    cos_ref,
    sin_ref,
    seg_column_ref,
    seg_row_ref,
    linear_hbm,
    heads_hbm,
    normed_hbm,
    gathered_hbm,
    y_hbm,
    output_ref,
    residual_grad_ref,
    share_ref,
    linear_grad_ref,
    rows_out_ref,
    heads_out_ref,
    narrow_out_ref,
    router_out_ref,
    y_in_hbm,
    branch_own,
    branch,
    out_weights,
    linear,
    heads,
    normed,
    upstream,
    out_low_grad,
    keys,
    values,
    key_sum,
    value_sum,
    query_sum,
    share_sum,
    second_sum,
    y_rows,
    partials,
    partials_in,
    result,
    choice,
    load_sem,
    y_sem,
    relay_right_send,
    relay_right_recv,
    relay_left_send,
    relay_left_recv,
    y_send,
    y_recv,
    partial_send,
    partial_recv,
):
    me, at_line = lax.axis_index("fsdp"), lax.axis_index("tensor")
    tokens, width = residual_ref.shape
    rank, query_columns = q_second_ref.shape
    head_dim = q_gain_ref.shape[1]
    slots = y_rows.shape[1]
    tile = 256

    greet_line_and_plane(line, plane)

    def y_copy(r, d):
        target = lax.rem(me + d, plane)
        return pltpu.make_async_remote_copy(
            src_ref=y_hbm.at[target, r],
            dst_ref=y_in_hbm.at[r, me],
            send_sem=y_send.at[r, d],
            recv_sem=y_recv.at[r, d],
            device_id={"fsdp": target},
        )

    def own_y(r):
        return pltpu.make_async_copy(y_hbm.at[me, r], y_in_hbm.at[r, me], y_sem.at[r])

    def partial_copy(r):
        return pltpu.make_async_remote_copy(
            src_ref=partials.at[r - 1],
            dst_ref=partials_in.at[r - 1],
            send_sem=partial_send.at[r - 1],
            recv_sem=partial_recv.at[r - 1],
            device_id={"tensor": lax.rem(at_line + r, line)},
        )

    for r in list(range(1, line)) + [0]:

        @pl.loop(1, plane)
        def _(d):
            y_copy(r, d).start()

    for r in range(line):
        own_y(r).start()
    loads = [
        pltpu.make_async_copy(source, target, load_sem.at[at])
        for at, (source, target) in enumerate(
            [
                (gathered_hbm.at[:, :, pl.ds(places[1], query_columns)], out_weights),
                (linear_hbm, linear),
                (heads_hbm, heads),
                (normed_hbm, normed),
            ]
        )
    ]
    for each in loads:
        each.start()

    def combine(r):
        @pl.loop(1, plane)
        def _(d):
            y_copy(r, d).wait_recv()

        own_y(r).wait()
        load = pltpu.make_async_copy(y_in_hbm.at[r], y_rows, y_sem.at[line])
        load.start()
        choice[...] = slot_choice(ranks_ref[lax.rem(at_line + r, line)], slots)
        load.wait()

        def combined(columns):
            total = flipped_left_operand(
                choice[...], y_rows[:, :, columns].reshape(plane * slots, 2 * tile)
            )
            if r == 0:
                result[:, columns] = total
            else:
                partials[r - 1, :, columns] = total.astype(BF16)

        tiles(width, 2 * tile, combined)
        if r > 0:
            partial_copy(r).start()

    gates = gates_ref[...]
    dots = dots_ref[...]
    logit_grad = (gates * (dots - jnp.sum(gates * dots, axis=0, keepdims=True))).astype(BF16)
    router_low_grad = matrix_product(router_second_ref[...], logit_grad).astype(BF16)
    rows_out_ref[4 * rank :, :] = matrix_product(router_low_grad, moe_rows_ref[...]).astype(BF16)
    router_out_ref[...] = flipped_right_operand(router_low_ref[...], logit_grad)
    half = tokens // 2
    for part in range(2):
        rows = pl.ds(part * half, half)
        columns = slice(part * half, (part + 1) * half)
        moe_grad = (
            moe_total_ref[rows, :]
            + flipped_left_operand(logit_grad[:, columns], router_ref[...])
            + flipped_left_operand(router_low_grad[:, columns], router_first_ref[...])
        )
        residual = residual_ref[rows, :]
        factor = lax.rsqrt(
            jnp.mean(residual * residual, axis=-1, keepdims=True) + NORM_EPSILON
        )
        residual_grad = cotangent_ref[rows, :].astype(F32) + norm_backward(
            residual, factor, moe_gain_ref[...], moe_grad
        )
        residual_grad_ref[rows, :] = residual_grad
        branch_own[rows, :] = residual_grad.astype(BF16)
    branch[at_line] = branch_own[...]

    advance, finish_relay = line_relay(
        at_line,
        line,
        [branch_own],
        [branch],
        (4,),
        (relay_right_send, relay_right_recv, relay_left_send, relay_left_recv),
    )
    advance(0, (0,))
    second_sum[...] = jnp.zeros_like(second_sum)
    loads[0].wait()

    def head_gradients(block):
        at = pl.ds(pl.multiple_of(block * tokens, tokens), tokens)
        low_grad = flipped_right_operand(branch[block], second_out_ref[...]).astype(BF16)
        out_low_grad[at, :] = low_grad
        second_sum[...] += flipped_left_operand(out_low_ref[at, :], branch[block])

        def project(columns):
            upstream[at, columns] = (
                matrix_product(branch[block], out_weights[:, :, columns].reshape(width, tile))
                + matrix_product(low_grad, first_out_ref[:, columns])
            ).astype(BF16)

        tiles(query_columns, tile, project)

    head_gradients(at_line)
    for each in loads[1:]:
        each.wait()
    cosine, sine = cos_ref[...], sin_ref[...]
    key_columns = slice(query_columns, query_columns + head_dim)
    value_columns = slice(query_columns + head_dim, query_columns + 2 * head_dim)
    keys[...] = head_values(
        linear[:, key_columns],
        low_ref[:, rank : 2 * rank],
        k_second_ref[...],
        k_gain_ref[...],
        cosine,
        sine,
    )[2]
    values[...] = (
        linear[:, value_columns]
        + matrix_product(low_ref[:, 2 * rank : 3 * rank], v_second_ref[...])
    ).astype(BF16)
    key_sum[...] = jnp.zeros_like(key_sum)
    value_sum[...] = jnp.zeros_like(value_sum)
    share_sum[...] = jnp.zeros_like(share_sum)
    for hop in range(1, line):
        advance(hop, (0,))

        @pl.when(at_line - hop >= 0)
        def _():
            head_gradients(at_line - hop)

        @pl.when(at_line + hop < line)
        def _():
            head_gradients(at_line + hop)

        if hop < line - 1:
            combine(hop)
    rows_out_ref[3 * rank : 4 * rank, :] = second_sum[...].astype(BF16)

    head_count = query_columns // head_dim

    @pl.loop(0, head_count)
    def _(head):
        columns = pl.ds(pl.multiple_of(head * head_dim, head_dim), head_dim)
        low_q = low_ref[:, :rank]
        lines, factor, query = head_values(
            linear[:, columns],
            low_q,
            q_second_ref[:, columns],
            q_gain_ref[...],
            cos_ref[...],
            sin_ref[...],
        )
        heads_out_ref[rank:, columns] = flipped_left_operand(
            out_low_grad[...], heads[:, columns]
        ).astype(BF16)
        seg_column, seg_row = seg_column_ref[...], seg_row_ref[...]
        for block in range(query.shape[0] // WINDOW):
            start, span = block_bounds(block)
            at, near = pl.ds(block * WINDOW, WINDOW), pl.ds(start, span)
            query_block = query[block * WINDOW : (block + 1) * WINDOW]
            upstream_block = upstream[at, columns]
            scores = flipped_right_operand(query_block, keys[near]) * scale
            scores = jnp.where(
                allowed_keys(block, start, span, seg_column, seg_row), scores, -1e30
            )
            expo = jnp.exp(scores - jnp.max(scores, axis=-1, keepdims=True))
            probs = expo / jnp.sum(expo, axis=-1, keepdims=True)
            prob_grad = flipped_right_operand(upstream_block, values[near])
            score_grad = (
                probs * (prob_grad - jnp.sum(probs * prob_grad, axis=-1, keepdims=True))
            ).astype(BF16)
            value_sum[near, :] += flipped_left_operand(probs.astype(BF16), upstream_block)
            key_sum[near, :] += flipped_left_operand(score_grad, query_block)
            query_sum[at, :] = matrix_product(score_grad, keys[near]) * scale
        q_grad = head_values_gradient(
            lines, factor, q_gain_ref[...], cos_ref[...], sin_ref[...], query_sum[...]
        )
        linear_grad_ref[:, columns] = q_grad
        heads_out_ref[:rank, columns] = flipped_left_operand(low_q, q_grad).astype(BF16)
        share_sum[:, :rank] += flipped_right_operand(q_grad, q_second_ref[:, columns])

        @pl.when(head == head_count // 2 - 1)
        def _():
            combine(line - 1)

    low_k = low_ref[:, rank : 2 * rank]
    low_v = low_ref[:, 2 * rank : 3 * rank]
    key_lines, key_factor, _turned = head_values(
        linear[:, key_columns], low_k, k_second_ref[...], k_gain_ref[...], cosine, sine
    )
    k_grad = head_values_gradient(
        key_lines, key_factor, k_gain_ref[...], cosine, sine, key_sum[...] * scale
    )
    v_grad = value_sum[...].astype(BF16)
    linear_grad_ref[:, key_columns] = k_grad
    linear_grad_ref[:, value_columns] = v_grad
    narrow_out_ref[:rank, :] = flipped_left_operand(low_k, k_grad).astype(BF16)
    narrow_out_ref[rank:, :] = flipped_left_operand(low_v, v_grad).astype(BF16)
    share_sum[:, rank : 2 * rank] = flipped_right_operand(k_grad, k_second_ref[...])
    share_sum[:, 2 * rank :] = flipped_right_operand(v_grad, v_second_ref[...])
    share_ref[...] = share_sum[...].astype(BF16)

    def first_gradient(columns):
        rows_out_ref[: 3 * rank, columns] = flipped_left_operand(
            share_ref[...], normed[:, columns]
        ).astype(BF16)

    tiles(width, 2 * tile, first_gradient)
    combine(0)
    for r in range(1, line):
        partial_copy(r).wait_recv()
        result[...] += partials_in[r - 1].astype(F32)
    output_ref[...] = (residual_ref[...] + result[...]).astype(BF16)
    finish_relay((0,), range(line - 1))
    for r in range(1, line):
        partial_copy(r).wait_send()
    for r in range(line):

        @pl.loop(1, plane)
        def _(d):
            y_copy(r, d).wait_send()


def back(scale, places, slots, identity, hbm_operands, operands):
    line, plane = lax.axis_size("tensor"), lax.axis_size("fsdp")
    linear, heads, normed, gathered, _y = hbm_operands
    count, width = operands[0].shape
    all_rows, linear_columns = linear.shape
    query_columns = heads.shape[1]
    head_dim = (linear_columns - query_columns) // 2
    rank = operands[13].shape[1]
    experts_count = line * plane
    anywhere = pl.BlockSpec(memory_space=pl.ANY)
    local = pl.BlockSpec(memory_space=pltpu.VMEM)
    dma = pltpu.SemaphoreType.DMA
    single = (all_rows, head_dim)
    block = (count, width)
    return pl.pallas_call(
        functools.partial(back_body, plane, line, scale, places),
        out_shape=[
            jax.ShapeDtypeStruct(block, BF16),
            jax.ShapeDtypeStruct(block, F32),
            jax.ShapeDtypeStruct((all_rows, 3 * rank), BF16),
            jax.ShapeDtypeStruct((all_rows, linear_columns), BF16),
            jax.ShapeDtypeStruct((5 * rank, width), BF16),
            jax.ShapeDtypeStruct((2 * rank, query_columns), BF16),
            jax.ShapeDtypeStruct((2 * rank, head_dim), BF16),
            jax.ShapeDtypeStruct((rank, experts_count), F32),
            jax.ShapeDtypeStruct((line, plane, slots, width), BF16),
        ],
        in_specs=[local] * len(operands) + [anywhere] * len(hbm_operands),
        out_specs=[local] * 8 + [anywhere],
        scratch_shapes=[
            pltpu.VMEM(block, BF16),
            pltpu.VMEM((line,) + block, BF16),
            pltpu.VMEM((plane, width // plane, query_columns), BF16),
            pltpu.VMEM((all_rows, linear_columns), F32),
            pltpu.VMEM((all_rows, query_columns), BF16),
            pltpu.VMEM((all_rows, width), BF16),
            pltpu.VMEM((all_rows, query_columns), BF16),
            pltpu.VMEM((all_rows, rank), BF16),
            pltpu.VMEM(single, BF16),
            pltpu.VMEM(single, BF16),
            pltpu.VMEM(single, F32),
            pltpu.VMEM(single, F32),
            pltpu.VMEM(single, F32),
            pltpu.VMEM((all_rows, 3 * rank), F32),
            pltpu.VMEM((rank, width), F32),
            pltpu.VMEM((plane, slots, width), BF16),
            pltpu.VMEM((line - 1,) + block, BF16),
            pltpu.VMEM((line - 1,) + block, BF16),
            pltpu.VMEM(block, F32),
            pltpu.VMEM((plane * slots, count), BF16),
            dma((4,)),
            dma((line + 1,)),
        ]
        + [dma((line - 1, 4))] * 4
        + [dma((line, plane))] * 2
        + [dma((line - 1,))] * 2,
        compiler_params=pltpu.CompilerParams(
            collective_id=identity, has_side_effects=True, vmem_limit_bytes=63 * MEBI
        ),
        name="back",
    )(*operands, *hbm_operands)


def last_body(
    line,
    linear_grad_ref,
    share_ref,
    first_ref,
    residual_grad_ref,
    tokens_ref,
    gain_ref,
    gathered_hbm,
    input_grad_ref,
    weights,
    part,
    left_buf,
    right_buf,
    load_sem,
    *semaphores,
):
    at_line = lax.axis_index("tensor")
    tokens, width = tokens_ref.shape
    linear_columns = linear_grad_ref.shape[1]
    load = pltpu.make_async_copy(
        gathered_hbm.at[:, :, pl.ds(0, linear_columns)], weights, load_sem
    )
    load.start()
    greet_line(at_line, line)
    load.wait()
    shards, wide = weights.shape[:2]

    def normed_gradient(block):
        at = pl.ds(pl.multiple_of(block * tokens, tokens), tokens)

        @pl.loop(0, shards)
        def _(shard):
            columns = pl.ds(pl.multiple_of(shard * wide, wide), wide)
            part[block, :, columns] = (
                flipped_right_operand(linear_grad_ref[at, :], weights[shard])
                + matrix_product(share_ref[at, :], first_ref[:, columns])
            ).astype(BF16)

    advance, finish = line_sum(
        at_line, line, 4, part, input_grad_ref, left_buf, right_buf, semaphores
    )
    for far in range(line - 1, 0, -1):

        @pl.when(at_line + far < line)
        def _():
            normed_gradient(at_line + far)

        @pl.when(at_line - far >= 0)
        def _():
            normed_gradient(at_line - far)

        advance(far)
    normed_gradient(at_line)
    finish()
    half = tokens // 2
    for at in range(2):
        rows = pl.ds(at * half, half)
        values = tokens_ref[rows, :].astype(F32)
        factor = lax.rsqrt(jnp.mean(values * values, axis=-1, keepdims=True) + NORM_EPSILON)
        input_grad_ref[rows, :] = residual_grad_ref[rows, :] + norm_backward(
            values, factor, gain_ref[...], input_grad_ref[rows, :]
        )


def last(linear_grad, share, first, residual_grad, tokens, gain, gathered, identity):
    line = lax.axis_size("tensor")
    count, width = tokens.shape
    anywhere = pl.BlockSpec(memory_space=pl.ANY)
    local = pl.BlockSpec(memory_space=pltpu.VMEM)
    dma = pltpu.SemaphoreType.DMA
    return pl.pallas_call(
        functools.partial(last_body, line),
        out_shape=jax.ShapeDtypeStruct((count, width), F32),
        in_specs=[local] * 6 + [anywhere],
        out_specs=local,
        scratch_shapes=[
            pltpu.VMEM(gathered.shape[:2] + (linear_grad.shape[1],), BF16),
            pltpu.VMEM((line, count, width), BF16),
            pltpu.VMEM((line - 1, count, width), BF16),
            pltpu.VMEM((line - 1, count, width), BF16),
            dma,
        ]
        + [dma((line - 1, 4))] * 4,
        compiler_params=pltpu.CompilerParams(
            collective_id=identity, has_side_effects=True, vmem_limit_bytes=48 * MEBI
        ),
        name="last",
    )(linear_grad, share, first, residual_grad, tokens, gain, gathered)


def per_device(
    tokens,
    segments,
    routes,
    adapter_index,
    cotangent,
    attn_gain,
    moe_gain,
    q_gain,
    key_norm_gain,
    w_query,
    key_projection_weight,
    value_projection_weight,
    w_out,
    w_router,
    expert_gate_weight,
    expert_up_weight,
    expert_down_weight,
    query_in,
    query_out,
    key_in,
    key_second_weight,
    value_in,
    value_second_weight,
    attn_in,
    attn_out,
    router_in,
    router_out,
    gate_in,
    gate_out,
    upward_in,
    upward_out,
    downward_in,
    downward_out,
):
    tensor_count = lax.axis_size("tensor")
    fsdp_count = lax.axis_size("fsdp")
    device_count = fsdp_count * tensor_count
    tensor_pos = lax.axis_index("tensor")
    fsdp_pos = lax.axis_index("fsdp")
    zero_pos = fsdp_pos * 0
    tok_rows, model_width = tokens.shape
    seq_rows = tok_rows * tensor_count
    rank = query_in.shape[2]
    adapter_count = query_in.shape[0]
    head_dim = q_gain.shape[0]
    local_cols = query_out.shape[2]
    local_kv_cols = key_second_weight.shape[2]
    expert_count = w_router.shape[1]
    top_count = routes.shape[1]
    capacity = 5 * tok_rows * top_count // (4 * expert_count)
    slots = -(-capacity // 16) * 16
    score_scale = 1.0 / math.sqrt(head_dim)
    adapter_pick = lax.dynamic_index_in_dim(adapter_index, fsdp_pos, 0, keepdims=False)

    def select_adapter(adapter_table):
        return lax.dynamic_index_in_dim(adapter_table, adapter_pick, 0, keepdims=False)

    def transposed(adapter_table):
        return jnp.swapaxes(adapter_table, -1, -2)

    input_first = jnp.concatenate(
        [select_adapter(transposed(table)) for table in (query_in, key_in, value_in)], axis=0
    )
    q_second = select_adapter(query_out)
    k_second = select_adapter(key_second_weight)
    v_second = select_adapter(value_second_weight)
    attention_first = select_adapter(transposed(attn_in))
    attention_second = select_adapter(attn_out)
    router_first = select_adapter(transposed(router_in))
    router_second = select_adapter(router_out)
    gain_attn = attn_gain.astype(F32)
    gain_moe = moe_gain.astype(F32)
    gain_query = q_gain.astype(F32)[None, :]
    gain_key = key_norm_gain.astype(F32)[None, :]

    in_kernel = fsdp_count * slots <= 640
    linear_cols = local_cols + 2 * local_kv_cols
    router_pad = -(-expert_count // 128) * 128
    out_start = linear_cols + router_pad
    packed = jnp.concatenate(
        [
            w_query,
            key_projection_weight,
            value_projection_weight,
            jnp.pad(w_router, ((0, 0), (0, router_pad - expert_count))),
            jnp.transpose(w_out, (1, 0)),
        ],
        axis=1,
    )
    tables = rope_tables(seq_rows, head_dim)
    seg_row = segments
    seg_column = jnp.transpose(segments, (1, 0))
    token_values = tokens.astype(F32)
    attn_normed, attn_factor = norm_forward(token_values, gain_attn)
    offsets = [0] + [sign * step for step in range(1, tensor_count) for sign in (1, -1)]
    offsets = [offset % tensor_count for offset in offsets[:tensor_count]]
    line_blocks = [((tensor_pos + offset) % tensor_count)[None] for offset in offsets]

    def fetched(block, offset):
        if offset == 0:
            return block
        pairs = [((at + offset) % tensor_count, at) for at in range(tensor_count)]
        return lax.ppermute(block, "tensor", pairs)

    def delivered(block, offset):
        if offset == 0:
            return block
        pairs = [(at, (at + offset) % tensor_count) for at in range(tensor_count)]
        return lax.ppermute(block, "tensor", pairs)

    def dispatched(block):
        return [
            plane_rows(to_slots(at, plane_ranks, fetched(block, offset), slots))
            for offset, at in zip(offsets, line_blocks)
        ]

    if in_kernel:
        (
            attention_total,
            plane_ranks,
            low,
            attention_low,
            linear,
            heads_narrow,
            sequence_normalized,
            gathered,
            up_rows,
        ) = front(
            tokens,
            cotangent,
            jnp.transpose(routes, (1, 0)),
            packed,
            gain_attn[None, :],
            input_first,
            q_second,
            k_second,
            v_second,
            gain_query,
            gain_key,
            tables,
            seg_column,
            seg_row,
            attention_first,
            attention_second,
            score_scale,
            slots,
            (linear_cols, out_start),
            0,
        )
        sequence_normalized = sequence_normalized.reshape(seq_rows, model_width)
        gathered_blocks = gathered
        gathered = gathered.reshape(model_width, -1)
    else:
        gathered = lax.all_gather(packed, "fsdp", axis=0, tiled=True)
        sequence_tokens, sequence_routes = gather_line(
            [tokens, jnp.transpose(routes, (1, 0))], (4, 1), 0
        )
        sequence_tokens = sequence_tokens.reshape(seq_rows, model_width)
        plane_experts = jnp.arange(fsdp_count, dtype=jnp.int32) * tensor_count + tensor_pos
        plane_ranks = ranks_of(
            jnp.any(
                sequence_routes[:, None, :, :] == plane_experts[None, :, None, None], axis=2
            )
        )
        up_rows = dispatched(cotangent)
        sequence_normalized = norm_forward(sequence_tokens.astype(F32), gain_attn)[0].astype(
            BF16
        )
        linear = matrix_product(sequence_normalized, gathered[:, :linear_cols])
        low = flipped_right_operand(sequence_normalized, input_first).astype(BF16)
    complete_linear = gathered[:, :linear_cols]
    complete_router = gathered[:, linear_cols : linear_cols + expert_count]
    full_out_t = gathered[:, out_start:]
    attention_operands = (
        linear,
        low,
        q_second,
        k_second,
        v_second,
        gain_query,
        gain_key,
        tables,
        seg_column,
        seg_row,
        score_scale,
    )
    if not in_kernel:
        heads_narrow = attention_forward(*attention_operands)
        attention_low = flipped_right_operand(heads_narrow, attention_first).astype(BF16)
        out_part = flipped_right_operand(heads_narrow, full_out_t) + matrix_product(
            attention_low, attention_second
        )
        attention_total = sum_line(
            out_part.astype(BF16).reshape(tensor_count, tok_rows, model_width), 4, 1
        )
    residual_stream = token_values + attention_total
    moe_normed, moe_factor = norm_forward(residual_stream, gain_moe)
    experts_narrow = moe_normed.astype(BF16)

    router_low = flipped_right_operand(experts_narrow, router_first).astype(BF16)
    router_logits = matrix_product(experts_narrow, complete_router) + matrix_product(
        router_low, router_second
    )
    expert_ids = jnp.arange(expert_count, dtype=jnp.int32)
    chosen = jnp.any(routes[:, :, None] == expert_ids[None, None, :], axis=1)
    chosen_logits = jnp.where(chosen, router_logits, -jnp.inf)
    chosen_exp = jnp.exp(chosen_logits - jnp.max(chosen_logits, axis=-1, keepdims=True))
    gate_weights = chosen_exp / jnp.sum(chosen_exp, axis=-1, keepdims=True)
    sent_weights = jnp.transpose(jnp.where(chosen, gate_weights, -1.0), (1, 0))
    own_weights = jnp.transpose(
        route_rows(sent_weights).reshape(fsdp_count, tensor_count, tok_rows), (1, 0, 2)
    )
    own_ranks = ranks_of(own_weights >= 0.0)

    broad = adapter_count * rank
    gate_in_t, upward_in_t = transposed(gate_in[0]), transposed(upward_in[0])
    expert_tables = (
        expert_gate_weight[0],
        expert_up_weight[0],
        expert_down_weight[0],
        jnp.concatenate(
            [gate_in_t.reshape(broad, model_width), upward_in_t.reshape(broad, model_width)],
            axis=0,
        ),
        gate_out[0].reshape(broad, -1),
        upward_out[0].reshape(broad, -1),
        transposed(downward_in[0]).reshape(broad, -1),
        downward_out[0].reshape(broad, model_width),
    )
    column_adapter = jnp.arange(broad, dtype=jnp.int32) // rank
    adapter_mask = jnp.repeat(
        (adapter_index[:, None] == column_adapter[None, :]).astype(BF16), slots, axis=0
    )
    ordered = [None] * tensor_count
    if in_kernel:
        moe_grad, gate_dots, expert_output, _landed, *sums = moe_layer(
            experts_narrow,
            up_rows,
            plane_ranks,
            own_ranks,
            own_weights,
            adapter_mask,
            expert_tables,
            3,
        )
    else:
        expert_rows = dispatched(experts_narrow)
        expert_output, rows_grad, gate_dots = [], [], []
        sums = [jnp.zeros(each.shape, F32) for each in expert_sums(expert_tables)]
        for at, rows, upstream in zip(line_blocks, expert_rows, up_rows):
            y_rows, grad_rows, dots, *sums = experts(
                at, rows, upstream, own_ranks, own_weights, adapter_mask, expert_tables, sums
            )
            expert_output.append(y_rows)
            rows_grad.append(grad_rows)
            gate_dots.append(dots)
        for offset, dots in zip(offsets, gate_dots):
            ordered[offset] = dots
        gate_dots = jnp.roll(jnp.stack(ordered), tensor_pos, axis=0)
    pair_in_grad, gate_out_grad, upward_out_grad, downward_in_grad, downward_out_grad = sums
    if in_kernel:

        def by_line(table):
            lines = table.reshape(fsdp_count, tensor_count, -1)
            return jnp.transpose(lines, (1, 0, 2)).reshape(expert_count, -1)

        (
            output,
            residual_grad,
            low_share,
            linear_grad,
            row_grads,
            head_grads,
            narrow_grads,
            router_grads,
            _landed,
        ) = back(
            score_scale,
            (linear_cols, out_start),
            slots,
            4,
            (linear, heads_narrow, sequence_normalized, gathered_blocks, expert_output),
            (
                moe_grad,
                gate_dots.reshape(expert_count, tok_rows),
                by_line(jnp.transpose(gate_weights, (1, 0))),
                residual_stream,
                cotangent,
                gain_moe[None, :],
                by_line(jnp.transpose(complete_router, (1, 0))),
                router_first,
                jnp.transpose(by_line(jnp.transpose(router_second, (1, 0))), (1, 0)),
                jnp.transpose(router_low, (1, 0)),
                experts_narrow,
                plane_ranks,
                low,
                attention_low,
                attention_first,
                attention_second,
                q_second,
                k_second,
                v_second,
                gain_query,
                gain_key,
                *tables,
                seg_column,
                seg_row,
            ),
        )
        router_second_gradient = jnp.transpose(
            router_grads.reshape(rank, tensor_count, fsdp_count), (0, 2, 1)
        ).reshape(rank, expert_count)
        input_grad = last(
            linear_grad,
            low_share,
            input_first,
            residual_grad,
            tokens,
            gain_attn[None, :],
            gathered_blocks,
            5,
        )
    else:
        gate_grad = jnp.transpose(
            route_rows(jnp.transpose(gate_dots, (1, 0, 2)).reshape(device_count, tok_rows)), (1, 0)
        )

        def returned(slotted):
            total = 0.0
            for offset, at, rows in zip(offsets, line_blocks, slotted):
                combined = from_slots(at, plane_ranks, plane_rows(rows))
                total = total + delivered(combined, offset).astype(F32)
            return total

        moe_grad = returned(rows_grad)

        out_grad = cotangent.astype(F32)
        logit_gradient = (
            gate_weights * (gate_grad - jnp.sum(gate_weights * gate_grad, axis=-1, keepdims=True))
        ).astype(BF16)
        router_low_gradient = flipped_right_operand(logit_gradient, router_second).astype(BF16)
        moe_grad = (
            moe_grad
            + flipped_right_operand(logit_gradient, complete_router)
            + matrix_product(router_low_gradient, router_first)
        )
        router_first_gradient = flipped_left_operand(router_low_gradient, experts_narrow)
        router_second_gradient = flipped_left_operand(router_low, logit_gradient)
        residual_grad = out_grad + norm_backward(residual_stream, moe_factor, gain_moe, moe_grad)

        (sequence_branch,) = gather_line([residual_grad.astype(BF16)], (4,), 2)
        sequence_branch = sequence_branch.reshape(seq_rows, model_width)
        output = (residual_stream + returned(expert_output)).astype(BF16)
        attention_low_grad = flipped_right_operand(sequence_branch, attention_second).astype(BF16)
        attention_second_gradient = flipped_left_operand(attention_low, sequence_branch)
        heads_grad = matrix_product(sequence_branch, full_out_t)
        (
            q_grad,
            k_grad,
            v_grad,
            low_share,
            q_second_gradient,
            k_second_gradient,
            v_second_gradient,
            attention_first_gradient,
        ) = attention_backward(
            *attention_operands,
            heads_narrow,
            heads_grad,
            attention_low_grad,
            attention_first,
        )
        linear_grad = jnp.concatenate([q_grad, k_grad, v_grad], axis=1)
        normed_part = flipped_right_operand(linear_grad, complete_linear) + matrix_product(
            low_share, input_first
        )
        input_first_gradient = flipped_left_operand(low_share, sequence_normalized)
        normalized_gradient = sum_line(
            normed_part.astype(BF16).reshape(tensor_count, tok_rows, model_width), 4, 1
        )
        input_grad = residual_grad + norm_backward(
            token_values, attn_factor, gain_attn, normalized_gradient
        )
        row_grads = jnp.concatenate(
            [input_first_gradient, attention_second_gradient, router_first_gradient], axis=0
        )
        head_grads = jnp.concatenate([q_second_gradient, attention_first_gradient], axis=0)
        narrow_grads = jnp.concatenate([k_second_gradient, v_second_gradient], axis=0)

    source_adapter = jnp.repeat(adapter_index, tensor_count)
    owner_onehot = (
        jnp.arange(adapter_count, dtype=jnp.int32)[:, None] == source_adapter[None, :]
    ).astype(BF16)

    def to_all(addend):
        lines = addend.shape[0]
        return jnp.transpose(
            addend.astype(BF16).reshape(lines, device_count, -1), (1, 0, 2)
        ).reshape(device_count, -1)

    def to_head_owners(addend):
        lines = addend.shape[0]
        pieces = jnp.transpose(
            addend.astype(BF16).reshape(lines, fsdp_count, -1), (1, 0, 2)
        ).reshape(fsdp_count, -1)
        holder = jnp.zeros((device_count, pieces.shape[1]), BF16)
        return lax.dynamic_update_slice(holder, pieces, (tensor_pos * fsdp_count, zero_pos))

    def owner_sums(parts):
        widths = [part.shape[1] for part in parts]
        total = matrix_product(owner_onehot, route_rows(jnp.concatenate(parts, axis=1)))
        pieces = []
        start = 0
        for width in widths:
            pieces.append(total[:, start : start + width])
            start += width
        return pieces

    row_sums, head_sums, narrow_sums, router_sums = owner_sums(
        [
            to_all(row_grads),
            to_head_owners(head_grads),
            to_head_owners(narrow_grads),
            to_all(router_second_gradient),
        ]
    )

    def lines_of(piece, lines):
        return piece.reshape(adapter_count, lines, -1)

    row_sums = lines_of(row_sums, 5 * rank)
    head_sums = lines_of(head_sums, 2 * rank)
    narrow_sums = lines_of(narrow_sums, 2 * rank)

    def factor_rows(at):
        return row_sums[:, at * rank : (at + 1) * rank]

    return (
        output,
        input_grad,
        transposed(factor_rows(0)),
        head_sums[:, :rank],
        transposed(factor_rows(1)),
        narrow_sums[:, :rank],
        transposed(factor_rows(2)),
        narrow_sums[:, rank:],
        transposed(head_sums[:, rank:]),
        factor_rows(3),
        transposed(factor_rows(4)),
        lines_of(router_sums, rank),
        transposed(lines_of(pair_in_grad[:broad], rank))[None],
        lines_of(gate_out_grad, rank)[None],
        transposed(lines_of(pair_in_grad[broad:], rank))[None],
        lines_of(upward_out_grad, rank)[None],
        transposed(lines_of(downward_in_grad, rank))[None],
        lines_of(downward_out_grad, rank)[None],
    )


def solution(mesh):
    placed = (
        P(("fsdp", "tensor"), None),
        P("fsdp", None),
        P(("fsdp", "tensor"), None),
        P(),
        P(("fsdp", "tensor"), None),
        P(),
        P(),
        P(),
        P(),
        P("fsdp", "tensor"),
        P("fsdp", "tensor"),
        P("fsdp", "tensor"),
        P("tensor", "fsdp"),
        P("fsdp", None),
        P(("fsdp", "tensor"), None, None),
        P(("fsdp", "tensor"), None, None),
        P(("fsdp", "tensor"), None, None),
        P(),
        P(None, None, "tensor"),
        P(),
        P(None, None, "tensor"),
        P(),
        P(None, None, "tensor"),
        P(None, "tensor", None),
        P(),
        P(),
        P(),
        P(("fsdp", "tensor"), None, None, None),
        P(("fsdp", "tensor"), None, None, None),
        P(("fsdp", "tensor"), None, None, None),
        P(("fsdp", "tensor"), None, None, None),
        P(("fsdp", "tensor"), None, None, None),
        P(("fsdp", "tensor"), None, None, None),
    )
    return jax.shard_map(
        per_device,
        mesh=mesh,
        in_specs=placed,
        out_specs=(
            P(("fsdp", "tensor"), None),
            P(("fsdp", "tensor"), None),
            P(None, ("fsdp", "tensor"), None),
            P(None, None, ("fsdp", "tensor")),
            P(None, ("fsdp", "tensor"), None),
            P(None, None, ("fsdp", "tensor")),
            P(None, ("fsdp", "tensor"), None),
            P(None, None, ("fsdp", "tensor")),
            P(None, ("fsdp", "tensor"), None),
            P(None, None, ("fsdp", "tensor")),
            P(None, ("fsdp", "tensor"), None),
            P(None, None, ("fsdp", "tensor")),
            P(("fsdp", "tensor"), None, None, None),
            P(("fsdp", "tensor"), None, None, None),
            P(("fsdp", "tensor"), None, None, None),
            P(("fsdp", "tensor"), None, None, None),
            P(("fsdp", "tensor"), None, None, None),
            P(("fsdp", "tensor"), None, None, None),
        ),
        check_vma=False,
    )
```

```python
import functools
import math

import jax
import jax.numpy as jnp
from jax import lax
from jax.experimental import pallas as pl
from jax.experimental.pallas import tpu as pltpu
from jax.sharding import PartitionSpec as P

NORM_EPSILON = 1e-06
ROPE_THETA = 1000000.0
BF16 = jnp.bfloat16
F32 = jnp.float32
WINDOW = 256
MEBI = 1 << 20


def matrix_product(first_op, second_op):
    return jnp.dot(first_op, second_op, preferred_element_type=F32)


def flipped_left_operand(first_op, second_op):
    return lax.dot_general(
        first_op, second_op, (((0,), (0,)), ((), ())), preferred_element_type=F32
    )


def flipped_right_operand(first_op, second_op):
    return lax.dot_general(
        first_op, second_op, (((1,), (1,)), ((), ())), preferred_element_type=F32
    )


def norm_forward(values, gain_vec):
    factor = lax.rsqrt(jnp.mean(values * values, axis=-1, keepdims=True) + NORM_EPSILON)
    return (values * factor * gain_vec, factor)


def norm_backward(values, factor, gain_vec, upstream):
    scaled = upstream * gain_vec
    return factor * scaled - values * (factor * factor * factor) * jnp.mean(
        values * scaled, axis=-1, keepdims=True
    )


def rope_tables(sequence_length, head_width):
    half_width = head_width // 2
    inverse = jnp.power(ROPE_THETA, -2.0 * jnp.arange(half_width, dtype=F32) / head_width)
    angles = jnp.arange(sequence_length, dtype=F32)[:, None] * inverse[None, :]
    cosine, sine = jnp.cos(angles), jnp.sin(angles)
    return (
        jnp.concatenate([cosine, cosine], axis=1),
        jnp.concatenate([-sine, sine], axis=1),
    )


def swapped(values):
    return pltpu.roll(values, values.shape[-1] // 2, 1)


def route_rows(block_rows):
    return lax.all_to_all(block_rows, ("fsdp", "tensor"), split_axis=0, concat_axis=0, tiled=True)


def plane_rows(block_rows):
    return lax.all_to_all(block_rows, "fsdp", split_axis=0, concat_axis=0, tiled=True)


def params(mebibytes, axes=1):
    return pltpu.CompilerParams(
        vmem_limit_bytes=mebibytes * MEBI, dimension_semantics=("arbitrary",) * axes
    )


def whole(shape):
    rank = len(shape)
    return pl.BlockSpec(shape, lambda *_: (0,) * rank)


def head_values(linear, low, second, gain, cosine, sine):
    values = linear + matrix_product(low, second)
    normed, factor = norm_forward(values, gain)
    turned = (normed * cosine + swapped(normed) * sine).astype(BF16)
    return values, factor, turned


def head_values_gradient(values, factor, gain, cosine, sine, upstream):
    back = upstream * cosine - swapped(upstream) * sine
    return norm_backward(values, factor, gain, back).astype(BF16)


def allowed_keys(block, start, width, seg_column, seg_row):
    rows = block * WINDOW + lax.broadcasted_iota(jnp.int32, (WINDOW, width), 0)
    keys = start + lax.broadcasted_iota(jnp.int32, (WINDOW, width), 1)
    mine = seg_column[block * WINDOW : (block + 1) * WINDOW]
    theirs = seg_row[:, start : start + width]
    return (keys == rows) | ((keys < rows) & (mine == theirs) & (theirs != 0))


def block_bounds(block):
    start = max(block - 1, 0) * WINDOW
    return start, (block + 1) * WINDOW - start


def attention_forward_body(
    rank,
    scale,
    lin_ref,
    key_lin_ref,
    value_lin_ref,
    low_ref,
    q_second_ref,
    k_second_ref,
    v_second_ref,
    q_gain_ref,
    k_gain_ref,
    cos_ref,
    sin_ref,
    seg_column_ref,
    seg_row_ref,
    heads_ref,
    key_scratch,
    value_scratch,
):
    cosine, sine = cos_ref[...], sin_ref[...]

    @pl.when(pl.program_id(0) == 0)
    def _():
        key_scratch[...] = head_values(
            key_lin_ref[...],
            low_ref[:, rank : 2 * rank],
            k_second_ref[...],
            k_gain_ref[...],
            cosine,
            sine,
        )[2]
        value_scratch[...] = (
            value_lin_ref[...]
            + matrix_product(low_ref[:, 2 * rank : 3 * rank], v_second_ref[...])
        ).astype(BF16)

    query = head_values(
        lin_ref[...], low_ref[:, :rank], q_second_ref[...], q_gain_ref[...], cosine, sine
    )[2]
    seg_column, seg_row = seg_column_ref[...], seg_row_ref[...]
    for block in range(query.shape[0] // WINDOW):
        start, width = block_bounds(block)
        rows = pl.ds(block * WINDOW, WINDOW)
        scores = (
            flipped_right_operand(
                query[block * WINDOW : (block + 1) * WINDOW], key_scratch[pl.ds(start, width)]
            )
            * scale
        )
        scores = jnp.where(
            allowed_keys(block, start, width, seg_column, seg_row), scores, -1e30
        )
        expo = jnp.exp(scores - jnp.max(scores, axis=-1, keepdims=True))
        probs = (expo / jnp.sum(expo, axis=-1, keepdims=True)).astype(BF16)
        heads_ref[rows, :] = matrix_product(probs, value_scratch[pl.ds(start, width)]).astype(
            BF16
        )


def attention_forward(
    linear, low, q_second, k_second, v_second, q_gain, k_gain, tables, seg_column, seg_row, scale
):
    rows, head_dim = linear.shape[0], q_gain.shape[1]
    heads = q_second.shape[1] // head_dim
    rank = q_second.shape[0]
    column = pl.BlockSpec((rows, head_dim), lambda h: (0, h))
    return pl.pallas_call(
        functools.partial(attention_forward_body, rank, scale),
        grid=(heads,),
        out_shape=jax.ShapeDtypeStruct((rows, heads * head_dim), BF16),
        in_specs=[
            column,
            pl.BlockSpec((rows, head_dim), lambda h: (0, heads)),
            pl.BlockSpec((rows, head_dim), lambda h: (0, heads + 1)),
            whole(low.shape),
            pl.BlockSpec((rank, head_dim), lambda h: (0, h)),
            whole(k_second.shape),
            whole(v_second.shape),
            whole(q_gain.shape),
            whole(k_gain.shape),
            whole(tables[0].shape),
            whole(tables[1].shape),
            whole(seg_column.shape),
            whole(seg_row.shape),
        ],
        out_specs=column,
        scratch_shapes=[pltpu.VMEM((rows, head_dim), BF16), pltpu.VMEM((rows, head_dim), BF16)],
        compiler_params=params(40),
        cost_estimate=pl.CostEstimate(
            flops=8 * heads * rows * WINDOW * head_dim,
            transcendentals=2 * heads * rows * WINDOW,
            bytes_accessed=6 * rows * heads * head_dim,
        ),
        name="attention_forward",
    )(
        linear,
        linear,
        linear,
        low,
        q_second,
        k_second,
        v_second,
        q_gain,
        k_gain,
        *tables,
        seg_column,
        seg_row,
    )


def attention_backward_body(
    rank,
    scale,
    lin_ref,
    key_lin_ref,
    value_lin_ref,
    low_ref,
    q_second_ref,
    k_second_ref,
    v_second_ref,
    q_gain_ref,
    k_gain_ref,
    cos_ref,
    sin_ref,
    seg_column_ref,
    seg_row_ref,
    heads_ref,
    heads_grad_ref,
    low_grad_ref,
    down_ref,
    q_grad_ref,
    k_grad_ref,
    v_grad_ref,
    share_ref,
    q_second_grad_ref,
    k_second_grad_ref,
    v_second_grad_ref,
    down_grad_ref,
    key_scratch,
    value_scratch,
    key_sum,
    value_sum,
    query_sum,
    share_sum,
):
    cosine, sine = cos_ref[...], sin_ref[...]
    head = pl.program_id(0)

    @pl.when(head == 0)
    def _():
        key_scratch[...] = head_values(
            key_lin_ref[...],
            low_ref[:, rank : 2 * rank],
            k_second_ref[...],
            k_gain_ref[...],
            cosine,
            sine,
        )[2]
        value_scratch[...] = (
            value_lin_ref[...]
            + matrix_product(low_ref[:, 2 * rank : 3 * rank], v_second_ref[...])
        ).astype(BF16)
        key_sum[...] = jnp.zeros_like(key_sum)
        value_sum[...] = jnp.zeros_like(value_sum)
        share_sum[...] = jnp.zeros_like(share_sum)

    low_q = low_ref[:, :rank]
    values, factor, query = head_values(
        lin_ref[...], low_q, q_second_ref[...], q_gain_ref[...], cosine, sine
    )
    low_grad = low_grad_ref[...]
    upstream = (heads_grad_ref[...] + matrix_product(low_grad, down_ref[...])).astype(BF16)
    down_grad_ref[...] = flipped_left_operand(low_grad, heads_ref[...])
    seg_column, seg_row = seg_column_ref[...], seg_row_ref[...]
    for block in range(query.shape[0] // WINDOW):
        start, width = block_bounds(block)
        rows = pl.ds(block * WINDOW, WINDOW)
        keys = pl.ds(start, width)
        query_block = query[block * WINDOW : (block + 1) * WINDOW]
        upstream_block = upstream[block * WINDOW : (block + 1) * WINDOW]
        scores = flipped_right_operand(query_block, key_scratch[keys]) * scale
        scores = jnp.where(
            allowed_keys(block, start, width, seg_column, seg_row), scores, -1e30
        )
        expo = jnp.exp(scores - jnp.max(scores, axis=-1, keepdims=True))
        probs = expo / jnp.sum(expo, axis=-1, keepdims=True)
        prob_grad = flipped_right_operand(upstream_block, value_scratch[keys])
        score_grad = (
            probs * (prob_grad - jnp.sum(probs * prob_grad, axis=-1, keepdims=True))
        ).astype(BF16)
        value_sum[keys, :] += flipped_left_operand(probs.astype(BF16), upstream_block)
        key_sum[keys, :] += flipped_left_operand(score_grad, query_block)
        query_sum[rows, :] = matrix_product(score_grad, key_scratch[keys]) * scale
    q_grad = head_values_gradient(
        values, factor, q_gain_ref[...], cosine, sine, query_sum[...]
    )
    q_grad_ref[...] = q_grad
    q_second_grad_ref[...] = flipped_left_operand(low_q, q_grad)
    share_sum[:, :rank] += flipped_right_operand(q_grad, q_second_ref[...])

    @pl.when(head == pl.num_programs(0) - 1)
    def _():
        low_k = low_ref[:, rank : 2 * rank]
        low_v = low_ref[:, 2 * rank : 3 * rank]
        key_values, key_factor, _turned = head_values(
            key_lin_ref[...], low_k, k_second_ref[...], k_gain_ref[...], cosine, sine
        )
        k_grad = head_values_gradient(
            key_values, key_factor, k_gain_ref[...], cosine, sine, key_sum[...] * scale
        )
        v_grad = value_sum[...].astype(BF16)
        k_grad_ref[...] = k_grad
        v_grad_ref[...] = v_grad
        k_second_grad_ref[...] = flipped_left_operand(low_k, k_grad)
        v_second_grad_ref[...] = flipped_left_operand(low_v, v_grad)
        share_sum[:, rank : 2 * rank] = flipped_right_operand(k_grad, k_second_ref[...])
        share_sum[:, 2 * rank : 3 * rank] = flipped_right_operand(v_grad, v_second_ref[...])
        share_ref[...] = share_sum[...].astype(BF16)


def attention_backward(
    linear,
    low,
    q_second,
    k_second,
    v_second,
    q_gain,
    k_gain,
    tables,
    seg_column,
    seg_row,
    scale,
    heads_low,
    heads_grad,
    low_grad,
    down_first,
):
    rows, head_dim = linear.shape[0], q_gain.shape[1]
    rank, columns = q_second.shape
    heads = columns // head_dim
    column = pl.BlockSpec((rows, head_dim), lambda h: (0, h))
    narrow = pl.BlockSpec((rank, head_dim), lambda h: (0, h))
    single = (rows, head_dim)
    return pl.pallas_call(
        functools.partial(attention_backward_body, rank, scale),
        grid=(heads,),
        out_shape=(
            jax.ShapeDtypeStruct((rows, columns), BF16),
            jax.ShapeDtypeStruct(single, BF16),
            jax.ShapeDtypeStruct(single, BF16),
            jax.ShapeDtypeStruct((rows, 3 * rank), BF16),
            jax.ShapeDtypeStruct((rank, columns), F32),
            jax.ShapeDtypeStruct((rank, head_dim), F32),
            jax.ShapeDtypeStruct((rank, head_dim), F32),
            jax.ShapeDtypeStruct((rank, columns), F32),
        ),
        in_specs=[
            column,
            pl.BlockSpec((rows, head_dim), lambda h: (0, heads)),
            pl.BlockSpec((rows, head_dim), lambda h: (0, heads + 1)),
            whole(low.shape),
            narrow,
            whole(k_second.shape),
            whole(v_second.shape),
            whole(q_gain.shape),
            whole(k_gain.shape),
            whole(tables[0].shape),
            whole(tables[1].shape),
            whole(seg_column.shape),
            whole(seg_row.shape),
            column,
            column,
            whole(low_grad.shape),
            narrow,
        ],
        out_specs=(
            column,
            whole(single),
            whole(single),
            whole((rows, 3 * rank)),
            narrow,
            whole((rank, head_dim)),
            whole((rank, head_dim)),
            narrow,
        ),
        scratch_shapes=[
            pltpu.VMEM(single, BF16),
            pltpu.VMEM(single, BF16),
            pltpu.VMEM(single, F32),
            pltpu.VMEM(single, F32),
            pltpu.VMEM(single, F32),
            pltpu.VMEM((rows, 3 * rank), F32),
        ],
        compiler_params=params(48),
        cost_estimate=pl.CostEstimate(
            flops=20 * heads * rows * WINDOW * head_dim,
            transcendentals=2 * heads * rows * WINDOW,
            bytes_accessed=12 * rows * columns,
        ),
        name="attention_backward",
    )(
        linear,
        linear,
        linear,
        low,
        q_second,
        k_second,
        v_second,
        q_gain,
        k_gain,
        *tables,
        seg_column,
        seg_row,
        heads_low,
        heads_grad,
        low_grad,
        down_first,
    )


def slot_choice(ranks, slots):
    experts, tokens = ranks.shape
    places = lax.broadcasted_iota(jnp.int32, (slots, tokens), 0).astype(ranks.dtype)
    return jnp.concatenate(
        [(places == ranks[e : e + 1, :]).astype(F32) for e in range(experts)], axis=0
    ).astype(BF16)


def to_slots_body(_block_ref, rank_ref, rows_ref, out_ref):
    slots = out_ref.shape[1]
    chosen = matrix_product(slot_choice(rank_ref[0], slots), rows_ref[...])
    out_ref[...] = chosen.astype(BF16).reshape(out_ref.shape)


def to_slots(block, ranks, rows, slots):
    experts, tokens = ranks.shape[1:]
    width = rows.shape[1]
    half = width // 2
    return pl.pallas_call(
        to_slots_body,
        grid_spec=pltpu.PrefetchScalarGridSpec(
            num_scalar_prefetch=1,
            grid=(2,),
            in_specs=[
                pl.BlockSpec((1, experts, tokens), lambda j, at: (at[0], 0, 0)),
                pl.BlockSpec((tokens, half), lambda j, at: (0, j)),
            ],
            out_specs=pl.BlockSpec((experts, slots, half), lambda j, at: (0, 0, j)),
        ),
        out_shape=jax.ShapeDtypeStruct((experts, slots, width), BF16),
        compiler_params=params(32),
        cost_estimate=pl.CostEstimate(
            flops=2 * experts * slots * tokens * width,
            transcendentals=0,
            bytes_accessed=2 * width * (experts * slots + tokens),
        ),
        name="to_slots",
    )(block, ranks, rows)


def from_slots_body(_block_ref, rank_ref, slot_ref, out_ref):
    experts, slots, width = slot_ref.shape
    choice = slot_choice(rank_ref[0], slots)
    out_ref[...] = flipped_left_operand(
        choice, slot_ref[...].reshape(experts * slots, width)
    ).astype(BF16)


def from_slots(block, ranks, slotted):
    experts, tokens = ranks.shape[1:]
    slots, width = slotted.shape[1:]
    half = width // 2
    return pl.pallas_call(
        from_slots_body,
        grid_spec=pltpu.PrefetchScalarGridSpec(
            num_scalar_prefetch=1,
            grid=(2,),
            in_specs=[
                pl.BlockSpec((1, experts, tokens), lambda j, at: (at[0], 0, 0)),
                pl.BlockSpec((experts, slots, half), lambda j, at: (0, 0, j)),
            ],
            out_specs=pl.BlockSpec((tokens, half), lambda j, at: (0, j)),
        ),
        out_shape=jax.ShapeDtypeStruct((tokens, width), BF16),
        compiler_params=params(32),
        cost_estimate=pl.CostEstimate(
            flops=2 * experts * slots * tokens * width,
            transcendentals=0,
            bytes_accessed=2 * width * (experts * slots + tokens),
        ),
        name="from_slots",
    )(block, ranks, slotted)


def all_to_slots_body(rank_ref, rows_ref, out_ref):
    slots = out_ref.shape[2]
    chosen = matrix_product(slot_choice(rank_ref[0], slots), rows_ref[...])
    out_ref[...] = chosen.astype(BF16).reshape(out_ref.shape)


def all_to_slots(ranks, rows, slots):
    blocks, experts, tokens = ranks.shape
    width = rows.shape[1]
    return pl.pallas_call(
        all_to_slots_body,
        grid=(blocks,),
        out_shape=jax.ShapeDtypeStruct((experts, blocks, slots, width), BF16),
        in_specs=[
            pl.BlockSpec((1, experts, tokens), lambda z: (z, 0, 0)),
            pl.BlockSpec((tokens, width), lambda z: (z, 0)),
        ],
        out_specs=pl.BlockSpec((experts, 1, slots, width), lambda z: (0, z, 0, 0)),
        compiler_params=params(40),
        cost_estimate=pl.CostEstimate(
            flops=2 * blocks * experts * slots * tokens * width,
            transcendentals=0,
            bytes_accessed=2 * blocks * width * (experts * slots + tokens),
        ),
        name="all_to_slots",
    )(ranks, rows)


def all_from_slots_body(_start_ref, rank_ref, slot_ref, out_ref):
    experts, _, slots, width = slot_ref.shape
    choice = slot_choice(rank_ref[0], slots)
    out_ref[...] = flipped_left_operand(
        choice, slot_ref[...].reshape(experts * slots, width)
    ).astype(BF16)


def all_from_slots(start, ranks, slotted):
    blocks, experts, tokens = ranks.shape
    slots, width = slotted.shape[2:]
    return pl.pallas_call(
        all_from_slots_body,
        grid_spec=pltpu.PrefetchScalarGridSpec(
            num_scalar_prefetch=1,
            grid=(blocks,),
            in_specs=[
                pl.BlockSpec((1, experts, tokens), lambda z, at: ((at[0] + z) % blocks, 0, 0)),
                pl.BlockSpec((experts, 1, slots, width), lambda z, at: (0, z, 0, 0)),
            ],
            out_specs=pl.BlockSpec((tokens, width), lambda z, at: ((at[0] + z) % blocks, 0)),
        ),
        out_shape=jax.ShapeDtypeStruct((blocks * tokens, width), BF16),
        compiler_params=params(40),
        cost_estimate=pl.CostEstimate(
            flops=2 * blocks * experts * slots * tokens * width,
            transcendentals=0,
            bytes_accessed=2 * blocks * width * (experts * slots + tokens),
        ),
        name="all_from_slots",
    )(start, ranks, slotted)


def ranks_of(mask):
    tokens = mask.shape[-1]
    order = jnp.arange(tokens, dtype=jnp.int32)
    before = (order[:, None] < order[None, :]).astype(BF16)
    counts = matrix_product(mask.astype(BF16), before)
    return jnp.where(mask, counts, -1.0).astype(jnp.int32)


def line_relay(me, count, ins, outs, chunks, semaphores):
    right_send, right_recv, left_send, left_recv = semaphores
    pieces = []
    for at in range(len(ins)):
        size = ins[at].shape[0] // chunks[at]
        for piece in range(chunks[at]):
            pieces.append((at, pl.ds(piece * size, size)))

    def copy(place, hop, origin, target, send, recv):
        at, rows = pieces[place]
        source = ins[at].at[rows] if hop == 0 else outs[at].at[origin, rows]
        return pltpu.make_async_remote_copy(
            src_ref=source,
            dst_ref=outs[at].at[origin, rows],
            send_sem=send.at[hop, place],
            recv_sem=recv.at[hop, place],
            device_id={"tensor": target},
        )

    def places(arrays):
        return [place for place in range(len(pieces)) if pieces[place][0] in arrays]

    def advance(hop, arrays):
        for place in places(arrays):
            if hop > 0:

                @pl.when(me - hop >= 0)
                def _():
                    copy(place, hop - 1, me - hop, me - 1, right_send, right_recv).wait_recv()

            if hop < count - 1:

                @pl.when((me - hop >= 0) & (me + 1 < count))
                def _():
                    copy(place, hop, me - hop, me + 1, right_send, right_recv).start()

            if hop > 0:

                @pl.when(me + hop < count)
                def _():
                    copy(place, hop - 1, me + hop, me + 1, left_send, left_recv).wait_recv()

            if hop < count - 1:

                @pl.when((me + hop < count) & (me > 0))
                def _():
                    copy(place, hop, me + hop, me - 1, left_send, left_recv).start()

    def finish(arrays, hops):
        for hop in hops:
            for place in places(arrays):

                @pl.when((me - hop >= 0) & (me + 1 < count))
                def _():
                    copy(place, hop, me - hop, me + 1, right_send, right_recv).wait_send()

                @pl.when((me + hop < count) & (me > 0))
                def _():
                    copy(place, hop, me + hop, me - 1, left_send, left_recv).wait_send()

    return advance, finish


def line_sum(me, count, chunks, part_ref, out_ref, left_buf, right_buf, semaphores):
    right_send, right_recv, left_send, left_recv = semaphores
    size = part_ref.shape[1] // chunks

    def rightward(rows, piece, far, source):
        return pltpu.make_async_remote_copy(
            src_ref=source,
            dst_ref=left_buf.at[far - 1, rows],
            send_sem=right_send.at[far - 1, piece],
            recv_sem=right_recv.at[far - 1, piece],
            device_id={"tensor": me + 1},
        )

    def leftward(rows, piece, far, source):
        return pltpu.make_async_remote_copy(
            src_ref=source,
            dst_ref=right_buf.at[far - 1, rows],
            send_sem=left_send.at[far - 1, piece],
            recv_sem=left_recv.at[far - 1, piece],
            device_id={"tensor": me - 1},
        )

    def added(buffer, far, rows, block):
        buffer[far, rows, :] = (
            buffer[far, rows, :].astype(F32) + part_ref[block, rows, :].astype(F32)
        ).astype(BF16)

    def advance(far):
        for piece in range(chunks):
            rows = pl.ds(piece * size, size)

            @pl.when((me == 0) & (me + far < count))
            def _():
                rightward(rows, piece, far, part_ref.at[me + far, rows]).start()

            @pl.when((me == count - 1) & (me - far >= 0))
            def _():
                leftward(rows, piece, far, part_ref.at[me - far, rows]).start()

            if far < count - 1:

                @pl.when((me > 0) & (me + far < count))
                def _():
                    rightward(rows, piece, far + 1, left_buf.at[far, rows]).wait_recv()
                    added(left_buf, far, rows, me + far)
                    rightward(rows, piece, far, left_buf.at[far, rows]).start()

                @pl.when((me < count - 1) & (me - far >= 0))
                def _():
                    leftward(rows, piece, far + 1, right_buf.at[far, rows]).wait_recv()
                    added(right_buf, far, rows, me - far)
                    leftward(rows, piece, far, right_buf.at[far, rows]).start()

    def finish():
        for piece in range(chunks):
            rows = pl.ds(piece * size, size)
            out_ref[rows, :] = part_ref[me, rows, :].astype(F32)

            @pl.when(me > 0)
            def _():
                rightward(rows, piece, 1, left_buf.at[0, rows]).wait_recv()
                out_ref[rows, :] += left_buf[0, rows, :].astype(F32)

            @pl.when(me < count - 1)
            def _():
                leftward(rows, piece, 1, right_buf.at[0, rows]).wait_recv()
                out_ref[rows, :] += right_buf[0, rows, :].astype(F32)

        for far in range(count - 1, 0, -1):
            for piece in range(chunks):
                rows = pl.ds(piece * size, size)

                @pl.when((me == 0) & (me + far < count))
                def _():
                    rightward(rows, piece, far, part_ref.at[me + far, rows]).wait_send()

                @pl.when((me == count - 1) & (me - far >= 0))
                def _():
                    leftward(rows, piece, far, part_ref.at[me - far, rows]).wait_send()

                if far < count - 1:

                    @pl.when((me > 0) & (me + far < count))
                    def _():
                        rightward(rows, piece, far, left_buf.at[far, rows]).wait_send()

                    @pl.when((me < count - 1) & (me - far >= 0))
                    def _():
                        leftward(rows, piece, far, right_buf.at[far, rows]).wait_send()

    return advance, finish


def greet_line_and_plane(line, plane):
    me, at_line = lax.axis_index("fsdp"), lax.axis_index("tensor")
    barrier = pltpu.get_barrier_semaphore()

    @pl.loop(1, plane)
    def _(d):
        pl.semaphore_signal(barrier, inc=1, device_id={"fsdp": lax.rem(me + d, plane)})

    @pl.loop(1, line)
    def _(d):
        pl.semaphore_signal(barrier, inc=1, device_id={"tensor": lax.rem(at_line + d, line)})

    pl.semaphore_wait(barrier, plane + line - 2)


def tiles(width, tile, body):
    @pl.loop(0, width // tile)
    def _(j):
        body(pl.ds(pl.multiple_of(j * tile, tile), tile))


def expert_math(
    tile, rows_ref, up_ref, ranks, weights, keep_dots, sent_y, mask_ref, tables, sums, scratch
):
    gate_w, up_w, down_w, pair_in, gate_out, up_out, down_in, down_out = tables
    pair_in_sum, gate_out_sum, up_out_sum, down_in_sum, down_out_sum = sums
    gate_lin_ref, up_lin_ref, inner_ref, route_ref, gate_grad_ref, up_grad_ref = scratch
    sources, slots, width = rows_ref.shape
    row_count = sources * slots
    hidden = gate_w.shape[1]
    broad = gate_out.shape[0]
    places = lax.broadcasted_iota(jnp.int32, (slots, ranks.shape[1]), 0)

    def held(source):
        return places == ranks[source : source + 1, :]

    def all_rows():
        return rows_ref[...].reshape(row_count, width)

    def pair_mask():
        mask = mask_ref[...].astype(F32)
        return jnp.concatenate([mask, mask], axis=1)

    weight = jnp.concatenate(
        [
            jnp.sum(
                jnp.where(held(source), weights[source : source + 1, :], 0.0),
                axis=1,
                keepdims=True,
            )
            for source in range(sources)
        ],
        axis=0,
    )
    pair = (flipped_right_operand(all_rows(), pair_in[...]) * pair_mask()).astype(BF16)
    gate_low, up_low = pair[:, :broad], pair[:, broad:]

    def inner_step(columns):
        rows = all_rows()
        gate_lin = matrix_product(rows, gate_w[:, columns]) + matrix_product(
            gate_low, gate_out[:, columns]
        )
        up_lin = matrix_product(rows, up_w[:, columns]) + matrix_product(
            up_low, up_out[:, columns]
        )
        gate_lin_ref[:, columns] = gate_lin
        up_lin_ref[:, columns] = up_lin
        inner_ref[:, columns] = (gate_lin * jax.nn.sigmoid(gate_lin) * up_lin).astype(BF16)

    tiles(hidden, tile, inner_step)
    down_low = (
        flipped_right_operand(inner_ref[...], down_in[...]) * mask_ref[...].astype(F32)
    ).astype(BF16)

    def down_step(j, total):
        columns = pl.ds(pl.multiple_of(j * tile, tile), tile)
        result = (
            matrix_product(inner_ref[...], down_w[:, columns])
            + matrix_product(down_low, down_out[:, columns])
        ).astype(BF16)
        wide = result.astype(F32)
        upstream = up_ref[:, :, columns].reshape(row_count, tile).astype(F32)
        up_ref[:, :, columns] = (weight * wide).astype(BF16).reshape(sources, slots, tile)
        route_ref[:, columns] = (weight * upstream).astype(BF16)
        return total + jnp.sum(upstream * wide, axis=1, keepdims=True)

    gate_dots = lax.fori_loop(0, width // tile, down_step, jnp.zeros((row_count, 1), F32))
    sent_y()
    for source in range(sources):
        keep_dots(
            source,
            jnp.sum(
                jnp.where(held(source), gate_dots[source * slots : (source + 1) * slots], 0.0),
                axis=0,
                keepdims=True,
            ),
        )
    down_low_grad = (
        flipped_right_operand(route_ref[...], down_out[...]) * mask_ref[...].astype(F32)
    ).astype(BF16)
    down_in_sum[...] += flipped_left_operand(down_low_grad, inner_ref[...])

    def down_out_step(columns):
        down_out_sum[:, columns] += flipped_left_operand(down_low, route_ref[:, columns])

    tiles(width, 2 * tile, down_out_step)

    def inner_grad_step(columns):
        inner_grad = flipped_right_operand(route_ref[...], down_w[columns, :]) + matrix_product(
            down_low_grad, down_in[:, columns]
        )
        gate_lin, up_lin = gate_lin_ref[:, columns], up_lin_ref[:, columns]
        sig = jax.nn.sigmoid(gate_lin)
        gate_grad_ref[:, columns] = (
            inner_grad * up_lin * (sig * (1.0 + gate_lin * (1.0 - sig)))
        ).astype(BF16)
        up_grad_ref[:, columns] = (inner_grad * (gate_lin * sig)).astype(BF16)

    tiles(hidden, tile, inner_grad_step)
    pair_grad = (
        jnp.concatenate(
            [
                flipped_right_operand(gate_grad_ref[...], gate_out[...]),
                flipped_right_operand(up_grad_ref[...], up_out[...]),
            ],
            axis=1,
        )
        * pair_mask()
    ).astype(BF16)
    gate_out_sum[...] += flipped_left_operand(gate_low, gate_grad_ref[...])
    up_out_sum[...] += flipped_left_operand(up_low, up_grad_ref[...])

    def rows_grad_step(columns):
        before = rows_ref[:, :, columns].reshape(row_count, tile)
        pair_in_sum[:, columns] += flipped_left_operand(pair_grad, before)
        rows_ref[:, :, columns] = (
            (
                flipped_right_operand(gate_grad_ref[...], gate_w[columns, :])
                + flipped_right_operand(up_grad_ref[...], up_w[columns, :])
                + matrix_product(pair_grad, pair_in[:, columns])
            )
            .astype(BF16)
            .reshape(sources, slots, tile)
        )

    tiles(width, tile, rows_grad_step)


def expert_sums(tables):
    gate_w, _up_w, _down_w, pair_in, gate_out, _up_out, down_in, down_out = tables
    return [
        jax.ShapeDtypeStruct(table.shape, F32)
        for table in (pair_in, gate_out, gate_out, down_in, down_out)
    ]


def expert_scratch(row_count, hidden, width):
    return [
        pltpu.VMEM((row_count, hidden), F32),
        pltpu.VMEM((row_count, hidden), F32),
        pltpu.VMEM((row_count, hidden), BF16),
        pltpu.VMEM((row_count, width), BF16),
        pltpu.VMEM((row_count, hidden), BF16),
        pltpu.VMEM((row_count, hidden), BF16),
    ]


def experts_body(_block_ref, rows_in, up_in, rank_ref, weight_ref, mask_ref, *rest):
    tables, sums_before, rest = rest[:8], rest[8:13], rest[13:]
    y_ref, rows_grad_ref, dots_ref = rest[:3]
    sums, rest = rest[3:8], rest[8:]
    for total, before in zip(sums, sums_before):
        total[...] = before[...]
    rows_grad_ref[...] = rows_in[...]
    y_ref[...] = up_in[...]

    def keep_dots(source, dots):
        dots_ref[source : source + 1, :] = dots

    expert_math(
        256,
        rows_grad_ref,
        y_ref,
        rank_ref[0],
        weight_ref[0],
        keep_dots,
        lambda: None,
        mask_ref,
        tables,
        sums,
        rest,
    )


def experts(block, rows, up_rows, ranks, weights, mask, tables, sums_before):
    sources, slots, width = rows.shape
    hidden = tables[0].shape[1]
    tokens = ranks.shape[2]
    token_spec = pl.BlockSpec((1, sources, tokens), lambda _, at: (at[0], 0, 0))

    def resident(array):
        return pl.BlockSpec(
            array.shape, lambda *_: (0,) * len(array.shape), pipeline_mode=pl.Buffered(1)
        )

    sums = expert_sums(tables)
    outs = [
        jax.ShapeDtypeStruct(rows.shape, BF16),
        jax.ShapeDtypeStruct(rows.shape, BF16),
        jax.ShapeDtypeStruct((sources, tokens), F32),
    ] + sums
    operands = [rows, up_rows, ranks, weights, mask, *tables, *sums_before]
    specs = (
        [resident(rows), resident(up_rows), token_spec, token_spec, resident(mask)]
        + [resident(table) for table in tables]
        + [resident(each) for each in sums_before]
    )
    return pl.pallas_call(
        experts_body,
        grid_spec=pltpu.PrefetchScalarGridSpec(
            num_scalar_prefetch=1,
            grid=(1,),
            in_specs=specs,
            out_specs=[resident(out) for out in outs],
            scratch_shapes=expert_scratch(sources * slots, hidden, width),
        ),
        out_shape=outs,
        input_output_aliases={
            1 + len(operands) - len(sums) + at: 3 + at for at in range(len(sums))
        },
        compiler_params=params(63),
        name="experts",
    )(block, *operands)


def moe_body(
    plane,
    line,
    own_ref,
    up_hbm,
    plane_rank_ref,
    rank_ref,
    weight_ref,
    mask_ref,
    *rest,
):
    tables_hbm, rest = rest[:8], rest[8:]
    total_ref, dots_ref, y_hbm, back_hbm = rest[:4]
    sums, rest = rest[4:9], rest[9:]
    tables, rest = rest[:8], rest[8:]
    (
        blocks,
        partials,
        partials_in,
        sent_slots,
        rows,
        up_rows,
        back_rows,
        choice,
        dots,
        dots_back,
        dots_pass,
        dots_in,
    ) = rest[:12]
    scratch, rest = rest[12:18], rest[18:]
    (
        table_sem,
        up_sem,
        y_sem,
        back_sem,
        own_sem,
        relay_right_send,
        relay_right_recv,
        relay_left_send,
        relay_left_recv,
        row_send,
        row_recv,
        back_send,
        back_recv,
        partial_send,
        partial_recv,
        dots_send,
        dots_recv,
        dots_in_send,
        dots_in_recv,
    ) = rest
    width = own_ref.shape[1]
    slots = rows.shape[2]
    tile = 256
    me, at_line = lax.axis_index("fsdp"), lax.axis_index("tensor")

    greet_line_and_plane(line, plane)

    orders = [sorted(range(line), key=lambda block: abs(block - at)) for at in range(line)]

    def place_of(step):
        result = 0
        for at in range(line):
            for k in range(line):
                result = jnp.where((at_line == at) & (step == k), orders[at][k], result)
        return result

    advance, finish_relay = line_relay(
        at_line,
        line,
        [own_ref],
        [blocks],
        (4,),
        (relay_right_send, relay_right_recv, relay_left_send, relay_left_recv),
    )

    def row_copy(step, block, d):
        target = lax.rem(me + d, plane)
        return pltpu.make_async_remote_copy(
            src_ref=sent_slots.at[lax.rem(step, 2), target],
            dst_ref=rows.at[block, me],
            send_sem=row_send.at[block, d],
            recv_sem=row_recv.at[block, d],
            device_id={"fsdp": target},
        )

    def own_rows(step, block):
        return pltpu.make_async_copy(
            sent_slots.at[lax.rem(step, 2), me], rows.at[block, me], own_sem.at[0]
        )

    def back_copy(block, d):
        target = lax.rem(me + d, plane)
        return pltpu.make_async_remote_copy(
            src_ref=rows.at[block, target],
            dst_ref=back_hbm.at[block, me],
            send_sem=back_send.at[block, d],
            recv_sem=back_recv.at[block, d],
            device_id={"fsdp": target},
        )

    def own_back(block):
        return pltpu.make_async_copy(
            rows.at[block, me], back_hbm.at[block, me], own_sem.at[1]
        )

    def dots_copy(block, d):
        target = lax.rem(me + d, plane)
        return pltpu.make_async_remote_copy(
            src_ref=dots.at[block, target],
            dst_ref=dots_back.at[block, me],
            send_sem=dots_send.at[block, d],
            recv_sem=dots_recv.at[block, d],
            device_id={"fsdp": target},
        )

    def dots_in_copy(block, sender):
        return pltpu.make_async_remote_copy(
            src_ref=dots_pass.at[block],
            dst_ref=dots_in.at[sender],
            send_sem=dots_in_send.at[block],
            recv_sem=dots_in_recv.at[sender],
            device_id={"tensor": block},
        )

    def partial_copy(block, sender):
        return pltpu.make_async_remote_copy(
            src_ref=partials.at[block],
            dst_ref=partials_in.at[sender],
            send_sem=partial_send.at[block],
            recv_sem=partial_recv.at[sender],
            device_id={"tensor": block},
        )

    def up_copy(block):
        return pltpu.make_async_copy(up_hbm.at[:, block], up_rows, up_sem)

    def y_copy(block):
        return pltpu.make_async_copy(up_rows, y_hbm.at[:, block], y_sem)

    advance(0, (0,))
    first_block = pltpu.make_async_copy(own_ref, blocks.at[at_line], own_sem.at[2])
    first_block.start()
    up_copy(at_line).start()
    table_copies = [
        pltpu.make_async_copy(source, target, table_sem.at[at])
        for at, (source, target) in enumerate(zip(tables_hbm, tables))
    ]
    for each in table_copies:
        each.start()
    first_block.wait()

    def dispatch(step):
        block = place_of(step)
        if step > 1:
            before = place_of(step - 2)

            @pl.loop(1, plane)
            def _(d):
                row_copy(step - 2, before, d).wait_send()

        choice[...] = slot_choice(plane_rank_ref[block], slots)

        def slot_step(columns):
            sent_slots[step % 2, :, :, columns] = (
                matrix_product(choice[...], blocks[block, :, columns])
                .astype(BF16)
                .reshape(plane, slots, 2 * tile)
            )

        tiles(width, 2 * tile, slot_step)

        @pl.loop(1, plane)
        def _(d):
            row_copy(step, block, d).start()

        own = own_rows(step, block)
        own.start()
        own.wait()

    dispatch(0)
    for total in sums:
        total[...] = jnp.zeros_like(total)
    advance(1, (0,))
    dispatch(1)
    for each in table_copies:
        each.wait()

    def send_back(block):
        @pl.loop(1, plane)
        def _(d):
            dots_copy(block, d).start()
            back_copy(block, d).start()

        own = own_back(block)
        own.start()
        dots_back[block, me] = dots[block, me]
        own.wait()

    @pl.loop(0, line + 2)
    def _(step):
        @pl.when(step < line)
        def _():
            block = place_of(step)

            @pl.loop(1, plane)
            def _(d):
                row_copy(step, block, d).wait_recv()

            up_copy(block).wait()

            def keep_dots(source, values):
                dots[block, source] = jnp.broadcast_to(values, (8, values.shape[1]))

            expert_math(
                tile,
                rows.at[block],
                up_rows,
                rank_ref[block],
                weight_ref[block],
                keep_dots,
                lambda: y_copy(block).start(),
                mask_ref,
                tables,
                sums,
                scratch,
            )

            @pl.when(step > 0)
            def _():
                send_back(block)

            @pl.when(step == line - 1)
            def _():
                send_back(at_line)

            y_copy(block).wait()

            @pl.when(step + 1 < line)
            def _():
                up_copy(place_of(step + 1)).start()

            for late in range(2, line):

                @pl.when(step == late - 2)
                def _():
                    advance(late, (0,))
                    dispatch(late)

        @pl.when(step >= 2)
        def _():
            block = place_of(lax.rem(step - 1, line))

            @pl.loop(1, plane)
            def _(d):
                dots_copy(block, d).wait_recv()
                back_copy(block, d).wait_recv()

            dots_pass[block] = dots_back[block, :, 0, :]
            load = pltpu.make_async_copy(back_hbm.at[block], back_rows, back_sem)
            load.start()
            choice[...] = slot_choice(plane_rank_ref[block], slots)
            load.wait()

            def combined(columns):
                return flipped_left_operand(
                    choice[...], back_rows[:, :, columns].reshape(plane * slots, 2 * tile)
                )

            @pl.when(step == line + 1)
            def _():
                def keep(columns):
                    total_ref[:, columns] = combined(columns)

                tiles(width, 2 * tile, keep)
                dots_ref[at_line] = dots_pass[at_line]

            @pl.when(step < line + 1)
            def _():
                dots_in_copy(block, at_line).start()

                def pass_on(columns):
                    partials[block, :, columns] = combined(columns).astype(BF16)

                tiles(width, 2 * tile, pass_on)
                partial_copy(block, at_line).start()

    @pl.loop(1, line)
    def _(step):
        sender = place_of(step)
        dots_in_copy(sender, sender).wait_recv()
        dots_ref[sender] = dots_in[sender]
        partial_copy(sender, sender).wait_recv()
        total_ref[...] += partials_in[sender].astype(F32)

    @pl.loop(1, line)
    def _(step):
        block = place_of(step)
        partial_copy(block, at_line).wait_send()
        dots_in_copy(block, at_line).wait_send()

    finish_relay((0,), range(line - 1))
    for step in (line - 2, line - 1):

        @pl.loop(1, plane)
        def _(d):
            row_copy(step, place_of(step), d).wait_send()

    @pl.loop(0, line)
    def _(block):
        @pl.loop(1, plane)
        def _(d):
            back_copy(block, d).wait_send()
            dots_copy(block, d).wait_send()


def moe_layer(own, up_rows, plane_ranks, ranks, weights, mask, tables, identity):
    line, plane, tokens = plane_ranks.shape
    slots, width = up_rows.shape[2:]
    hidden = tables[0].shape[1]
    sums = expert_sums(tables)
    anywhere = pl.BlockSpec(memory_space=pl.ANY)
    local = pl.BlockSpec(memory_space=pltpu.VMEM)
    grouped = (plane, slots, width)
    dma = pltpu.SemaphoreType.DMA
    return pl.pallas_call(
        functools.partial(moe_body, plane, line),
        out_shape=[
            jax.ShapeDtypeStruct((tokens, width), F32),
            jax.ShapeDtypeStruct((line, plane, tokens), F32),
            jax.ShapeDtypeStruct((plane, line, slots, width), BF16),
            jax.ShapeDtypeStruct((line,) + grouped, BF16),
        ]
        + sums,
        in_specs=[anywhere, anywhere, local, local, local, local] + [anywhere] * len(tables),
        out_specs=[local, local, anywhere, anywhere] + [local] * len(sums),
        scratch_shapes=[pltpu.VMEM(table.shape, table.dtype) for table in tables]
        + [
            pltpu.VMEM((line, tokens, width), BF16),
            pltpu.VMEM((line, tokens, width), BF16),
            pltpu.VMEM((line, tokens, width), BF16),
            pltpu.VMEM((2,) + grouped, BF16),
            pltpu.VMEM((line,) + grouped, BF16),
            pltpu.VMEM(grouped, BF16),
            pltpu.VMEM(grouped, BF16),
            pltpu.VMEM((plane * slots, tokens), BF16),
            pltpu.VMEM((line, plane, 8, tokens), F32),
            pltpu.VMEM((line, plane, 8, tokens), F32),
            pltpu.VMEM((line, plane, tokens), F32),
            pltpu.VMEM((line, plane, tokens), F32),
        ]
        + expert_scratch(plane * slots, hidden, width)
        + [dma((len(tables),)), dma, dma, dma, dma((3,))]
        + [dma((line - 1, 4))] * 4
        + [dma((line, plane))] * 4
        + [dma((line,))] * 2
        + [dma((line, plane))] * 2
        + [dma((line,))] * 2,
        compiler_params=pltpu.CompilerParams(
            collective_id=identity, has_side_effects=True, vmem_limit_bytes=63 * MEBI
        ),
        name="moe_layer",
    )(own, up_rows, plane_ranks, ranks, weights, mask, *tables)


def greet_line(me, count):
    barrier = pltpu.get_barrier_semaphore()

    @pl.when(me > 0)
    def _():
        pl.semaphore_signal(barrier, inc=1, device_id={"tensor": me - 1})

    @pl.when(me < count - 1)
    def _():
        pl.semaphore_signal(barrier, inc=1, device_id={"tensor": me + 1})

    @pl.when((me > 0) & (me < count - 1))
    def _():
        pl.semaphore_wait(barrier, 2)

    @pl.when((me == 0) | (me == count - 1))
    def _():
        pl.semaphore_wait(barrier, 1)


def gather_line_body(count, chunks, *refs):
    arrays = len(chunks)
    ins, outs = refs[:arrays], refs[arrays : 2 * arrays]
    semaphores, own_sem = refs[2 * arrays : -1], refs[-1]
    me = lax.axis_index("tensor")
    advance, finish = line_relay(me, count, ins, outs, chunks, semaphores)
    greet_line(me, count)
    own = [
        pltpu.make_async_copy(ins[at], outs[at].at[me], own_sem.at[at]) for at in range(arrays)
    ]
    everything = tuple(range(arrays))
    advance(0, everything)
    for each in own:
        each.start()
    for hop in range(1, count):
        advance(hop, everything)
    for each in own:
        each.wait()
    finish(everything, range(count - 1))


def gather_line(arrays, chunks, identity):
    count = lax.axis_size("tensor")
    total = sum(chunks)
    anywhere = pl.BlockSpec(memory_space=pl.ANY)
    return pl.pallas_call(
        functools.partial(gather_line_body, count, chunks),
        out_shape=[jax.ShapeDtypeStruct((count,) + a.shape, a.dtype) for a in arrays],
        in_specs=[anywhere] * len(arrays),
        out_specs=[anywhere] * len(arrays),
        scratch_shapes=[pltpu.SemaphoreType.DMA((count - 1, total))] * 4
        + [pltpu.SemaphoreType.DMA((len(arrays),))],
        compiler_params=pltpu.CompilerParams(collective_id=identity, has_side_effects=True),
        name="gather_line",
    )(*arrays)


def sum_line_body(count, chunks, part_ref, out_ref, left_buf, right_buf, *semaphores):
    me = lax.axis_index("tensor")
    advance, finish = line_sum(
        me, count, chunks, part_ref, out_ref, left_buf, right_buf, semaphores
    )
    greet_line(me, count)
    for far in range(count - 1, 0, -1):
        advance(far)
    finish()


def sum_line(part, chunks, identity):
    count, rows, width = part.shape
    semaphores = pltpu.SemaphoreType.DMA((count - 1, chunks))
    return pl.pallas_call(
        functools.partial(sum_line_body, count, chunks),
        out_shape=jax.ShapeDtypeStruct((rows, width), F32),
        in_specs=[pl.BlockSpec(memory_space=pltpu.VMEM)],
        out_specs=pl.BlockSpec(memory_space=pltpu.VMEM),
        scratch_shapes=[
            pltpu.VMEM((count - 1, rows, width), BF16),
            pltpu.VMEM((count - 1, rows, width), BF16),
        ]
        + [semaphores] * 4,
        compiler_params=pltpu.CompilerParams(
            collective_id=identity, has_side_effects=True, vmem_limit_bytes=32 * MEBI
        ),
        name="sum_line",
    )(part)


def front_body(
    plane,
    line,
    scale,
    places,
    tokens_hbm,
    cotangent_hbm,
    routes_hbm,
    weights_hbm,
    gain_ref,
    first_ref,
    q_second_ref,
    k_second_ref,
    v_second_ref,
    q_gain_ref,
    k_gain_ref,
    cos_ref,
    sin_ref,
    seg_column_ref,
    seg_row_ref,
    out_first_ref,
    out_second_ref,
    before_ref,
    total_ref,
    ranks_ref,
    low_ref,
    out_low_ref,
    linear_hbm,
    heads_hbm,
    normed_hbm,
    gathered_hbm,
    up_hbm,
    rows,
    upstream,
    routes,
    weights,
    linear,
    heads,
    keys,
    values,
    part,
    left_buf,
    right_buf,
    sent_slots,
    choice,
    own_sem,
    save_sem,
    relay_right_send,
    relay_right_recv,
    relay_left_send,
    relay_left_recv,
    weight_send,
    weight_recv,
    pass_send,
    pass_recv,
    sum_right_send,
    sum_right_recv,
    sum_left_send,
    sum_left_recv,
    slot_send,
    slot_recv,
):
    me, at_line = lax.axis_index("fsdp"), lax.axis_index("tensor")
    rank = q_second_ref.shape[0]
    head_dim = q_gain_ref.shape[1]
    tokens, width = tokens_hbm.shape
    slots = sent_slots.shape[2]
    tile = 256
    query_columns = q_second_ref.shape[1]
    linear_columns = linear.shape[1]
    out_start = places[1]

    greet_line_and_plane(line, plane)

    beside = me + 1 - 2 * lax.rem(me, 2)

    def weight_copy(k):
        target = lax.rem(me + 2 * k, plane)
        return pltpu.make_async_remote_copy(
            src_ref=weights_hbm,
            dst_ref=weights.at[me],
            send_sem=weight_send.at[k],
            recv_sem=weight_recv.at[k],
            device_id={"fsdp": target},
        )

    def weight_pass(k):
        origin = lax.rem(me + plane - 2 * k, plane)
        return pltpu.make_async_remote_copy(
            src_ref=weights_hbm if k == 0 else weights.at[origin],
            dst_ref=weights.at[origin],
            send_sem=pass_send.at[k],
            recv_sem=pass_recv.at[k],
            device_id={"fsdp": beside},
        )

    peers = plane // 2
    for k in range(1, peers):
        weight_copy(k).start()
    weight_pass(0).start()
    locals_in = [
        pltpu.make_async_copy(source, target, own_sem.at[at])
        for at, (source, target) in enumerate(
            [
                (tokens_hbm, rows.at[at_line]),
                (routes_hbm, routes.at[at_line]),
                (cotangent_hbm, upstream.at[at_line]),
                (weights_hbm, weights.at[me]),
            ]
        )
    ]
    advance, finish_relay = line_relay(
        at_line,
        line,
        [tokens_hbm, routes_hbm, cotangent_hbm],
        [rows, routes, upstream],
        (4, 1, 4),
        (relay_right_send, relay_right_recv, relay_left_send, relay_left_recv),
    )
    advance(0, (0, 1))
    for each in locals_in:
        each.start()
    advance(1, (0, 1))
    advance(2, (0, 1))
    advance(0, (2,))
    for k in range(1, peers):
        weight_copy(k).wait_recv()
        weight_pass(k).start()
    advance(3, (0, 1))
    for each in locals_in:
        each.wait()

    for block in range(line):
        named = [
            jnp.max(
                (routes[block] == expert * line + at_line).astype(F32), axis=0, keepdims=True
            )
            for expert in range(plane)
        ]
        mask = jnp.concatenate(named, axis=0)
        counts = matrix_product(mask.astype(BF16), before_ref[...])
        ranks_ref[block] = jnp.where(mask > 0.0, counts, -1.0)

    def slot_copy(block, d):
        target = lax.rem(me + d, plane)
        return pltpu.make_async_remote_copy(
            src_ref=sent_slots.at[block, target],
            dst_ref=up_hbm.at[me, block],
            send_sem=slot_send.at[block, d],
            recv_sem=slot_recv.at[block, d],
            device_id={"fsdp": target},
        )

    def own_slots(block):
        return pltpu.make_async_copy(
            sent_slots.at[block, me], up_hbm.at[me, block], save_sem.at[4 + block]
        )

    def dispatch(block):
        choice[...] = slot_choice(ranks_ref[block], slots)

        def slot_step(columns):
            sent_slots[block, :, :, columns] = (
                matrix_product(choice[...], upstream[block, :, columns])
                .astype(BF16)
                .reshape(plane, slots, 2 * tile)
            )

        tiles(width, 2 * tile, slot_step)

        @pl.loop(1, plane)
        def _(d):
            slot_copy(block, d).start()

    def dispatch_at(distance):
        if distance == 0:
            dispatch(at_line)
            return

        @pl.when(at_line - distance >= 0)
        def _():
            dispatch(at_line - distance)

        @pl.when(at_line + distance < line)
        def _():
            dispatch(at_line + distance)

    dispatch_at(0)

    finish_relay((0,), range(1, line - 1))

    @pl.loop(0, line * tokens // 128)
    def _(j):
        block, at = j // (tokens // 128), pl.ds((j % (tokens // 128)) * 128, 128)
        wide = rows[block, at, :].astype(F32)
        rows[block, at, :] = norm_forward(wide, gain_ref[...])[0].astype(BF16)

    for k in range(peers):
        weight_pass(k).wait_recv()
    saves = [
        pltpu.make_async_copy(rows, normed_hbm, save_sem.at[0]),
        pltpu.make_async_copy(weights, gathered_hbm, save_sem.at[1]),
        pltpu.make_async_copy(linear, linear_hbm, save_sem.at[2]),
        pltpu.make_async_copy(heads, heads_hbm, save_sem.at[3]),
    ]
    saves[0].start()
    saves[1].start()

    @pl.loop(0, line)
    def _(block):
        at = pl.ds(pl.multiple_of(block * tokens, tokens), tokens)
        low_ref[at, :] = flipped_right_operand(rows[block], first_ref[...]).astype(BF16)

        def project(columns):
            linear[at, columns] = matrix_product(
                rows[block], weights[:, :, columns].reshape(width, tile)
            )

        tiles(linear_columns, tile, project)

    saves[2].start()
    advance(1, (2,))
    dispatch_at(1)

    cosine, sine = cos_ref[...], sin_ref[...]
    keys[...] = head_values(
        linear[:, query_columns : query_columns + head_dim],
        low_ref[:, rank : 2 * rank],
        k_second_ref[...],
        k_gain_ref[...],
        cosine,
        sine,
    )[2]
    values[...] = (
        linear[:, query_columns + head_dim : query_columns + 2 * head_dim]
        + matrix_product(low_ref[:, 2 * rank : 3 * rank], v_second_ref[...])
    ).astype(BF16)

    @pl.loop(0, query_columns // head_dim)
    def _(head):
        columns = pl.ds(pl.multiple_of(head * head_dim, head_dim), head_dim)
        query = head_values(
            linear[:, columns],
            low_ref[:, :rank],
            q_second_ref[:, columns],
            q_gain_ref[...],
            cos_ref[...],
            sin_ref[...],
        )[2]
        seg_column, seg_row = seg_column_ref[...], seg_row_ref[...]
        for block in range(query.shape[0] // WINDOW):
            start, span = block_bounds(block)
            scores = (
                flipped_right_operand(
                    query[block * WINDOW : (block + 1) * WINDOW], keys[pl.ds(start, span)]
                )
                * scale
            )
            scores = jnp.where(
                allowed_keys(block, start, span, seg_column, seg_row), scores, -1e30
            )
            expo = jnp.exp(scores - jnp.max(scores, axis=-1, keepdims=True))
            probs = (expo / jnp.sum(expo, axis=-1, keepdims=True)).astype(BF16)
            heads[pl.ds(block * WINDOW, WINDOW), columns] = matrix_product(
                probs, values[pl.ds(start, span)]
            ).astype(BF16)

    saves[3].start()
    advance(2, (2,))
    dispatch_at(2)

    out_low_ref[...] = flipped_right_operand(heads[...], out_first_ref[...]).astype(BF16)

    @pl.loop(0, line)
    def _(block):
        at = pl.ds(pl.multiple_of(block * tokens, tokens), tokens)

        @pl.loop(0, plane)
        def _(shard):
            wide = width // plane
            columns = pl.ds(pl.multiple_of(shard * wide, wide), wide)
            part[block, :, columns] = (
                flipped_right_operand(heads[at, :], weights[shard, :, out_start:])
                + matrix_product(out_low_ref[at, :], out_second_ref[:, columns])
            ).astype(BF16)

    advance_sum, finish_sum = line_sum(
        at_line,
        line,
        4,
        part,
        total_ref,
        left_buf,
        right_buf,
        (sum_right_send, sum_right_recv, sum_left_send, sum_left_recv),
    )
    for far in range(line - 1, 0, -1):
        advance_sum(far)
        if far == 2:
            advance(3, (2,))
            dispatch_at(3)
    finish_sum()

    for block in range(line):
        own_slots(block).start()
    for each in saves:
        each.wait()
    finish_relay((0,), (0,))
    finish_relay((1, 2), range(line - 1))
    for k in range(1, peers):
        weight_copy(k).wait_send()
    for k in range(peers):
        weight_pass(k).wait_send()

    @pl.loop(0, line)
    def _(block):
        @pl.loop(1, plane)
        def _(d):
            slot_copy(block, d).wait_recv()
            slot_copy(block, d).wait_send()

    for block in range(line):
        own_slots(block).wait()


def front(
    tokens,
    cotangent,
    routes,
    packed,
    gain,
    first,
    q_second,
    k_second,
    v_second,
    q_gain,
    k_gain,
    tables,
    seg_column,
    seg_row,
    out_first,
    out_second,
    scale,
    slots,
    places,
    identity,
):
    line, plane = lax.axis_size("tensor"), lax.axis_size("fsdp")
    count, width = tokens.shape
    all_rows = line * count
    rank, query_columns = q_second.shape
    head_dim = q_gain.shape[1]
    linear_columns = query_columns + 2 * head_dim
    order = jnp.arange(count, dtype=jnp.int32)
    before = (order[:, None] < order[None, :]).astype(BF16)
    anywhere = pl.BlockSpec(memory_space=pl.ANY)
    local = pl.BlockSpec(memory_space=pltpu.VMEM)
    dma = pltpu.SemaphoreType.DMA
    up_shape = (plane, line, slots, width)
    operands = [
        gain,
        first,
        q_second,
        k_second,
        v_second,
        q_gain,
        k_gain,
        *tables,
        seg_column,
        seg_row,
        out_first,
        out_second,
        before,
    ]
    return pl.pallas_call(
        functools.partial(front_body, plane, line, scale, places),
        out_shape=[
            jax.ShapeDtypeStruct((count, width), F32),
            jax.ShapeDtypeStruct((line, plane, count), F32),
            jax.ShapeDtypeStruct((all_rows, 3 * rank), BF16),
            jax.ShapeDtypeStruct((all_rows, rank), BF16),
            jax.ShapeDtypeStruct((all_rows, linear_columns), F32),
            jax.ShapeDtypeStruct((all_rows, query_columns), BF16),
            jax.ShapeDtypeStruct((line, count, width), BF16),
            jax.ShapeDtypeStruct((plane,) + packed.shape, BF16),
            jax.ShapeDtypeStruct(up_shape, BF16),
        ],
        in_specs=[anywhere] * 4 + [local] * len(operands),
        out_specs=[local] * 4 + [anywhere] * 5,
        scratch_shapes=[
            pltpu.VMEM((line, count, width), BF16),
            pltpu.VMEM((line, count, width), BF16),
            pltpu.VMEM((line,) + routes.shape, jnp.int32),
            pltpu.VMEM((plane,) + packed.shape, BF16),
            pltpu.VMEM((all_rows, linear_columns), F32),
            pltpu.VMEM((all_rows, query_columns), BF16),
            pltpu.VMEM((all_rows, head_dim), BF16),
            pltpu.VMEM((all_rows, head_dim), BF16),
            pltpu.VMEM((line, count, width), BF16),
            pltpu.VMEM((line - 1, count, width), BF16),
            pltpu.VMEM((line - 1, count, width), BF16),
            pltpu.VMEM((line, plane, slots, width), BF16),
            pltpu.VMEM((plane * slots, count), BF16),
            dma((4,)),
            dma((4 + line,)),
        ]
        + [dma((line - 1, 9))] * 4
        + [dma((plane // 2,))] * 4
        + [dma((line - 1, 4))] * 4
        + [dma((line, plane))] * 2,
        compiler_params=pltpu.CompilerParams(
            collective_id=identity, has_side_effects=True, vmem_limit_bytes=63 * MEBI
        ),
        name="front",
    )(tokens, cotangent, routes, packed, *operands)


def back_body(
    plane,
    line,
    scale,
    places,
    moe_total_ref,
    dots_ref,
    gates_ref,
    residual_ref,
    cotangent_ref,
    moe_gain_ref,
    router_ref,
    router_first_ref,
    router_second_ref,
    router_low_ref,
    moe_rows_ref,
    ranks_ref,
    low_ref,
    out_low_ref,
    first_out_ref,
    second_out_ref,
    q_second_ref,
    k_second_ref,
    v_second_ref,
    q_gain_ref,
    k_gain_ref,
    cos_ref,
    sin_ref,
    seg_column_ref,
    seg_row_ref,
    linear_hbm,
    heads_hbm,
    normed_hbm,
    gathered_hbm,
    y_hbm,
    output_ref,
    residual_grad_ref,
    share_ref,
    linear_grad_ref,
    rows_out_ref,
    heads_out_ref,
    narrow_out_ref,
    router_out_ref,
    y_in_hbm,
    branch_own,
    branch,
    out_weights,
    linear,
    heads,
    normed,
    upstream,
    out_low_grad,
    keys,
    values,
    key_sum,
    value_sum,
    query_sum,
    share_sum,
    second_sum,
    y_rows,
    partials,
    left_buf,
    right_buf,
    result,
    choice,
    load_sem,
    y_sem,
    relay_right_send,
    relay_right_recv,
    relay_left_send,
    relay_left_recv,
    y_send,
    y_recv,
    sum_right_send,
    sum_right_recv,
    sum_left_send,
    sum_left_recv,
):
    me, at_line = lax.axis_index("fsdp"), lax.axis_index("tensor")
    tokens, width = residual_ref.shape
    rank, query_columns = q_second_ref.shape
    head_dim = q_gain_ref.shape[1]
    slots = y_rows.shape[1]
    tile = 256

    greet_line_and_plane(line, plane)

    orders = [sorted(range(line), key=lambda block: abs(block - at)) for at in range(line)]

    def place_of(step):
        result = 0
        for at in range(line):
            result = jnp.where(at_line == at, orders[at][step], result)
        return result

    def y_copy(block, d):
        target = lax.rem(me + d, plane)
        return pltpu.make_async_remote_copy(
            src_ref=y_hbm.at[target, block],
            dst_ref=y_in_hbm.at[block, me],
            send_sem=y_send.at[block, d],
            recv_sem=y_recv.at[block, d],
            device_id={"fsdp": target},
        )

    def own_y(block):
        return pltpu.make_async_copy(
            y_hbm.at[me, block], y_in_hbm.at[block, me], y_sem.at[block]
        )

    def send_y(step):
        block = place_of(step)

        @pl.loop(1, plane)
        def _(d):
            y_copy(block, d).start()

        own_y(block).start()

    send_y(line - 1)
    send_y(line - 2)
    advance_sum, finish_sum = line_sum(
        at_line,
        line,
        4,
        partials,
        result,
        left_buf,
        right_buf,
        (sum_right_send, sum_right_recv, sum_left_send, sum_left_recv),
    )
    loads = [
        pltpu.make_async_copy(source, target, load_sem.at[at])
        for at, (source, target) in enumerate(
            [
                (gathered_hbm.at[:, :, pl.ds(places[1], query_columns)], out_weights),
                (linear_hbm, linear),
                (heads_hbm, heads),
                (normed_hbm, normed),
            ]
        )
    ]
    for each in loads:
        each.start()

    def combine(step):
        block = place_of(step)

        @pl.loop(1, plane)
        def _(d):
            y_copy(block, d).wait_recv()

        own_y(block).wait()
        if step > 1:
            send_y(step - 2)
        load = pltpu.make_async_copy(y_in_hbm.at[block], y_rows, y_sem.at[line])
        load.start()
        choice[...] = slot_choice(ranks_ref[block], slots)
        load.wait()

        def combined(columns):
            total = flipped_left_operand(
                choice[...], y_rows[:, :, columns].reshape(plane * slots, 2 * tile)
            )
            partials[block, :, columns] = total.astype(BF16)

        tiles(width, 2 * tile, combined)
        if step > 0:
            advance_sum(step)

    gates = gates_ref[...]
    dots = dots_ref[...]
    logit_grad = (gates * (dots - jnp.sum(gates * dots, axis=0, keepdims=True))).astype(BF16)
    router_low_grad = matrix_product(router_second_ref[...], logit_grad).astype(BF16)
    rows_out_ref[4 * rank :, :] = matrix_product(router_low_grad, moe_rows_ref[...]).astype(BF16)
    router_out_ref[...] = flipped_right_operand(router_low_ref[...], logit_grad)
    half = tokens // 2
    for part in range(2):
        rows = pl.ds(part * half, half)
        columns = slice(part * half, (part + 1) * half)
        moe_grad = (
            moe_total_ref[rows, :]
            + flipped_left_operand(logit_grad[:, columns], router_ref[...])
            + flipped_left_operand(router_low_grad[:, columns], router_first_ref[...])
        )
        residual = residual_ref[rows, :]
        factor = lax.rsqrt(
            jnp.mean(residual * residual, axis=-1, keepdims=True) + NORM_EPSILON
        )
        residual_grad = cotangent_ref[rows, :].astype(F32) + norm_backward(
            residual, factor, moe_gain_ref[...], moe_grad
        )
        residual_grad_ref[rows, :] = residual_grad
        branch_own[rows, :] = residual_grad.astype(BF16)
    branch[at_line] = branch_own[...]

    advance, finish_relay = line_relay(
        at_line,
        line,
        [branch_own],
        [branch],
        (4,),
        (relay_right_send, relay_right_recv, relay_left_send, relay_left_recv),
    )
    advance(0, (0,))
    second_sum[...] = jnp.zeros_like(second_sum)
    loads[0].wait()

    def head_gradients(block):
        at = pl.ds(pl.multiple_of(block * tokens, tokens), tokens)
        low_grad = flipped_right_operand(branch[block], second_out_ref[...]).astype(BF16)
        out_low_grad[at, :] = low_grad
        second_sum[...] += flipped_left_operand(out_low_ref[at, :], branch[block])

        def project(columns):
            upstream[at, columns] = (
                matrix_product(branch[block], out_weights[:, :, columns].reshape(width, tile))
                + matrix_product(low_grad, first_out_ref[:, columns])
            ).astype(BF16)

        tiles(query_columns, tile, project)

    head_gradients(at_line)
    for each in loads[1:]:
        each.wait()
    cosine, sine = cos_ref[...], sin_ref[...]
    key_columns = slice(query_columns, query_columns + head_dim)
    value_columns = slice(query_columns + head_dim, query_columns + 2 * head_dim)
    keys[...] = head_values(
        linear[:, key_columns],
        low_ref[:, rank : 2 * rank],
        k_second_ref[...],
        k_gain_ref[...],
        cosine,
        sine,
    )[2]
    values[...] = (
        linear[:, value_columns]
        + matrix_product(low_ref[:, 2 * rank : 3 * rank], v_second_ref[...])
    ).astype(BF16)
    key_sum[...] = jnp.zeros_like(key_sum)
    value_sum[...] = jnp.zeros_like(value_sum)
    share_sum[...] = jnp.zeros_like(share_sum)
    for hop in range(1, line):
        advance(hop, (0,))

        @pl.when(at_line - hop >= 0)
        def _():
            head_gradients(at_line - hop)

        @pl.when(at_line + hop < line)
        def _():
            head_gradients(at_line + hop)

        if hop < line - 1:
            combine(line - hop)
    rows_out_ref[3 * rank : 4 * rank, :] = second_sum[...].astype(BF16)

    head_count = query_columns // head_dim

    @pl.loop(0, head_count)
    def _(head):
        columns = pl.ds(pl.multiple_of(head * head_dim, head_dim), head_dim)
        low_q = low_ref[:, :rank]
        lines, factor, query = head_values(
            linear[:, columns],
            low_q,
            q_second_ref[:, columns],
            q_gain_ref[...],
            cos_ref[...],
            sin_ref[...],
        )
        heads_out_ref[rank:, columns] = flipped_left_operand(
            out_low_grad[...], heads[:, columns]
        ).astype(BF16)
        seg_column, seg_row = seg_column_ref[...], seg_row_ref[...]
        for block in range(query.shape[0] // WINDOW):
            start, span = block_bounds(block)
            at, near = pl.ds(block * WINDOW, WINDOW), pl.ds(start, span)
            query_block = query[block * WINDOW : (block + 1) * WINDOW]
            upstream_block = upstream[at, columns]
            scores = flipped_right_operand(query_block, keys[near]) * scale
            scores = jnp.where(
                allowed_keys(block, start, span, seg_column, seg_row), scores, -1e30
            )
            expo = jnp.exp(scores - jnp.max(scores, axis=-1, keepdims=True))
            probs = expo / jnp.sum(expo, axis=-1, keepdims=True)
            prob_grad = flipped_right_operand(upstream_block, values[near])
            score_grad = (
                probs * (prob_grad - jnp.sum(probs * prob_grad, axis=-1, keepdims=True))
            ).astype(BF16)
            value_sum[near, :] += flipped_left_operand(probs.astype(BF16), upstream_block)
            key_sum[near, :] += flipped_left_operand(score_grad, query_block)
            query_sum[at, :] = matrix_product(score_grad, keys[near]) * scale
        q_grad = head_values_gradient(
            lines, factor, q_gain_ref[...], cos_ref[...], sin_ref[...], query_sum[...]
        )
        linear_grad_ref[:, columns] = q_grad
        heads_out_ref[:rank, columns] = flipped_left_operand(low_q, q_grad).astype(BF16)
        share_sum[:, :rank] += flipped_right_operand(q_grad, q_second_ref[:, columns])

        @pl.when(head == head_count // 2 - 1)
        def _():
            combine(1)

    low_k = low_ref[:, rank : 2 * rank]
    low_v = low_ref[:, 2 * rank : 3 * rank]
    key_lines, key_factor, _turned = head_values(
        linear[:, key_columns], low_k, k_second_ref[...], k_gain_ref[...], cosine, sine
    )
    k_grad = head_values_gradient(
        key_lines, key_factor, k_gain_ref[...], cosine, sine, key_sum[...] * scale
    )
    v_grad = value_sum[...].astype(BF16)
    linear_grad_ref[:, key_columns] = k_grad
    linear_grad_ref[:, value_columns] = v_grad
    narrow_out_ref[:rank, :] = flipped_left_operand(low_k, k_grad).astype(BF16)
    narrow_out_ref[rank:, :] = flipped_left_operand(low_v, v_grad).astype(BF16)
    share_sum[:, rank : 2 * rank] = flipped_right_operand(k_grad, k_second_ref[...])
    share_sum[:, 2 * rank :] = flipped_right_operand(v_grad, v_second_ref[...])
    share_ref[...] = share_sum[...].astype(BF16)

    def first_gradient(columns):
        rows_out_ref[: 3 * rank, columns] = flipped_left_operand(
            share_ref[...], normed[:, columns]
        ).astype(BF16)

    tiles(width, 2 * tile, first_gradient)
    combine(0)
    finish_sum()
    output_ref[...] = (residual_ref[...] + result[...]).astype(BF16)
    finish_relay((0,), range(line - 1))
    for block in range(line):

        @pl.loop(1, plane)
        def _(d):
            y_copy(block, d).wait_send()


def back(scale, places, slots, identity, hbm_operands, operands):
    line, plane = lax.axis_size("tensor"), lax.axis_size("fsdp")
    linear, heads, normed, gathered, _y = hbm_operands
    count, width = operands[0].shape
    all_rows, linear_columns = linear.shape
    query_columns = heads.shape[1]
    head_dim = (linear_columns - query_columns) // 2
    rank = operands[13].shape[1]
    experts_count = line * plane
    anywhere = pl.BlockSpec(memory_space=pl.ANY)
    local = pl.BlockSpec(memory_space=pltpu.VMEM)
    dma = pltpu.SemaphoreType.DMA
    single = (all_rows, head_dim)
    block = (count, width)
    return pl.pallas_call(
        functools.partial(back_body, plane, line, scale, places),
        out_shape=[
            jax.ShapeDtypeStruct(block, BF16),
            jax.ShapeDtypeStruct(block, F32),
            jax.ShapeDtypeStruct((all_rows, 3 * rank), BF16),
            jax.ShapeDtypeStruct((all_rows, linear_columns), BF16),
            jax.ShapeDtypeStruct((5 * rank, width), BF16),
            jax.ShapeDtypeStruct((2 * rank, query_columns), BF16),
            jax.ShapeDtypeStruct((2 * rank, head_dim), BF16),
            jax.ShapeDtypeStruct((rank, experts_count), F32),
            jax.ShapeDtypeStruct((line, plane, slots, width), BF16),
        ],
        in_specs=[local] * len(operands) + [anywhere] * len(hbm_operands),
        out_specs=[local] * 8 + [anywhere],
        scratch_shapes=[
            pltpu.VMEM(block, BF16),
            pltpu.VMEM((line,) + block, BF16),
            pltpu.VMEM((plane, width // plane, query_columns), BF16),
            pltpu.VMEM((all_rows, linear_columns), F32),
            pltpu.VMEM((all_rows, query_columns), BF16),
            pltpu.VMEM((all_rows, width), BF16),
            pltpu.VMEM((all_rows, query_columns), BF16),
            pltpu.VMEM((all_rows, rank), BF16),
            pltpu.VMEM(single, BF16),
            pltpu.VMEM(single, BF16),
            pltpu.VMEM(single, F32),
            pltpu.VMEM(single, F32),
            pltpu.VMEM(single, F32),
            pltpu.VMEM((all_rows, 3 * rank), F32),
            pltpu.VMEM((rank, width), F32),
            pltpu.VMEM((plane, slots, width), BF16),
            pltpu.VMEM((line,) + block, BF16),
            pltpu.VMEM((line - 1,) + block, BF16),
            pltpu.VMEM((line - 1,) + block, BF16),
            pltpu.VMEM(block, F32),
            pltpu.VMEM((plane * slots, count), BF16),
            dma((4,)),
            dma((line + 1,)),
        ]
        + [dma((line - 1, 4))] * 4
        + [dma((line, plane))] * 2
        + [dma((line - 1, 4))] * 4,
        compiler_params=pltpu.CompilerParams(
            collective_id=identity, has_side_effects=True, vmem_limit_bytes=63 * MEBI
        ),
        name="back",
    )(*operands, *hbm_operands)


def last_body(
    line,
    linear_grad_ref,
    share_ref,
    first_ref,
    residual_grad_ref,
    tokens_ref,
    gain_ref,
    gathered_hbm,
    input_grad_ref,
    weights,
    part,
    left_buf,
    right_buf,
    load_sem,
    *semaphores,
):
    at_line = lax.axis_index("tensor")
    tokens, width = tokens_ref.shape
    linear_columns = linear_grad_ref.shape[1]
    load = pltpu.make_async_copy(
        gathered_hbm.at[:, :, pl.ds(0, linear_columns)], weights, load_sem
    )
    load.start()
    greet_line(at_line, line)
    load.wait()
    shards, wide = weights.shape[:2]

    def normed_gradient(block):
        at = pl.ds(pl.multiple_of(block * tokens, tokens), tokens)

        @pl.loop(0, shards)
        def _(shard):
            columns = pl.ds(pl.multiple_of(shard * wide, wide), wide)
            part[block, :, columns] = (
                flipped_right_operand(linear_grad_ref[at, :], weights[shard])
                + matrix_product(share_ref[at, :], first_ref[:, columns])
            ).astype(BF16)

    advance, finish = line_sum(
        at_line, line, 4, part, input_grad_ref, left_buf, right_buf, semaphores
    )
    for far in range(line - 1, 0, -1):

        @pl.when(at_line + far < line)
        def _():
            normed_gradient(at_line + far)

        @pl.when(at_line - far >= 0)
        def _():
            normed_gradient(at_line - far)

        advance(far)
    normed_gradient(at_line)
    finish()
    half = tokens // 2
    for at in range(2):
        rows = pl.ds(at * half, half)
        values = tokens_ref[rows, :].astype(F32)
        factor = lax.rsqrt(jnp.mean(values * values, axis=-1, keepdims=True) + NORM_EPSILON)
        input_grad_ref[rows, :] = residual_grad_ref[rows, :] + norm_backward(
            values, factor, gain_ref[...], input_grad_ref[rows, :]
        )


def last(linear_grad, share, first, residual_grad, tokens, gain, gathered, identity):
    line = lax.axis_size("tensor")
    count, width = tokens.shape
    anywhere = pl.BlockSpec(memory_space=pl.ANY)
    local = pl.BlockSpec(memory_space=pltpu.VMEM)
    dma = pltpu.SemaphoreType.DMA
    return pl.pallas_call(
        functools.partial(last_body, line),
        out_shape=jax.ShapeDtypeStruct((count, width), F32),
        in_specs=[local] * 6 + [anywhere],
        out_specs=local,
        scratch_shapes=[
            pltpu.VMEM(gathered.shape[:2] + (linear_grad.shape[1],), BF16),
            pltpu.VMEM((line, count, width), BF16),
            pltpu.VMEM((line - 1, count, width), BF16),
            pltpu.VMEM((line - 1, count, width), BF16),
            dma,
        ]
        + [dma((line - 1, 4))] * 4,
        compiler_params=pltpu.CompilerParams(
            collective_id=identity, has_side_effects=True, vmem_limit_bytes=48 * MEBI
        ),
        name="last",
    )(linear_grad, share, first, residual_grad, tokens, gain, gathered)


def per_device(
    tokens,
    segments,
    routes,
    adapter_index,
    cotangent,
    attn_gain,
    moe_gain,
    q_gain,
    key_norm_gain,
    w_query,
    key_projection_weight,
    value_projection_weight,
    w_out,
    w_router,
    expert_gate_weight,
    expert_up_weight,
    expert_down_weight,
    query_in,
    query_out,
    key_in,
    key_second_weight,
    value_in,
    value_second_weight,
    attn_in,
    attn_out,
    router_in,
    router_out,
    gate_in,
    gate_out,
    upward_in,
    upward_out,
    downward_in,
    downward_out,
):
    tensor_count = lax.axis_size("tensor")
    fsdp_count = lax.axis_size("fsdp")
    device_count = fsdp_count * tensor_count
    tensor_pos = lax.axis_index("tensor")
    fsdp_pos = lax.axis_index("fsdp")
    zero_pos = fsdp_pos * 0
    tok_rows, model_width = tokens.shape
    seq_rows = tok_rows * tensor_count
    rank = query_in.shape[2]
    adapter_count = query_in.shape[0]
    head_dim = q_gain.shape[0]
    local_cols = query_out.shape[2]
    local_kv_cols = key_second_weight.shape[2]
    expert_count = w_router.shape[1]
    top_count = routes.shape[1]
    capacity = 5 * tok_rows * top_count // (4 * expert_count)
    slots = -(-capacity // 16) * 16
    score_scale = 1.0 / math.sqrt(head_dim)
    adapter_pick = lax.dynamic_index_in_dim(adapter_index, fsdp_pos, 0, keepdims=False)

    def select_adapter(adapter_table):
        return lax.dynamic_index_in_dim(adapter_table, adapter_pick, 0, keepdims=False)

    def transposed(adapter_table):
        return jnp.swapaxes(adapter_table, -1, -2)

    input_first = jnp.concatenate(
        [select_adapter(transposed(table)) for table in (query_in, key_in, value_in)], axis=0
    )
    q_second = select_adapter(query_out)
    k_second = select_adapter(key_second_weight)
    v_second = select_adapter(value_second_weight)
    attention_first = select_adapter(transposed(attn_in))
    attention_second = select_adapter(attn_out)
    router_first = select_adapter(transposed(router_in))
    router_second = select_adapter(router_out)
    gain_attn = attn_gain.astype(F32)
    gain_moe = moe_gain.astype(F32)
    gain_query = q_gain.astype(F32)[None, :]
    gain_key = key_norm_gain.astype(F32)[None, :]

    in_kernel = fsdp_count * slots <= 640
    linear_cols = local_cols + 2 * local_kv_cols
    router_pad = -(-expert_count // 128) * 128
    out_start = linear_cols + router_pad
    packed = jnp.concatenate(
        [
            w_query,
            key_projection_weight,
            value_projection_weight,
            jnp.pad(w_router, ((0, 0), (0, router_pad - expert_count))),
            jnp.transpose(w_out, (1, 0)),
        ],
        axis=1,
    )
    tables = rope_tables(seq_rows, head_dim)
    seg_row = segments
    seg_column = jnp.transpose(segments, (1, 0))
    token_values = tokens.astype(F32)
    attn_normed, attn_factor = norm_forward(token_values, gain_attn)
    offsets = [0] + [sign * step for step in range(1, tensor_count) for sign in (1, -1)]
    offsets = [offset % tensor_count for offset in offsets[:tensor_count]]
    line_blocks = [((tensor_pos + offset) % tensor_count)[None] for offset in offsets]

    def fetched(block, offset):
        if offset == 0:
            return block
        pairs = [((at + offset) % tensor_count, at) for at in range(tensor_count)]
        return lax.ppermute(block, "tensor", pairs)

    def delivered(block, offset):
        if offset == 0:
            return block
        pairs = [(at, (at + offset) % tensor_count) for at in range(tensor_count)]
        return lax.ppermute(block, "tensor", pairs)

    def dispatched(block):
        return [
            plane_rows(to_slots(at, plane_ranks, fetched(block, offset), slots))
            for offset, at in zip(offsets, line_blocks)
        ]

    if in_kernel:
        (
            attention_total,
            plane_ranks,
            low,
            attention_low,
            linear,
            heads_narrow,
            sequence_normalized,
            gathered,
            up_rows,
        ) = front(
            tokens,
            cotangent,
            jnp.transpose(routes, (1, 0)),
            packed,
            gain_attn[None, :],
            input_first,
            q_second,
            k_second,
            v_second,
            gain_query,
            gain_key,
            tables,
            seg_column,
            seg_row,
            attention_first,
            attention_second,
            score_scale,
            slots,
            (linear_cols, out_start),
            0,
        )
        sequence_normalized = sequence_normalized.reshape(seq_rows, model_width)
        gathered_blocks = gathered
        gathered = gathered.reshape(model_width, -1)
    else:
        gathered = lax.all_gather(packed, "fsdp", axis=0, tiled=True)
        sequence_tokens, sequence_routes = gather_line(
            [tokens, jnp.transpose(routes, (1, 0))], (4, 1), 0
        )
        sequence_tokens = sequence_tokens.reshape(seq_rows, model_width)
        plane_experts = jnp.arange(fsdp_count, dtype=jnp.int32) * tensor_count + tensor_pos
        plane_ranks = ranks_of(
            jnp.any(
                sequence_routes[:, None, :, :] == plane_experts[None, :, None, None], axis=2
            )
        )
        up_rows = dispatched(cotangent)
        sequence_normalized = norm_forward(sequence_tokens.astype(F32), gain_attn)[0].astype(
            BF16
        )
        linear = matrix_product(sequence_normalized, gathered[:, :linear_cols])
        low = flipped_right_operand(sequence_normalized, input_first).astype(BF16)
    complete_linear = gathered[:, :linear_cols]
    complete_router = gathered[:, linear_cols : linear_cols + expert_count]
    full_out_t = gathered[:, out_start:]
    attention_operands = (
        linear,
        low,
        q_second,
        k_second,
        v_second,
        gain_query,
        gain_key,
        tables,
        seg_column,
        seg_row,
        score_scale,
    )
    if not in_kernel:
        heads_narrow = attention_forward(*attention_operands)
        attention_low = flipped_right_operand(heads_narrow, attention_first).astype(BF16)
        out_part = flipped_right_operand(heads_narrow, full_out_t) + matrix_product(
            attention_low, attention_second
        )
        attention_total = sum_line(
            out_part.astype(BF16).reshape(tensor_count, tok_rows, model_width), 4, 1
        )
    residual_stream = token_values + attention_total
    moe_normed, moe_factor = norm_forward(residual_stream, gain_moe)
    experts_narrow = moe_normed.astype(BF16)

    router_low = flipped_right_operand(experts_narrow, router_first).astype(BF16)
    router_logits = matrix_product(experts_narrow, complete_router) + matrix_product(
        router_low, router_second
    )
    expert_ids = jnp.arange(expert_count, dtype=jnp.int32)
    chosen = jnp.any(routes[:, :, None] == expert_ids[None, None, :], axis=1)
    chosen_logits = jnp.where(chosen, router_logits, -jnp.inf)
    chosen_exp = jnp.exp(chosen_logits - jnp.max(chosen_logits, axis=-1, keepdims=True))
    gate_weights = chosen_exp / jnp.sum(chosen_exp, axis=-1, keepdims=True)
    sent_weights = jnp.transpose(jnp.where(chosen, gate_weights, -1.0), (1, 0))
    own_weights = jnp.transpose(
        route_rows(sent_weights).reshape(fsdp_count, tensor_count, tok_rows), (1, 0, 2)
    )
    own_ranks = ranks_of(own_weights >= 0.0)

    broad = adapter_count * rank
    gate_in_t, upward_in_t = transposed(gate_in[0]), transposed(upward_in[0])
    expert_tables = (
        expert_gate_weight[0],
        expert_up_weight[0],
        expert_down_weight[0],
        jnp.concatenate(
            [gate_in_t.reshape(broad, model_width), upward_in_t.reshape(broad, model_width)],
            axis=0,
        ),
        gate_out[0].reshape(broad, -1),
        upward_out[0].reshape(broad, -1),
        transposed(downward_in[0]).reshape(broad, -1),
        downward_out[0].reshape(broad, model_width),
    )
    column_adapter = jnp.arange(broad, dtype=jnp.int32) // rank
    adapter_mask = jnp.repeat(
        (adapter_index[:, None] == column_adapter[None, :]).astype(BF16), slots, axis=0
    )
    ordered = [None] * tensor_count
    if in_kernel:
        moe_grad, gate_dots, expert_output, _landed, *sums = moe_layer(
            experts_narrow,
            up_rows,
            plane_ranks,
            own_ranks,
            own_weights,
            adapter_mask,
            expert_tables,
            3,
        )
    else:
        expert_rows = dispatched(experts_narrow)
        expert_output, rows_grad, gate_dots = [], [], []
        sums = [jnp.zeros(each.shape, F32) for each in expert_sums(expert_tables)]
        for at, rows, upstream in zip(line_blocks, expert_rows, up_rows):
            y_rows, grad_rows, dots, *sums = experts(
                at, rows, upstream, own_ranks, own_weights, adapter_mask, expert_tables, sums
            )
            expert_output.append(y_rows)
            rows_grad.append(grad_rows)
            gate_dots.append(dots)
        for offset, dots in zip(offsets, gate_dots):
            ordered[offset] = dots
        gate_dots = jnp.roll(jnp.stack(ordered), tensor_pos, axis=0)
    pair_in_grad, gate_out_grad, upward_out_grad, downward_in_grad, downward_out_grad = sums
    if in_kernel:

        def by_line(table):
            lines = table.reshape(fsdp_count, tensor_count, -1)
            return jnp.transpose(lines, (1, 0, 2)).reshape(expert_count, -1)

        (
            output,
            residual_grad,
            low_share,
            linear_grad,
            row_grads,
            head_grads,
            narrow_grads,
            router_grads,
            _landed,
        ) = back(
            score_scale,
            (linear_cols, out_start),
            slots,
            4,
            (linear, heads_narrow, sequence_normalized, gathered_blocks, expert_output),
            (
                moe_grad,
                gate_dots.reshape(expert_count, tok_rows),
                by_line(jnp.transpose(gate_weights, (1, 0))),
                residual_stream,
                cotangent,
                gain_moe[None, :],
                by_line(jnp.transpose(complete_router, (1, 0))),
                router_first,
                jnp.transpose(by_line(jnp.transpose(router_second, (1, 0))), (1, 0)),
                jnp.transpose(router_low, (1, 0)),
                experts_narrow,
                plane_ranks,
                low,
                attention_low,
                attention_first,
                attention_second,
                q_second,
                k_second,
                v_second,
                gain_query,
                gain_key,
                *tables,
                seg_column,
                seg_row,
            ),
        )
        router_second_gradient = jnp.transpose(
            router_grads.reshape(rank, tensor_count, fsdp_count), (0, 2, 1)
        ).reshape(rank, expert_count)
        input_grad = last(
            linear_grad,
            low_share,
            input_first,
            residual_grad,
            tokens,
            gain_attn[None, :],
            gathered_blocks,
            5,
        )
    else:
        gate_grad = jnp.transpose(
            route_rows(jnp.transpose(gate_dots, (1, 0, 2)).reshape(device_count, tok_rows)), (1, 0)
        )

        def returned(slotted):
            total = 0.0
            for offset, at, rows in zip(offsets, line_blocks, slotted):
                combined = from_slots(at, plane_ranks, plane_rows(rows))
                total = total + delivered(combined, offset).astype(F32)
            return total

        moe_grad = returned(rows_grad)

        out_grad = cotangent.astype(F32)
        logit_gradient = (
            gate_weights * (gate_grad - jnp.sum(gate_weights * gate_grad, axis=-1, keepdims=True))
        ).astype(BF16)
        router_low_gradient = flipped_right_operand(logit_gradient, router_second).astype(BF16)
        moe_grad = (
            moe_grad
            + flipped_right_operand(logit_gradient, complete_router)
            + matrix_product(router_low_gradient, router_first)
        )
        router_first_gradient = flipped_left_operand(router_low_gradient, experts_narrow)
        router_second_gradient = flipped_left_operand(router_low, logit_gradient)
        residual_grad = out_grad + norm_backward(residual_stream, moe_factor, gain_moe, moe_grad)

        (sequence_branch,) = gather_line([residual_grad.astype(BF16)], (4,), 2)
        sequence_branch = sequence_branch.reshape(seq_rows, model_width)
        output = (residual_stream + returned(expert_output)).astype(BF16)
        attention_low_grad = flipped_right_operand(sequence_branch, attention_second).astype(BF16)
        attention_second_gradient = flipped_left_operand(attention_low, sequence_branch)
        heads_grad = matrix_product(sequence_branch, full_out_t)
        (
            q_grad,
            k_grad,
            v_grad,
            low_share,
            q_second_gradient,
            k_second_gradient,
            v_second_gradient,
            attention_first_gradient,
        ) = attention_backward(
            *attention_operands,
            heads_narrow,
            heads_grad,
            attention_low_grad,
            attention_first,
        )
        linear_grad = jnp.concatenate([q_grad, k_grad, v_grad], axis=1)
        normed_part = flipped_right_operand(linear_grad, complete_linear) + matrix_product(
            low_share, input_first
        )
        input_first_gradient = flipped_left_operand(low_share, sequence_normalized)
        normalized_gradient = sum_line(
            normed_part.astype(BF16).reshape(tensor_count, tok_rows, model_width), 4, 1
        )
        input_grad = residual_grad + norm_backward(
            token_values, attn_factor, gain_attn, normalized_gradient
        )
        row_grads = jnp.concatenate(
            [input_first_gradient, attention_second_gradient, router_first_gradient], axis=0
        )
        head_grads = jnp.concatenate([q_second_gradient, attention_first_gradient], axis=0)
        narrow_grads = jnp.concatenate([k_second_gradient, v_second_gradient], axis=0)

    source_adapter = jnp.repeat(adapter_index, tensor_count)
    owner_onehot = (
        jnp.arange(adapter_count, dtype=jnp.int32)[:, None] == source_adapter[None, :]
    ).astype(BF16)

    def to_all(addend):
        lines = addend.shape[0]
        return jnp.transpose(
            addend.astype(BF16).reshape(lines, device_count, -1), (1, 0, 2)
        ).reshape(device_count, -1)

    def to_head_owners(addend):
        lines = addend.shape[0]
        pieces = jnp.transpose(
            addend.astype(BF16).reshape(lines, fsdp_count, -1), (1, 0, 2)
        ).reshape(fsdp_count, -1)
        holder = jnp.zeros((device_count, pieces.shape[1]), BF16)
        return lax.dynamic_update_slice(holder, pieces, (tensor_pos * fsdp_count, zero_pos))

    def owner_sums(parts):
        widths = [part.shape[1] for part in parts]
        total = matrix_product(owner_onehot, route_rows(jnp.concatenate(parts, axis=1)))
        pieces = []
        start = 0
        for width in widths:
            pieces.append(total[:, start : start + width])
            start += width
        return pieces

    row_sums, head_sums, narrow_sums, router_sums = owner_sums(
        [
            to_all(row_grads),
            to_head_owners(head_grads),
            to_head_owners(narrow_grads),
            to_all(router_second_gradient),
        ]
    )

    def lines_of(piece, lines):
        return piece.reshape(adapter_count, lines, -1)

    row_sums = lines_of(row_sums, 5 * rank)
    head_sums = lines_of(head_sums, 2 * rank)
    narrow_sums = lines_of(narrow_sums, 2 * rank)

    def factor_rows(at):
        return row_sums[:, at * rank : (at + 1) * rank]

    return (
        output,
        input_grad,
        transposed(factor_rows(0)),
        head_sums[:, :rank],
        transposed(factor_rows(1)),
        narrow_sums[:, :rank],
        transposed(factor_rows(2)),
        narrow_sums[:, rank:],
        transposed(head_sums[:, rank:]),
        factor_rows(3),
        transposed(factor_rows(4)),
        lines_of(router_sums, rank),
        transposed(lines_of(pair_in_grad[:broad], rank))[None],
        lines_of(gate_out_grad, rank)[None],
        transposed(lines_of(pair_in_grad[broad:], rank))[None],
        lines_of(upward_out_grad, rank)[None],
        transposed(lines_of(downward_in_grad, rank))[None],
        lines_of(downward_out_grad, rank)[None],
    )


def solution(mesh):
    placed = (
        P(("fsdp", "tensor"), None),
        P("fsdp", None),
        P(("fsdp", "tensor"), None),
        P(),
        P(("fsdp", "tensor"), None),
        P(),
        P(),
        P(),
        P(),
        P("fsdp", "tensor"),
        P("fsdp", "tensor"),
        P("fsdp", "tensor"),
        P("tensor", "fsdp"),
        P("fsdp", None),
        P(("fsdp", "tensor"), None, None),
        P(("fsdp", "tensor"), None, None),
        P(("fsdp", "tensor"), None, None),
        P(),
        P(None, None, "tensor"),
        P(),
        P(None, None, "tensor"),
        P(),
        P(None, None, "tensor"),
        P(None, "tensor", None),
        P(),
        P(),
        P(),
        P(("fsdp", "tensor"), None, None, None),
        P(("fsdp", "tensor"), None, None, None),
        P(("fsdp", "tensor"), None, None, None),
        P(("fsdp", "tensor"), None, None, None),
        P(("fsdp", "tensor"), None, None, None),
        P(("fsdp", "tensor"), None, None, None),
    )
    return jax.shard_map(
        per_device,
        mesh=mesh,
        in_specs=placed,
        out_specs=(
            P(("fsdp", "tensor"), None),
            P(("fsdp", "tensor"), None),
            P(None, ("fsdp", "tensor"), None),
            P(None, None, ("fsdp", "tensor")),
            P(None, ("fsdp", "tensor"), None),
            P(None, None, ("fsdp", "tensor")),
            P(None, ("fsdp", "tensor"), None),
            P(None, None, ("fsdp", "tensor")),
            P(None, ("fsdp", "tensor"), None),
            P(None, None, ("fsdp", "tensor")),
            P(None, ("fsdp", "tensor"), None),
            P(None, None, ("fsdp", "tensor")),
            P(("fsdp", "tensor"), None, None, None),
            P(("fsdp", "tensor"), None, None, None),
            P(("fsdp", "tensor"), None, None, None),
            P(("fsdp", "tensor"), None, None, None),
            P(("fsdp", "tensor"), None, None, None),
            P(("fsdp", "tensor"), None, None, None),
        ),
        check_vma=False,
    )
```

```python
import functools
import math

import jax
import jax.numpy as jnp
import numpy as np
from jax import lax
from jax.experimental import pallas as pl
from jax.experimental.pallas import tpu as pltpu
from jax.sharding import PartitionSpec as P

NORM_EPSILON = 1e-06
ROPE_THETA = 1000000.0
BF16 = jnp.bfloat16
F32 = jnp.float32
WINDOW = 256
MEBI = 1 << 20


def matrix_product(first_op, second_op):
    return jnp.dot(first_op, second_op, preferred_element_type=F32)


def flipped_left_operand(first_op, second_op):
    return lax.dot_general(
        first_op, second_op, (((0,), (0,)), ((), ())), preferred_element_type=F32
    )


def flipped_right_operand(first_op, second_op):
    return lax.dot_general(
        first_op, second_op, (((1,), (1,)), ((), ())), preferred_element_type=F32
    )


def norm_forward(values, gain_vec):
    factor = lax.rsqrt(jnp.mean(values * values, axis=-1, keepdims=True) + NORM_EPSILON)
    return (values * factor * gain_vec, factor)


def norm_backward(values, factor, gain_vec, upstream):
    scaled = upstream * gain_vec
    return factor * scaled - values * (factor * factor * factor) * jnp.mean(
        values * scaled, axis=-1, keepdims=True
    )


def rope_tables(sequence_length, head_width):
    half_width = head_width // 2
    inverse = np.power(
        np.float32(ROPE_THETA), -2.0 * np.arange(half_width, dtype=np.float32) / head_width
    ).astype(np.float32)
    angles = np.arange(sequence_length, dtype=np.float32)[:, None] * inverse[None, :]
    cosine, sine = np.cos(angles), np.sin(angles)
    return (
        jnp.asarray(np.concatenate([cosine, cosine], axis=1)),
        jnp.asarray(np.concatenate([-sine, sine], axis=1)),
    )


def swapped(values):
    return pltpu.roll(values, values.shape[-1] // 2, 1)


def route_rows(block_rows):
    return lax.all_to_all(block_rows, ("fsdp", "tensor"), split_axis=0, concat_axis=0, tiled=True)


def plane_rows(block_rows):
    return lax.all_to_all(block_rows, "fsdp", split_axis=0, concat_axis=0, tiled=True)


def params(mebibytes, axes=1):
    return pltpu.CompilerParams(
        vmem_limit_bytes=mebibytes * MEBI, dimension_semantics=("arbitrary",) * axes
    )


def staged(body, lead, count):
    def kernel(*refs):
        semaphores, held = refs[-1], refs[-1 - count : -1]
        copies = [
            pltpu.make_async_copy(source, target, semaphores.at[at])
            for at, (source, target) in enumerate(zip(refs[lead : lead + count], held))
        ]
        for each in copies:
            each.start()

        def ready():
            for each in copies:
                each.wait()

        body(ready, *refs[:lead], *held, *refs[lead + count : -1 - count])

    return kernel


def staging(operands):
    return [pltpu.VMEM(operand.shape, operand.dtype) for operand in operands] + [
        pltpu.SemaphoreType.DMA((len(operands),))
    ]


def whole(shape):
    rank = len(shape)
    return pl.BlockSpec(shape, lambda *_: (0,) * rank)


def head_values(linear, low, second, gain, cosine, sine):
    values = linear + matrix_product(low, second)
    normed, factor = norm_forward(values, gain)
    turned = (normed * cosine + swapped(normed) * sine).astype(BF16)
    return values, factor, turned


def head_values_gradient(values, factor, gain, cosine, sine, upstream):
    back = upstream * cosine - swapped(upstream) * sine
    return norm_backward(values, factor, gain, back).astype(BF16)


def allowed_keys(block, start, width, seg_column, seg_row):
    rows = block * WINDOW + lax.broadcasted_iota(jnp.int32, (WINDOW, width), 0)
    keys = start + lax.broadcasted_iota(jnp.int32, (WINDOW, width), 1)
    mine = seg_column[block * WINDOW : (block + 1) * WINDOW]
    theirs = seg_row[:, start : start + width]
    return (keys == rows) | ((keys < rows) & (mine == theirs) & (theirs != 0))


def block_bounds(block):
    start = max(block - 1, 0) * WINDOW
    return start, (block + 1) * WINDOW - start


def attention_forward_body(
    rank,
    scale,
    lin_ref,
    key_lin_ref,
    value_lin_ref,
    low_ref,
    q_second_ref,
    k_second_ref,
    v_second_ref,
    q_gain_ref,
    k_gain_ref,
    cos_ref,
    sin_ref,
    seg_column_ref,
    seg_row_ref,
    heads_ref,
    key_scratch,
    value_scratch,
):
    cosine, sine = cos_ref[...], sin_ref[...]

    @pl.when(pl.program_id(0) == 0)
    def _():
        key_scratch[...] = head_values(
            key_lin_ref[...],
            low_ref[:, rank : 2 * rank],
            k_second_ref[...],
            k_gain_ref[...],
            cosine,
            sine,
        )[2]
        value_scratch[...] = (
            value_lin_ref[...]
            + matrix_product(low_ref[:, 2 * rank : 3 * rank], v_second_ref[...])
        ).astype(BF16)

    query = head_values(
        lin_ref[...], low_ref[:, :rank], q_second_ref[...], q_gain_ref[...], cosine, sine
    )[2]
    seg_column, seg_row = seg_column_ref[...], seg_row_ref[...]
    for block in range(query.shape[0] // WINDOW):
        start, width = block_bounds(block)
        rows = pl.ds(block * WINDOW, WINDOW)
        scores = (
            flipped_right_operand(
                query[block * WINDOW : (block + 1) * WINDOW], key_scratch[pl.ds(start, width)]
            )
            * scale
        )
        scores = jnp.where(
            allowed_keys(block, start, width, seg_column, seg_row), scores, -1e30
        )
        expo = jnp.exp(scores - jnp.max(scores, axis=-1, keepdims=True))
        probs = (expo / jnp.sum(expo, axis=-1, keepdims=True)).astype(BF16)
        heads_ref[rows, :] = matrix_product(probs, value_scratch[pl.ds(start, width)]).astype(
            BF16
        )


def attention_forward(
    linear, low, q_second, k_second, v_second, q_gain, k_gain, tables, seg_column, seg_row, scale
):
    rows, head_dim = linear.shape[0], q_gain.shape[1]
    heads = q_second.shape[1] // head_dim
    rank = q_second.shape[0]
    column = pl.BlockSpec((rows, head_dim), lambda h: (0, h))
    return pl.pallas_call(
        functools.partial(attention_forward_body, rank, scale),
        grid=(heads,),
        out_shape=jax.ShapeDtypeStruct((rows, heads * head_dim), BF16),
        in_specs=[
            column,
            pl.BlockSpec((rows, head_dim), lambda h: (0, heads)),
            pl.BlockSpec((rows, head_dim), lambda h: (0, heads + 1)),
            whole(low.shape),
            pl.BlockSpec((rank, head_dim), lambda h: (0, h)),
            whole(k_second.shape),
            whole(v_second.shape),
            whole(q_gain.shape),
            whole(k_gain.shape),
            whole(tables[0].shape),
            whole(tables[1].shape),
            whole(seg_column.shape),
            whole(seg_row.shape),
        ],
        out_specs=column,
        scratch_shapes=[pltpu.VMEM((rows, head_dim), BF16), pltpu.VMEM((rows, head_dim), BF16)],
        compiler_params=params(40),
        cost_estimate=pl.CostEstimate(
            flops=8 * heads * rows * WINDOW * head_dim,
            transcendentals=2 * heads * rows * WINDOW,
            bytes_accessed=6 * rows * heads * head_dim,
        ),
        name="attention_forward",
    )(
        linear,
        linear,
        linear,
        low,
        q_second,
        k_second,
        v_second,
        q_gain,
        k_gain,
        *tables,
        seg_column,
        seg_row,
    )


def attention_backward_body(
    rank,
    scale,
    lin_ref,
    key_lin_ref,
    value_lin_ref,
    low_ref,
    q_second_ref,
    k_second_ref,
    v_second_ref,
    q_gain_ref,
    k_gain_ref,
    cos_ref,
    sin_ref,
    seg_column_ref,
    seg_row_ref,
    heads_ref,
    heads_grad_ref,
    low_grad_ref,
    down_ref,
    q_grad_ref,
    k_grad_ref,
    v_grad_ref,
    share_ref,
    q_second_grad_ref,
    k_second_grad_ref,
    v_second_grad_ref,
    down_grad_ref,
    key_scratch,
    value_scratch,
    key_sum,
    value_sum,
    query_sum,
    share_sum,
):
    cosine, sine = cos_ref[...], sin_ref[...]
    head = pl.program_id(0)

    @pl.when(head == 0)
    def _():
        key_scratch[...] = head_values(
            key_lin_ref[...],
            low_ref[:, rank : 2 * rank],
            k_second_ref[...],
            k_gain_ref[...],
            cosine,
            sine,
        )[2]
        value_scratch[...] = (
            value_lin_ref[...]
            + matrix_product(low_ref[:, 2 * rank : 3 * rank], v_second_ref[...])
        ).astype(BF16)
        key_sum[...] = jnp.zeros_like(key_sum)
        value_sum[...] = jnp.zeros_like(value_sum)
        share_sum[...] = jnp.zeros_like(share_sum)

    low_q = low_ref[:, :rank]
    values, factor, query = head_values(
        lin_ref[...], low_q, q_second_ref[...], q_gain_ref[...], cosine, sine
    )
    low_grad = low_grad_ref[...]
    upstream = (heads_grad_ref[...] + matrix_product(low_grad, down_ref[...])).astype(BF16)
    down_grad_ref[...] = flipped_left_operand(low_grad, heads_ref[...])
    seg_column, seg_row = seg_column_ref[...], seg_row_ref[...]
    for block in range(query.shape[0] // WINDOW):
        start, width = block_bounds(block)
        rows = pl.ds(block * WINDOW, WINDOW)
        keys = pl.ds(start, width)
        query_block = query[block * WINDOW : (block + 1) * WINDOW]
        upstream_block = upstream[block * WINDOW : (block + 1) * WINDOW]
        scores = flipped_right_operand(query_block, key_scratch[keys]) * scale
        scores = jnp.where(
            allowed_keys(block, start, width, seg_column, seg_row), scores, -1e30
        )
        expo = jnp.exp(scores - jnp.max(scores, axis=-1, keepdims=True))
        probs = expo / jnp.sum(expo, axis=-1, keepdims=True)
        prob_grad = flipped_right_operand(upstream_block, value_scratch[keys])
        score_grad = (
            probs * (prob_grad - jnp.sum(probs * prob_grad, axis=-1, keepdims=True))
        ).astype(BF16)
        value_sum[keys, :] += flipped_left_operand(probs.astype(BF16), upstream_block)
        key_sum[keys, :] += flipped_left_operand(score_grad, query_block)
        query_sum[rows, :] = matrix_product(score_grad, key_scratch[keys]) * scale
    q_grad = head_values_gradient(
        values, factor, q_gain_ref[...], cosine, sine, query_sum[...]
    )
    q_grad_ref[...] = q_grad
    q_second_grad_ref[...] = flipped_left_operand(low_q, q_grad)
    share_sum[:, :rank] += flipped_right_operand(q_grad, q_second_ref[...])

    @pl.when(head == pl.num_programs(0) - 1)
    def _():
        low_k = low_ref[:, rank : 2 * rank]
        low_v = low_ref[:, 2 * rank : 3 * rank]
        key_values, key_factor, _turned = head_values(
            key_lin_ref[...], low_k, k_second_ref[...], k_gain_ref[...], cosine, sine
        )
        k_grad = head_values_gradient(
            key_values, key_factor, k_gain_ref[...], cosine, sine, key_sum[...] * scale
        )
        v_grad = value_sum[...].astype(BF16)
        k_grad_ref[...] = k_grad
        v_grad_ref[...] = v_grad
        k_second_grad_ref[...] = flipped_left_operand(low_k, k_grad)
        v_second_grad_ref[...] = flipped_left_operand(low_v, v_grad)
        share_sum[:, rank : 2 * rank] = flipped_right_operand(k_grad, k_second_ref[...])
        share_sum[:, 2 * rank : 3 * rank] = flipped_right_operand(v_grad, v_second_ref[...])
        share_ref[...] = share_sum[...].astype(BF16)


def attention_backward(
    linear,
    low,
    q_second,
    k_second,
    v_second,
    q_gain,
    k_gain,
    tables,
    seg_column,
    seg_row,
    scale,
    heads_low,
    heads_grad,
    low_grad,
    down_first,
):
    rows, head_dim = linear.shape[0], q_gain.shape[1]
    rank, columns = q_second.shape
    heads = columns // head_dim
    column = pl.BlockSpec((rows, head_dim), lambda h: (0, h))
    narrow = pl.BlockSpec((rank, head_dim), lambda h: (0, h))
    single = (rows, head_dim)
    return pl.pallas_call(
        functools.partial(attention_backward_body, rank, scale),
        grid=(heads,),
        out_shape=(
            jax.ShapeDtypeStruct((rows, columns), BF16),
            jax.ShapeDtypeStruct(single, BF16),
            jax.ShapeDtypeStruct(single, BF16),
            jax.ShapeDtypeStruct((rows, 3 * rank), BF16),
            jax.ShapeDtypeStruct((rank, columns), F32),
            jax.ShapeDtypeStruct((rank, head_dim), F32),
            jax.ShapeDtypeStruct((rank, head_dim), F32),
            jax.ShapeDtypeStruct((rank, columns), F32),
        ),
        in_specs=[
            column,
            pl.BlockSpec((rows, head_dim), lambda h: (0, heads)),
            pl.BlockSpec((rows, head_dim), lambda h: (0, heads + 1)),
            whole(low.shape),
            narrow,
            whole(k_second.shape),
            whole(v_second.shape),
            whole(q_gain.shape),
            whole(k_gain.shape),
            whole(tables[0].shape),
            whole(tables[1].shape),
            whole(seg_column.shape),
            whole(seg_row.shape),
            column,
            column,
            whole(low_grad.shape),
            narrow,
        ],
        out_specs=(
            column,
            whole(single),
            whole(single),
            whole((rows, 3 * rank)),
            narrow,
            whole((rank, head_dim)),
            whole((rank, head_dim)),
            narrow,
        ),
        scratch_shapes=[
            pltpu.VMEM(single, BF16),
            pltpu.VMEM(single, BF16),
            pltpu.VMEM(single, F32),
            pltpu.VMEM(single, F32),
            pltpu.VMEM(single, F32),
            pltpu.VMEM((rows, 3 * rank), F32),
        ],
        compiler_params=params(48),
        cost_estimate=pl.CostEstimate(
            flops=20 * heads * rows * WINDOW * head_dim,
            transcendentals=2 * heads * rows * WINDOW,
            bytes_accessed=12 * rows * columns,
        ),
        name="attention_backward",
    )(
        linear,
        linear,
        linear,
        low,
        q_second,
        k_second,
        v_second,
        q_gain,
        k_gain,
        *tables,
        seg_column,
        seg_row,
        heads_low,
        heads_grad,
        low_grad,
        down_first,
    )


def slot_choice(ranks, slots):
    experts, tokens = ranks.shape
    places = lax.broadcasted_iota(jnp.int32, (slots, tokens), 0).astype(ranks.dtype)
    return jnp.concatenate(
        [(places == ranks[e : e + 1, :]).astype(F32) for e in range(experts)], axis=0
    ).astype(BF16)


def to_slots_body(_block_ref, rank_ref, rows_ref, out_ref):
    slots = out_ref.shape[1]
    chosen = matrix_product(slot_choice(rank_ref[0], slots), rows_ref[...])
    out_ref[...] = chosen.astype(BF16).reshape(out_ref.shape)


def to_slots(block, ranks, rows, slots):
    experts, tokens = ranks.shape[1:]
    width = rows.shape[1]
    half = width // 2
    return pl.pallas_call(
        to_slots_body,
        grid_spec=pltpu.PrefetchScalarGridSpec(
            num_scalar_prefetch=1,
            grid=(2,),
            in_specs=[
                pl.BlockSpec((1, experts, tokens), lambda j, at: (at[0], 0, 0)),
                pl.BlockSpec((tokens, half), lambda j, at: (0, j)),
            ],
            out_specs=pl.BlockSpec((experts, slots, half), lambda j, at: (0, 0, j)),
        ),
        out_shape=jax.ShapeDtypeStruct((experts, slots, width), BF16),
        compiler_params=params(32),
        cost_estimate=pl.CostEstimate(
            flops=2 * experts * slots * tokens * width,
            transcendentals=0,
            bytes_accessed=2 * width * (experts * slots + tokens),
        ),
        name="to_slots",
    )(block, ranks, rows)


def from_slots_body(_block_ref, rank_ref, slot_ref, out_ref):
    experts, slots, width = slot_ref.shape
    choice = slot_choice(rank_ref[0], slots)
    out_ref[...] = flipped_left_operand(
        choice, slot_ref[...].reshape(experts * slots, width)
    ).astype(BF16)


def from_slots(block, ranks, slotted):
    experts, tokens = ranks.shape[1:]
    slots, width = slotted.shape[1:]
    half = width // 2
    return pl.pallas_call(
        from_slots_body,
        grid_spec=pltpu.PrefetchScalarGridSpec(
            num_scalar_prefetch=1,
            grid=(2,),
            in_specs=[
                pl.BlockSpec((1, experts, tokens), lambda j, at: (at[0], 0, 0)),
                pl.BlockSpec((experts, slots, half), lambda j, at: (0, 0, j)),
            ],
            out_specs=pl.BlockSpec((tokens, half), lambda j, at: (0, j)),
        ),
        out_shape=jax.ShapeDtypeStruct((tokens, width), BF16),
        compiler_params=params(32),
        cost_estimate=pl.CostEstimate(
            flops=2 * experts * slots * tokens * width,
            transcendentals=0,
            bytes_accessed=2 * width * (experts * slots + tokens),
        ),
        name="from_slots",
    )(block, ranks, slotted)


def all_to_slots_body(rank_ref, rows_ref, out_ref):
    slots = out_ref.shape[2]
    chosen = matrix_product(slot_choice(rank_ref[0], slots), rows_ref[...])
    out_ref[...] = chosen.astype(BF16).reshape(out_ref.shape)


def all_to_slots(ranks, rows, slots):
    blocks, experts, tokens = ranks.shape
    width = rows.shape[1]
    return pl.pallas_call(
        all_to_slots_body,
        grid=(blocks,),
        out_shape=jax.ShapeDtypeStruct((experts, blocks, slots, width), BF16),
        in_specs=[
            pl.BlockSpec((1, experts, tokens), lambda z: (z, 0, 0)),
            pl.BlockSpec((tokens, width), lambda z: (z, 0)),
        ],
        out_specs=pl.BlockSpec((experts, 1, slots, width), lambda z: (0, z, 0, 0)),
        compiler_params=params(40),
        cost_estimate=pl.CostEstimate(
            flops=2 * blocks * experts * slots * tokens * width,
            transcendentals=0,
            bytes_accessed=2 * blocks * width * (experts * slots + tokens),
        ),
        name="all_to_slots",
    )(ranks, rows)


def all_from_slots_body(_start_ref, rank_ref, slot_ref, out_ref):
    experts, _, slots, width = slot_ref.shape
    choice = slot_choice(rank_ref[0], slots)
    out_ref[...] = flipped_left_operand(
        choice, slot_ref[...].reshape(experts * slots, width)
    ).astype(BF16)


def all_from_slots(start, ranks, slotted):
    blocks, experts, tokens = ranks.shape
    slots, width = slotted.shape[2:]
    return pl.pallas_call(
        all_from_slots_body,
        grid_spec=pltpu.PrefetchScalarGridSpec(
            num_scalar_prefetch=1,
            grid=(blocks,),
            in_specs=[
                pl.BlockSpec((1, experts, tokens), lambda z, at: ((at[0] + z) % blocks, 0, 0)),
                pl.BlockSpec((experts, 1, slots, width), lambda z, at: (0, z, 0, 0)),
            ],
            out_specs=pl.BlockSpec((tokens, width), lambda z, at: ((at[0] + z) % blocks, 0)),
        ),
        out_shape=jax.ShapeDtypeStruct((blocks * tokens, width), BF16),
        compiler_params=params(40),
        cost_estimate=pl.CostEstimate(
            flops=2 * blocks * experts * slots * tokens * width,
            transcendentals=0,
            bytes_accessed=2 * blocks * width * (experts * slots + tokens),
        ),
        name="all_from_slots",
    )(start, ranks, slotted)


def ranks_of(mask):
    tokens = mask.shape[-1]
    order = jnp.arange(tokens, dtype=jnp.int32)
    before = (order[:, None] < order[None, :]).astype(BF16)
    counts = matrix_product(mask.astype(BF16), before)
    return jnp.where(mask, counts, -1.0).astype(jnp.int32)


def line_relay(me, count, ins, outs, chunks, semaphores):
    right_send, right_recv, left_send, left_recv = semaphores
    pieces = []
    for at in range(len(ins)):
        size = ins[at].shape[0] // chunks[at]
        for piece in range(chunks[at]):
            pieces.append((at, pl.ds(piece * size, size)))

    def copy(place, hop, origin, target, send, recv):
        at, rows = pieces[place]
        source = ins[at].at[rows] if hop == 0 else outs[at].at[origin, rows]
        return pltpu.make_async_remote_copy(
            src_ref=source,
            dst_ref=outs[at].at[origin, rows],
            send_sem=send.at[hop, place],
            recv_sem=recv.at[hop, place],
            device_id={"tensor": target},
        )

    def places(arrays):
        return [place for place in range(len(pieces)) if pieces[place][0] in arrays]

    def advance(hop, arrays):
        for place in places(arrays):
            if hop > 0:

                @pl.when(me - hop >= 0)
                def _():
                    copy(place, hop - 1, me - hop, me - 1, right_send, right_recv).wait_recv()

            if hop < count - 1:

                @pl.when((me - hop >= 0) & (me + 1 < count))
                def _():
                    copy(place, hop, me - hop, me + 1, right_send, right_recv).start()

            if hop > 0:

                @pl.when(me + hop < count)
                def _():
                    copy(place, hop - 1, me + hop, me + 1, left_send, left_recv).wait_recv()

            if hop < count - 1:

                @pl.when((me + hop < count) & (me > 0))
                def _():
                    copy(place, hop, me + hop, me - 1, left_send, left_recv).start()

    def finish(arrays, hops):
        for hop in hops:
            for place in places(arrays):

                @pl.when((me - hop >= 0) & (me + 1 < count))
                def _():
                    copy(place, hop, me - hop, me + 1, right_send, right_recv).wait_send()

                @pl.when((me + hop < count) & (me > 0))
                def _():
                    copy(place, hop, me + hop, me - 1, left_send, left_recv).wait_send()

    return advance, finish


def line_sum(me, count, chunks, part_ref, out_ref, left_buf, right_buf, semaphores):
    right_send, right_recv, left_send, left_recv = semaphores
    size = part_ref.shape[1] // chunks

    def rightward(rows, piece, far, source):
        return pltpu.make_async_remote_copy(
            src_ref=source,
            dst_ref=left_buf.at[far - 1, rows],
            send_sem=right_send.at[far - 1, piece],
            recv_sem=right_recv.at[far - 1, piece],
            device_id={"tensor": me + 1},
        )

    def leftward(rows, piece, far, source):
        return pltpu.make_async_remote_copy(
            src_ref=source,
            dst_ref=right_buf.at[far - 1, rows],
            send_sem=left_send.at[far - 1, piece],
            recv_sem=left_recv.at[far - 1, piece],
            device_id={"tensor": me - 1},
        )

    def added(buffer, far, rows, block):
        buffer[far, rows, :] = (
            buffer[far, rows, :].astype(F32) + part_ref[block, rows, :].astype(F32)
        ).astype(BF16)

    def advance(far):
        for piece in range(chunks):
            rows = pl.ds(piece * size, size)

            @pl.when((me == 0) & (me + far < count))
            def _():
                rightward(rows, piece, far, part_ref.at[me + far, rows]).start()

            @pl.when((me == count - 1) & (me - far >= 0))
            def _():
                leftward(rows, piece, far, part_ref.at[me - far, rows]).start()

            if far < count - 1:

                @pl.when((me > 0) & (me + far < count))
                def _():
                    rightward(rows, piece, far + 1, left_buf.at[far, rows]).wait_recv()
                    added(left_buf, far, rows, me + far)
                    rightward(rows, piece, far, left_buf.at[far, rows]).start()

                @pl.when((me < count - 1) & (me - far >= 0))
                def _():
                    leftward(rows, piece, far + 1, right_buf.at[far, rows]).wait_recv()
                    added(right_buf, far, rows, me - far)
                    leftward(rows, piece, far, right_buf.at[far, rows]).start()

    def finish():
        for piece in range(chunks):
            rows = pl.ds(piece * size, size)
            out_ref[rows, :] = part_ref[me, rows, :].astype(F32)

            @pl.when(me > 0)
            def _():
                rightward(rows, piece, 1, left_buf.at[0, rows]).wait_recv()
                out_ref[rows, :] += left_buf[0, rows, :].astype(F32)

            @pl.when(me < count - 1)
            def _():
                leftward(rows, piece, 1, right_buf.at[0, rows]).wait_recv()
                out_ref[rows, :] += right_buf[0, rows, :].astype(F32)

        for far in range(count - 1, 0, -1):
            for piece in range(chunks):
                rows = pl.ds(piece * size, size)

                @pl.when((me == 0) & (me + far < count))
                def _():
                    rightward(rows, piece, far, part_ref.at[me + far, rows]).wait_send()

                @pl.when((me == count - 1) & (me - far >= 0))
                def _():
                    leftward(rows, piece, far, part_ref.at[me - far, rows]).wait_send()

                if far < count - 1:

                    @pl.when((me > 0) & (me + far < count))
                    def _():
                        rightward(rows, piece, far, left_buf.at[far, rows]).wait_send()

                    @pl.when((me < count - 1) & (me - far >= 0))
                    def _():
                        leftward(rows, piece, far, right_buf.at[far, rows]).wait_send()

    return advance, finish


def greet_line_and_plane(line, plane):
    me, at_line = lax.axis_index("fsdp"), lax.axis_index("tensor")
    barrier = pltpu.get_barrier_semaphore()

    @pl.loop(1, plane)
    def _(d):
        pl.semaphore_signal(barrier, inc=1, device_id={"fsdp": lax.rem(me + d, plane)})

    @pl.loop(1, line)
    def _(d):
        pl.semaphore_signal(barrier, inc=1, device_id={"tensor": lax.rem(at_line + d, line)})

    pl.semaphore_wait(barrier, plane + line - 2)


def tiles(width, tile, body):
    @pl.loop(0, width // tile)
    def _(j):
        body(pl.ds(pl.multiple_of(j * tile, tile), tile))


def expert_math(
    tile, rows_ref, up_ref, ranks, weights, keep_dots, sent_y, mask_ref, tables, sums, scratch
):
    gate_w, up_w, down_w, pair_in, gate_out, up_out, down_in, down_out = tables
    pair_in_sum, gate_out_sum, up_out_sum, down_in_sum, down_out_sum = sums
    gate_lin_ref, up_lin_ref, inner_ref, route_ref, gate_grad_ref, up_grad_ref = scratch
    sources, slots, width = rows_ref.shape
    row_count = sources * slots
    hidden = gate_w.shape[1]
    broad = gate_out.shape[0]
    places = lax.broadcasted_iota(jnp.int32, (slots, ranks.shape[1]), 0).astype(ranks.dtype)

    def held(source):
        return places == ranks[source : source + 1, :]

    def all_rows():
        return rows_ref[...].reshape(row_count, width)

    def pair_mask():
        mask = mask_ref[...].astype(F32)
        return jnp.concatenate([mask, mask], axis=1)

    weight = jnp.concatenate(
        [
            jnp.sum(
                jnp.where(held(source), weights[source : source + 1, :], 0.0),
                axis=1,
                keepdims=True,
            )
            for source in range(sources)
        ],
        axis=0,
    )
    pair = (flipped_right_operand(all_rows(), pair_in[...]) * pair_mask()).astype(BF16)
    gate_low, up_low = pair[:, :broad], pair[:, broad:]

    def inner_step(columns):
        rows = all_rows()
        gate_lin = matrix_product(rows, gate_w[:, columns]) + matrix_product(
            gate_low, gate_out[:, columns]
        )
        up_lin = matrix_product(rows, up_w[:, columns]) + matrix_product(
            up_low, up_out[:, columns]
        )
        gate_lin_ref[:, columns] = gate_lin
        up_lin_ref[:, columns] = up_lin
        inner_ref[:, columns] = (gate_lin * jax.nn.sigmoid(gate_lin) * up_lin).astype(BF16)

    tiles(hidden, tile, inner_step)
    down_low = (
        flipped_right_operand(inner_ref[...], down_in[...]) * mask_ref[...].astype(F32)
    ).astype(BF16)

    def down_step(j, total):
        columns = pl.ds(pl.multiple_of(j * tile, tile), tile)
        result = (
            matrix_product(inner_ref[...], down_w[:, columns])
            + matrix_product(down_low, down_out[:, columns])
        ).astype(BF16)
        wide = result.astype(F32)
        upstream = up_ref[:, :, columns].reshape(row_count, tile).astype(F32)
        up_ref[:, :, columns] = (weight * wide).astype(BF16).reshape(sources, slots, tile)
        route_ref[:, columns] = (weight * upstream).astype(BF16)
        return total + jnp.sum(upstream * wide, axis=1, keepdims=True)

    gate_dots = lax.fori_loop(0, width // tile, down_step, jnp.zeros((row_count, 1), F32))
    sent_y()
    for source in range(sources):
        keep_dots(
            source,
            jnp.sum(
                jnp.where(held(source), gate_dots[source * slots : (source + 1) * slots], 0.0),
                axis=0,
                keepdims=True,
            ),
        )
    down_low_grad = (
        flipped_right_operand(route_ref[...], down_out[...]) * mask_ref[...].astype(F32)
    ).astype(BF16)
    down_in_sum[...] += flipped_left_operand(down_low_grad, inner_ref[...])

    def down_out_step(columns):
        down_out_sum[:, columns] += flipped_left_operand(down_low, route_ref[:, columns])

    tiles(width, 2 * tile, down_out_step)

    def inner_grad_step(columns):
        inner_grad = flipped_right_operand(route_ref[...], down_w[columns, :]) + matrix_product(
            down_low_grad, down_in[:, columns]
        )
        gate_lin, up_lin = gate_lin_ref[:, columns], up_lin_ref[:, columns]
        sig = jax.nn.sigmoid(gate_lin)
        gate_grad_ref[:, columns] = (
            inner_grad * up_lin * (sig * (1.0 + gate_lin * (1.0 - sig)))
        ).astype(BF16)
        up_grad_ref[:, columns] = (inner_grad * (gate_lin * sig)).astype(BF16)

    tiles(hidden, tile, inner_grad_step)
    pair_grad = (
        jnp.concatenate(
            [
                flipped_right_operand(gate_grad_ref[...], gate_out[...]),
                flipped_right_operand(up_grad_ref[...], up_out[...]),
            ],
            axis=1,
        )
        * pair_mask()
    ).astype(BF16)
    gate_out_sum[...] += flipped_left_operand(gate_low, gate_grad_ref[...])
    up_out_sum[...] += flipped_left_operand(up_low, up_grad_ref[...])

    def rows_grad_step(columns):
        before = rows_ref[:, :, columns].reshape(row_count, tile)
        pair_in_sum[:, columns] += flipped_left_operand(pair_grad, before)
        rows_ref[:, :, columns] = (
            (
                flipped_right_operand(gate_grad_ref[...], gate_w[columns, :])
                + flipped_right_operand(up_grad_ref[...], up_w[columns, :])
                + matrix_product(pair_grad, pair_in[:, columns])
            )
            .astype(BF16)
            .reshape(sources, slots, tile)
        )

    tiles(width, tile, rows_grad_step)


def expert_sums(tables):
    gate_w, _up_w, _down_w, pair_in, gate_out, _up_out, down_in, down_out = tables
    return [
        jax.ShapeDtypeStruct(table.shape, F32)
        for table in (pair_in, gate_out, gate_out, down_in, down_out)
    ]


def expert_scratch(row_count, hidden, width):
    return [
        pltpu.VMEM((row_count, hidden), F32),
        pltpu.VMEM((row_count, hidden), F32),
        pltpu.VMEM((row_count, hidden), BF16),
        pltpu.VMEM((row_count, width), BF16),
        pltpu.VMEM((row_count, hidden), BF16),
        pltpu.VMEM((row_count, hidden), BF16),
    ]


def experts_body(_block_ref, rows_in, up_in, rank_ref, weight_ref, mask_ref, *rest):
    tables, sums_before, rest = rest[:8], rest[8:13], rest[13:]
    y_ref, rows_grad_ref, dots_ref = rest[:3]
    sums, rest = rest[3:8], rest[8:]
    for total, before in zip(sums, sums_before):
        total[...] = before[...]
    rows_grad_ref[...] = rows_in[...]
    y_ref[...] = up_in[...]

    def keep_dots(source, dots):
        dots_ref[source : source + 1, :] = dots

    expert_math(
        256,
        rows_grad_ref,
        y_ref,
        rank_ref[0],
        weight_ref[0],
        keep_dots,
        lambda: None,
        mask_ref,
        tables,
        sums,
        rest,
    )


def experts(block, rows, up_rows, ranks, weights, mask, tables, sums_before):
    sources, slots, width = rows.shape
    hidden = tables[0].shape[1]
    tokens = ranks.shape[2]
    token_spec = pl.BlockSpec((1, sources, tokens), lambda _, at: (at[0], 0, 0))

    def resident(array):
        return pl.BlockSpec(
            array.shape, lambda *_: (0,) * len(array.shape), pipeline_mode=pl.Buffered(1)
        )

    sums = expert_sums(tables)
    outs = [
        jax.ShapeDtypeStruct(rows.shape, BF16),
        jax.ShapeDtypeStruct(rows.shape, BF16),
        jax.ShapeDtypeStruct((sources, tokens), F32),
    ] + sums
    operands = [rows, up_rows, ranks, weights, mask, *tables, *sums_before]
    specs = (
        [resident(rows), resident(up_rows), token_spec, token_spec, resident(mask)]
        + [resident(table) for table in tables]
        + [resident(each) for each in sums_before]
    )
    return pl.pallas_call(
        experts_body,
        grid_spec=pltpu.PrefetchScalarGridSpec(
            num_scalar_prefetch=1,
            grid=(1,),
            in_specs=specs,
            out_specs=[resident(out) for out in outs],
            scratch_shapes=expert_scratch(sources * slots, hidden, width),
        ),
        out_shape=outs,
        input_output_aliases={
            1 + len(operands) - len(sums) + at: 3 + at for at in range(len(sums))
        },
        compiler_params=params(63),
        name="experts",
    )(block, *operands)


def moe_body(
    plane,
    line,
    ready,
    own_ref,
    up_hbm,
    plane_rank_ref,
    weight_ref,
    mask_ref,
    *rest,
):
    tables_hbm, rest = rest[:8], rest[8:]
    total_ref, dots_ref, y_hbm, back_hbm = rest[:4]
    sums, rest = rest[4:9], rest[9:]
    tables, rest = rest[:8], rest[8:]
    (
        blocks,
        partials,
        partials_in,
        sent_slots,
        rows,
        up_rows,
        back_rows,
        choice,
        dots,
        dots_back,
        dots_pass,
        dots_in,
        line_weights,
        weight_pass,
        weight_land,
    ) = rest[:15]
    scratch, rest = rest[15:21], rest[21:]
    (
        table_sem,
        up_sem,
        y_sem,
        back_sem,
        own_sem,
        relay_right_send,
        relay_right_recv,
        relay_left_send,
        relay_left_recv,
        row_send,
        row_recv,
        back_send,
        back_recv,
        partial_send,
        partial_recv,
        dots_send,
        dots_recv,
        dots_in_send,
        dots_in_recv,
        line_weight_send,
        line_weight_recv,
        weight_send,
        weight_recv,
    ) = rest
    width = own_ref.shape[1]
    slots = rows.shape[2]
    tile = 256
    me, at_line = lax.axis_index("fsdp"), lax.axis_index("tensor")

    greet_line_and_plane(line, plane)

    orders = [sorted(range(line), key=lambda block: abs(block - at)) for at in range(line)]

    def place_of(step):
        result = 0
        for at in range(line):
            for k in range(line):
                result = jnp.where((at_line == at) & (step == k), orders[at][k], result)
        return result

    advance, finish_relay = line_relay(
        at_line,
        line,
        [own_ref],
        [blocks],
        (4,),
        (relay_right_send, relay_right_recv, relay_left_send, relay_left_recv),
    )

    def row_copy(step, block, d):
        target = lax.rem(me + d, plane)
        return pltpu.make_async_remote_copy(
            src_ref=sent_slots.at[lax.rem(step, 2), target],
            dst_ref=rows.at[block, me],
            send_sem=row_send.at[block, d],
            recv_sem=row_recv.at[block, d],
            device_id={"fsdp": target},
        )

    def own_rows(step, block):
        return pltpu.make_async_copy(
            sent_slots.at[lax.rem(step, 2), me], rows.at[block, me], own_sem.at[0]
        )

    def back_copy(block, d):
        target = lax.rem(me + d, plane)
        return pltpu.make_async_remote_copy(
            src_ref=rows.at[block, target],
            dst_ref=back_hbm.at[block, me],
            send_sem=back_send.at[block, d],
            recv_sem=back_recv.at[block, d],
            device_id={"fsdp": target},
        )

    def own_back(block):
        return pltpu.make_async_copy(
            rows.at[block, me], back_hbm.at[block, me], own_sem.at[1]
        )

    def dots_copy(block, d):
        target = lax.rem(me + d, plane)
        return pltpu.make_async_remote_copy(
            src_ref=dots.at[block, target],
            dst_ref=dots_back.at[block, me],
            send_sem=dots_send.at[block, d],
            recv_sem=dots_recv.at[block, d],
            device_id={"fsdp": target},
        )

    def dots_in_copy(block, sender):
        return pltpu.make_async_remote_copy(
            src_ref=dots_pass.at[block],
            dst_ref=dots_in.at[sender],
            send_sem=dots_in_send.at[block],
            recv_sem=dots_in_recv.at[sender],
            device_id={"tensor": block},
        )

    def partial_copy(block, sender):
        return pltpu.make_async_remote_copy(
            src_ref=partials.at[block],
            dst_ref=partials_in.at[sender],
            send_sem=partial_send.at[block],
            recv_sem=partial_recv.at[sender],
            device_id={"tensor": block},
        )

    def up_copy(block):
        return pltpu.make_async_copy(up_hbm.at[:, block], up_rows, up_sem)

    def y_copy(block):
        return pltpu.make_async_copy(up_rows, y_hbm.at[:, block], y_sem)

    def line_weight_copy(target, sender):
        return pltpu.make_async_remote_copy(
            src_ref=weight_ref.at[target],
            dst_ref=line_weights.at[sender],
            send_sem=line_weight_send.at[target],
            recv_sem=line_weight_recv.at[sender],
            device_id={"tensor": target},
        )

    def weight_copy(block, d):
        target = lax.rem(me + d, plane)
        return pltpu.make_async_remote_copy(
            src_ref=weight_pass.at[block, target],
            dst_ref=weight_land.at[block, me],
            send_sem=weight_send.at[block, d],
            recv_sem=weight_recv.at[block, d],
            device_id={"fsdp": target},
        )

    ready()
    for step in range(1, line):
        line_weight_copy(place_of(step), at_line).start()
    line_weights[at_line] = weight_ref[at_line]
    advance(0, (0,))
    first_block = pltpu.make_async_copy(own_ref, blocks.at[at_line], own_sem.at[2])
    first_block.start()
    up_copy(at_line).start()
    table_copies = [
        pltpu.make_async_copy(source, target, table_sem.at[at])
        for at, (source, target) in enumerate(zip(tables_hbm, tables))
    ]
    for each in table_copies:
        each.start()
    first_block.wait()

    def dispatch(step):
        block = place_of(step)
        if step > 1:
            before = place_of(step - 2)

            @pl.loop(1, plane)
            def _(d):
                row_copy(step - 2, before, d).wait_send()

        if step > 0:
            line_weight_copy(block, block).wait_recv()
        for target in range(plane):
            weight_pass[block, target] = jnp.broadcast_to(
                line_weights[block, target : target + 1, :], weight_pass.shape[2:]
            )
        weight_land[block, me] = weight_pass[block, me]

        @pl.loop(1, plane)
        def _(d):
            weight_copy(block, d).start()

        choice[...] = slot_choice(plane_rank_ref[block], slots)

        def slot_step(columns):
            sent_slots[step % 2, :, :, columns] = (
                matrix_product(choice[...], blocks[block, :, columns])
                .astype(BF16)
                .reshape(plane, slots, 2 * tile)
            )

        tiles(width, 2 * tile, slot_step)

        @pl.loop(1, plane)
        def _(d):
            row_copy(step, block, d).start()

        own = own_rows(step, block)
        own.start()
        own.wait()

    dispatch(0)
    for total in sums:
        total[...] = jnp.zeros_like(total)
    advance(1, (0,))
    dispatch(1)
    for each in table_copies:
        each.wait()

    def send_back(block):
        @pl.loop(1, plane)
        def _(d):
            dots_copy(block, d).start()
            back_copy(block, d).start()

        own = own_back(block)
        own.start()
        dots_back[block, me] = dots[block, me]
        own.wait()

    @pl.loop(0, line + 2)
    def _(step):
        @pl.when(step < line)
        def _():
            block = place_of(step)

            @pl.loop(1, plane)
            def _(d):
                weight_copy(block, d).wait_recv()
                row_copy(step, block, d).wait_recv()

            gates = weight_land[block, :, 0, :]
            count = gates.shape[1]
            earlier = lax.broadcasted_iota(jnp.int32, (count, count), 0)
            before = (
                (earlier < lax.broadcasted_iota(jnp.int32, (count, count), 1))
                .astype(F32)
                .astype(BF16)
            )
            held = gates >= 0.0
            ranks = jnp.where(
                held, matrix_product(held.astype(F32).astype(BF16), before), -1.0
            )
            up_copy(block).wait()

            def keep_dots(source, values):
                dots[block, source] = jnp.broadcast_to(values, (8, values.shape[1]))

            expert_math(
                tile,
                rows.at[block],
                up_rows,
                ranks,
                gates,
                keep_dots,
                lambda: y_copy(block).start(),
                mask_ref,
                tables,
                sums,
                scratch,
            )

            @pl.when(step > 0)
            def _():
                send_back(block)

            @pl.when(step == line - 1)
            def _():
                send_back(at_line)

            y_copy(block).wait()

            @pl.when(step + 1 < line)
            def _():
                up_copy(place_of(step + 1)).start()

            for late in range(2, line):

                @pl.when(step == late - 2)
                def _():
                    advance(late, (0,))
                    dispatch(late)

        @pl.when(step >= 2)
        def _():
            block = place_of(lax.rem(step - 1, line))

            @pl.loop(1, plane)
            def _(d):
                dots_copy(block, d).wait_recv()
                back_copy(block, d).wait_recv()

            dots_pass[block] = dots_back[block, :, 0, :]
            load = pltpu.make_async_copy(back_hbm.at[block], back_rows, back_sem)
            load.start()
            choice[...] = slot_choice(plane_rank_ref[block], slots)
            load.wait()

            def combined(columns):
                return flipped_left_operand(
                    choice[...], back_rows[:, :, columns].reshape(plane * slots, 2 * tile)
                )

            @pl.when(step == line + 1)
            def _():
                def keep(columns):
                    total_ref[:, columns] = combined(columns)

                tiles(width, 2 * tile, keep)
                dots_ref[at_line] = dots_pass[at_line]

            @pl.when(step < line + 1)
            def _():
                dots_in_copy(block, at_line).start()

                def pass_on(columns):
                    partials[block, :, columns] = combined(columns).astype(BF16)

                tiles(width, 2 * tile, pass_on)
                partial_copy(block, at_line).start()

    @pl.loop(1, line)
    def _(step):
        sender = place_of(step)
        dots_in_copy(sender, sender).wait_recv()
        dots_ref[sender] = dots_in[sender]
        partial_copy(sender, sender).wait_recv()
        total_ref[...] += partials_in[sender].astype(F32)

    @pl.loop(1, line)
    def _(step):
        block = place_of(step)
        partial_copy(block, at_line).wait_send()
        dots_in_copy(block, at_line).wait_send()

    finish_relay((0,), range(line - 1))
    for step in (line - 2, line - 1):

        @pl.loop(1, plane)
        def _(d):
            row_copy(step, place_of(step), d).wait_send()

    @pl.loop(0, line)
    def _(block):
        @pl.loop(1, plane)
        def _(d):
            back_copy(block, d).wait_send()
            dots_copy(block, d).wait_send()
            weight_copy(block, d).wait_send()

    for step in range(1, line):
        line_weight_copy(place_of(step), at_line).wait_send()


def moe_layer(own, up_rows, plane_ranks, weights, mask, tables, identity):
    line, plane, tokens = plane_ranks.shape
    slots, width = up_rows.shape[2:]
    hidden = tables[0].shape[1]
    sums = expert_sums(tables)
    anywhere = pl.BlockSpec(memory_space=pl.ANY)
    local = pl.BlockSpec(memory_space=pltpu.VMEM)
    grouped = (plane, slots, width)
    dma = pltpu.SemaphoreType.DMA
    return pl.pallas_call(
        staged(functools.partial(moe_body, plane, line), 2, 3),
        out_shape=[
            jax.ShapeDtypeStruct((tokens, width), F32),
            jax.ShapeDtypeStruct((line, plane, tokens), F32),
            jax.ShapeDtypeStruct((plane, line, slots, width), BF16),
            jax.ShapeDtypeStruct((line,) + grouped, BF16),
        ]
        + sums,
        in_specs=[anywhere] * (5 + len(tables)),
        out_specs=[local, local, anywhere, anywhere] + [local] * len(sums),
        scratch_shapes=[pltpu.VMEM(table.shape, table.dtype) for table in tables]
        + [
            pltpu.VMEM((line, tokens, width), BF16),
            pltpu.VMEM((line, tokens, width), BF16),
            pltpu.VMEM((line, tokens, width), BF16),
            pltpu.VMEM((2,) + grouped, BF16),
            pltpu.VMEM((line,) + grouped, BF16),
            pltpu.VMEM(grouped, BF16),
            pltpu.VMEM(grouped, BF16),
            pltpu.VMEM((plane * slots, tokens), BF16),
            pltpu.VMEM((line, plane, 8, tokens), F32),
            pltpu.VMEM((line, plane, 8, tokens), F32),
            pltpu.VMEM((line, plane, tokens), F32),
            pltpu.VMEM((line, plane, tokens), F32),
            pltpu.VMEM((line, plane, tokens), F32),
            pltpu.VMEM((line, plane, 8, tokens), F32),
            pltpu.VMEM((line, plane, 8, tokens), F32),
        ]
        + expert_scratch(plane * slots, hidden, width)
        + [dma((len(tables),)), dma, dma, dma, dma((3,))]
        + [dma((line - 1, 4))] * 4
        + [dma((line, plane))] * 4
        + [dma((line,))] * 2
        + [dma((line, plane))] * 2
        + [dma((line,))] * 4
        + [dma((line, plane))] * 2
        + staging([plane_ranks, weights, mask]),
        compiler_params=pltpu.CompilerParams(
            collective_id=identity, has_side_effects=True, vmem_limit_bytes=63 * MEBI
        ),
        name="moe_layer",
    )(own, up_rows, plane_ranks, weights, mask, *tables)


def greet_line(me, count):
    barrier = pltpu.get_barrier_semaphore()

    @pl.when(me > 0)
    def _():
        pl.semaphore_signal(barrier, inc=1, device_id={"tensor": me - 1})

    @pl.when(me < count - 1)
    def _():
        pl.semaphore_signal(barrier, inc=1, device_id={"tensor": me + 1})

    @pl.when((me > 0) & (me < count - 1))
    def _():
        pl.semaphore_wait(barrier, 2)

    @pl.when((me == 0) | (me == count - 1))
    def _():
        pl.semaphore_wait(barrier, 1)


def gather_line_body(count, chunks, *refs):
    arrays = len(chunks)
    ins, outs = refs[:arrays], refs[arrays : 2 * arrays]
    semaphores, own_sem = refs[2 * arrays : -1], refs[-1]
    me = lax.axis_index("tensor")
    advance, finish = line_relay(me, count, ins, outs, chunks, semaphores)
    greet_line(me, count)
    own = [
        pltpu.make_async_copy(ins[at], outs[at].at[me], own_sem.at[at]) for at in range(arrays)
    ]
    everything = tuple(range(arrays))
    advance(0, everything)
    for each in own:
        each.start()
    for hop in range(1, count):
        advance(hop, everything)
    for each in own:
        each.wait()
    finish(everything, range(count - 1))


def gather_line(arrays, chunks, identity):
    count = lax.axis_size("tensor")
    total = sum(chunks)
    anywhere = pl.BlockSpec(memory_space=pl.ANY)
    return pl.pallas_call(
        functools.partial(gather_line_body, count, chunks),
        out_shape=[jax.ShapeDtypeStruct((count,) + a.shape, a.dtype) for a in arrays],
        in_specs=[anywhere] * len(arrays),
        out_specs=[anywhere] * len(arrays),
        scratch_shapes=[pltpu.SemaphoreType.DMA((count - 1, total))] * 4
        + [pltpu.SemaphoreType.DMA((len(arrays),))],
        compiler_params=pltpu.CompilerParams(collective_id=identity, has_side_effects=True),
        name="gather_line",
    )(*arrays)


def sum_line_body(count, chunks, part_ref, out_ref, left_buf, right_buf, *semaphores):
    me = lax.axis_index("tensor")
    advance, finish = line_sum(
        me, count, chunks, part_ref, out_ref, left_buf, right_buf, semaphores
    )
    greet_line(me, count)
    for far in range(count - 1, 0, -1):
        advance(far)
    finish()


def sum_line(part, chunks, identity):
    count, rows, width = part.shape
    semaphores = pltpu.SemaphoreType.DMA((count - 1, chunks))
    return pl.pallas_call(
        functools.partial(sum_line_body, count, chunks),
        out_shape=jax.ShapeDtypeStruct((rows, width), F32),
        in_specs=[pl.BlockSpec(memory_space=pltpu.VMEM)],
        out_specs=pl.BlockSpec(memory_space=pltpu.VMEM),
        scratch_shapes=[
            pltpu.VMEM((count - 1, rows, width), BF16),
            pltpu.VMEM((count - 1, rows, width), BF16),
        ]
        + [semaphores] * 4,
        compiler_params=pltpu.CompilerParams(
            collective_id=identity, has_side_effects=True, vmem_limit_bytes=32 * MEBI
        ),
        name="sum_line",
    )(part)


def front_body(
    plane,
    line,
    scale,
    places,
    ready,
    tokens_hbm,
    cotangent_hbm,
    routes_hbm,
    weights_hbm,
    gain_ref,
    first_ref,
    q_second_ref,
    k_second_ref,
    v_second_ref,
    q_gain_ref,
    k_gain_ref,
    cos_ref,
    sin_ref,
    seg_column_ref,
    seg_row_ref,
    out_first_ref,
    out_second_ref,
    before_ref,
    total_ref,
    ranks_ref,
    low_ref,
    out_low_ref,
    linear_hbm,
    heads_hbm,
    normed_hbm,
    gathered_hbm,
    up_hbm,
    rows,
    upstream,
    routes,
    weights,
    linear,
    heads,
    keys,
    values,
    part,
    left_buf,
    right_buf,
    sent_slots,
    choice,
    own_sem,
    save_sem,
    relay_right_send,
    relay_right_recv,
    relay_left_send,
    relay_left_recv,
    weight_send,
    weight_recv,
    pass_send,
    pass_recv,
    sum_right_send,
    sum_right_recv,
    sum_left_send,
    sum_left_recv,
    slot_send,
    slot_recv,
):
    me, at_line = lax.axis_index("fsdp"), lax.axis_index("tensor")
    rank = q_second_ref.shape[0]
    head_dim = q_gain_ref.shape[1]
    tokens, width = tokens_hbm.shape
    slots = sent_slots.shape[2]
    tile = 256
    query_columns = q_second_ref.shape[1]
    linear_columns = linear.shape[1]
    out_start = places[1]

    greet_line_and_plane(line, plane)

    beside = me + 1 - 2 * lax.rem(me, 2)

    def weight_copy(k):
        target = lax.rem(me + 2 * k, plane)
        return pltpu.make_async_remote_copy(
            src_ref=weights_hbm,
            dst_ref=weights.at[me],
            send_sem=weight_send.at[k],
            recv_sem=weight_recv.at[k],
            device_id={"fsdp": target},
        )

    def weight_pass(k):
        origin = lax.rem(me + plane - 2 * k, plane)
        return pltpu.make_async_remote_copy(
            src_ref=weights_hbm if k == 0 else weights.at[origin],
            dst_ref=weights.at[origin],
            send_sem=pass_send.at[k],
            recv_sem=pass_recv.at[k],
            device_id={"fsdp": beside},
        )

    peers = plane // 2
    for k in range(1, peers):
        weight_copy(k).start()
    weight_pass(0).start()
    locals_in = [
        pltpu.make_async_copy(source, target, own_sem.at[at])
        for at, (source, target) in enumerate(
            [
                (tokens_hbm, rows.at[at_line]),
                (routes_hbm, routes.at[at_line]),
                (cotangent_hbm, upstream.at[at_line]),
                (weights_hbm, weights.at[me]),
            ]
        )
    ]
    advance, finish_relay = line_relay(
        at_line,
        line,
        [tokens_hbm, routes_hbm, cotangent_hbm],
        [rows, routes, upstream],
        (4, 1, 4),
        (relay_right_send, relay_right_recv, relay_left_send, relay_left_recv),
    )
    advance(0, (0, 1))
    for each in locals_in:
        each.start()
    advance(1, (0, 1))
    advance(2, (0, 1))
    advance(0, (2,))
    for k in range(1, peers):
        weight_copy(k).wait_recv()
        weight_pass(k).start()
    advance(3, (0, 1))
    for each in locals_in:
        each.wait()

    ready()

    for block in range(line):
        named = [
            jnp.max(
                (routes[block] == expert * line + at_line).astype(F32), axis=0, keepdims=True
            )
            for expert in range(plane)
        ]
        mask = jnp.concatenate(named, axis=0)
        counts = matrix_product(mask.astype(BF16), before_ref[...])
        ranks_ref[block] = jnp.where(mask > 0.0, counts, -1.0)

    def slot_copy(block, d):
        target = lax.rem(me + d, plane)
        return pltpu.make_async_remote_copy(
            src_ref=sent_slots.at[block, target],
            dst_ref=up_hbm.at[me, block],
            send_sem=slot_send.at[block, d],
            recv_sem=slot_recv.at[block, d],
            device_id={"fsdp": target},
        )

    def own_slots(block):
        return pltpu.make_async_copy(
            sent_slots.at[block, me], up_hbm.at[me, block], save_sem.at[4 + block]
        )

    def dispatch(block):
        choice[...] = slot_choice(ranks_ref[block], slots)

        def slot_step(columns):
            sent_slots[block, :, :, columns] = (
                matrix_product(choice[...], upstream[block, :, columns])
                .astype(BF16)
                .reshape(plane, slots, 2 * tile)
            )

        tiles(width, 2 * tile, slot_step)

        @pl.loop(1, plane)
        def _(d):
            slot_copy(block, d).start()

    def dispatch_at(distance):
        if distance == 0:
            dispatch(at_line)
            return

        @pl.when(at_line - distance >= 0)
        def _():
            dispatch(at_line - distance)

        @pl.when(at_line + distance < line)
        def _():
            dispatch(at_line + distance)

    dispatch_at(0)

    finish_relay((0,), range(1, line - 1))

    @pl.loop(0, line * tokens // 128)
    def _(j):
        block, at = j // (tokens // 128), pl.ds((j % (tokens // 128)) * 128, 128)
        wide = rows[block, at, :].astype(F32)
        rows[block, at, :] = norm_forward(wide, gain_ref[...])[0].astype(BF16)

    for k in range(peers):
        weight_pass(k).wait_recv()
    saves = [
        pltpu.make_async_copy(rows, normed_hbm, save_sem.at[0]),
        pltpu.make_async_copy(weights, gathered_hbm, save_sem.at[1]),
        pltpu.make_async_copy(linear, linear_hbm, save_sem.at[2]),
        pltpu.make_async_copy(heads, heads_hbm, save_sem.at[3]),
    ]
    saves[0].start()
    saves[1].start()

    @pl.loop(0, line)
    def _(block):
        at = pl.ds(pl.multiple_of(block * tokens, tokens), tokens)
        low_ref[at, :] = flipped_right_operand(rows[block], first_ref[...]).astype(BF16)

        def project(columns):
            linear[at, columns] = matrix_product(
                rows[block], weights[:, :, columns].reshape(width, tile)
            )

        tiles(linear_columns, tile, project)

    saves[2].start()
    advance(1, (2,))
    dispatch_at(1)

    cosine, sine = cos_ref[...], sin_ref[...]
    keys[...] = head_values(
        linear[:, query_columns : query_columns + head_dim],
        low_ref[:, rank : 2 * rank],
        k_second_ref[...],
        k_gain_ref[...],
        cosine,
        sine,
    )[2]
    values[...] = (
        linear[:, query_columns + head_dim : query_columns + 2 * head_dim]
        + matrix_product(low_ref[:, 2 * rank : 3 * rank], v_second_ref[...])
    ).astype(BF16)

    @pl.loop(0, query_columns // head_dim)
    def _(head):
        columns = pl.ds(pl.multiple_of(head * head_dim, head_dim), head_dim)
        query = head_values(
            linear[:, columns],
            low_ref[:, :rank],
            q_second_ref[:, columns],
            q_gain_ref[...],
            cos_ref[...],
            sin_ref[...],
        )[2]
        seg_column, seg_row = seg_column_ref[...], seg_row_ref[...]
        for block in range(query.shape[0] // WINDOW):
            start, span = block_bounds(block)
            scores = (
                flipped_right_operand(
                    query[block * WINDOW : (block + 1) * WINDOW], keys[pl.ds(start, span)]
                )
                * scale
            )
            scores = jnp.where(
                allowed_keys(block, start, span, seg_column, seg_row), scores, -1e30
            )
            expo = jnp.exp(scores - jnp.max(scores, axis=-1, keepdims=True))
            probs = (expo / jnp.sum(expo, axis=-1, keepdims=True)).astype(BF16)
            heads[pl.ds(block * WINDOW, WINDOW), columns] = matrix_product(
                probs, values[pl.ds(start, span)]
            ).astype(BF16)

    saves[3].start()
    advance(2, (2,))
    dispatch_at(2)

    out_low_ref[...] = flipped_right_operand(heads[...], out_first_ref[...]).astype(BF16)

    @pl.loop(0, line)
    def _(block):
        at = pl.ds(pl.multiple_of(block * tokens, tokens), tokens)

        @pl.loop(0, plane)
        def _(shard):
            wide = width // plane
            columns = pl.ds(pl.multiple_of(shard * wide, wide), wide)
            part[block, :, columns] = (
                flipped_right_operand(heads[at, :], weights[shard, :, out_start:])
                + matrix_product(out_low_ref[at, :], out_second_ref[:, columns])
            ).astype(BF16)

    advance_sum, finish_sum = line_sum(
        at_line,
        line,
        4,
        part,
        total_ref,
        left_buf,
        right_buf,
        (sum_right_send, sum_right_recv, sum_left_send, sum_left_recv),
    )
    for far in range(line - 1, 0, -1):
        advance_sum(far)
        if far == 2:
            advance(3, (2,))
            dispatch_at(3)
    finish_sum()

    for block in range(line):
        own_slots(block).start()
    for each in saves:
        each.wait()
    finish_relay((0,), (0,))
    finish_relay((1, 2), range(line - 1))
    for k in range(1, peers):
        weight_copy(k).wait_send()
    for k in range(peers):
        weight_pass(k).wait_send()

    @pl.loop(0, line)
    def _(block):
        @pl.loop(1, plane)
        def _(d):
            slot_copy(block, d).wait_recv()
            slot_copy(block, d).wait_send()

    for block in range(line):
        own_slots(block).wait()


def front(
    tokens,
    cotangent,
    routes,
    packed,
    gain,
    first,
    q_second,
    k_second,
    v_second,
    q_gain,
    k_gain,
    tables,
    seg_column,
    seg_row,
    out_first,
    out_second,
    scale,
    slots,
    places,
    identity,
):
    line, plane = lax.axis_size("tensor"), lax.axis_size("fsdp")
    count, width = tokens.shape
    all_rows = line * count
    rank, query_columns = q_second.shape
    head_dim = q_gain.shape[1]
    linear_columns = query_columns + 2 * head_dim
    order = jnp.arange(count, dtype=jnp.int32)
    before = (order[:, None] < order[None, :]).astype(BF16)
    anywhere = pl.BlockSpec(memory_space=pl.ANY)
    local = pl.BlockSpec(memory_space=pltpu.VMEM)
    dma = pltpu.SemaphoreType.DMA
    up_shape = (plane, line, slots, width)
    operands = [
        gain,
        first,
        q_second,
        k_second,
        v_second,
        q_gain,
        k_gain,
        *tables,
        seg_column,
        seg_row,
        out_first,
        out_second,
        before,
    ]
    return pl.pallas_call(
        staged(
            functools.partial(front_body, plane, line, scale, places), 4, len(operands)
        ),
        out_shape=[
            jax.ShapeDtypeStruct((count, width), F32),
            jax.ShapeDtypeStruct((line, plane, count), F32),
            jax.ShapeDtypeStruct((all_rows, 3 * rank), BF16),
            jax.ShapeDtypeStruct((all_rows, rank), BF16),
            jax.ShapeDtypeStruct((all_rows, linear_columns), F32),
            jax.ShapeDtypeStruct((all_rows, query_columns), BF16),
            jax.ShapeDtypeStruct((line, count, width), BF16),
            jax.ShapeDtypeStruct((plane,) + packed.shape, BF16),
            jax.ShapeDtypeStruct(up_shape, BF16),
        ],
        in_specs=[anywhere] * (4 + len(operands)),
        out_specs=[local] * 4 + [anywhere] * 5,
        scratch_shapes=[
            pltpu.VMEM((line, count, width), BF16),
            pltpu.VMEM((line, count, width), BF16),
            pltpu.VMEM((line,) + routes.shape, jnp.int32),
            pltpu.VMEM((plane,) + packed.shape, BF16),
            pltpu.VMEM((all_rows, linear_columns), F32),
            pltpu.VMEM((all_rows, query_columns), BF16),
            pltpu.VMEM((all_rows, head_dim), BF16),
            pltpu.VMEM((all_rows, head_dim), BF16),
            pltpu.VMEM((line, count, width), BF16),
            pltpu.VMEM((line - 1, count, width), BF16),
            pltpu.VMEM((line - 1, count, width), BF16),
            pltpu.VMEM((line, plane, slots, width), BF16),
            pltpu.VMEM((plane * slots, count), BF16),
            dma((4,)),
            dma((4 + line,)),
        ]
        + [dma((line - 1, 9))] * 4
        + [dma((plane // 2,))] * 4
        + [dma((line - 1, 4))] * 4
        + [dma((line, plane))] * 2
        + staging(operands),
        compiler_params=pltpu.CompilerParams(
            collective_id=identity, has_side_effects=True, vmem_limit_bytes=63 * MEBI
        ),
        name="front",
    )(tokens, cotangent, routes, packed, *operands)


def back_body(
    plane,
    line,
    scale,
    places,
    moe_total_ref,
    dots_ref,
    gates_ref,
    residual_ref,
    cotangent_ref,
    moe_gain_ref,
    router_first_ref,
    router_second_ref,
    router_low_ref,
    moe_rows_ref,
    ranks_ref,
    low_ref,
    out_low_ref,
    first_out_ref,
    second_out_ref,
    q_second_ref,
    k_second_ref,
    v_second_ref,
    q_gain_ref,
    k_gain_ref,
    cos_ref,
    sin_ref,
    seg_column_ref,
    seg_row_ref,
    linear_hbm,
    heads_hbm,
    normed_hbm,
    gathered_hbm,
    y_hbm,
    output_ref,
    residual_grad_ref,
    share_ref,
    linear_grad_ref,
    owned_ref,
    y_in_hbm,
    branch_own,
    branch,
    out_weights,
    router_weights,
    linear,
    heads,
    normed,
    upstream,
    out_low_grad,
    keys,
    values,
    key_sum,
    value_sum,
    query_sum,
    share_sum,
    second_sum,
    y_rows,
    partials,
    left_buf,
    right_buf,
    result,
    choice,
    rows_out_ref,
    heads_out_ref,
    narrow_out_ref,
    router_out_ref,
    load_sem,
    y_sem,
    relay_right_send,
    relay_right_recv,
    relay_left_send,
    relay_left_recv,
    y_send,
    y_recv,
    sum_right_send,
    sum_right_recv,
    sum_left_send,
    sum_left_recv,
):
    me, at_line = lax.axis_index("fsdp"), lax.axis_index("tensor")
    tokens, width = residual_ref.shape
    rank, query_columns = q_second_ref.shape
    head_dim = q_gain_ref.shape[1]
    slots = y_rows.shape[1]
    tile = 256

    greet_line_and_plane(line, plane)

    orders = [sorted(range(line), key=lambda block: abs(block - at)) for at in range(line)]

    def place_of(step):
        result = 0
        for at in range(line):
            result = jnp.where(at_line == at, orders[at][step], result)
        return result

    def y_copy(block, d):
        target = lax.rem(me + d, plane)
        return pltpu.make_async_remote_copy(
            src_ref=y_hbm.at[target, block],
            dst_ref=y_in_hbm.at[block, me],
            send_sem=y_send.at[block, d],
            recv_sem=y_recv.at[block, d],
            device_id={"fsdp": target},
        )

    def own_y(block):
        return pltpu.make_async_copy(
            y_hbm.at[me, block], y_in_hbm.at[block, me], y_sem.at[block]
        )

    def send_y(step):
        block = place_of(step)

        @pl.loop(1, plane)
        def _(d):
            y_copy(block, d).start()

        own_y(block).start()

    send_y(line - 1)
    send_y(line - 2)
    advance_sum, finish_sum = line_sum(
        at_line,
        line,
        4,
        partials,
        result,
        left_buf,
        right_buf,
        (sum_right_send, sum_right_recv, sum_left_send, sum_left_recv),
    )
    loads = [
        pltpu.make_async_copy(source, target, load_sem.at[at])
        for at, (source, target) in enumerate(
            [
                (
                    gathered_hbm.at[:, :, pl.ds(places[0], places[1] - places[0])],
                    router_weights,
                ),
                (gathered_hbm.at[:, :, pl.ds(places[1], query_columns)], out_weights),
                (linear_hbm, linear),
                (heads_hbm, heads),
                (normed_hbm, normed),
            ]
        )
    ]
    for each in loads:
        each.start()

    def combine(step):
        block = place_of(step)

        @pl.loop(1, plane)
        def _(d):
            y_copy(block, d).wait_recv()

        own_y(block).wait()
        if step > 1:
            send_y(step - 2)
        load = pltpu.make_async_copy(y_in_hbm.at[block], y_rows, y_sem.at[line])
        load.start()
        choice[...] = slot_choice(ranks_ref[block], slots)
        load.wait()

        def combined(columns):
            total = flipped_left_operand(
                choice[...], y_rows[:, :, columns].reshape(plane * slots, 2 * tile)
            )
            partials[block, :, columns] = total.astype(BF16)

        tiles(width, 2 * tile, combined)
        if step > 0:
            advance_sum(step)

    loads[0].wait()
    router_ref = router_weights[...].reshape(width, -1)
    gates = gates_ref[...]
    dots = dots_ref[...]
    logit_grad = (gates * (dots - jnp.sum(gates * dots, axis=0, keepdims=True))).astype(BF16)
    experts_count, lanes = gates.shape[0], router_ref.shape[1]
    wide_logit_grad = jnp.transpose(
        jnp.concatenate(
            [
                logit_grad.astype(F32),
                jnp.zeros((lanes - experts_count, tokens), F32),
            ],
            axis=0,
        ),
        (1, 0),
    ).astype(BF16)
    router_low_grad = matrix_product(
        router_second_ref[:, :experts_count], logit_grad
    ).astype(BF16)
    rows_out_ref[4 * rank :, :] = matrix_product(router_low_grad, moe_rows_ref[...]).astype(BF16)
    router_out_ref[...] = flipped_right_operand(router_low_ref[...], logit_grad)
    half = tokens // 2
    for part in range(2):
        rows = pl.ds(part * half, half)
        columns = slice(part * half, (part + 1) * half)
        moe_grad = (
            moe_total_ref[rows, :]
            + flipped_right_operand(wide_logit_grad[columns], router_ref)
            + flipped_left_operand(router_low_grad[:, columns], router_first_ref[...])
        )
        residual = residual_ref[rows, :]
        factor = lax.rsqrt(
            jnp.mean(residual * residual, axis=-1, keepdims=True) + NORM_EPSILON
        )
        residual_grad = cotangent_ref[rows, :].astype(F32) + norm_backward(
            residual, factor, moe_gain_ref[...], moe_grad
        )
        residual_grad_ref[rows, :] = residual_grad
        branch_own[rows, :] = residual_grad.astype(BF16)
    branch[at_line] = branch_own[...]

    advance, finish_relay = line_relay(
        at_line,
        line,
        [branch_own],
        [branch],
        (4,),
        (relay_right_send, relay_right_recv, relay_left_send, relay_left_recv),
    )
    advance(0, (0,))
    second_sum[...] = jnp.zeros_like(second_sum)
    loads[1].wait()

    def head_gradients(block):
        at = pl.ds(pl.multiple_of(block * tokens, tokens), tokens)
        low_grad = flipped_right_operand(branch[block], second_out_ref[...]).astype(BF16)
        out_low_grad[at, :] = low_grad
        second_sum[...] += flipped_left_operand(out_low_ref[at, :], branch[block])

        def project(columns):
            upstream[at, columns] = (
                matrix_product(branch[block], out_weights[:, :, columns].reshape(width, tile))
                + matrix_product(low_grad, first_out_ref[:, columns])
            ).astype(BF16)

        tiles(query_columns, tile, project)

    head_gradients(at_line)
    for each in loads[2:]:
        each.wait()
    cosine, sine = cos_ref[...], sin_ref[...]
    key_columns = slice(query_columns, query_columns + head_dim)
    value_columns = slice(query_columns + head_dim, query_columns + 2 * head_dim)
    keys[...] = head_values(
        linear[:, key_columns],
        low_ref[:, rank : 2 * rank],
        k_second_ref[...],
        k_gain_ref[...],
        cosine,
        sine,
    )[2]
    values[...] = (
        linear[:, value_columns]
        + matrix_product(low_ref[:, 2 * rank : 3 * rank], v_second_ref[...])
    ).astype(BF16)
    key_sum[...] = jnp.zeros_like(key_sum)
    value_sum[...] = jnp.zeros_like(value_sum)
    share_sum[...] = jnp.zeros_like(share_sum)
    for hop in range(1, line):
        advance(hop, (0,))

        @pl.when(at_line - hop >= 0)
        def _():
            head_gradients(at_line - hop)

        @pl.when(at_line + hop < line)
        def _():
            head_gradients(at_line + hop)

        if hop < line - 1:
            combine(line - hop)
    rows_out_ref[3 * rank : 4 * rank, :] = second_sum[...].astype(BF16)

    head_count = query_columns // head_dim

    @pl.loop(0, head_count)
    def _(head):
        columns = pl.ds(pl.multiple_of(head * head_dim, head_dim), head_dim)
        low_q = low_ref[:, :rank]
        lines, factor, query = head_values(
            linear[:, columns],
            low_q,
            q_second_ref[:, columns],
            q_gain_ref[...],
            cos_ref[...],
            sin_ref[...],
        )
        heads_out_ref[rank:, columns] = flipped_left_operand(
            out_low_grad[...], heads[:, columns]
        ).astype(BF16)
        seg_column, seg_row = seg_column_ref[...], seg_row_ref[...]
        for block in range(query.shape[0] // WINDOW):
            start, span = block_bounds(block)
            at, near = pl.ds(block * WINDOW, WINDOW), pl.ds(start, span)
            query_block = query[block * WINDOW : (block + 1) * WINDOW]
            upstream_block = upstream[at, columns]
            scores = flipped_right_operand(query_block, keys[near]) * scale
            scores = jnp.where(
                allowed_keys(block, start, span, seg_column, seg_row), scores, -1e30
            )
            expo = jnp.exp(scores - jnp.max(scores, axis=-1, keepdims=True))
            probs = expo / jnp.sum(expo, axis=-1, keepdims=True)
            prob_grad = flipped_right_operand(upstream_block, values[near])
            score_grad = (
                probs * (prob_grad - jnp.sum(probs * prob_grad, axis=-1, keepdims=True))
            ).astype(BF16)
            value_sum[near, :] += flipped_left_operand(probs.astype(BF16), upstream_block)
            key_sum[near, :] += flipped_left_operand(score_grad, query_block)
            query_sum[at, :] = matrix_product(score_grad, keys[near]) * scale
        q_grad = head_values_gradient(
            lines, factor, q_gain_ref[...], cos_ref[...], sin_ref[...], query_sum[...]
        )
        linear_grad_ref[:, columns] = q_grad
        heads_out_ref[:rank, columns] = flipped_left_operand(low_q, q_grad).astype(BF16)
        share_sum[:, :rank] += flipped_right_operand(q_grad, q_second_ref[:, columns])

        @pl.when(head == head_count // 2 - 1)
        def _():
            combine(1)

    low_k = low_ref[:, rank : 2 * rank]
    low_v = low_ref[:, 2 * rank : 3 * rank]
    key_lines, key_factor, _turned = head_values(
        linear[:, key_columns], low_k, k_second_ref[...], k_gain_ref[...], cosine, sine
    )
    k_grad = head_values_gradient(
        key_lines, key_factor, k_gain_ref[...], cosine, sine, key_sum[...] * scale
    )
    v_grad = value_sum[...].astype(BF16)
    linear_grad_ref[:, key_columns] = k_grad
    linear_grad_ref[:, value_columns] = v_grad
    narrow_out_ref[:rank, :] = flipped_left_operand(low_k, k_grad).astype(BF16)
    narrow_out_ref[rank:, :] = flipped_left_operand(low_v, v_grad).astype(BF16)
    share_sum[:, rank : 2 * rank] = flipped_right_operand(k_grad, k_second_ref[...])
    share_sum[:, 2 * rank :] = flipped_right_operand(v_grad, v_second_ref[...])
    share_ref[...] = share_sum[...].astype(BF16)

    def first_gradient(columns):
        rows_out_ref[: 3 * rank, columns] = flipped_left_operand(
            share_ref[...], normed[:, columns]
        ).astype(BF16)

    tiles(width, 2 * tile, first_gradient)

    pieces, lines, lanes_out = owned_ref.shape
    row_lines, span = rows_out_ref.shape[0], width // pieces
    owned_ref[...] = jnp.zeros_like(owned_ref)
    for piece in range(pieces):
        owned_ref[piece, :row_lines, :span] = rows_out_ref[:, piece * span : (piece + 1) * span]
        at = (piece % line) * plane + piece // line
        owned_ref[piece, :rank, span : span + 1] = router_out_ref[:, at : at + 1].astype(BF16)
    narrow_span = head_dim // plane
    for piece in range(plane):
        owner = at_line * plane + piece
        owned_ref[owner, row_lines:, :] = heads_out_ref[
            :, piece * lanes_out : (piece + 1) * lanes_out
        ]
        owned_ref[owner, : 2 * rank, span + rank : span + rank + narrow_span] = narrow_out_ref[
            :, piece * narrow_span : (piece + 1) * narrow_span
        ]
    combine(0)
    finish_sum()
    output_ref[...] = (residual_ref[...] + result[...]).astype(BF16)
    finish_relay((0,), range(line - 1))
    for block in range(line):

        @pl.loop(1, plane)
        def _(d):
            y_copy(block, d).wait_send()


def back(scale, places, slots, identity, hbm_operands, operands):
    line, plane = lax.axis_size("tensor"), lax.axis_size("fsdp")
    linear, heads, normed, gathered, _y = hbm_operands
    count, width = operands[0].shape
    all_rows, linear_columns = linear.shape
    query_columns = heads.shape[1]
    head_dim = (linear_columns - query_columns) // 2
    rank = operands[12].shape[1]
    experts_count = line * plane
    anywhere = pl.BlockSpec(memory_space=pl.ANY)
    local = pl.BlockSpec(memory_space=pltpu.VMEM)
    dma = pltpu.SemaphoreType.DMA
    single = (all_rows, head_dim)
    block = (count, width)
    return pl.pallas_call(
        functools.partial(back_body, plane, line, scale, places),
        out_shape=[
            jax.ShapeDtypeStruct(block, BF16),
            jax.ShapeDtypeStruct(block, F32),
            jax.ShapeDtypeStruct((all_rows, 3 * rank), BF16),
            jax.ShapeDtypeStruct((all_rows, linear_columns), BF16),
            jax.ShapeDtypeStruct((experts_count, 7 * rank, head_dim), BF16),
            jax.ShapeDtypeStruct((line, plane, slots, width), BF16),
        ],
        in_specs=[local] * len(operands) + [anywhere] * len(hbm_operands),
        out_specs=[local] * 5 + [anywhere],
        scratch_shapes=[
            pltpu.VMEM(block, BF16),
            pltpu.VMEM((line,) + block, BF16),
            pltpu.VMEM((plane, width // plane, query_columns), BF16),
            pltpu.VMEM((plane, width // plane, places[1] - places[0]), BF16),
            pltpu.VMEM((all_rows, linear_columns), F32),
            pltpu.VMEM((all_rows, query_columns), BF16),
            pltpu.VMEM((all_rows, width), BF16),
            pltpu.VMEM((all_rows, query_columns), BF16),
            pltpu.VMEM((all_rows, rank), BF16),
            pltpu.VMEM(single, BF16),
            pltpu.VMEM(single, BF16),
            pltpu.VMEM(single, F32),
            pltpu.VMEM(single, F32),
            pltpu.VMEM(single, F32),
            pltpu.VMEM((all_rows, 3 * rank), F32),
            pltpu.VMEM((rank, width), F32),
            pltpu.VMEM((plane, slots, width), BF16),
            pltpu.VMEM((line,) + block, BF16),
            pltpu.VMEM((line - 1,) + block, BF16),
            pltpu.VMEM((line - 1,) + block, BF16),
            pltpu.VMEM(block, F32),
            pltpu.VMEM((plane * slots, count), BF16),
            pltpu.VMEM((5 * rank, width), BF16),
            pltpu.VMEM((2 * rank, query_columns), BF16),
            pltpu.VMEM((2 * rank, head_dim), BF16),
            pltpu.VMEM((rank, experts_count), F32),
            dma((5,)),
            dma((line + 1,)),
        ]
        + [dma((line - 1, 4))] * 4
        + [dma((line, plane))] * 2
        + [dma((line - 1, 4))] * 4,
        compiler_params=pltpu.CompilerParams(
            collective_id=identity, has_side_effects=True, vmem_limit_bytes=63 * MEBI
        ),
        name="back",
    )(*operands, *hbm_operands)


def last_body(
    line,
    ready,
    linear_grad_ref,
    share_ref,
    first_ref,
    residual_grad_ref,
    tokens_ref,
    gain_ref,
    gathered_hbm,
    input_grad_ref,
    weights,
    part,
    left_buf,
    right_buf,
    load_sem,
    *semaphores,
):
    at_line = lax.axis_index("tensor")
    tokens, width = tokens_ref.shape
    linear_columns = linear_grad_ref.shape[1]
    load = pltpu.make_async_copy(
        gathered_hbm.at[:, :, pl.ds(0, linear_columns)], weights, load_sem
    )
    load.start()
    greet_line(at_line, line)
    ready()
    load.wait()
    shards, wide = weights.shape[:2]

    def normed_gradient(block):
        at = pl.ds(pl.multiple_of(block * tokens, tokens), tokens)

        @pl.loop(0, shards)
        def _(shard):
            columns = pl.ds(pl.multiple_of(shard * wide, wide), wide)
            part[block, :, columns] = (
                flipped_right_operand(linear_grad_ref[at, :], weights[shard])
                + matrix_product(share_ref[at, :], first_ref[:, columns])
            ).astype(BF16)

    advance, finish = line_sum(
        at_line, line, 4, part, input_grad_ref, left_buf, right_buf, semaphores
    )
    for far in range(line - 1, 0, -1):

        @pl.when(at_line + far < line)
        def _():
            normed_gradient(at_line + far)

        @pl.when(at_line - far >= 0)
        def _():
            normed_gradient(at_line - far)

        advance(far)
    normed_gradient(at_line)
    finish()
    half = tokens // 2
    for at in range(2):
        rows = pl.ds(at * half, half)
        values = tokens_ref[rows, :].astype(F32)
        factor = lax.rsqrt(jnp.mean(values * values, axis=-1, keepdims=True) + NORM_EPSILON)
        input_grad_ref[rows, :] = residual_grad_ref[rows, :] + norm_backward(
            values, factor, gain_ref[...], input_grad_ref[rows, :]
        )


def last(linear_grad, share, first, residual_grad, tokens, gain, gathered, identity):
    line = lax.axis_size("tensor")
    count, width = tokens.shape
    anywhere = pl.BlockSpec(memory_space=pl.ANY)
    local = pl.BlockSpec(memory_space=pltpu.VMEM)
    dma = pltpu.SemaphoreType.DMA
    operands = [linear_grad, share, first, residual_grad, tokens, gain]
    return pl.pallas_call(
        staged(functools.partial(last_body, line), 0, 6),
        out_shape=jax.ShapeDtypeStruct((count, width), F32),
        in_specs=[anywhere] * 7,
        out_specs=local,
        scratch_shapes=[
            pltpu.VMEM(gathered.shape[:2] + (linear_grad.shape[1],), BF16),
            pltpu.VMEM((line, count, width), BF16),
            pltpu.VMEM((line - 1, count, width), BF16),
            pltpu.VMEM((line - 1, count, width), BF16),
            dma,
        ]
        + [dma((line - 1, 4))] * 4
        + staging(operands),
        compiler_params=pltpu.CompilerParams(
            collective_id=identity, has_side_effects=True, vmem_limit_bytes=63 * MEBI
        ),
        name="last",
    )(*operands, gathered)


def prepare_body(
    _adapters_ref,
    _place_ref,
    query_in_ref,
    key_in_ref,
    value_in_ref,
    query_out_ref,
    key_out_ref,
    value_out_ref,
    attn_in_ref,
    attn_out_ref,
    router_in_ref,
    router_out_ref,
    w_query_ref,
    w_key_ref,
    w_value_ref,
    w_router_ref,
    w_out_ref,
    order_ref,
    segments_ref,
    first_ref,
    q_second_ref,
    k_second_ref,
    v_second_ref,
    out_first_ref,
    out_second_ref,
    router_first_ref,
    router_second_ref,
    packed_ref,
    seg_column_ref,
):
    rank = query_in_ref.shape[1]
    for at, ref in enumerate((query_in_ref, key_in_ref, value_in_ref)):
        first_ref[at * rank : (at + 1) * rank, :] = ref[0]
    q_second_ref[...] = query_out_ref[0]
    k_second_ref[...] = key_out_ref[0]
    v_second_ref[...] = value_out_ref[0]
    out_first_ref[...] = attn_in_ref[0]
    out_second_ref[...] = attn_out_ref[0]
    router_first_ref[...] = router_in_ref[0]
    router_second_ref[...] = matrix_product(router_out_ref[0], order_ref[...]).astype(BF16)
    start = 0
    for ref in (w_query_ref, w_key_ref, w_value_ref):
        width = ref.shape[1]
        packed_ref[:, start : start + width] = ref[...]
        start += width
    width = order_ref.shape[1]
    packed_ref[:, start : start + width] = flipped_left_operand(
        w_router_ref[...], order_ref[...]
    ).astype(BF16)
    start += width
    for at in range(0, w_out_ref.shape[0], 256):
        packed_ref[:, start + at : start + at + 256] = jnp.transpose(
            w_out_ref[at : at + 256, :], (1, 0)
        )
    marks = jnp.broadcast_to(segments_ref[...].astype(F32), (8, segments_ref.shape[1]))
    seg_column_ref[...] = jnp.transpose(marks, (1, 0))[:, :1].astype(jnp.int32)


def prepare(adapters, place, tables, weights, order, segments):
    def chosen(table):
        return pl.BlockSpec(
            (1,) + table.shape[1:], lambda _, adapter, at: (adapter[at[0]], 0, 0)
        )

    def resident(shape):
        return pl.BlockSpec(tuple(shape), lambda *_: (0,) * len(shape))

    rank = tables[0].shape[1]
    columns = sum(w.shape[1] for w in weights[:3]) + order.shape[1] + weights[4].shape[0]
    shapes = [
        ((3 * rank, tables[0].shape[2]), BF16),
        (tables[3].shape[1:], BF16),
        (tables[4].shape[1:], BF16),
        (tables[5].shape[1:], BF16),
        (tables[6].shape[1:], BF16),
        (tables[7].shape[1:], BF16),
        (tables[8].shape[1:], BF16),
        ((rank, order.shape[1]), BF16),
        ((weights[0].shape[0], columns), BF16),
        ((segments.shape[1], 1), jnp.int32),
    ]
    return pl.pallas_call(
        prepare_body,
        grid_spec=pltpu.PrefetchScalarGridSpec(
            num_scalar_prefetch=2,
            grid=(1,),
            in_specs=[chosen(table) for table in tables]
            + [resident(w.shape) for w in weights]
            + [resident(order.shape), resident(segments.shape)],
            out_specs=[resident(shape) for shape, _ in shapes],
        ),
        out_shape=[jax.ShapeDtypeStruct(shape, dtype) for shape, dtype in shapes],
        compiler_params=params(63),
        name="prepare",
    )(adapters, place, *tables, *weights, order, segments)


def router_body(
    line,
    total_ref,
    tokens_ref,
    gain_ref,
    weights_ref,
    first_ref,
    second_ref,
    routes_ref,
    residual_ref,
    rows_ref,
    gates_ref,
    sent_ref,
    low_ref,
):
    count, width = tokens_ref.shape
    residual = total_ref[...] + tokens_ref[...].astype(F32)
    residual_ref[...] = residual
    rows_ref[...] = norm_forward(residual, gain_ref[...])[0].astype(BF16)
    low_ref[...] = flipped_right_operand(first_ref[...], rows_ref[...]).astype(BF16)
    logits = matrix_product(rows_ref[...], weights_ref[...].reshape(width, -1))
    logits = jnp.transpose(logits, (1, 0)) + flipped_left_operand(second_ref[...], low_ref[...])
    experts_count = gates_ref.shape[0]
    plane = experts_count // line
    logits = logits[:experts_count]
    at = lax.broadcasted_iota(jnp.int32, (experts_count, count), 0)
    names = (at % plane) * line + at // plane
    chosen = jnp.zeros((experts_count, count), jnp.bool_)
    for k in range(routes_ref.shape[0]):
        chosen = chosen | (names == routes_ref[k : k + 1, :])
    peak = jnp.max(jnp.where(chosen, logits, -jnp.inf), axis=0, keepdims=True)
    expo = jnp.where(chosen, jnp.exp(jnp.where(chosen, logits - peak, 0.0)), 0.0)
    gates = expo / jnp.sum(expo, axis=0, keepdims=True)
    gates_ref[...] = gates
    sent = jnp.where(chosen, gates, -1.0)
    for group in range(line):
        sent_ref[group] = sent[group * plane : (group + 1) * plane]


def router(total, tokens, gain, gathered, column, first, second, routes):
    line, plane = lax.axis_size("tensor"), lax.axis_size("fsdp")
    count, width = tokens.shape
    lanes = second.shape[1]

    def resident(shape):
        return pl.BlockSpec(tuple(shape), lambda *_: (0,) * len(shape))

    shapes = [
        ((count, width), F32),
        ((count, width), BF16),
        ((line * plane, count), F32),
        ((line, plane, count), F32),
        ((first.shape[0], count), BF16),
    ]
    return pl.pallas_call(
        functools.partial(router_body, line),
        grid=(1,),
        in_specs=[
            resident(total.shape),
            resident(tokens.shape),
            resident(gain.shape),
            pl.BlockSpec(gathered.shape[:2] + (lanes,), lambda _: (0, 0, column // lanes)),
            resident(first.shape),
            resident(second.shape),
            resident(routes.shape),
        ],
        out_specs=[resident(shape) for shape, _ in shapes],
        out_shape=[jax.ShapeDtypeStruct(shape, dtype) for shape, dtype in shapes],
        compiler_params=params(63),
        name="router",
    )(total, tokens, gain, gathered, first, second, routes)


def owners_body(spans, adapters_ref, pieces_ref, *refs):
    outs, total = refs[:-1], refs[-1]
    span, narrow_span = spans
    sources = adapters_ref.shape[0]
    group = pieces_ref.shape[0] // sources
    rank = outs[0].shape[1]
    total[...] = jnp.zeros_like(total)

    @pl.loop(0, sources)
    def _(source):
        addend = pieces_ref[source * group].astype(F32)
        for at in range(1, group):
            addend = addend + pieces_ref[source * group + at].astype(F32)
        total[adapters_ref[source]] += addend

    for at in range(5):
        outs[at][...] = total[:, at * rank : (at + 1) * rank, :span]
    outs[5][...] = total[:, :rank, span : span + 1]
    outs[6][...] = total[:, 5 * rank : 6 * rank, :]
    outs[7][...] = total[:, 6 * rank :, :]
    columns = slice(span + rank, span + rank + narrow_span)
    outs[8][...] = total[:, :rank, columns]
    outs[9][...] = total[:, rank : 2 * rank, columns]


def owners(adapters, pieces, adapter_count, rank, span, narrow_span):
    lanes = pieces.shape[2]
    shapes = (
        [(adapter_count, rank, span)] * 5
        + [(adapter_count, rank, 1)]
        + [(adapter_count, rank, lanes)] * 2
        + [(adapter_count, rank, narrow_span)] * 2
    )

    def resident(shape):
        return pl.BlockSpec(tuple(shape), lambda *_: (0,) * len(shape))

    return pl.pallas_call(
        functools.partial(owners_body, (span, narrow_span)),
        grid_spec=pltpu.PrefetchScalarGridSpec(
            num_scalar_prefetch=1,
            grid=(1,),
            in_specs=[resident(pieces.shape)],
            out_specs=[resident(shape) for shape in shapes],
            scratch_shapes=[pltpu.VMEM((adapter_count,) + pieces.shape[1:], F32)],
        ),
        out_shape=[jax.ShapeDtypeStruct(shape, F32) for shape in shapes],
        compiler_params=params(63),
        name="owners",
    )(adapters, pieces)


def per_device(
    tokens,
    segments,
    routes,
    adapter_index,
    cotangent,
    attn_gain,
    moe_gain,
    q_gain,
    key_norm_gain,
    w_query,
    key_projection_weight,
    value_projection_weight,
    w_out,
    w_router,
    expert_gate_weight,
    expert_up_weight,
    expert_down_weight,
    query_in,
    query_out,
    key_in,
    key_second_weight,
    value_in,
    value_second_weight,
    attn_in,
    attn_out,
    router_in,
    router_out,
    gate_in,
    gate_out,
    upward_in,
    upward_out,
    downward_in,
    downward_out,
):
    tensor_count = lax.axis_size("tensor")
    fsdp_count = lax.axis_size("fsdp")
    device_count = fsdp_count * tensor_count
    tensor_pos = lax.axis_index("tensor")
    fsdp_pos = lax.axis_index("fsdp")
    zero_pos = fsdp_pos * 0
    tok_rows, model_width = tokens.shape
    seq_rows = tok_rows * tensor_count
    rank = query_in.shape[2]
    adapter_count = query_in.shape[0]
    head_dim = q_gain.shape[0]
    local_cols = query_out.shape[2]
    local_kv_cols = key_second_weight.shape[2]
    expert_count = w_router.shape[1]
    top_count = routes.shape[1]
    capacity = 5 * tok_rows * top_count // (4 * expert_count)
    slots = -(-capacity // 16) * 16
    score_scale = 1.0 / math.sqrt(head_dim)
    adapter_pick = lax.dynamic_index_in_dim(adapter_index, fsdp_pos, 0, keepdims=False)

    def select_adapter(adapter_table):
        return lax.dynamic_index_in_dim(adapter_table, adapter_pick, 0, keepdims=False)

    def transposed(adapter_table):
        return jnp.swapaxes(adapter_table, -1, -2)

    gain_attn = attn_gain.astype(F32)
    gain_moe = moe_gain.astype(F32)
    gain_query = q_gain.astype(F32)[None, :]
    gain_key = key_norm_gain.astype(F32)[None, :]

    in_kernel = fsdp_count * slots <= 640
    linear_cols = local_cols + 2 * local_kv_cols
    router_pad = -(-expert_count // 128) * 128
    out_start = linear_cols + router_pad
    tables = rope_tables(seq_rows, head_dim)
    seg_row = segments
    routes_t = jnp.transpose(routes, (1, 0))
    if in_kernel:
        expert_order = np.zeros((expert_count, router_pad), np.float32)
        places = np.arange(expert_count)
        expert_order[
            (places % fsdp_count) * tensor_count + places // fsdp_count, places
        ] = 1.0
        (
            input_first,
            q_second,
            k_second,
            v_second,
            attention_first,
            attention_second,
            router_first,
            router_second,
            packed,
            seg_column,
        ) = prepare(
            adapter_index,
            fsdp_pos[None],
            [
                transposed(query_in),
                transposed(key_in),
                transposed(value_in),
                query_out,
                key_second_weight,
                value_second_weight,
                transposed(attn_in),
                attn_out,
                transposed(router_in),
                router_out,
            ],
            [
                w_query,
                key_projection_weight,
                value_projection_weight,
                jnp.transpose(w_router, (1, 0)),
                w_out,
            ],
            jnp.asarray(expert_order, BF16),
            segments,
        )
    else:
        input_first = jnp.concatenate(
            [select_adapter(transposed(table)) for table in (query_in, key_in, value_in)], axis=0
        )
        q_second = select_adapter(query_out)
        k_second = select_adapter(key_second_weight)
        v_second = select_adapter(value_second_weight)
        attention_first = select_adapter(transposed(attn_in))
        attention_second = select_adapter(attn_out)
        router_first = select_adapter(transposed(router_in))
        router_second = select_adapter(router_out)
        packed = jnp.concatenate(
            [
                w_query,
                key_projection_weight,
                value_projection_weight,
                jnp.pad(w_router, ((0, 0), (0, router_pad - expert_count))),
                jnp.transpose(w_out, (1, 0)),
            ],
            axis=1,
        )
        seg_column = jnp.transpose(segments, (1, 0))
    token_values = tokens.astype(F32)
    attn_normed, attn_factor = norm_forward(token_values, gain_attn)
    offsets = [0] + [sign * step for step in range(1, tensor_count) for sign in (1, -1)]
    offsets = [offset % tensor_count for offset in offsets[:tensor_count]]
    line_blocks = [((tensor_pos + offset) % tensor_count)[None] for offset in offsets]

    def fetched(block, offset):
        if offset == 0:
            return block
        pairs = [((at + offset) % tensor_count, at) for at in range(tensor_count)]
        return lax.ppermute(block, "tensor", pairs)

    def delivered(block, offset):
        if offset == 0:
            return block
        pairs = [(at, (at + offset) % tensor_count) for at in range(tensor_count)]
        return lax.ppermute(block, "tensor", pairs)

    def dispatched(block):
        return [
            plane_rows(to_slots(at, plane_ranks, fetched(block, offset), slots))
            for offset, at in zip(offsets, line_blocks)
        ]

    if in_kernel:
        (
            attention_total,
            plane_ranks,
            low,
            attention_low,
            linear,
            heads_narrow,
            sequence_normalized,
            gathered,
            up_rows,
        ) = front(
            tokens,
            cotangent,
            routes_t,
            packed,
            gain_attn[None, :],
            input_first,
            q_second,
            k_second,
            v_second,
            gain_query,
            gain_key,
            tables,
            seg_column,
            seg_row,
            attention_first,
            attention_second,
            score_scale,
            slots,
            (linear_cols, out_start),
            0,
        )
        sequence_normalized = sequence_normalized.reshape(seq_rows, model_width)
    else:
        gathered = lax.all_gather(packed, "fsdp", axis=0, tiled=True)
        sequence_tokens, sequence_routes = gather_line(
            [tokens, jnp.transpose(routes, (1, 0))], (4, 1), 0
        )
        sequence_tokens = sequence_tokens.reshape(seq_rows, model_width)
        plane_experts = jnp.arange(fsdp_count, dtype=jnp.int32) * tensor_count + tensor_pos
        plane_ranks = ranks_of(
            jnp.any(
                sequence_routes[:, None, :, :] == plane_experts[None, :, None, None], axis=2
            )
        )
        up_rows = dispatched(cotangent)
        sequence_normalized = norm_forward(sequence_tokens.astype(F32), gain_attn)[0].astype(
            BF16
        )
        linear = matrix_product(sequence_normalized, gathered[:, :linear_cols])
        low = flipped_right_operand(sequence_normalized, input_first).astype(BF16)
        complete_linear = gathered[:, :linear_cols]
        complete_router = gathered[:, linear_cols : linear_cols + expert_count]
        full_out_t = gathered[:, out_start:]
    attention_operands = (
        linear,
        low,
        q_second,
        k_second,
        v_second,
        gain_query,
        gain_key,
        tables,
        seg_column,
        seg_row,
        score_scale,
    )
    if not in_kernel:
        heads_narrow = attention_forward(*attention_operands)
        attention_low = flipped_right_operand(heads_narrow, attention_first).astype(BF16)
        out_part = flipped_right_operand(heads_narrow, full_out_t) + matrix_product(
            attention_low, attention_second
        )
        attention_total = sum_line(
            out_part.astype(BF16).reshape(tensor_count, tok_rows, model_width), 4, 1
        )
    if in_kernel:
        residual_stream, experts_narrow, gate_weights, sent_weights, router_low = router(
            attention_total,
            tokens,
            gain_moe[None, :],
            gathered,
            linear_cols,
            router_first,
            router_second,
            routes_t,
        )
    else:
        residual_stream = token_values + attention_total
        moe_normed, moe_factor = norm_forward(residual_stream, gain_moe)
        experts_narrow = moe_normed.astype(BF16)

        router_low = flipped_right_operand(experts_narrow, router_first).astype(BF16)
        router_logits = matrix_product(experts_narrow, complete_router) + matrix_product(
            router_low, router_second
        )
        expert_ids = jnp.arange(expert_count, dtype=jnp.int32)
        chosen = jnp.any(routes[:, :, None] == expert_ids[None, None, :], axis=1)
        chosen_logits = jnp.where(chosen, router_logits, -jnp.inf)
        chosen_exp = jnp.exp(chosen_logits - jnp.max(chosen_logits, axis=-1, keepdims=True))
        gate_weights = chosen_exp / jnp.sum(chosen_exp, axis=-1, keepdims=True)
        sent_weights = jnp.transpose(jnp.where(chosen, gate_weights, -1.0), (1, 0))
        own_weights = jnp.transpose(
            route_rows(sent_weights).reshape(fsdp_count, tensor_count, tok_rows), (1, 0, 2)
        )
        own_ranks = ranks_of(own_weights >= 0.0)

    broad = adapter_count * rank
    gate_in_t, upward_in_t = transposed(gate_in[0]), transposed(upward_in[0])
    expert_tables = (
        expert_gate_weight[0],
        expert_up_weight[0],
        expert_down_weight[0],
        jnp.concatenate(
            [gate_in_t.reshape(broad, model_width), upward_in_t.reshape(broad, model_width)],
            axis=0,
        ),
        gate_out[0].reshape(broad, -1),
        upward_out[0].reshape(broad, -1),
        transposed(downward_in[0]).reshape(broad, -1),
        downward_out[0].reshape(broad, model_width),
    )
    column_adapter = jnp.arange(broad, dtype=jnp.int32) // rank
    adapter_mask = jnp.repeat(
        (adapter_index[:, None] == column_adapter[None, :]).astype(BF16), slots, axis=0
    )
    ordered = [None] * tensor_count
    if in_kernel:
        moe_grad, gate_dots, expert_output, _landed, *sums = moe_layer(
            experts_narrow,
            up_rows,
            plane_ranks,
            sent_weights,
            adapter_mask,
            expert_tables,
            3,
        )
    else:
        expert_rows = dispatched(experts_narrow)
        expert_output, rows_grad, gate_dots = [], [], []
        sums = [jnp.zeros(each.shape, F32) for each in expert_sums(expert_tables)]
        for at, rows, upstream in zip(line_blocks, expert_rows, up_rows):
            y_rows, grad_rows, dots, *sums = experts(
                at, rows, upstream, own_ranks, own_weights, adapter_mask, expert_tables, sums
            )
            expert_output.append(y_rows)
            rows_grad.append(grad_rows)
            gate_dots.append(dots)
        for offset, dots in zip(offsets, gate_dots):
            ordered[offset] = dots
        gate_dots = jnp.roll(jnp.stack(ordered), tensor_pos, axis=0)
    pair_in_grad, gate_out_grad, upward_out_grad, downward_in_grad, downward_out_grad = sums
    if in_kernel:
        (
            output,
            residual_grad,
            low_share,
            linear_grad,
            owned,
            _landed,
        ) = back(
            score_scale,
            (linear_cols, out_start),
            slots,
            4,
            (linear, heads_narrow, sequence_normalized, gathered, expert_output),
            (
                moe_grad,
                gate_dots.reshape(expert_count, tok_rows),
                gate_weights,
                residual_stream,
                cotangent,
                gain_moe[None, :],
                router_first,
                router_second,
                router_low,
                experts_narrow,
                plane_ranks,
                low,
                attention_low,
                attention_first,
                attention_second,
                q_second,
                k_second,
                v_second,
                gain_query,
                gain_key,
                *tables,
                seg_column,
                seg_row,
            ),
        )
        owned = route_rows(owned)
        input_grad = last(
            linear_grad,
            low_share,
            input_first,
            residual_grad,
            tokens,
            gain_attn[None, :],
            gathered,
            5,
        )
    else:
        gate_grad = jnp.transpose(
            route_rows(jnp.transpose(gate_dots, (1, 0, 2)).reshape(device_count, tok_rows)), (1, 0)
        )

        def returned(slotted):
            total = 0.0
            for offset, at, rows in zip(offsets, line_blocks, slotted):
                combined = from_slots(at, plane_ranks, plane_rows(rows))
                total = total + delivered(combined, offset).astype(F32)
            return total

        moe_grad = returned(rows_grad)

        out_grad = cotangent.astype(F32)
        logit_gradient = (
            gate_weights * (gate_grad - jnp.sum(gate_weights * gate_grad, axis=-1, keepdims=True))
        ).astype(BF16)
        router_low_gradient = flipped_right_operand(logit_gradient, router_second).astype(BF16)
        moe_grad = (
            moe_grad
            + flipped_right_operand(logit_gradient, complete_router)
            + matrix_product(router_low_gradient, router_first)
        )
        router_first_gradient = flipped_left_operand(router_low_gradient, experts_narrow)
        router_second_gradient = flipped_left_operand(router_low, logit_gradient)
        residual_grad = out_grad + norm_backward(residual_stream, moe_factor, gain_moe, moe_grad)

        (sequence_branch,) = gather_line([residual_grad.astype(BF16)], (4,), 2)
        sequence_branch = sequence_branch.reshape(seq_rows, model_width)
        output = (residual_stream + returned(expert_output)).astype(BF16)
        attention_low_grad = flipped_right_operand(sequence_branch, attention_second).astype(BF16)
        attention_second_gradient = flipped_left_operand(attention_low, sequence_branch)
        heads_grad = matrix_product(sequence_branch, full_out_t)
        (
            q_grad,
            k_grad,
            v_grad,
            low_share,
            q_second_gradient,
            k_second_gradient,
            v_second_gradient,
            attention_first_gradient,
        ) = attention_backward(
            *attention_operands,
            heads_narrow,
            heads_grad,
            attention_low_grad,
            attention_first,
        )
        linear_grad = jnp.concatenate([q_grad, k_grad, v_grad], axis=1)
        normed_part = flipped_right_operand(linear_grad, complete_linear) + matrix_product(
            low_share, input_first
        )
        input_first_gradient = flipped_left_operand(low_share, sequence_normalized)
        normalized_gradient = sum_line(
            normed_part.astype(BF16).reshape(tensor_count, tok_rows, model_width), 4, 1
        )
        input_grad = residual_grad + norm_backward(
            token_values, attn_factor, gain_attn, normalized_gradient
        )
        row_grads = jnp.concatenate(
            [input_first_gradient, attention_second_gradient, router_first_gradient], axis=0
        )
        head_grads = jnp.concatenate([q_second_gradient, attention_first_gradient], axis=0)
        narrow_grads = jnp.concatenate([k_second_gradient, v_second_gradient], axis=0)

    def lines_of(piece, lines):
        return piece.reshape(adapter_count, lines, -1)

    if in_kernel:
        (
            query_in_sum,
            key_in_sum,
            value_in_sum,
            attn_out_sum,
            router_in_sum,
            router_out_sum,
            query_out_sum,
            attn_in_sum,
            key_out_sum,
            value_out_sum,
        ) = owners(
            adapter_index,
            owned,
            adapter_count,
            rank,
            model_width // device_count,
            local_kv_cols // fsdp_count,
        )
    else:
        source_adapter = jnp.repeat(adapter_index, tensor_count)
        owner_onehot = (
            jnp.arange(adapter_count, dtype=jnp.int32)[:, None] == source_adapter[None, :]
        ).astype(BF16)

        def to_all(addend):
            lines = addend.shape[0]
            return jnp.transpose(
                addend.astype(BF16).reshape(lines, device_count, -1), (1, 0, 2)
            ).reshape(device_count, -1)

        def to_head_owners(addend):
            lines = addend.shape[0]
            pieces = jnp.transpose(
                addend.astype(BF16).reshape(lines, fsdp_count, -1), (1, 0, 2)
            ).reshape(fsdp_count, -1)
            holder = jnp.zeros((device_count, pieces.shape[1]), BF16)
            return lax.dynamic_update_slice(holder, pieces, (tensor_pos * fsdp_count, zero_pos))

        def owner_sums(parts):
            widths = [part.shape[1] for part in parts]
            total = matrix_product(owner_onehot, route_rows(jnp.concatenate(parts, axis=1)))
            pieces = []
            start = 0
            for width in widths:
                pieces.append(total[:, start : start + width])
                start += width
            return pieces

        row_sums, head_sums, narrow_sums, router_sums = owner_sums(
            [
                to_all(row_grads),
                to_head_owners(head_grads),
                to_head_owners(narrow_grads),
                to_all(router_second_gradient),
            ]
        )
        row_sums = lines_of(row_sums, 5 * rank)
        head_sums = lines_of(head_sums, 2 * rank)
        narrow_sums = lines_of(narrow_sums, 2 * rank)
        query_in_sum, key_in_sum, value_in_sum, attn_out_sum, router_in_sum = [
            row_sums[:, at * rank : (at + 1) * rank] for at in range(5)
        ]
        query_out_sum, attn_in_sum = head_sums[:, :rank], head_sums[:, rank:]
        key_out_sum, value_out_sum = narrow_sums[:, :rank], narrow_sums[:, rank:]
        router_out_sum = lines_of(router_sums, rank)
    return (
        output,
        input_grad,
        transposed(query_in_sum),
        query_out_sum,
        transposed(key_in_sum),
        key_out_sum,
        transposed(value_in_sum),
        value_out_sum,
        transposed(attn_in_sum),
        attn_out_sum,
        transposed(router_in_sum),
        router_out_sum,
        transposed(lines_of(pair_in_grad[:broad], rank))[None],
        lines_of(gate_out_grad, rank)[None],
        transposed(lines_of(pair_in_grad[broad:], rank))[None],
        lines_of(upward_out_grad, rank)[None],
        transposed(lines_of(downward_in_grad, rank))[None],
        lines_of(downward_out_grad, rank)[None],
    )


def solution(mesh):
    placed = (
        P(("fsdp", "tensor"), None),
        P("fsdp", None),
        P(("fsdp", "tensor"), None),
        P(),
        P(("fsdp", "tensor"), None),
        P(),
        P(),
        P(),
        P(),
        P("fsdp", "tensor"),
        P("fsdp", "tensor"),
        P("fsdp", "tensor"),
        P("tensor", "fsdp"),
        P("fsdp", None),
        P(("fsdp", "tensor"), None, None),
        P(("fsdp", "tensor"), None, None),
        P(("fsdp", "tensor"), None, None),
        P(),
        P(None, None, "tensor"),
        P(),
        P(None, None, "tensor"),
        P(),
        P(None, None, "tensor"),
        P(None, "tensor", None),
        P(),
        P(),
        P(),
        P(("fsdp", "tensor"), None, None, None),
        P(("fsdp", "tensor"), None, None, None),
        P(("fsdp", "tensor"), None, None, None),
        P(("fsdp", "tensor"), None, None, None),
        P(("fsdp", "tensor"), None, None, None),
        P(("fsdp", "tensor"), None, None, None),
    )
    return jax.shard_map(
        per_device,
        mesh=mesh,
        in_specs=placed,
        out_specs=(
            P(("fsdp", "tensor"), None),
            P(("fsdp", "tensor"), None),
            P(None, ("fsdp", "tensor"), None),
            P(None, None, ("fsdp", "tensor")),
            P(None, ("fsdp", "tensor"), None),
            P(None, None, ("fsdp", "tensor")),
            P(None, ("fsdp", "tensor"), None),
            P(None, None, ("fsdp", "tensor")),
            P(None, ("fsdp", "tensor"), None),
            P(None, None, ("fsdp", "tensor")),
            P(None, ("fsdp", "tensor"), None),
            P(None, None, ("fsdp", "tensor")),
            P(("fsdp", "tensor"), None, None, None),
            P(("fsdp", "tensor"), None, None, None),
            P(("fsdp", "tensor"), None, None, None),
            P(("fsdp", "tensor"), None, None, None),
            P(("fsdp", "tensor"), None, None, None),
            P(("fsdp", "tensor"), None, None, None),
        ),
        check_vma=False,
    )
```

```python
import functools
import math

import jax
import jax.numpy as jnp
import numpy as np
from jax import lax
from jax.experimental import pallas as pl
from jax.experimental.pallas import tpu as pltpu
from jax.sharding import PartitionSpec as P

NORM_EPSILON = 1e-06
ROPE_THETA = 1000000.0
BF16 = jnp.bfloat16
F32 = jnp.float32
WINDOW = 256
MEBI = 1 << 20


def matrix_product(first_op, second_op):
    return jnp.dot(first_op, second_op, preferred_element_type=F32)


def flipped_left_operand(first_op, second_op):
    return lax.dot_general(
        first_op, second_op, (((0,), (0,)), ((), ())), preferred_element_type=F32
    )


def flipped_right_operand(first_op, second_op):
    return lax.dot_general(
        first_op, second_op, (((1,), (1,)), ((), ())), preferred_element_type=F32
    )


def norm_forward(values, gain_vec):
    factor = lax.rsqrt(jnp.mean(values * values, axis=-1, keepdims=True) + NORM_EPSILON)
    return (values * factor * gain_vec, factor)


def norm_backward(values, factor, gain_vec, upstream):
    scaled = upstream * gain_vec
    return factor * scaled - values * (factor * factor * factor) * jnp.mean(
        values * scaled, axis=-1, keepdims=True
    )


def rope_tables(sequence_length, head_width):
    half_width = head_width // 2
    inverse = np.power(
        np.float32(ROPE_THETA), -2.0 * np.arange(half_width, dtype=np.float32) / head_width
    ).astype(np.float32)
    angles = np.arange(sequence_length, dtype=np.float32)[:, None] * inverse[None, :]
    cosine, sine = np.cos(angles), np.sin(angles)
    return (
        jnp.asarray(np.concatenate([cosine, cosine], axis=1)),
        jnp.asarray(np.concatenate([-sine, sine], axis=1)),
    )


def swapped(values):
    return pltpu.roll(values, values.shape[-1] // 2, 1)


def route_rows(block_rows):
    return lax.all_to_all(block_rows, ("fsdp", "tensor"), split_axis=0, concat_axis=0, tiled=True)


def plane_rows(block_rows):
    return lax.all_to_all(block_rows, "fsdp", split_axis=0, concat_axis=0, tiled=True)


def params(mebibytes, axes=1):
    return pltpu.CompilerParams(
        vmem_limit_bytes=mebibytes * MEBI, dimension_semantics=("arbitrary",) * axes
    )


def staged(body, lead, count):
    def kernel(*refs):
        semaphores, held = refs[-1], refs[-1 - count : -1]
        copies = [
            pltpu.make_async_copy(source, target, semaphores.at[at])
            for at, (source, target) in enumerate(zip(refs[lead : lead + count], held))
        ]
        for each in copies:
            each.start()

        def ready():
            for each in copies:
                each.wait()

        body(ready, *refs[:lead], *held, *refs[lead + count : -1 - count])

    return kernel


def staging(operands):
    return [pltpu.VMEM(operand.shape, operand.dtype) for operand in operands] + [
        pltpu.SemaphoreType.DMA((len(operands),))
    ]


def whole(shape):
    rank = len(shape)
    return pl.BlockSpec(shape, lambda *_: (0,) * rank)


def head_values(linear, low, second, gain, cosine, sine):
    values = linear + matrix_product(low, second)
    normed, factor = norm_forward(values, gain)
    turned = (normed * cosine + swapped(normed) * sine).astype(BF16)
    return values, factor, turned


def head_values_gradient(values, factor, gain, cosine, sine, upstream):
    back = upstream * cosine - swapped(upstream) * sine
    return norm_backward(values, factor, gain, back).astype(BF16)


def allowed_keys(block, start, width, seg_column, seg_row):
    rows = block * WINDOW + lax.broadcasted_iota(jnp.int32, (WINDOW, width), 0)
    keys = start + lax.broadcasted_iota(jnp.int32, (WINDOW, width), 1)
    mine = seg_column[block * WINDOW : (block + 1) * WINDOW]
    theirs = seg_row[:, start : start + width]
    return (keys == rows) | ((keys < rows) & (mine == theirs) & (theirs != 0))


def block_bounds(block):
    start = max(block - 1, 0) * WINDOW
    return start, (block + 1) * WINDOW - start


def attention_forward_body(
    rank,
    scale,
    lin_ref,
    key_lin_ref,
    value_lin_ref,
    low_ref,
    q_second_ref,
    k_second_ref,
    v_second_ref,
    q_gain_ref,
    k_gain_ref,
    cos_ref,
    sin_ref,
    seg_column_ref,
    seg_row_ref,
    heads_ref,
    key_scratch,
    value_scratch,
):
    cosine, sine = cos_ref[...], sin_ref[...]

    @pl.when(pl.program_id(0) == 0)
    def _():
        key_scratch[...] = head_values(
            key_lin_ref[...],
            low_ref[:, rank : 2 * rank],
            k_second_ref[...],
            k_gain_ref[...],
            cosine,
            sine,
        )[2]
        value_scratch[...] = (
            value_lin_ref[...]
            + matrix_product(low_ref[:, 2 * rank : 3 * rank], v_second_ref[...])
        ).astype(BF16)

    query = head_values(
        lin_ref[...], low_ref[:, :rank], q_second_ref[...], q_gain_ref[...], cosine, sine
    )[2]
    seg_column, seg_row = seg_column_ref[...], seg_row_ref[...]
    for block in range(query.shape[0] // WINDOW):
        start, width = block_bounds(block)
        rows = pl.ds(block * WINDOW, WINDOW)
        scores = (
            flipped_right_operand(
                query[block * WINDOW : (block + 1) * WINDOW], key_scratch[pl.ds(start, width)]
            )
            * scale
        )
        scores = jnp.where(
            allowed_keys(block, start, width, seg_column, seg_row), scores, -1e30
        )
        expo = jnp.exp(scores - jnp.max(scores, axis=-1, keepdims=True))
        probs = (expo / jnp.sum(expo, axis=-1, keepdims=True)).astype(BF16)
        heads_ref[rows, :] = matrix_product(probs, value_scratch[pl.ds(start, width)]).astype(
            BF16
        )


def attention_forward(
    linear, low, q_second, k_second, v_second, q_gain, k_gain, tables, seg_column, seg_row, scale
):
    rows, head_dim = linear.shape[0], q_gain.shape[1]
    heads = q_second.shape[1] // head_dim
    rank = q_second.shape[0]
    column = pl.BlockSpec((rows, head_dim), lambda h: (0, h))
    return pl.pallas_call(
        functools.partial(attention_forward_body, rank, scale),
        grid=(heads,),
        out_shape=jax.ShapeDtypeStruct((rows, heads * head_dim), BF16),
        in_specs=[
            column,
            pl.BlockSpec((rows, head_dim), lambda h: (0, heads)),
            pl.BlockSpec((rows, head_dim), lambda h: (0, heads + 1)),
            whole(low.shape),
            pl.BlockSpec((rank, head_dim), lambda h: (0, h)),
            whole(k_second.shape),
            whole(v_second.shape),
            whole(q_gain.shape),
            whole(k_gain.shape),
            whole(tables[0].shape),
            whole(tables[1].shape),
            whole(seg_column.shape),
            whole(seg_row.shape),
        ],
        out_specs=column,
        scratch_shapes=[pltpu.VMEM((rows, head_dim), BF16), pltpu.VMEM((rows, head_dim), BF16)],
        compiler_params=params(40),
        cost_estimate=pl.CostEstimate(
            flops=8 * heads * rows * WINDOW * head_dim,
            transcendentals=2 * heads * rows * WINDOW,
            bytes_accessed=6 * rows * heads * head_dim,
        ),
        name="attention_forward",
    )(
        linear,
        linear,
        linear,
        low,
        q_second,
        k_second,
        v_second,
        q_gain,
        k_gain,
        *tables,
        seg_column,
        seg_row,
    )


def attention_backward_body(
    rank,
    scale,
    lin_ref,
    key_lin_ref,
    value_lin_ref,
    low_ref,
    q_second_ref,
    k_second_ref,
    v_second_ref,
    q_gain_ref,
    k_gain_ref,
    cos_ref,
    sin_ref,
    seg_column_ref,
    seg_row_ref,
    heads_ref,
    heads_grad_ref,
    low_grad_ref,
    down_ref,
    q_grad_ref,
    k_grad_ref,
    v_grad_ref,
    share_ref,
    q_second_grad_ref,
    k_second_grad_ref,
    v_second_grad_ref,
    down_grad_ref,
    key_scratch,
    value_scratch,
    key_sum,
    value_sum,
    query_sum,
    share_sum,
):
    cosine, sine = cos_ref[...], sin_ref[...]
    head = pl.program_id(0)

    @pl.when(head == 0)
    def _():
        key_scratch[...] = head_values(
            key_lin_ref[...],
            low_ref[:, rank : 2 * rank],
            k_second_ref[...],
            k_gain_ref[...],
            cosine,
            sine,
        )[2]
        value_scratch[...] = (
            value_lin_ref[...]
            + matrix_product(low_ref[:, 2 * rank : 3 * rank], v_second_ref[...])
        ).astype(BF16)
        key_sum[...] = jnp.zeros_like(key_sum)
        value_sum[...] = jnp.zeros_like(value_sum)
        share_sum[...] = jnp.zeros_like(share_sum)

    low_q = low_ref[:, :rank]
    values, factor, query = head_values(
        lin_ref[...], low_q, q_second_ref[...], q_gain_ref[...], cosine, sine
    )
    low_grad = low_grad_ref[...]
    upstream = (heads_grad_ref[...] + matrix_product(low_grad, down_ref[...])).astype(BF16)
    down_grad_ref[...] = flipped_left_operand(low_grad, heads_ref[...])
    seg_column, seg_row = seg_column_ref[...], seg_row_ref[...]
    for block in range(query.shape[0] // WINDOW):
        start, width = block_bounds(block)
        rows = pl.ds(block * WINDOW, WINDOW)
        keys = pl.ds(start, width)
        query_block = query[block * WINDOW : (block + 1) * WINDOW]
        upstream_block = upstream[block * WINDOW : (block + 1) * WINDOW]
        scores = flipped_right_operand(query_block, key_scratch[keys]) * scale
        scores = jnp.where(
            allowed_keys(block, start, width, seg_column, seg_row), scores, -1e30
        )
        expo = jnp.exp(scores - jnp.max(scores, axis=-1, keepdims=True))
        probs = expo / jnp.sum(expo, axis=-1, keepdims=True)
        prob_grad = flipped_right_operand(upstream_block, value_scratch[keys])
        score_grad = (
            probs * (prob_grad - jnp.sum(probs * prob_grad, axis=-1, keepdims=True))
        ).astype(BF16)
        value_sum[keys, :] += flipped_left_operand(probs.astype(BF16), upstream_block)
        key_sum[keys, :] += flipped_left_operand(score_grad, query_block)
        query_sum[rows, :] = matrix_product(score_grad, key_scratch[keys]) * scale
    q_grad = head_values_gradient(
        values, factor, q_gain_ref[...], cosine, sine, query_sum[...]
    )
    q_grad_ref[...] = q_grad
    q_second_grad_ref[...] = flipped_left_operand(low_q, q_grad)
    share_sum[:, :rank] += flipped_right_operand(q_grad, q_second_ref[...])

    @pl.when(head == pl.num_programs(0) - 1)
    def _():
        low_k = low_ref[:, rank : 2 * rank]
        low_v = low_ref[:, 2 * rank : 3 * rank]
        key_values, key_factor, _turned = head_values(
            key_lin_ref[...], low_k, k_second_ref[...], k_gain_ref[...], cosine, sine
        )
        k_grad = head_values_gradient(
            key_values, key_factor, k_gain_ref[...], cosine, sine, key_sum[...] * scale
        )
        v_grad = value_sum[...].astype(BF16)
        k_grad_ref[...] = k_grad
        v_grad_ref[...] = v_grad
        k_second_grad_ref[...] = flipped_left_operand(low_k, k_grad)
        v_second_grad_ref[...] = flipped_left_operand(low_v, v_grad)
        share_sum[:, rank : 2 * rank] = flipped_right_operand(k_grad, k_second_ref[...])
        share_sum[:, 2 * rank : 3 * rank] = flipped_right_operand(v_grad, v_second_ref[...])
        share_ref[...] = share_sum[...].astype(BF16)


def attention_backward(
    linear,
    low,
    q_second,
    k_second,
    v_second,
    q_gain,
    k_gain,
    tables,
    seg_column,
    seg_row,
    scale,
    heads_low,
    heads_grad,
    low_grad,
    down_first,
):
    rows, head_dim = linear.shape[0], q_gain.shape[1]
    rank, columns = q_second.shape
    heads = columns // head_dim
    column = pl.BlockSpec((rows, head_dim), lambda h: (0, h))
    narrow = pl.BlockSpec((rank, head_dim), lambda h: (0, h))
    single = (rows, head_dim)
    return pl.pallas_call(
        functools.partial(attention_backward_body, rank, scale),
        grid=(heads,),
        out_shape=(
            jax.ShapeDtypeStruct((rows, columns), BF16),
            jax.ShapeDtypeStruct(single, BF16),
            jax.ShapeDtypeStruct(single, BF16),
            jax.ShapeDtypeStruct((rows, 3 * rank), BF16),
            jax.ShapeDtypeStruct((rank, columns), F32),
            jax.ShapeDtypeStruct((rank, head_dim), F32),
            jax.ShapeDtypeStruct((rank, head_dim), F32),
            jax.ShapeDtypeStruct((rank, columns), F32),
        ),
        in_specs=[
            column,
            pl.BlockSpec((rows, head_dim), lambda h: (0, heads)),
            pl.BlockSpec((rows, head_dim), lambda h: (0, heads + 1)),
            whole(low.shape),
            narrow,
            whole(k_second.shape),
            whole(v_second.shape),
            whole(q_gain.shape),
            whole(k_gain.shape),
            whole(tables[0].shape),
            whole(tables[1].shape),
            whole(seg_column.shape),
            whole(seg_row.shape),
            column,
            column,
            whole(low_grad.shape),
            narrow,
        ],
        out_specs=(
            column,
            whole(single),
            whole(single),
            whole((rows, 3 * rank)),
            narrow,
            whole((rank, head_dim)),
            whole((rank, head_dim)),
            narrow,
        ),
        scratch_shapes=[
            pltpu.VMEM(single, BF16),
            pltpu.VMEM(single, BF16),
            pltpu.VMEM(single, F32),
            pltpu.VMEM(single, F32),
            pltpu.VMEM(single, F32),
            pltpu.VMEM((rows, 3 * rank), F32),
        ],
        compiler_params=params(48),
        cost_estimate=pl.CostEstimate(
            flops=20 * heads * rows * WINDOW * head_dim,
            transcendentals=2 * heads * rows * WINDOW,
            bytes_accessed=12 * rows * columns,
        ),
        name="attention_backward",
    )(
        linear,
        linear,
        linear,
        low,
        q_second,
        k_second,
        v_second,
        q_gain,
        k_gain,
        *tables,
        seg_column,
        seg_row,
        heads_low,
        heads_grad,
        low_grad,
        down_first,
    )


def slot_choice(ranks, slots):
    experts, tokens = ranks.shape
    places = lax.broadcasted_iota(jnp.int32, (slots, tokens), 0).astype(ranks.dtype)
    return jnp.concatenate(
        [(places == ranks[e : e + 1, :]).astype(F32) for e in range(experts)], axis=0
    ).astype(BF16)


def to_slots_body(_block_ref, rank_ref, rows_ref, out_ref):
    slots = out_ref.shape[1]
    chosen = matrix_product(slot_choice(rank_ref[0], slots), rows_ref[...])
    out_ref[...] = chosen.astype(BF16).reshape(out_ref.shape)


def to_slots(block, ranks, rows, slots):
    experts, tokens = ranks.shape[1:]
    width = rows.shape[1]
    half = width // 2
    return pl.pallas_call(
        to_slots_body,
        grid_spec=pltpu.PrefetchScalarGridSpec(
            num_scalar_prefetch=1,
            grid=(2,),
            in_specs=[
                pl.BlockSpec((1, experts, tokens), lambda j, at: (at[0], 0, 0)),
                pl.BlockSpec((tokens, half), lambda j, at: (0, j)),
            ],
            out_specs=pl.BlockSpec((experts, slots, half), lambda j, at: (0, 0, j)),
        ),
        out_shape=jax.ShapeDtypeStruct((experts, slots, width), BF16),
        compiler_params=params(32),
        cost_estimate=pl.CostEstimate(
            flops=2 * experts * slots * tokens * width,
            transcendentals=0,
            bytes_accessed=2 * width * (experts * slots + tokens),
        ),
        name="to_slots",
    )(block, ranks, rows)


def from_slots_body(_block_ref, rank_ref, slot_ref, out_ref):
    experts, slots, width = slot_ref.shape
    choice = slot_choice(rank_ref[0], slots)
    out_ref[...] = flipped_left_operand(
        choice, slot_ref[...].reshape(experts * slots, width)
    ).astype(BF16)


def from_slots(block, ranks, slotted):
    experts, tokens = ranks.shape[1:]
    slots, width = slotted.shape[1:]
    half = width // 2
    return pl.pallas_call(
        from_slots_body,
        grid_spec=pltpu.PrefetchScalarGridSpec(
            num_scalar_prefetch=1,
            grid=(2,),
            in_specs=[
                pl.BlockSpec((1, experts, tokens), lambda j, at: (at[0], 0, 0)),
                pl.BlockSpec((experts, slots, half), lambda j, at: (0, 0, j)),
            ],
            out_specs=pl.BlockSpec((tokens, half), lambda j, at: (0, j)),
        ),
        out_shape=jax.ShapeDtypeStruct((tokens, width), BF16),
        compiler_params=params(32),
        cost_estimate=pl.CostEstimate(
            flops=2 * experts * slots * tokens * width,
            transcendentals=0,
            bytes_accessed=2 * width * (experts * slots + tokens),
        ),
        name="from_slots",
    )(block, ranks, slotted)


def all_to_slots_body(rank_ref, rows_ref, out_ref):
    slots = out_ref.shape[2]
    chosen = matrix_product(slot_choice(rank_ref[0], slots), rows_ref[...])
    out_ref[...] = chosen.astype(BF16).reshape(out_ref.shape)


def all_to_slots(ranks, rows, slots):
    blocks, experts, tokens = ranks.shape
    width = rows.shape[1]
    return pl.pallas_call(
        all_to_slots_body,
        grid=(blocks,),
        out_shape=jax.ShapeDtypeStruct((experts, blocks, slots, width), BF16),
        in_specs=[
            pl.BlockSpec((1, experts, tokens), lambda z: (z, 0, 0)),
            pl.BlockSpec((tokens, width), lambda z: (z, 0)),
        ],
        out_specs=pl.BlockSpec((experts, 1, slots, width), lambda z: (0, z, 0, 0)),
        compiler_params=params(40),
        cost_estimate=pl.CostEstimate(
            flops=2 * blocks * experts * slots * tokens * width,
            transcendentals=0,
            bytes_accessed=2 * blocks * width * (experts * slots + tokens),
        ),
        name="all_to_slots",
    )(ranks, rows)


def all_from_slots_body(_start_ref, rank_ref, slot_ref, out_ref):
    experts, _, slots, width = slot_ref.shape
    choice = slot_choice(rank_ref[0], slots)
    out_ref[...] = flipped_left_operand(
        choice, slot_ref[...].reshape(experts * slots, width)
    ).astype(BF16)


def all_from_slots(start, ranks, slotted):
    blocks, experts, tokens = ranks.shape
    slots, width = slotted.shape[2:]
    return pl.pallas_call(
        all_from_slots_body,
        grid_spec=pltpu.PrefetchScalarGridSpec(
            num_scalar_prefetch=1,
            grid=(blocks,),
            in_specs=[
                pl.BlockSpec((1, experts, tokens), lambda z, at: ((at[0] + z) % blocks, 0, 0)),
                pl.BlockSpec((experts, 1, slots, width), lambda z, at: (0, z, 0, 0)),
            ],
            out_specs=pl.BlockSpec((tokens, width), lambda z, at: ((at[0] + z) % blocks, 0)),
        ),
        out_shape=jax.ShapeDtypeStruct((blocks * tokens, width), BF16),
        compiler_params=params(40),
        cost_estimate=pl.CostEstimate(
            flops=2 * blocks * experts * slots * tokens * width,
            transcendentals=0,
            bytes_accessed=2 * blocks * width * (experts * slots + tokens),
        ),
        name="all_from_slots",
    )(start, ranks, slotted)


def ranks_of(mask):
    tokens = mask.shape[-1]
    order = jnp.arange(tokens, dtype=jnp.int32)
    before = (order[:, None] < order[None, :]).astype(BF16)
    counts = matrix_product(mask.astype(BF16), before)
    return jnp.where(mask, counts, -1.0).astype(jnp.int32)


def line_relay(me, count, ins, outs, chunks, semaphores):
    right_send, right_recv, left_send, left_recv = semaphores
    pieces = []
    for at in range(len(ins)):
        size = ins[at].shape[0] // chunks[at]
        for piece in range(chunks[at]):
            pieces.append((at, pl.ds(piece * size, size)))

    def copy(place, hop, origin, target, send, recv):
        at, rows = pieces[place]
        source = ins[at].at[rows] if hop == 0 else outs[at].at[origin, rows]
        return pltpu.make_async_remote_copy(
            src_ref=source,
            dst_ref=outs[at].at[origin, rows],
            send_sem=send.at[hop, place],
            recv_sem=recv.at[hop, place],
            device_id={"tensor": target},
        )

    def places(arrays):
        return [place for place in range(len(pieces)) if pieces[place][0] in arrays]

    def advance(hop, arrays):
        for place in places(arrays):
            if hop > 0:

                @pl.when(me - hop >= 0)
                def _():
                    copy(place, hop - 1, me - hop, me - 1, right_send, right_recv).wait_recv()

            if hop < count - 1:

                @pl.when((me - hop >= 0) & (me + 1 < count))
                def _():
                    copy(place, hop, me - hop, me + 1, right_send, right_recv).start()

            if hop > 0:

                @pl.when(me + hop < count)
                def _():
                    copy(place, hop - 1, me + hop, me + 1, left_send, left_recv).wait_recv()

            if hop < count - 1:

                @pl.when((me + hop < count) & (me > 0))
                def _():
                    copy(place, hop, me + hop, me - 1, left_send, left_recv).start()

    def finish(arrays, hops):
        for hop in hops:
            for place in places(arrays):

                @pl.when((me - hop >= 0) & (me + 1 < count))
                def _():
                    copy(place, hop, me - hop, me + 1, right_send, right_recv).wait_send()

                @pl.when((me + hop < count) & (me > 0))
                def _():
                    copy(place, hop, me + hop, me - 1, left_send, left_recv).wait_send()

    return advance, finish


def line_sum(me, count, chunks, part_ref, out_ref, left_buf, right_buf, semaphores):
    right_send, right_recv, left_send, left_recv = semaphores
    size = part_ref.shape[1] // chunks

    def rightward(rows, piece, far, source):
        return pltpu.make_async_remote_copy(
            src_ref=source,
            dst_ref=left_buf.at[far - 1, rows],
            send_sem=right_send.at[far - 1, piece],
            recv_sem=right_recv.at[far - 1, piece],
            device_id={"tensor": me + 1},
        )

    def leftward(rows, piece, far, source):
        return pltpu.make_async_remote_copy(
            src_ref=source,
            dst_ref=right_buf.at[far - 1, rows],
            send_sem=left_send.at[far - 1, piece],
            recv_sem=left_recv.at[far - 1, piece],
            device_id={"tensor": me - 1},
        )

    def added(buffer, far, rows, block):
        buffer[far, rows, :] = (
            buffer[far, rows, :].astype(F32) + part_ref[block, rows, :].astype(F32)
        ).astype(BF16)

    def advance(far):
        for piece in range(chunks):
            rows = pl.ds(piece * size, size)

            @pl.when((me == 0) & (me + far < count))
            def _():
                rightward(rows, piece, far, part_ref.at[me + far, rows]).start()

            @pl.when((me == count - 1) & (me - far >= 0))
            def _():
                leftward(rows, piece, far, part_ref.at[me - far, rows]).start()

            if far < count - 1:

                @pl.when((me > 0) & (me + far < count))
                def _():
                    rightward(rows, piece, far + 1, left_buf.at[far, rows]).wait_recv()
                    added(left_buf, far, rows, me + far)
                    rightward(rows, piece, far, left_buf.at[far, rows]).start()

                @pl.when((me < count - 1) & (me - far >= 0))
                def _():
                    leftward(rows, piece, far + 1, right_buf.at[far, rows]).wait_recv()
                    added(right_buf, far, rows, me - far)
                    leftward(rows, piece, far, right_buf.at[far, rows]).start()

    def finish():
        for piece in range(chunks):
            rows = pl.ds(piece * size, size)
            out_ref[rows, :] = part_ref[me, rows, :].astype(F32)

            @pl.when(me > 0)
            def _():
                rightward(rows, piece, 1, left_buf.at[0, rows]).wait_recv()
                out_ref[rows, :] += left_buf[0, rows, :].astype(F32)

            @pl.when(me < count - 1)
            def _():
                leftward(rows, piece, 1, right_buf.at[0, rows]).wait_recv()
                out_ref[rows, :] += right_buf[0, rows, :].astype(F32)

        for far in range(count - 1, 0, -1):
            for piece in range(chunks):
                rows = pl.ds(piece * size, size)

                @pl.when((me == 0) & (me + far < count))
                def _():
                    rightward(rows, piece, far, part_ref.at[me + far, rows]).wait_send()

                @pl.when((me == count - 1) & (me - far >= 0))
                def _():
                    leftward(rows, piece, far, part_ref.at[me - far, rows]).wait_send()

                if far < count - 1:

                    @pl.when((me > 0) & (me + far < count))
                    def _():
                        rightward(rows, piece, far, left_buf.at[far, rows]).wait_send()

                    @pl.when((me < count - 1) & (me - far >= 0))
                    def _():
                        leftward(rows, piece, far, right_buf.at[far, rows]).wait_send()

    return advance, finish


def greet_line_and_plane(line, plane):
    me, at_line = lax.axis_index("fsdp"), lax.axis_index("tensor")
    barrier = pltpu.get_barrier_semaphore()

    @pl.loop(1, plane)
    def _(d):
        pl.semaphore_signal(barrier, inc=1, device_id={"fsdp": lax.rem(me + d, plane)})

    @pl.loop(1, line)
    def _(d):
        pl.semaphore_signal(barrier, inc=1, device_id={"tensor": lax.rem(at_line + d, line)})

    pl.semaphore_wait(barrier, plane + line - 2)


def tiles(width, tile, body):
    @pl.loop(0, width // tile)
    def _(j):
        body(pl.ds(pl.multiple_of(j * tile, tile), tile))


def expert_math(
    tile, rows_ref, up_ref, ranks, weights, keep_dots, sent_y, mask_ref, tables, sums, scratch
):
    gate_w, up_w, down_w, pair_in, gate_out, up_out, down_in, down_out = tables
    pair_in_sum, gate_out_sum, up_out_sum, down_in_sum, down_out_sum = sums
    gate_lin_ref, up_lin_ref, inner_ref, route_ref, gate_grad_ref, up_grad_ref = scratch
    sources, slots, width = rows_ref.shape
    row_count = sources * slots
    hidden = gate_w.shape[1]
    broad = gate_out.shape[0]
    places = lax.broadcasted_iota(jnp.int32, (slots, ranks.shape[1]), 0).astype(ranks.dtype)

    def held(source):
        return places == ranks[source : source + 1, :]

    def all_rows():
        return rows_ref[...].reshape(row_count, width)

    def pair_mask():
        mask = mask_ref[...].astype(F32)
        return jnp.concatenate([mask, mask], axis=1)

    weight = jnp.concatenate(
        [
            jnp.sum(
                jnp.where(held(source), weights[source : source + 1, :], 0.0),
                axis=1,
                keepdims=True,
            )
            for source in range(sources)
        ],
        axis=0,
    )
    pair = (flipped_right_operand(all_rows(), pair_in[...]) * pair_mask()).astype(BF16)
    gate_low, up_low = pair[:, :broad], pair[:, broad:]

    def inner_step(columns):
        rows = all_rows()
        gate_lin = matrix_product(rows, gate_w[:, columns]) + matrix_product(
            gate_low, gate_out[:, columns]
        )
        up_lin = matrix_product(rows, up_w[:, columns]) + matrix_product(
            up_low, up_out[:, columns]
        )
        gate_lin_ref[:, columns] = gate_lin
        up_lin_ref[:, columns] = up_lin
        inner_ref[:, columns] = (gate_lin * jax.nn.sigmoid(gate_lin) * up_lin).astype(BF16)

    tiles(hidden, tile, inner_step)
    down_low = (
        flipped_right_operand(inner_ref[...], down_in[...]) * mask_ref[...].astype(F32)
    ).astype(BF16)

    def down_step(j, total):
        columns = pl.ds(pl.multiple_of(j * tile, tile), tile)
        result = (
            matrix_product(inner_ref[...], down_w[:, columns])
            + matrix_product(down_low, down_out[:, columns])
        ).astype(BF16)
        wide = result.astype(F32)
        upstream = up_ref[:, :, columns].reshape(row_count, tile).astype(F32)
        up_ref[:, :, columns] = (weight * wide).astype(BF16).reshape(sources, slots, tile)
        route_ref[:, columns] = (weight * upstream).astype(BF16)
        return total + jnp.sum(upstream * wide, axis=1, keepdims=True)

    gate_dots = lax.fori_loop(0, width // tile, down_step, jnp.zeros((row_count, 1), F32))
    sent_y()
    for source in range(sources):
        keep_dots(
            source,
            jnp.sum(
                jnp.where(held(source), gate_dots[source * slots : (source + 1) * slots], 0.0),
                axis=0,
                keepdims=True,
            ),
        )
    down_low_grad = (
        flipped_right_operand(route_ref[...], down_out[...]) * mask_ref[...].astype(F32)
    ).astype(BF16)
    down_in_sum[...] += flipped_left_operand(down_low_grad, inner_ref[...])

    def down_out_step(columns):
        down_out_sum[:, columns] += flipped_left_operand(down_low, route_ref[:, columns])

    tiles(width, 2 * tile, down_out_step)

    def inner_grad_step(columns):
        inner_grad = flipped_right_operand(route_ref[...], down_w[columns, :]) + matrix_product(
            down_low_grad, down_in[:, columns]
        )
        gate_lin, up_lin = gate_lin_ref[:, columns], up_lin_ref[:, columns]
        sig = jax.nn.sigmoid(gate_lin)
        gate_grad_ref[:, columns] = (
            inner_grad * up_lin * (sig * (1.0 + gate_lin * (1.0 - sig)))
        ).astype(BF16)
        up_grad_ref[:, columns] = (inner_grad * (gate_lin * sig)).astype(BF16)

    tiles(hidden, tile, inner_grad_step)
    pair_grad = (
        jnp.concatenate(
            [
                flipped_right_operand(gate_grad_ref[...], gate_out[...]),
                flipped_right_operand(up_grad_ref[...], up_out[...]),
            ],
            axis=1,
        )
        * pair_mask()
    ).astype(BF16)
    gate_out_sum[...] += flipped_left_operand(gate_low, gate_grad_ref[...])
    up_out_sum[...] += flipped_left_operand(up_low, up_grad_ref[...])

    def rows_grad_step(columns):
        before = rows_ref[:, :, columns].reshape(row_count, tile)
        pair_in_sum[:, columns] += flipped_left_operand(pair_grad, before)
        rows_ref[:, :, columns] = (
            (
                flipped_right_operand(gate_grad_ref[...], gate_w[columns, :])
                + flipped_right_operand(up_grad_ref[...], up_w[columns, :])
                + matrix_product(pair_grad, pair_in[:, columns])
            )
            .astype(BF16)
            .reshape(sources, slots, tile)
        )

    tiles(width, tile, rows_grad_step)


def expert_sums(tables):
    gate_w, _up_w, _down_w, pair_in, gate_out, _up_out, down_in, down_out = tables
    return [
        jax.ShapeDtypeStruct(table.shape, F32)
        for table in (pair_in, gate_out, gate_out, down_in, down_out)
    ]


def expert_scratch(row_count, hidden, width):
    return [
        pltpu.VMEM((row_count, hidden), F32),
        pltpu.VMEM((row_count, hidden), F32),
        pltpu.VMEM((row_count, hidden), BF16),
        pltpu.VMEM((row_count, width), BF16),
        pltpu.VMEM((row_count, hidden), BF16),
        pltpu.VMEM((row_count, hidden), BF16),
    ]


def experts_body(_block_ref, rows_in, up_in, rank_ref, weight_ref, mask_ref, *rest):
    tables, sums_before, rest = rest[:8], rest[8:13], rest[13:]
    y_ref, rows_grad_ref, dots_ref = rest[:3]
    sums, rest = rest[3:8], rest[8:]
    for total, before in zip(sums, sums_before):
        total[...] = before[...]
    rows_grad_ref[...] = rows_in[...]
    y_ref[...] = up_in[...]

    def keep_dots(source, dots):
        dots_ref[source : source + 1, :] = dots

    expert_math(
        256,
        rows_grad_ref,
        y_ref,
        rank_ref[0],
        weight_ref[0],
        keep_dots,
        lambda: None,
        mask_ref,
        tables,
        sums,
        rest,
    )


def experts(block, rows, up_rows, ranks, weights, mask, tables, sums_before):
    sources, slots, width = rows.shape
    hidden = tables[0].shape[1]
    tokens = ranks.shape[2]
    token_spec = pl.BlockSpec((1, sources, tokens), lambda _, at: (at[0], 0, 0))

    def resident(array):
        return pl.BlockSpec(
            array.shape, lambda *_: (0,) * len(array.shape), pipeline_mode=pl.Buffered(1)
        )

    sums = expert_sums(tables)
    outs = [
        jax.ShapeDtypeStruct(rows.shape, BF16),
        jax.ShapeDtypeStruct(rows.shape, BF16),
        jax.ShapeDtypeStruct((sources, tokens), F32),
    ] + sums
    operands = [rows, up_rows, ranks, weights, mask, *tables, *sums_before]
    specs = (
        [resident(rows), resident(up_rows), token_spec, token_spec, resident(mask)]
        + [resident(table) for table in tables]
        + [resident(each) for each in sums_before]
    )
    return pl.pallas_call(
        experts_body,
        grid_spec=pltpu.PrefetchScalarGridSpec(
            num_scalar_prefetch=1,
            grid=(1,),
            in_specs=specs,
            out_specs=[resident(out) for out in outs],
            scratch_shapes=expert_scratch(sources * slots, hidden, width),
        ),
        out_shape=outs,
        input_output_aliases={
            1 + len(operands) - len(sums) + at: 3 + at for at in range(len(sums))
        },
        compiler_params=params(63),
        name="experts",
    )(block, *operands)


def moe_body(
    plane,
    line,
    ready,
    own_ref,
    up_hbm,
    plane_rank_ref,
    weight_ref,
    mask_ref,
    *rest,
):
    tables_hbm, rest = rest[:8], rest[8:]
    total_ref, dots_ref, y_hbm, back_hbm = rest[:4]
    sums, rest = rest[4:9], rest[9:]
    tables, rest = rest[:8], rest[8:]
    (
        blocks,
        partials,
        partials_in,
        sent_slots,
        rows,
        up_rows,
        back_rows,
        choice,
        dots,
        dots_back,
        dots_pass,
        dots_in,
        line_weights,
        weight_pass,
        weight_land,
    ) = rest[:15]
    scratch, rest = rest[15:21], rest[21:]
    (
        table_sem,
        up_sem,
        y_sem,
        back_sem,
        own_sem,
        relay_right_send,
        relay_right_recv,
        relay_left_send,
        relay_left_recv,
        row_send,
        row_recv,
        back_send,
        back_recv,
        partial_send,
        partial_recv,
        dots_send,
        dots_recv,
        dots_in_send,
        dots_in_recv,
        line_weight_send,
        line_weight_recv,
        weight_send,
        weight_recv,
    ) = rest
    width = own_ref.shape[1]
    slots = rows.shape[2]
    tile = 256
    me, at_line = lax.axis_index("fsdp"), lax.axis_index("tensor")

    greet_line_and_plane(line, plane)

    orders = [sorted(range(line), key=lambda block: abs(block - at)) for at in range(line)]

    def place_of(step):
        result = 0
        for at in range(line):
            for k in range(line):
                result = jnp.where((at_line == at) & (step == k), orders[at][k], result)
        return result

    advance, finish_relay = line_relay(
        at_line,
        line,
        [own_ref],
        [blocks],
        (4,),
        (relay_right_send, relay_right_recv, relay_left_send, relay_left_recv),
    )

    def row_copy(step, block, d):
        target = lax.rem(me + d, plane)
        return pltpu.make_async_remote_copy(
            src_ref=sent_slots.at[lax.rem(step, 2), target],
            dst_ref=rows.at[block, me],
            send_sem=row_send.at[block, d],
            recv_sem=row_recv.at[block, d],
            device_id={"fsdp": target},
        )

    def own_rows(step, block):
        return pltpu.make_async_copy(
            sent_slots.at[lax.rem(step, 2), me], rows.at[block, me], own_sem.at[0]
        )

    def back_copy(block, d):
        target = lax.rem(me + d, plane)
        return pltpu.make_async_remote_copy(
            src_ref=rows.at[block, target],
            dst_ref=back_hbm.at[block, me],
            send_sem=back_send.at[block, d],
            recv_sem=back_recv.at[block, d],
            device_id={"fsdp": target},
        )

    def own_back(block):
        return pltpu.make_async_copy(
            rows.at[block, me], back_hbm.at[block, me], own_sem.at[1]
        )

    def dots_copy(block, d):
        target = lax.rem(me + d, plane)
        return pltpu.make_async_remote_copy(
            src_ref=dots.at[block, target],
            dst_ref=dots_back.at[block, me],
            send_sem=dots_send.at[block, d],
            recv_sem=dots_recv.at[block, d],
            device_id={"fsdp": target},
        )

    def dots_in_copy(block, sender):
        return pltpu.make_async_remote_copy(
            src_ref=dots_pass.at[block],
            dst_ref=dots_in.at[sender],
            send_sem=dots_in_send.at[block],
            recv_sem=dots_in_recv.at[sender],
            device_id={"tensor": block},
        )

    def partial_copy(block, sender):
        return pltpu.make_async_remote_copy(
            src_ref=partials.at[block],
            dst_ref=partials_in.at[sender],
            send_sem=partial_send.at[block],
            recv_sem=partial_recv.at[sender],
            device_id={"tensor": block},
        )

    def up_copy(block):
        return pltpu.make_async_copy(up_hbm.at[:, block], up_rows, up_sem)

    def y_copy(block):
        return pltpu.make_async_copy(up_rows, y_hbm.at[:, block], y_sem)

    def line_weight_copy(target, sender):
        return pltpu.make_async_remote_copy(
            src_ref=weight_ref.at[target],
            dst_ref=line_weights.at[sender],
            send_sem=line_weight_send.at[target],
            recv_sem=line_weight_recv.at[sender],
            device_id={"tensor": target},
        )

    def weight_copy(block, d):
        target = lax.rem(me + d, plane)
        return pltpu.make_async_remote_copy(
            src_ref=weight_pass.at[block, target],
            dst_ref=weight_land.at[block, me],
            send_sem=weight_send.at[block, d],
            recv_sem=weight_recv.at[block, d],
            device_id={"fsdp": target},
        )

    ready()
    for step in range(1, line):
        line_weight_copy(place_of(step), at_line).start()
    line_weights[at_line] = weight_ref[at_line]
    advance(0, (0,))
    first_block = pltpu.make_async_copy(own_ref, blocks.at[at_line], own_sem.at[2])
    first_block.start()
    up_copy(at_line).start()
    table_copies = [
        pltpu.make_async_copy(source, target, table_sem.at[at])
        for at, (source, target) in enumerate(zip(tables_hbm, tables))
    ]
    for each in table_copies:
        each.start()
    first_block.wait()

    def dispatch(step):
        block = place_of(step)
        if step > 1:
            before = place_of(step - 2)

            @pl.loop(1, plane)
            def _(d):
                row_copy(step - 2, before, d).wait_send()

        if step > 0:
            line_weight_copy(block, block).wait_recv()
        for target in range(plane):
            weight_pass[block, target] = jnp.broadcast_to(
                line_weights[block, target : target + 1, :], weight_pass.shape[2:]
            )
        weight_land[block, me] = weight_pass[block, me]

        @pl.loop(1, plane)
        def _(d):
            weight_copy(block, d).start()

        choice[...] = slot_choice(plane_rank_ref[block], slots)

        def slot_step(columns):
            sent_slots[step % 2, :, :, columns] = (
                matrix_product(choice[...], blocks[block, :, columns])
                .astype(BF16)
                .reshape(plane, slots, 2 * tile)
            )

        tiles(width, 2 * tile, slot_step)

        @pl.loop(1, plane)
        def _(d):
            row_copy(step, block, d).start()

        own = own_rows(step, block)
        own.start()
        own.wait()

    dispatch(0)
    for total in sums:
        total[...] = jnp.zeros_like(total)
    advance(1, (0,))
    dispatch(1)
    for each in table_copies:
        each.wait()

    def send_back(block):
        @pl.loop(1, plane)
        def _(d):
            dots_copy(block, d).start()
            back_copy(block, d).start()

        own = own_back(block)
        own.start()
        dots_back[block, me] = dots[block, me]
        own.wait()

    @pl.loop(0, line + 2)
    def _(step):
        @pl.when(step < line)
        def _():
            block = place_of(step)

            @pl.loop(1, plane)
            def _(d):
                weight_copy(block, d).wait_recv()
                row_copy(step, block, d).wait_recv()

            gates = weight_land[block, :, 0, :]
            count = gates.shape[1]
            earlier = lax.broadcasted_iota(jnp.int32, (count, count), 0)
            before = (
                (earlier < lax.broadcasted_iota(jnp.int32, (count, count), 1))
                .astype(F32)
                .astype(BF16)
            )
            held = gates >= 0.0
            ranks = jnp.where(
                held, matrix_product(held.astype(F32).astype(BF16), before), -1.0
            )
            up_copy(block).wait()

            def keep_dots(source, values):
                dots[block, source] = jnp.broadcast_to(values, (8, values.shape[1]))

            expert_math(
                tile,
                rows.at[block],
                up_rows,
                ranks,
                gates,
                keep_dots,
                lambda: y_copy(block).start(),
                mask_ref,
                tables,
                sums,
                scratch,
            )

            @pl.when(step > 0)
            def _():
                send_back(block)

            @pl.when(step == line - 1)
            def _():
                send_back(at_line)

            y_copy(block).wait()

            @pl.when(step + 1 < line)
            def _():
                up_copy(place_of(step + 1)).start()

            for late in range(2, line):

                @pl.when(step == late - 2)
                def _():
                    advance(late, (0,))
                    dispatch(late)

        @pl.when(step >= 2)
        def _():
            block = place_of(lax.rem(step - 1, line))

            @pl.loop(1, plane)
            def _(d):
                dots_copy(block, d).wait_recv()
                back_copy(block, d).wait_recv()

            dots_pass[block] = dots_back[block, :, 0, :]
            load = pltpu.make_async_copy(back_hbm.at[block], back_rows, back_sem)
            load.start()
            choice[...] = slot_choice(plane_rank_ref[block], slots)
            load.wait()

            def combined(columns):
                return flipped_left_operand(
                    choice[...], back_rows[:, :, columns].reshape(plane * slots, 2 * tile)
                )

            @pl.when(step == line + 1)
            def _():
                def keep(columns):
                    total_ref[:, columns] = combined(columns)

                tiles(width, 2 * tile, keep)
                dots_ref[at_line] = dots_pass[at_line]

            @pl.when(step < line + 1)
            def _():
                dots_in_copy(block, at_line).start()

                def pass_on(columns):
                    partials[block, :, columns] = combined(columns).astype(BF16)

                tiles(width, 2 * tile, pass_on)
                partial_copy(block, at_line).start()

    @pl.loop(1, line)
    def _(step):
        sender = place_of(step)
        dots_in_copy(sender, sender).wait_recv()
        dots_ref[sender] = dots_in[sender]
        partial_copy(sender, sender).wait_recv()
        total_ref[...] += partials_in[sender].astype(F32)

    @pl.loop(1, line)
    def _(step):
        block = place_of(step)
        partial_copy(block, at_line).wait_send()
        dots_in_copy(block, at_line).wait_send()

    finish_relay((0,), range(line - 1))
    for step in (line - 2, line - 1):

        @pl.loop(1, plane)
        def _(d):
            row_copy(step, place_of(step), d).wait_send()

    @pl.loop(0, line)
    def _(block):
        @pl.loop(1, plane)
        def _(d):
            back_copy(block, d).wait_send()
            dots_copy(block, d).wait_send()
            weight_copy(block, d).wait_send()

    for step in range(1, line):
        line_weight_copy(place_of(step), at_line).wait_send()


def moe_layer(own, up_rows, plane_ranks, weights, mask, tables, identity):
    line, plane, tokens = plane_ranks.shape
    slots, width = up_rows.shape[2:]
    hidden = tables[0].shape[1]
    sums = expert_sums(tables)
    anywhere = pl.BlockSpec(memory_space=pl.ANY)
    local = pl.BlockSpec(memory_space=pltpu.VMEM)
    grouped = (plane, slots, width)
    dma = pltpu.SemaphoreType.DMA
    return pl.pallas_call(
        staged(functools.partial(moe_body, plane, line), 2, 3),
        out_shape=[
            jax.ShapeDtypeStruct((tokens, width), F32),
            jax.ShapeDtypeStruct((line, plane, tokens), F32),
            jax.ShapeDtypeStruct((plane, line, slots, width), BF16),
            jax.ShapeDtypeStruct((line,) + grouped, BF16),
        ]
        + sums,
        in_specs=[anywhere] * (5 + len(tables)),
        out_specs=[local, local, anywhere, anywhere] + [local] * len(sums),
        scratch_shapes=[pltpu.VMEM(table.shape, table.dtype) for table in tables]
        + [
            pltpu.VMEM((line, tokens, width), BF16),
            pltpu.VMEM((line, tokens, width), BF16),
            pltpu.VMEM((line, tokens, width), BF16),
            pltpu.VMEM((2,) + grouped, BF16),
            pltpu.VMEM((line,) + grouped, BF16),
            pltpu.VMEM(grouped, BF16),
            pltpu.VMEM(grouped, BF16),
            pltpu.VMEM((plane * slots, tokens), BF16),
            pltpu.VMEM((line, plane, 8, tokens), F32),
            pltpu.VMEM((line, plane, 8, tokens), F32),
            pltpu.VMEM((line, plane, tokens), F32),
            pltpu.VMEM((line, plane, tokens), F32),
            pltpu.VMEM((line, plane, tokens), F32),
            pltpu.VMEM((line, plane, 8, tokens), F32),
            pltpu.VMEM((line, plane, 8, tokens), F32),
        ]
        + expert_scratch(plane * slots, hidden, width)
        + [dma((len(tables),)), dma, dma, dma, dma((3,))]
        + [dma((line - 1, 4))] * 4
        + [dma((line, plane))] * 4
        + [dma((line,))] * 2
        + [dma((line, plane))] * 2
        + [dma((line,))] * 4
        + [dma((line, plane))] * 2
        + staging([plane_ranks, weights, mask]),
        compiler_params=pltpu.CompilerParams(
            collective_id=identity, has_side_effects=True, vmem_limit_bytes=63 * MEBI
        ),
        name="moe_layer",
    )(own, up_rows, plane_ranks, weights, mask, *tables)


def greet_line(me, count):
    barrier = pltpu.get_barrier_semaphore()

    @pl.when(me > 0)
    def _():
        pl.semaphore_signal(barrier, inc=1, device_id={"tensor": me - 1})

    @pl.when(me < count - 1)
    def _():
        pl.semaphore_signal(barrier, inc=1, device_id={"tensor": me + 1})

    @pl.when((me > 0) & (me < count - 1))
    def _():
        pl.semaphore_wait(barrier, 2)

    @pl.when((me == 0) | (me == count - 1))
    def _():
        pl.semaphore_wait(barrier, 1)


def gather_line_body(count, chunks, *refs):
    arrays = len(chunks)
    ins, outs = refs[:arrays], refs[arrays : 2 * arrays]
    semaphores, own_sem = refs[2 * arrays : -1], refs[-1]
    me = lax.axis_index("tensor")
    advance, finish = line_relay(me, count, ins, outs, chunks, semaphores)
    greet_line(me, count)
    own = [
        pltpu.make_async_copy(ins[at], outs[at].at[me], own_sem.at[at]) for at in range(arrays)
    ]
    everything = tuple(range(arrays))
    advance(0, everything)
    for each in own:
        each.start()
    for hop in range(1, count):
        advance(hop, everything)
    for each in own:
        each.wait()
    finish(everything, range(count - 1))


def gather_line(arrays, chunks, identity):
    count = lax.axis_size("tensor")
    total = sum(chunks)
    anywhere = pl.BlockSpec(memory_space=pl.ANY)
    return pl.pallas_call(
        functools.partial(gather_line_body, count, chunks),
        out_shape=[jax.ShapeDtypeStruct((count,) + a.shape, a.dtype) for a in arrays],
        in_specs=[anywhere] * len(arrays),
        out_specs=[anywhere] * len(arrays),
        scratch_shapes=[pltpu.SemaphoreType.DMA((count - 1, total))] * 4
        + [pltpu.SemaphoreType.DMA((len(arrays),))],
        compiler_params=pltpu.CompilerParams(collective_id=identity, has_side_effects=True),
        name="gather_line",
    )(*arrays)


def sum_line_body(count, chunks, part_ref, out_ref, left_buf, right_buf, *semaphores):
    me = lax.axis_index("tensor")
    advance, finish = line_sum(
        me, count, chunks, part_ref, out_ref, left_buf, right_buf, semaphores
    )
    greet_line(me, count)
    for far in range(count - 1, 0, -1):
        advance(far)
    finish()


def sum_line(part, chunks, identity):
    count, rows, width = part.shape
    semaphores = pltpu.SemaphoreType.DMA((count - 1, chunks))
    return pl.pallas_call(
        functools.partial(sum_line_body, count, chunks),
        out_shape=jax.ShapeDtypeStruct((rows, width), F32),
        in_specs=[pl.BlockSpec(memory_space=pltpu.VMEM)],
        out_specs=pl.BlockSpec(memory_space=pltpu.VMEM),
        scratch_shapes=[
            pltpu.VMEM((count - 1, rows, width), BF16),
            pltpu.VMEM((count - 1, rows, width), BF16),
        ]
        + [semaphores] * 4,
        compiler_params=pltpu.CompilerParams(
            collective_id=identity, has_side_effects=True, vmem_limit_bytes=32 * MEBI
        ),
        name="sum_line",
    )(part)


def front_body(
    plane,
    line,
    scale,
    places,
    ready,
    tokens_hbm,
    cotangent_hbm,
    routes_hbm,
    weights_hbm,
    gain_ref,
    first_ref,
    q_second_ref,
    k_second_ref,
    v_second_ref,
    q_gain_ref,
    k_gain_ref,
    cos_ref,
    sin_ref,
    seg_column_ref,
    seg_row_ref,
    out_first_ref,
    out_second_ref,
    before_ref,
    total_ref,
    ranks_ref,
    low_ref,
    out_low_ref,
    linear_hbm,
    heads_hbm,
    normed_hbm,
    gathered_hbm,
    up_hbm,
    rows,
    upstream,
    routes,
    weights,
    linear,
    heads,
    keys,
    values,
    part,
    left_buf,
    right_buf,
    sent_slots,
    choice,
    own_sem,
    save_sem,
    relay_right_send,
    relay_right_recv,
    relay_left_send,
    relay_left_recv,
    weight_send,
    weight_recv,
    pass_send,
    pass_recv,
    sum_right_send,
    sum_right_recv,
    sum_left_send,
    sum_left_recv,
    slot_send,
    slot_recv,
):
    me, at_line = lax.axis_index("fsdp"), lax.axis_index("tensor")
    rank = q_second_ref.shape[0]
    head_dim = q_gain_ref.shape[1]
    tokens, width = tokens_hbm.shape
    slots = sent_slots.shape[2]
    tile = 256
    query_columns = q_second_ref.shape[1]
    linear_columns = linear.shape[1]
    out_start = places[1]

    greet_line_and_plane(line, plane)

    beside = me + 1 - 2 * lax.rem(me, 2)

    def weight_copy(k):
        target = lax.rem(me + 2 * k, plane)
        return pltpu.make_async_remote_copy(
            src_ref=weights_hbm,
            dst_ref=weights.at[me],
            send_sem=weight_send.at[k],
            recv_sem=weight_recv.at[k],
            device_id={"fsdp": target},
        )

    def weight_pass(k):
        origin = lax.rem(me + plane - 2 * k, plane)
        return pltpu.make_async_remote_copy(
            src_ref=weights_hbm if k == 0 else weights.at[origin],
            dst_ref=weights.at[origin],
            send_sem=pass_send.at[k],
            recv_sem=pass_recv.at[k],
            device_id={"fsdp": beside},
        )

    peers = plane // 2
    for k in range(1, peers):
        weight_copy(k).start()
    weight_pass(0).start()
    locals_in = [
        pltpu.make_async_copy(source, target, own_sem.at[at])
        for at, (source, target) in enumerate(
            [
                (tokens_hbm, rows.at[at_line]),
                (routes_hbm, routes.at[at_line]),
                (cotangent_hbm, upstream.at[at_line]),
                (weights_hbm, weights.at[me]),
            ]
        )
    ]
    advance, finish_relay = line_relay(
        at_line,
        line,
        [tokens_hbm, routes_hbm, cotangent_hbm],
        [rows, routes, upstream],
        (4, 1, 4),
        (relay_right_send, relay_right_recv, relay_left_send, relay_left_recv),
    )
    advance(0, (0, 1))
    for each in locals_in:
        each.start()
    advance(1, (0, 1))
    advance(2, (0, 1))
    advance(0, (2,))
    for k in range(1, peers):
        weight_copy(k).wait_recv()
        weight_pass(k).start()
    advance(3, (0, 1))
    for each in locals_in:
        each.wait()

    ready()

    for block in range(line):
        named = [
            jnp.max(
                (routes[block] == expert * line + at_line).astype(F32), axis=0, keepdims=True
            )
            for expert in range(plane)
        ]
        mask = jnp.concatenate(named, axis=0)
        counts = matrix_product(mask.astype(BF16), before_ref[...])
        ranks_ref[block] = jnp.where(mask > 0.0, counts, -1.0)

    def slot_copy(block, d):
        target = lax.rem(me + d, plane)
        return pltpu.make_async_remote_copy(
            src_ref=sent_slots.at[block, target],
            dst_ref=up_hbm.at[me, block],
            send_sem=slot_send.at[block, d],
            recv_sem=slot_recv.at[block, d],
            device_id={"fsdp": target},
        )

    def own_slots(block):
        return pltpu.make_async_copy(
            sent_slots.at[block, me], up_hbm.at[me, block], save_sem.at[4 + block]
        )

    def dispatch(block):
        choice[...] = slot_choice(ranks_ref[block], slots)

        def slot_step(columns):
            sent_slots[block, :, :, columns] = (
                matrix_product(choice[...], upstream[block, :, columns])
                .astype(BF16)
                .reshape(plane, slots, 2 * tile)
            )

        tiles(width, 2 * tile, slot_step)

        @pl.loop(1, plane)
        def _(d):
            slot_copy(block, d).start()

    def dispatch_at(distance):
        if distance == 0:
            dispatch(at_line)
            return

        @pl.when(at_line - distance >= 0)
        def _():
            dispatch(at_line - distance)

        @pl.when(at_line + distance < line)
        def _():
            dispatch(at_line + distance)

    dispatch_at(0)

    finish_relay((0,), range(1, line - 1))

    @pl.loop(0, line * tokens // 128)
    def _(j):
        block, at = j // (tokens // 128), pl.ds((j % (tokens // 128)) * 128, 128)
        wide = rows[block, at, :].astype(F32)
        rows[block, at, :] = norm_forward(wide, gain_ref[...])[0].astype(BF16)

    for k in range(peers):
        weight_pass(k).wait_recv()
    saves = [
        pltpu.make_async_copy(rows, normed_hbm, save_sem.at[0]),
        pltpu.make_async_copy(weights, gathered_hbm, save_sem.at[1]),
        pltpu.make_async_copy(linear, linear_hbm, save_sem.at[2]),
        pltpu.make_async_copy(heads, heads_hbm, save_sem.at[3]),
    ]
    saves[0].start()
    saves[1].start()

    @pl.loop(0, line)
    def _(block):
        at = pl.ds(pl.multiple_of(block * tokens, tokens), tokens)
        low_ref[at, :] = flipped_right_operand(rows[block], first_ref[...]).astype(BF16)

        def project(columns):
            linear[at, columns] = matrix_product(
                rows[block], weights[:, :, columns].reshape(width, tile)
            )

        tiles(linear_columns, tile, project)

    saves[2].start()
    advance(1, (2,))
    dispatch_at(1)

    cosine, sine = cos_ref[...], sin_ref[...]
    keys[...] = head_values(
        linear[:, query_columns : query_columns + head_dim],
        low_ref[:, rank : 2 * rank],
        k_second_ref[...],
        k_gain_ref[...],
        cosine,
        sine,
    )[2]
    values[...] = (
        linear[:, query_columns + head_dim : query_columns + 2 * head_dim]
        + matrix_product(low_ref[:, 2 * rank : 3 * rank], v_second_ref[...])
    ).astype(BF16)

    @pl.loop(0, query_columns // head_dim)
    def _(head):
        columns = pl.ds(pl.multiple_of(head * head_dim, head_dim), head_dim)
        query = head_values(
            linear[:, columns],
            low_ref[:, :rank],
            q_second_ref[:, columns],
            q_gain_ref[...],
            cos_ref[...],
            sin_ref[...],
        )[2]
        seg_column, seg_row = seg_column_ref[...], seg_row_ref[...]
        for block in range(query.shape[0] // WINDOW):
            start, span = block_bounds(block)
            scores = (
                flipped_right_operand(
                    query[block * WINDOW : (block + 1) * WINDOW], keys[pl.ds(start, span)]
                )
                * scale
            )
            scores = jnp.where(
                allowed_keys(block, start, span, seg_column, seg_row), scores, -1e30
            )
            expo = jnp.exp(scores - jnp.max(scores, axis=-1, keepdims=True))
            probs = (expo / jnp.sum(expo, axis=-1, keepdims=True)).astype(BF16)
            heads[pl.ds(block * WINDOW, WINDOW), columns] = matrix_product(
                probs, values[pl.ds(start, span)]
            ).astype(BF16)

    saves[3].start()
    advance(2, (2,))
    dispatch_at(2)

    out_low_ref[...] = flipped_right_operand(heads[...], out_first_ref[...]).astype(BF16)

    def output_part(block):
        at = pl.ds(pl.multiple_of(block * tokens, tokens), tokens)

        @pl.loop(0, plane)
        def _(shard):
            wide = width // plane
            columns = pl.ds(pl.multiple_of(shard * wide, wide), wide)
            part[block, :, columns] = (
                flipped_right_operand(heads[at, :], weights[shard, :, out_start:])
                + matrix_product(out_low_ref[at, :], out_second_ref[:, columns])
            ).astype(BF16)

    advance_sum, finish_sum = line_sum(
        at_line,
        line,
        4,
        part,
        total_ref,
        left_buf,
        right_buf,
        (sum_right_send, sum_right_recv, sum_left_send, sum_left_recv),
    )
    for far in range(line - 1, 0, -1):

        @pl.when(at_line + far < line)
        def _():
            output_part(at_line + far)

        @pl.when(at_line - far >= 0)
        def _():
            output_part(at_line - far)

        advance_sum(far)
        if far == 2:
            advance(3, (2,))
            dispatch_at(3)
    output_part(at_line)
    finish_sum()

    for block in range(line):
        own_slots(block).start()
    for each in saves:
        each.wait()
    finish_relay((0,), (0,))
    finish_relay((1, 2), range(line - 1))
    for k in range(1, peers):
        weight_copy(k).wait_send()
    for k in range(peers):
        weight_pass(k).wait_send()

    @pl.loop(0, line)
    def _(block):
        @pl.loop(1, plane)
        def _(d):
            slot_copy(block, d).wait_recv()
            slot_copy(block, d).wait_send()

    for block in range(line):
        own_slots(block).wait()


def front(
    tokens,
    cotangent,
    routes,
    packed,
    gain,
    first,
    q_second,
    k_second,
    v_second,
    q_gain,
    k_gain,
    tables,
    seg_column,
    seg_row,
    out_first,
    out_second,
    scale,
    slots,
    places,
    identity,
):
    line, plane = lax.axis_size("tensor"), lax.axis_size("fsdp")
    count, width = tokens.shape
    all_rows = line * count
    rank, query_columns = q_second.shape
    head_dim = q_gain.shape[1]
    linear_columns = query_columns + 2 * head_dim
    order = jnp.arange(count, dtype=jnp.int32)
    before = (order[:, None] < order[None, :]).astype(BF16)
    anywhere = pl.BlockSpec(memory_space=pl.ANY)
    local = pl.BlockSpec(memory_space=pltpu.VMEM)
    dma = pltpu.SemaphoreType.DMA
    up_shape = (plane, line, slots, width)
    operands = [
        gain,
        first,
        q_second,
        k_second,
        v_second,
        q_gain,
        k_gain,
        *tables,
        seg_column,
        seg_row,
        out_first,
        out_second,
        before,
    ]
    return pl.pallas_call(
        staged(
            functools.partial(front_body, plane, line, scale, places), 4, len(operands)
        ),
        out_shape=[
            jax.ShapeDtypeStruct((count, width), F32),
            jax.ShapeDtypeStruct((line, plane, count), F32),
            jax.ShapeDtypeStruct((all_rows, 3 * rank), BF16),
            jax.ShapeDtypeStruct((all_rows, rank), BF16),
            jax.ShapeDtypeStruct((all_rows, linear_columns), F32),
            jax.ShapeDtypeStruct((all_rows, query_columns), BF16),
            jax.ShapeDtypeStruct((line, count, width), BF16),
            jax.ShapeDtypeStruct((plane,) + packed.shape, BF16),
            jax.ShapeDtypeStruct(up_shape, BF16),
        ],
        in_specs=[anywhere] * (4 + len(operands)),
        out_specs=[local] * 4 + [anywhere] * 5,
        scratch_shapes=[
            pltpu.VMEM((line, count, width), BF16),
            pltpu.VMEM((line, count, width), BF16),
            pltpu.VMEM((line,) + routes.shape, jnp.int32),
            pltpu.VMEM((plane,) + packed.shape, BF16),
            pltpu.VMEM((all_rows, linear_columns), F32),
            pltpu.VMEM((all_rows, query_columns), BF16),
            pltpu.VMEM((all_rows, head_dim), BF16),
            pltpu.VMEM((all_rows, head_dim), BF16),
            pltpu.VMEM((line, count, width), BF16),
            pltpu.VMEM((line - 1, count, width), BF16),
            pltpu.VMEM((line - 1, count, width), BF16),
            pltpu.VMEM((line, plane, slots, width), BF16),
            pltpu.VMEM((plane * slots, count), BF16),
            dma((4,)),
            dma((4 + line,)),
        ]
        + [dma((line - 1, 9))] * 4
        + [dma((plane // 2,))] * 4
        + [dma((line - 1, 4))] * 4
        + [dma((line, plane))] * 2
        + staging(operands),
        compiler_params=pltpu.CompilerParams(
            collective_id=identity, has_side_effects=True, vmem_limit_bytes=63 * MEBI
        ),
        name="front",
    )(tokens, cotangent, routes, packed, *operands)


def back_body(
    plane,
    line,
    scale,
    places,
    moe_total_ref,
    dots_ref,
    gates_ref,
    residual_ref,
    cotangent_ref,
    moe_gain_ref,
    router_first_ref,
    router_second_ref,
    router_low_ref,
    moe_rows_ref,
    ranks_ref,
    low_ref,
    out_low_ref,
    first_out_ref,
    second_out_ref,
    q_second_ref,
    k_second_ref,
    v_second_ref,
    q_gain_ref,
    k_gain_ref,
    cos_ref,
    sin_ref,
    seg_column_ref,
    seg_row_ref,
    linear_hbm,
    heads_hbm,
    normed_hbm,
    gathered_hbm,
    y_hbm,
    output_ref,
    residual_grad_ref,
    share_ref,
    linear_grad_ref,
    owned_ref,
    y_in_hbm,
    branch_own,
    branch,
    out_weights,
    router_weights,
    linear,
    heads,
    normed,
    upstream,
    out_low_grad,
    keys,
    values,
    key_sum,
    value_sum,
    query_sum,
    share_sum,
    second_sum,
    y_rows,
    partials,
    left_buf,
    right_buf,
    result,
    choice,
    rows_out_ref,
    heads_out_ref,
    narrow_out_ref,
    router_out_ref,
    load_sem,
    y_sem,
    relay_right_send,
    relay_right_recv,
    relay_left_send,
    relay_left_recv,
    y_send,
    y_recv,
    sum_right_send,
    sum_right_recv,
    sum_left_send,
    sum_left_recv,
):
    me, at_line = lax.axis_index("fsdp"), lax.axis_index("tensor")
    tokens, width = residual_ref.shape
    rank, query_columns = q_second_ref.shape
    head_dim = q_gain_ref.shape[1]
    slots = y_rows.shape[1]
    tile = 256

    greet_line_and_plane(line, plane)

    orders = [sorted(range(line), key=lambda block: abs(block - at)) for at in range(line)]

    def place_of(step):
        result = 0
        for at in range(line):
            result = jnp.where(at_line == at, orders[at][step], result)
        return result

    def y_copy(block, d):
        target = lax.rem(me + d, plane)
        return pltpu.make_async_remote_copy(
            src_ref=y_hbm.at[target, block],
            dst_ref=y_in_hbm.at[block, me],
            send_sem=y_send.at[block, d],
            recv_sem=y_recv.at[block, d],
            device_id={"fsdp": target},
        )

    def own_y(block):
        return pltpu.make_async_copy(
            y_hbm.at[me, block], y_in_hbm.at[block, me], y_sem.at[block]
        )

    def send_y(step):
        block = place_of(step)

        @pl.loop(1, plane)
        def _(d):
            y_copy(block, d).start()

        own_y(block).start()

    send_y(line - 1)
    send_y(line - 2)
    advance_sum, finish_sum = line_sum(
        at_line,
        line,
        4,
        partials,
        result,
        left_buf,
        right_buf,
        (sum_right_send, sum_right_recv, sum_left_send, sum_left_recv),
    )
    loads = [
        pltpu.make_async_copy(source, target, load_sem.at[at])
        for at, (source, target) in enumerate(
            [
                (
                    gathered_hbm.at[:, :, pl.ds(places[0], places[1] - places[0])],
                    router_weights,
                ),
                (gathered_hbm.at[:, :, pl.ds(places[1], query_columns)], out_weights),
                (linear_hbm, linear),
                (heads_hbm, heads),
                (normed_hbm, normed),
            ]
        )
    ]
    for each in loads:
        each.start()

    def combine(step):
        block = place_of(step)

        @pl.loop(1, plane)
        def _(d):
            y_copy(block, d).wait_recv()

        own_y(block).wait()
        if step > 1:
            send_y(step - 2)
        load = pltpu.make_async_copy(y_in_hbm.at[block], y_rows, y_sem.at[line])
        load.start()
        choice[...] = slot_choice(ranks_ref[block], slots)
        load.wait()

        def combined(columns):
            total = flipped_left_operand(
                choice[...], y_rows[:, :, columns].reshape(plane * slots, 2 * tile)
            )
            partials[block, :, columns] = total.astype(BF16)

        tiles(width, 2 * tile, combined)
        if step > 0:
            advance_sum(step)

    loads[0].wait()
    router_ref = router_weights[...].reshape(width, -1)
    gates = gates_ref[...]
    dots = dots_ref[...]
    logit_grad = (gates * (dots - jnp.sum(gates * dots, axis=0, keepdims=True))).astype(BF16)
    experts_count, lanes = gates.shape[0], router_ref.shape[1]
    wide_logit_grad = jnp.transpose(
        jnp.concatenate(
            [
                logit_grad.astype(F32),
                jnp.zeros((lanes - experts_count, tokens), F32),
            ],
            axis=0,
        ),
        (1, 0),
    ).astype(BF16)
    router_low_grad = matrix_product(
        router_second_ref[:, :experts_count], logit_grad
    ).astype(BF16)
    rows_out_ref[4 * rank :, :] = matrix_product(router_low_grad, moe_rows_ref[...]).astype(BF16)
    router_out_ref[...] = flipped_right_operand(router_low_ref[...], logit_grad)
    half = tokens // 2
    for part in range(2):
        rows = pl.ds(part * half, half)
        columns = slice(part * half, (part + 1) * half)
        moe_grad = (
            moe_total_ref[rows, :]
            + flipped_right_operand(wide_logit_grad[columns], router_ref)
            + flipped_left_operand(router_low_grad[:, columns], router_first_ref[...])
        )
        residual = residual_ref[rows, :]
        factor = lax.rsqrt(
            jnp.mean(residual * residual, axis=-1, keepdims=True) + NORM_EPSILON
        )
        residual_grad = cotangent_ref[rows, :].astype(F32) + norm_backward(
            residual, factor, moe_gain_ref[...], moe_grad
        )
        residual_grad_ref[rows, :] = residual_grad
        branch_own[rows, :] = residual_grad.astype(BF16)
    branch[at_line] = branch_own[...]

    advance, finish_relay = line_relay(
        at_line,
        line,
        [branch_own],
        [branch],
        (4,),
        (relay_right_send, relay_right_recv, relay_left_send, relay_left_recv),
    )
    advance(0, (0,))
    second_sum[...] = jnp.zeros_like(second_sum)
    loads[1].wait()

    def head_gradients(block):
        at = pl.ds(pl.multiple_of(block * tokens, tokens), tokens)
        low_grad = flipped_right_operand(branch[block], second_out_ref[...]).astype(BF16)
        out_low_grad[at, :] = low_grad
        second_sum[...] += flipped_left_operand(out_low_ref[at, :], branch[block])

        def project(columns):
            upstream[at, columns] = (
                matrix_product(branch[block], out_weights[:, :, columns].reshape(width, tile))
                + matrix_product(low_grad, first_out_ref[:, columns])
            ).astype(BF16)

        tiles(query_columns, tile, project)

    head_gradients(at_line)
    for each in loads[2:]:
        each.wait()
    cosine, sine = cos_ref[...], sin_ref[...]
    key_columns = slice(query_columns, query_columns + head_dim)
    value_columns = slice(query_columns + head_dim, query_columns + 2 * head_dim)
    keys[...] = head_values(
        linear[:, key_columns],
        low_ref[:, rank : 2 * rank],
        k_second_ref[...],
        k_gain_ref[...],
        cosine,
        sine,
    )[2]
    values[...] = (
        linear[:, value_columns]
        + matrix_product(low_ref[:, 2 * rank : 3 * rank], v_second_ref[...])
    ).astype(BF16)
    key_sum[...] = jnp.zeros_like(key_sum)
    value_sum[...] = jnp.zeros_like(value_sum)
    share_sum[...] = jnp.zeros_like(share_sum)
    for hop in range(1, line):
        advance(hop, (0,))

        @pl.when(at_line - hop >= 0)
        def _():
            head_gradients(at_line - hop)

        @pl.when(at_line + hop < line)
        def _():
            head_gradients(at_line + hop)

        if hop < line - 1:
            combine(line - hop)
    rows_out_ref[3 * rank : 4 * rank, :] = second_sum[...].astype(BF16)

    head_count = query_columns // head_dim

    @pl.loop(0, head_count)
    def _(head):
        columns = pl.ds(pl.multiple_of(head * head_dim, head_dim), head_dim)
        low_q = low_ref[:, :rank]
        lines, factor, query = head_values(
            linear[:, columns],
            low_q,
            q_second_ref[:, columns],
            q_gain_ref[...],
            cos_ref[...],
            sin_ref[...],
        )
        heads_out_ref[rank:, columns] = flipped_left_operand(
            out_low_grad[...], heads[:, columns]
        ).astype(BF16)
        seg_column, seg_row = seg_column_ref[...], seg_row_ref[...]
        for block in range(query.shape[0] // WINDOW):
            start, span = block_bounds(block)
            at, near = pl.ds(block * WINDOW, WINDOW), pl.ds(start, span)
            query_block = query[block * WINDOW : (block + 1) * WINDOW]
            upstream_block = upstream[at, columns]
            scores = flipped_right_operand(query_block, keys[near]) * scale
            scores = jnp.where(
                allowed_keys(block, start, span, seg_column, seg_row), scores, -1e30
            )
            expo = jnp.exp(scores - jnp.max(scores, axis=-1, keepdims=True))
            probs = expo / jnp.sum(expo, axis=-1, keepdims=True)
            prob_grad = flipped_right_operand(upstream_block, values[near])
            score_grad = (
                probs * (prob_grad - jnp.sum(probs * prob_grad, axis=-1, keepdims=True))
            ).astype(BF16)
            value_sum[near, :] += flipped_left_operand(probs.astype(BF16), upstream_block)
            key_sum[near, :] += flipped_left_operand(score_grad, query_block)
            query_sum[at, :] = matrix_product(score_grad, keys[near]) * scale
        q_grad = head_values_gradient(
            lines, factor, q_gain_ref[...], cos_ref[...], sin_ref[...], query_sum[...]
        )
        linear_grad_ref[:, columns] = q_grad
        heads_out_ref[:rank, columns] = flipped_left_operand(low_q, q_grad).astype(BF16)
        share_sum[:, :rank] += flipped_right_operand(q_grad, q_second_ref[:, columns])

        @pl.when(head == head_count // 2 - 1)
        def _():
            combine(1)

    low_k = low_ref[:, rank : 2 * rank]
    low_v = low_ref[:, 2 * rank : 3 * rank]
    key_lines, key_factor, _turned = head_values(
        linear[:, key_columns], low_k, k_second_ref[...], k_gain_ref[...], cosine, sine
    )
    k_grad = head_values_gradient(
        key_lines, key_factor, k_gain_ref[...], cosine, sine, key_sum[...] * scale
    )
    v_grad = value_sum[...].astype(BF16)
    linear_grad_ref[:, key_columns] = k_grad
    linear_grad_ref[:, value_columns] = v_grad
    narrow_out_ref[:rank, :] = flipped_left_operand(low_k, k_grad).astype(BF16)
    narrow_out_ref[rank:, :] = flipped_left_operand(low_v, v_grad).astype(BF16)
    share_sum[:, rank : 2 * rank] = flipped_right_operand(k_grad, k_second_ref[...])
    share_sum[:, 2 * rank :] = flipped_right_operand(v_grad, v_second_ref[...])
    share_ref[...] = share_sum[...].astype(BF16)

    def first_gradient(columns):
        rows_out_ref[: 3 * rank, columns] = flipped_left_operand(
            share_ref[...], normed[:, columns]
        ).astype(BF16)

    tiles(width, 2 * tile, first_gradient)

    pieces, lines, lanes_out = owned_ref.shape
    row_lines, span = rows_out_ref.shape[0], width // pieces
    owned_ref[...] = jnp.zeros_like(owned_ref)
    for piece in range(pieces):
        owned_ref[piece, :row_lines, :span] = rows_out_ref[:, piece * span : (piece + 1) * span]
        at = (piece % line) * plane + piece // line
        owned_ref[piece, :rank, span : span + 1] = router_out_ref[:, at : at + 1].astype(BF16)
    narrow_span = head_dim // plane
    for piece in range(plane):
        owner = at_line * plane + piece
        owned_ref[owner, row_lines:, :] = heads_out_ref[
            :, piece * lanes_out : (piece + 1) * lanes_out
        ]
        owned_ref[owner, : 2 * rank, span + rank : span + rank + narrow_span] = narrow_out_ref[
            :, piece * narrow_span : (piece + 1) * narrow_span
        ]
    combine(0)
    finish_sum()
    output_ref[...] = (residual_ref[...] + result[...]).astype(BF16)
    finish_relay((0,), range(line - 1))
    for block in range(line):

        @pl.loop(1, plane)
        def _(d):
            y_copy(block, d).wait_send()


def back(scale, places, slots, identity, hbm_operands, operands):
    line, plane = lax.axis_size("tensor"), lax.axis_size("fsdp")
    linear, heads, normed, gathered, _y = hbm_operands
    count, width = operands[0].shape
    all_rows, linear_columns = linear.shape
    query_columns = heads.shape[1]
    head_dim = (linear_columns - query_columns) // 2
    rank = operands[12].shape[1]
    experts_count = line * plane
    anywhere = pl.BlockSpec(memory_space=pl.ANY)
    local = pl.BlockSpec(memory_space=pltpu.VMEM)
    dma = pltpu.SemaphoreType.DMA
    single = (all_rows, head_dim)
    block = (count, width)
    return pl.pallas_call(
        functools.partial(back_body, plane, line, scale, places),
        out_shape=[
            jax.ShapeDtypeStruct(block, BF16),
            jax.ShapeDtypeStruct(block, F32),
            jax.ShapeDtypeStruct((all_rows, 3 * rank), BF16),
            jax.ShapeDtypeStruct((all_rows, linear_columns), BF16),
            jax.ShapeDtypeStruct((experts_count, 7 * rank, head_dim), BF16),
            jax.ShapeDtypeStruct((line, plane, slots, width), BF16),
        ],
        in_specs=[local] * len(operands) + [anywhere] * len(hbm_operands),
        out_specs=[local] * 5 + [anywhere],
        scratch_shapes=[
            pltpu.VMEM(block, BF16),
            pltpu.VMEM((line,) + block, BF16),
            pltpu.VMEM((plane, width // plane, query_columns), BF16),
            pltpu.VMEM((plane, width // plane, places[1] - places[0]), BF16),
            pltpu.VMEM((all_rows, linear_columns), F32),
            pltpu.VMEM((all_rows, query_columns), BF16),
            pltpu.VMEM((all_rows, width), BF16),
            pltpu.VMEM((all_rows, query_columns), BF16),
            pltpu.VMEM((all_rows, rank), BF16),
            pltpu.VMEM(single, BF16),
            pltpu.VMEM(single, BF16),
            pltpu.VMEM(single, F32),
            pltpu.VMEM(single, F32),
            pltpu.VMEM(single, F32),
            pltpu.VMEM((all_rows, 3 * rank), F32),
            pltpu.VMEM((rank, width), F32),
            pltpu.VMEM((plane, slots, width), BF16),
            pltpu.VMEM((line,) + block, BF16),
            pltpu.VMEM((line - 1,) + block, BF16),
            pltpu.VMEM((line - 1,) + block, BF16),
            pltpu.VMEM(block, F32),
            pltpu.VMEM((plane * slots, count), BF16),
            pltpu.VMEM((5 * rank, width), BF16),
            pltpu.VMEM((2 * rank, query_columns), BF16),
            pltpu.VMEM((2 * rank, head_dim), BF16),
            pltpu.VMEM((rank, experts_count), F32),
            dma((5,)),
            dma((line + 1,)),
        ]
        + [dma((line - 1, 4))] * 4
        + [dma((line, plane))] * 2
        + [dma((line - 1, 4))] * 4,
        compiler_params=pltpu.CompilerParams(
            collective_id=identity, has_side_effects=True, vmem_limit_bytes=63 * MEBI
        ),
        name="back",
    )(*operands, *hbm_operands)


def last_body(
    line,
    ready,
    linear_grad_ref,
    share_ref,
    first_ref,
    residual_grad_ref,
    tokens_ref,
    gain_ref,
    gathered_hbm,
    input_grad_ref,
    weights,
    part,
    left_buf,
    right_buf,
    load_sem,
    *semaphores,
):
    at_line = lax.axis_index("tensor")
    tokens, width = tokens_ref.shape
    linear_columns = linear_grad_ref.shape[1]
    load = pltpu.make_async_copy(
        gathered_hbm.at[:, :, pl.ds(0, linear_columns)], weights, load_sem
    )
    load.start()
    greet_line(at_line, line)
    ready()
    load.wait()
    shards, wide = weights.shape[:2]

    def normed_gradient(block):
        at = pl.ds(pl.multiple_of(block * tokens, tokens), tokens)

        @pl.loop(0, shards)
        def _(shard):
            columns = pl.ds(pl.multiple_of(shard * wide, wide), wide)
            part[block, :, columns] = (
                flipped_right_operand(linear_grad_ref[at, :], weights[shard])
                + matrix_product(share_ref[at, :], first_ref[:, columns])
            ).astype(BF16)

    advance, finish = line_sum(
        at_line, line, 4, part, input_grad_ref, left_buf, right_buf, semaphores
    )
    for far in range(line - 1, 0, -1):

        @pl.when(at_line + far < line)
        def _():
            normed_gradient(at_line + far)

        @pl.when(at_line - far >= 0)
        def _():
            normed_gradient(at_line - far)

        advance(far)
    normed_gradient(at_line)
    finish()
    half = tokens // 2
    for at in range(2):
        rows = pl.ds(at * half, half)
        values = tokens_ref[rows, :].astype(F32)
        factor = lax.rsqrt(jnp.mean(values * values, axis=-1, keepdims=True) + NORM_EPSILON)
        input_grad_ref[rows, :] = residual_grad_ref[rows, :] + norm_backward(
            values, factor, gain_ref[...], input_grad_ref[rows, :]
        )


def last(linear_grad, share, first, residual_grad, tokens, gain, gathered, identity):
    line = lax.axis_size("tensor")
    count, width = tokens.shape
    anywhere = pl.BlockSpec(memory_space=pl.ANY)
    local = pl.BlockSpec(memory_space=pltpu.VMEM)
    dma = pltpu.SemaphoreType.DMA
    operands = [linear_grad, share, first, residual_grad, tokens, gain]
    return pl.pallas_call(
        staged(functools.partial(last_body, line), 0, 6),
        out_shape=jax.ShapeDtypeStruct((count, width), F32),
        in_specs=[anywhere] * 7,
        out_specs=local,
        scratch_shapes=[
            pltpu.VMEM(gathered.shape[:2] + (linear_grad.shape[1],), BF16),
            pltpu.VMEM((line, count, width), BF16),
            pltpu.VMEM((line - 1, count, width), BF16),
            pltpu.VMEM((line - 1, count, width), BF16),
            dma,
        ]
        + [dma((line - 1, 4))] * 4
        + staging(operands),
        compiler_params=pltpu.CompilerParams(
            collective_id=identity, has_side_effects=True, vmem_limit_bytes=63 * MEBI
        ),
        name="last",
    )(*operands, gathered)


def prepare_body(
    _adapters_ref,
    _place_ref,
    query_in_ref,
    key_in_ref,
    value_in_ref,
    query_out_ref,
    key_out_ref,
    value_out_ref,
    attn_in_ref,
    attn_out_ref,
    router_in_ref,
    router_out_ref,
    w_query_ref,
    w_key_ref,
    w_value_ref,
    w_router_ref,
    w_out_ref,
    order_ref,
    segments_ref,
    first_ref,
    q_second_ref,
    k_second_ref,
    v_second_ref,
    out_first_ref,
    out_second_ref,
    router_first_ref,
    router_second_ref,
    packed_ref,
    seg_column_ref,
):
    rank = query_in_ref.shape[1]
    for at, ref in enumerate((query_in_ref, key_in_ref, value_in_ref)):
        first_ref[at * rank : (at + 1) * rank, :] = ref[0]
    q_second_ref[...] = query_out_ref[0]
    k_second_ref[...] = key_out_ref[0]
    v_second_ref[...] = value_out_ref[0]
    out_first_ref[...] = attn_in_ref[0]
    out_second_ref[...] = attn_out_ref[0]
    router_first_ref[...] = router_in_ref[0]
    router_second_ref[...] = matrix_product(router_out_ref[0], order_ref[...]).astype(BF16)
    start = 0
    for ref in (w_query_ref, w_key_ref, w_value_ref):
        width = ref.shape[1]
        packed_ref[:, start : start + width] = ref[...]
        start += width
    width = order_ref.shape[1]
    packed_ref[:, start : start + width] = flipped_left_operand(
        w_router_ref[...], order_ref[...]
    ).astype(BF16)
    start += width
    for at in range(0, w_out_ref.shape[0], 256):
        packed_ref[:, start + at : start + at + 256] = jnp.transpose(
            w_out_ref[at : at + 256, :], (1, 0)
        )
    marks = jnp.broadcast_to(segments_ref[...].astype(F32), (8, segments_ref.shape[1]))
    seg_column_ref[...] = jnp.transpose(marks, (1, 0))[:, :1].astype(jnp.int32)


def prepare(adapters, place, tables, weights, order, segments):
    def chosen(table):
        return pl.BlockSpec(
            (1,) + table.shape[1:], lambda _, adapter, at: (adapter[at[0]], 0, 0)
        )

    def resident(shape):
        return pl.BlockSpec(tuple(shape), lambda *_: (0,) * len(shape))

    rank = tables[0].shape[1]
    columns = sum(w.shape[1] for w in weights[:3]) + order.shape[1] + weights[4].shape[0]
    shapes = [
        ((3 * rank, tables[0].shape[2]), BF16),
        (tables[3].shape[1:], BF16),
        (tables[4].shape[1:], BF16),
        (tables[5].shape[1:], BF16),
        (tables[6].shape[1:], BF16),
        (tables[7].shape[1:], BF16),
        (tables[8].shape[1:], BF16),
        ((rank, order.shape[1]), BF16),
        ((weights[0].shape[0], columns), BF16),
        ((segments.shape[1], 1), jnp.int32),
    ]
    return pl.pallas_call(
        prepare_body,
        grid_spec=pltpu.PrefetchScalarGridSpec(
            num_scalar_prefetch=2,
            grid=(1,),
            in_specs=[chosen(table) for table in tables]
            + [resident(w.shape) for w in weights]
            + [resident(order.shape), resident(segments.shape)],
            out_specs=[resident(shape) for shape, _ in shapes],
        ),
        out_shape=[jax.ShapeDtypeStruct(shape, dtype) for shape, dtype in shapes],
        compiler_params=params(63),
        name="prepare",
    )(adapters, place, *tables, *weights, order, segments)


def router_body(
    line,
    total_ref,
    tokens_ref,
    gain_ref,
    weights_ref,
    first_ref,
    second_ref,
    routes_ref,
    residual_ref,
    rows_ref,
    gates_ref,
    sent_ref,
    low_ref,
):
    count, width = tokens_ref.shape
    residual = total_ref[...] + tokens_ref[...].astype(F32)
    residual_ref[...] = residual
    rows_ref[...] = norm_forward(residual, gain_ref[...])[0].astype(BF16)
    low_ref[...] = flipped_right_operand(first_ref[...], rows_ref[...]).astype(BF16)
    logits = matrix_product(rows_ref[...], weights_ref[...].reshape(width, -1))
    logits = jnp.transpose(logits, (1, 0)) + flipped_left_operand(second_ref[...], low_ref[...])
    experts_count = gates_ref.shape[0]
    plane = experts_count // line
    logits = logits[:experts_count]
    at = lax.broadcasted_iota(jnp.int32, (experts_count, count), 0)
    names = (at % plane) * line + at // plane
    chosen = jnp.zeros((experts_count, count), jnp.bool_)
    for k in range(routes_ref.shape[0]):
        chosen = chosen | (names == routes_ref[k : k + 1, :])
    peak = jnp.max(jnp.where(chosen, logits, -jnp.inf), axis=0, keepdims=True)
    expo = jnp.where(chosen, jnp.exp(jnp.where(chosen, logits - peak, 0.0)), 0.0)
    gates = expo / jnp.sum(expo, axis=0, keepdims=True)
    gates_ref[...] = gates
    sent = jnp.where(chosen, gates, -1.0)
    for group in range(line):
        sent_ref[group] = sent[group * plane : (group + 1) * plane]


def router(total, tokens, gain, gathered, column, first, second, routes):
    line, plane = lax.axis_size("tensor"), lax.axis_size("fsdp")
    count, width = tokens.shape
    lanes = second.shape[1]

    def resident(shape):
        return pl.BlockSpec(tuple(shape), lambda *_: (0,) * len(shape))

    shapes = [
        ((count, width), F32),
        ((count, width), BF16),
        ((line * plane, count), F32),
        ((line, plane, count), F32),
        ((first.shape[0], count), BF16),
    ]
    return pl.pallas_call(
        functools.partial(router_body, line),
        grid=(1,),
        in_specs=[
            resident(total.shape),
            resident(tokens.shape),
            resident(gain.shape),
            pl.BlockSpec(gathered.shape[:2] + (lanes,), lambda _: (0, 0, column // lanes)),
            resident(first.shape),
            resident(second.shape),
            resident(routes.shape),
        ],
        out_specs=[resident(shape) for shape, _ in shapes],
        out_shape=[jax.ShapeDtypeStruct(shape, dtype) for shape, dtype in shapes],
        compiler_params=params(63),
        name="router",
    )(total, tokens, gain, gathered, first, second, routes)


def owners_body(spans, adapters_ref, pieces_ref, *refs):
    outs, total = refs[:-1], refs[-1]
    span, narrow_span = spans
    sources = adapters_ref.shape[0]
    group = pieces_ref.shape[0] // sources
    rank = outs[0].shape[1]
    total[...] = jnp.zeros_like(total)

    @pl.loop(0, sources)
    def _(source):
        addend = pieces_ref[source * group].astype(F32)
        for at in range(1, group):
            addend = addend + pieces_ref[source * group + at].astype(F32)
        total[adapters_ref[source]] += addend

    for at in range(5):
        outs[at][...] = total[:, at * rank : (at + 1) * rank, :span]
    outs[5][...] = total[:, :rank, span : span + 1]
    outs[6][...] = total[:, 5 * rank : 6 * rank, :]
    outs[7][...] = total[:, 6 * rank :, :]
    columns = slice(span + rank, span + rank + narrow_span)
    outs[8][...] = total[:, :rank, columns]
    outs[9][...] = total[:, rank : 2 * rank, columns]


def owners(adapters, pieces, adapter_count, rank, span, narrow_span):
    lanes = pieces.shape[2]
    shapes = (
        [(adapter_count, rank, span)] * 5
        + [(adapter_count, rank, 1)]
        + [(adapter_count, rank, lanes)] * 2
        + [(adapter_count, rank, narrow_span)] * 2
    )

    def resident(shape):
        return pl.BlockSpec(tuple(shape), lambda *_: (0,) * len(shape))

    return pl.pallas_call(
        functools.partial(owners_body, (span, narrow_span)),
        grid_spec=pltpu.PrefetchScalarGridSpec(
            num_scalar_prefetch=1,
            grid=(1,),
            in_specs=[resident(pieces.shape)],
            out_specs=[resident(shape) for shape in shapes],
            scratch_shapes=[pltpu.VMEM((adapter_count,) + pieces.shape[1:], F32)],
        ),
        out_shape=[jax.ShapeDtypeStruct(shape, F32) for shape in shapes],
        compiler_params=params(63),
        name="owners",
    )(adapters, pieces)


def per_device(
    tokens,
    segments,
    routes,
    adapter_index,
    cotangent,
    attn_gain,
    moe_gain,
    q_gain,
    key_norm_gain,
    w_query,
    key_projection_weight,
    value_projection_weight,
    w_out,
    w_router,
    expert_gate_weight,
    expert_up_weight,
    expert_down_weight,
    query_in,
    query_out,
    key_in,
    key_second_weight,
    value_in,
    value_second_weight,
    attn_in,
    attn_out,
    router_in,
    router_out,
    gate_in,
    gate_out,
    upward_in,
    upward_out,
    downward_in,
    downward_out,
):
    tensor_count = lax.axis_size("tensor")
    fsdp_count = lax.axis_size("fsdp")
    device_count = fsdp_count * tensor_count
    tensor_pos = lax.axis_index("tensor")
    fsdp_pos = lax.axis_index("fsdp")
    zero_pos = fsdp_pos * 0
    tok_rows, model_width = tokens.shape
    seq_rows = tok_rows * tensor_count
    rank = query_in.shape[2]
    adapter_count = query_in.shape[0]
    head_dim = q_gain.shape[0]
    local_cols = query_out.shape[2]
    local_kv_cols = key_second_weight.shape[2]
    expert_count = w_router.shape[1]
    top_count = routes.shape[1]
    capacity = 5 * tok_rows * top_count // (4 * expert_count)
    slots = -(-capacity // 16) * 16
    score_scale = 1.0 / math.sqrt(head_dim)
    adapter_pick = lax.dynamic_index_in_dim(adapter_index, fsdp_pos, 0, keepdims=False)

    def select_adapter(adapter_table):
        return lax.dynamic_index_in_dim(adapter_table, adapter_pick, 0, keepdims=False)

    def transposed(adapter_table):
        return jnp.swapaxes(adapter_table, -1, -2)

    gain_attn = attn_gain.astype(F32)
    gain_moe = moe_gain.astype(F32)
    gain_query = q_gain.astype(F32)[None, :]
    gain_key = key_norm_gain.astype(F32)[None, :]

    in_kernel = fsdp_count * slots <= 640
    linear_cols = local_cols + 2 * local_kv_cols
    router_pad = -(-expert_count // 128) * 128
    out_start = linear_cols + router_pad
    tables = rope_tables(seq_rows, head_dim)
    seg_row = segments
    routes_t = jnp.transpose(routes, (1, 0))
    if in_kernel:
        expert_order = np.zeros((expert_count, router_pad), np.float32)
        places = np.arange(expert_count)
        expert_order[
            (places % fsdp_count) * tensor_count + places // fsdp_count, places
        ] = 1.0
        (
            input_first,
            q_second,
            k_second,
            v_second,
            attention_first,
            attention_second,
            router_first,
            router_second,
            packed,
            seg_column,
        ) = prepare(
            adapter_index,
            fsdp_pos[None],
            [
                transposed(query_in),
                transposed(key_in),
                transposed(value_in),
                query_out,
                key_second_weight,
                value_second_weight,
                transposed(attn_in),
                attn_out,
                transposed(router_in),
                router_out,
            ],
            [
                w_query,
                key_projection_weight,
                value_projection_weight,
                jnp.transpose(w_router, (1, 0)),
                w_out,
            ],
            jnp.asarray(expert_order, BF16),
            segments,
        )
    else:
        input_first = jnp.concatenate(
            [select_adapter(transposed(table)) for table in (query_in, key_in, value_in)], axis=0
        )
        q_second = select_adapter(query_out)
        k_second = select_adapter(key_second_weight)
        v_second = select_adapter(value_second_weight)
        attention_first = select_adapter(transposed(attn_in))
        attention_second = select_adapter(attn_out)
        router_first = select_adapter(transposed(router_in))
        router_second = select_adapter(router_out)
        packed = jnp.concatenate(
            [
                w_query,
                key_projection_weight,
                value_projection_weight,
                jnp.pad(w_router, ((0, 0), (0, router_pad - expert_count))),
                jnp.transpose(w_out, (1, 0)),
            ],
            axis=1,
        )
        seg_column = jnp.transpose(segments, (1, 0))
    token_values = tokens.astype(F32)
    attn_normed, attn_factor = norm_forward(token_values, gain_attn)
    offsets = [0] + [sign * step for step in range(1, tensor_count) for sign in (1, -1)]
    offsets = [offset % tensor_count for offset in offsets[:tensor_count]]
    line_blocks = [((tensor_pos + offset) % tensor_count)[None] for offset in offsets]

    def fetched(block, offset):
        if offset == 0:
            return block
        pairs = [((at + offset) % tensor_count, at) for at in range(tensor_count)]
        return lax.ppermute(block, "tensor", pairs)

    def delivered(block, offset):
        if offset == 0:
            return block
        pairs = [(at, (at + offset) % tensor_count) for at in range(tensor_count)]
        return lax.ppermute(block, "tensor", pairs)

    def dispatched(block):
        return [
            plane_rows(to_slots(at, plane_ranks, fetched(block, offset), slots))
            for offset, at in zip(offsets, line_blocks)
        ]

    if in_kernel:
        (
            attention_total,
            plane_ranks,
            low,
            attention_low,
            linear,
            heads_narrow,
            sequence_normalized,
            gathered,
            up_rows,
        ) = front(
            tokens,
            cotangent,
            routes_t,
            packed,
            gain_attn[None, :],
            input_first,
            q_second,
            k_second,
            v_second,
            gain_query,
            gain_key,
            tables,
            seg_column,
            seg_row,
            attention_first,
            attention_second,
            score_scale,
            slots,
            (linear_cols, out_start),
            0,
        )
        sequence_normalized = sequence_normalized.reshape(seq_rows, model_width)
    else:
        gathered = lax.all_gather(packed, "fsdp", axis=0, tiled=True)
        sequence_tokens, sequence_routes = gather_line(
            [tokens, jnp.transpose(routes, (1, 0))], (4, 1), 0
        )
        sequence_tokens = sequence_tokens.reshape(seq_rows, model_width)
        plane_experts = jnp.arange(fsdp_count, dtype=jnp.int32) * tensor_count + tensor_pos
        plane_ranks = ranks_of(
            jnp.any(
                sequence_routes[:, None, :, :] == plane_experts[None, :, None, None], axis=2
            )
        )
        up_rows = dispatched(cotangent)
        sequence_normalized = norm_forward(sequence_tokens.astype(F32), gain_attn)[0].astype(
            BF16
        )
        linear = matrix_product(sequence_normalized, gathered[:, :linear_cols])
        low = flipped_right_operand(sequence_normalized, input_first).astype(BF16)
        complete_linear = gathered[:, :linear_cols]
        complete_router = gathered[:, linear_cols : linear_cols + expert_count]
        full_out_t = gathered[:, out_start:]
    attention_operands = (
        linear,
        low,
        q_second,
        k_second,
        v_second,
        gain_query,
        gain_key,
        tables,
        seg_column,
        seg_row,
        score_scale,
    )
    if not in_kernel:
        heads_narrow = attention_forward(*attention_operands)
        attention_low = flipped_right_operand(heads_narrow, attention_first).astype(BF16)
        out_part = flipped_right_operand(heads_narrow, full_out_t) + matrix_product(
            attention_low, attention_second
        )
        attention_total = sum_line(
            out_part.astype(BF16).reshape(tensor_count, tok_rows, model_width), 4, 1
        )
    if in_kernel:
        residual_stream, experts_narrow, gate_weights, sent_weights, router_low = router(
            attention_total,
            tokens,
            gain_moe[None, :],
            gathered,
            linear_cols,
            router_first,
            router_second,
            routes_t,
        )
    else:
        residual_stream = token_values + attention_total
        moe_normed, moe_factor = norm_forward(residual_stream, gain_moe)
        experts_narrow = moe_normed.astype(BF16)

        router_low = flipped_right_operand(experts_narrow, router_first).astype(BF16)
        router_logits = matrix_product(experts_narrow, complete_router) + matrix_product(
            router_low, router_second
        )
        expert_ids = jnp.arange(expert_count, dtype=jnp.int32)
        chosen = jnp.any(routes[:, :, None] == expert_ids[None, None, :], axis=1)
        chosen_logits = jnp.where(chosen, router_logits, -jnp.inf)
        chosen_exp = jnp.exp(chosen_logits - jnp.max(chosen_logits, axis=-1, keepdims=True))
        gate_weights = chosen_exp / jnp.sum(chosen_exp, axis=-1, keepdims=True)
        sent_weights = jnp.transpose(jnp.where(chosen, gate_weights, -1.0), (1, 0))
        own_weights = jnp.transpose(
            route_rows(sent_weights).reshape(fsdp_count, tensor_count, tok_rows), (1, 0, 2)
        )
        own_ranks = ranks_of(own_weights >= 0.0)

    broad = adapter_count * rank
    gate_in_t, upward_in_t = transposed(gate_in[0]), transposed(upward_in[0])
    expert_tables = (
        expert_gate_weight[0],
        expert_up_weight[0],
        expert_down_weight[0],
        jnp.concatenate(
            [gate_in_t.reshape(broad, model_width), upward_in_t.reshape(broad, model_width)],
            axis=0,
        ),
        gate_out[0].reshape(broad, -1),
        upward_out[0].reshape(broad, -1),
        transposed(downward_in[0]).reshape(broad, -1),
        downward_out[0].reshape(broad, model_width),
    )
    column_adapter = jnp.arange(broad, dtype=jnp.int32) // rank
    adapter_mask = jnp.repeat(
        (adapter_index[:, None] == column_adapter[None, :]).astype(BF16), slots, axis=0
    )
    ordered = [None] * tensor_count
    if in_kernel:
        moe_grad, gate_dots, expert_output, _landed, *sums = moe_layer(
            experts_narrow,
            up_rows,
            plane_ranks,
            sent_weights,
            adapter_mask,
            expert_tables,
            3,
        )
    else:
        expert_rows = dispatched(experts_narrow)
        expert_output, rows_grad, gate_dots = [], [], []
        sums = [jnp.zeros(each.shape, F32) for each in expert_sums(expert_tables)]
        for at, rows, upstream in zip(line_blocks, expert_rows, up_rows):
            y_rows, grad_rows, dots, *sums = experts(
                at, rows, upstream, own_ranks, own_weights, adapter_mask, expert_tables, sums
            )
            expert_output.append(y_rows)
            rows_grad.append(grad_rows)
            gate_dots.append(dots)
        for offset, dots in zip(offsets, gate_dots):
            ordered[offset] = dots
        gate_dots = jnp.roll(jnp.stack(ordered), tensor_pos, axis=0)
    pair_in_grad, gate_out_grad, upward_out_grad, downward_in_grad, downward_out_grad = sums
    if in_kernel:
        (
            output,
            residual_grad,
            low_share,
            linear_grad,
            owned,
            _landed,
        ) = back(
            score_scale,
            (linear_cols, out_start),
            slots,
            4,
            (linear, heads_narrow, sequence_normalized, gathered, expert_output),
            (
                moe_grad,
                gate_dots.reshape(expert_count, tok_rows),
                gate_weights,
                residual_stream,
                cotangent,
                gain_moe[None, :],
                router_first,
                router_second,
                router_low,
                experts_narrow,
                plane_ranks,
                low,
                attention_low,
                attention_first,
                attention_second,
                q_second,
                k_second,
                v_second,
                gain_query,
                gain_key,
                *tables,
                seg_column,
                seg_row,
            ),
        )
        owned = route_rows(owned)
        input_grad = last(
            linear_grad,
            low_share,
            input_first,
            residual_grad,
            tokens,
            gain_attn[None, :],
            gathered,
            5,
        )
    else:
        gate_grad = jnp.transpose(
            route_rows(jnp.transpose(gate_dots, (1, 0, 2)).reshape(device_count, tok_rows)), (1, 0)
        )

        def returned(slotted):
            total = 0.0
            for offset, at, rows in zip(offsets, line_blocks, slotted):
                combined = from_slots(at, plane_ranks, plane_rows(rows))
                total = total + delivered(combined, offset).astype(F32)
            return total

        moe_grad = returned(rows_grad)

        out_grad = cotangent.astype(F32)
        logit_gradient = (
            gate_weights * (gate_grad - jnp.sum(gate_weights * gate_grad, axis=-1, keepdims=True))
        ).astype(BF16)
        router_low_gradient = flipped_right_operand(logit_gradient, router_second).astype(BF16)
        moe_grad = (
            moe_grad
            + flipped_right_operand(logit_gradient, complete_router)
            + matrix_product(router_low_gradient, router_first)
        )
        router_first_gradient = flipped_left_operand(router_low_gradient, experts_narrow)
        router_second_gradient = flipped_left_operand(router_low, logit_gradient)
        residual_grad = out_grad + norm_backward(residual_stream, moe_factor, gain_moe, moe_grad)

        (sequence_branch,) = gather_line([residual_grad.astype(BF16)], (4,), 2)
        sequence_branch = sequence_branch.reshape(seq_rows, model_width)
        output = (residual_stream + returned(expert_output)).astype(BF16)
        attention_low_grad = flipped_right_operand(sequence_branch, attention_second).astype(BF16)
        attention_second_gradient = flipped_left_operand(attention_low, sequence_branch)
        heads_grad = matrix_product(sequence_branch, full_out_t)
        (
            q_grad,
            k_grad,
            v_grad,
            low_share,
            q_second_gradient,
            k_second_gradient,
            v_second_gradient,
            attention_first_gradient,
        ) = attention_backward(
            *attention_operands,
            heads_narrow,
            heads_grad,
            attention_low_grad,
            attention_first,
        )
        linear_grad = jnp.concatenate([q_grad, k_grad, v_grad], axis=1)
        normed_part = flipped_right_operand(linear_grad, complete_linear) + matrix_product(
            low_share, input_first
        )
        input_first_gradient = flipped_left_operand(low_share, sequence_normalized)
        normalized_gradient = sum_line(
            normed_part.astype(BF16).reshape(tensor_count, tok_rows, model_width), 4, 1
        )
        input_grad = residual_grad + norm_backward(
            token_values, attn_factor, gain_attn, normalized_gradient
        )
        row_grads = jnp.concatenate(
            [input_first_gradient, attention_second_gradient, router_first_gradient], axis=0
        )
        head_grads = jnp.concatenate([q_second_gradient, attention_first_gradient], axis=0)
        narrow_grads = jnp.concatenate([k_second_gradient, v_second_gradient], axis=0)

    def lines_of(piece, lines):
        return piece.reshape(adapter_count, lines, -1)

    if in_kernel:
        (
            query_in_sum,
            key_in_sum,
            value_in_sum,
            attn_out_sum,
            router_in_sum,
            router_out_sum,
            query_out_sum,
            attn_in_sum,
            key_out_sum,
            value_out_sum,
        ) = owners(
            adapter_index,
            owned,
            adapter_count,
            rank,
            model_width // device_count,
            local_kv_cols // fsdp_count,
        )
    else:
        source_adapter = jnp.repeat(adapter_index, tensor_count)
        owner_onehot = (
            jnp.arange(adapter_count, dtype=jnp.int32)[:, None] == source_adapter[None, :]
        ).astype(BF16)

        def to_all(addend):
            lines = addend.shape[0]
            return jnp.transpose(
                addend.astype(BF16).reshape(lines, device_count, -1), (1, 0, 2)
            ).reshape(device_count, -1)

        def to_head_owners(addend):
            lines = addend.shape[0]
            pieces = jnp.transpose(
                addend.astype(BF16).reshape(lines, fsdp_count, -1), (1, 0, 2)
            ).reshape(fsdp_count, -1)
            holder = jnp.zeros((device_count, pieces.shape[1]), BF16)
            return lax.dynamic_update_slice(holder, pieces, (tensor_pos * fsdp_count, zero_pos))

        def owner_sums(parts):
            widths = [part.shape[1] for part in parts]
            total = matrix_product(owner_onehot, route_rows(jnp.concatenate(parts, axis=1)))
            pieces = []
            start = 0
            for width in widths:
                pieces.append(total[:, start : start + width])
                start += width
            return pieces

        row_sums, head_sums, narrow_sums, router_sums = owner_sums(
            [
                to_all(row_grads),
                to_head_owners(head_grads),
                to_head_owners(narrow_grads),
                to_all(router_second_gradient),
            ]
        )
        row_sums = lines_of(row_sums, 5 * rank)
        head_sums = lines_of(head_sums, 2 * rank)
        narrow_sums = lines_of(narrow_sums, 2 * rank)
        query_in_sum, key_in_sum, value_in_sum, attn_out_sum, router_in_sum = [
            row_sums[:, at * rank : (at + 1) * rank] for at in range(5)
        ]
        query_out_sum, attn_in_sum = head_sums[:, :rank], head_sums[:, rank:]
        key_out_sum, value_out_sum = narrow_sums[:, :rank], narrow_sums[:, rank:]
        router_out_sum = lines_of(router_sums, rank)
    return (
        output,
        input_grad,
        transposed(query_in_sum),
        query_out_sum,
        transposed(key_in_sum),
        key_out_sum,
        transposed(value_in_sum),
        value_out_sum,
        transposed(attn_in_sum),
        attn_out_sum,
        transposed(router_in_sum),
        router_out_sum,
        transposed(lines_of(pair_in_grad[:broad], rank))[None],
        lines_of(gate_out_grad, rank)[None],
        transposed(lines_of(pair_in_grad[broad:], rank))[None],
        lines_of(upward_out_grad, rank)[None],
        transposed(lines_of(downward_in_grad, rank))[None],
        lines_of(downward_out_grad, rank)[None],
    )


def solution(mesh):
    placed = (
        P(("fsdp", "tensor"), None),
        P("fsdp", None),
        P(("fsdp", "tensor"), None),
        P(),
        P(("fsdp", "tensor"), None),
        P(),
        P(),
        P(),
        P(),
        P("fsdp", "tensor"),
        P("fsdp", "tensor"),
        P("fsdp", "tensor"),
        P("tensor", "fsdp"),
        P("fsdp", None),
        P(("fsdp", "tensor"), None, None),
        P(("fsdp", "tensor"), None, None),
        P(("fsdp", "tensor"), None, None),
        P(),
        P(None, None, "tensor"),
        P(),
        P(None, None, "tensor"),
        P(),
        P(None, None, "tensor"),
        P(None, "tensor", None),
        P(),
        P(),
        P(),
        P(("fsdp", "tensor"), None, None, None),
        P(("fsdp", "tensor"), None, None, None),
        P(("fsdp", "tensor"), None, None, None),
        P(("fsdp", "tensor"), None, None, None),
        P(("fsdp", "tensor"), None, None, None),
        P(("fsdp", "tensor"), None, None, None),
    )
    return jax.shard_map(
        per_device,
        mesh=mesh,
        in_specs=placed,
        out_specs=(
            P(("fsdp", "tensor"), None),
            P(("fsdp", "tensor"), None),
            P(None, ("fsdp", "tensor"), None),
            P(None, None, ("fsdp", "tensor")),
            P(None, ("fsdp", "tensor"), None),
            P(None, None, ("fsdp", "tensor")),
            P(None, ("fsdp", "tensor"), None),
            P(None, None, ("fsdp", "tensor")),
            P(None, ("fsdp", "tensor"), None),
            P(None, None, ("fsdp", "tensor")),
            P(None, ("fsdp", "tensor"), None),
            P(None, None, ("fsdp", "tensor")),
            P(("fsdp", "tensor"), None, None, None),
            P(("fsdp", "tensor"), None, None, None),
            P(("fsdp", "tensor"), None, None, None),
            P(("fsdp", "tensor"), None, None, None),
            P(("fsdp", "tensor"), None, None, None),
            P(("fsdp", "tensor"), None, None, None),
        ),
        check_vma=False,
    )
```
